32 devices in a mesh: dp: 16 (over z, y, core), branch: 2 (over x).
Axes of the slice: x: 2, y: 2, z: 4, core: 2. Of those that a mesh axis runs over, the one named last changes fastest.
Arguments:
- tokens: bfloat16 [16384, 1024], P(('dp', 'branch')), may hold values from -6 to 6
- lengths: int32 [16], P('dp'), may hold values from 30 to 1024, as said below
- norm_gain: bfloat16 [1024], replicated, may hold values from 0.5 to 1.5
- norm_shift: bfloat16 [1024], replicated, may hold values from -3 to 3
- qkv_weight: bfloat16 [1024, 3072], replicated, may hold values from -0.1875 to 0.1875
- proj_weight: bfloat16 [1024, 1024], replicated, may hold values from -2 to 2
- up_weight: bfloat16 [1024, 4096], replicated, may hold values from -0.1875 to 0.1875
- inner_bias: bfloat16 [4096], replicated, may hold values from -3 to 3
- down_weight: bfloat16 [4096, 1024], replicated, may hold values from -0.09375 to 0.09375
- outer_bias: bfloat16 [1024], replicated, may hold values from -3 to 3
- cotangent: bfloat16 [16384, 1024], P(('dp', 'branch')), may hold values from -6 to 6
Outputs:
- layer_out: bfloat16 [16384, 1024], P(('dp', 'branch'))
- tokens_grad: float32 [16384, 1024], P(('dp', 'branch'))
- gain_grad: float32 [1024], P(('dp', 'branch'))
- shift_grad: float32 [1024], P(('dp', 'branch'))
- qkv_grad: float32 [1024, 3072], P(('dp', 'branch'))
- proj_grad: float32 [1024, 1024], P(('dp', 'branch'))
- up_grad: float32 [1024, 4096], P(('dp', 'branch'))
- inner_grad: float32 [4096], P(('dp', 'branch'))
- down_grad: float32 [4096, 1024], P(('dp', 'branch'))
- outer_grad: float32 [1024], P(('dp', 'branch'))
The draws below stay inside these ranges and needn't reach their ends.
Inputs may be any that keep to these rules, and one draw needn't show every extreme that they name: `lengths`: length of each sequence; some sequence has length 1024 in every draw.
All inputs are finite; a program needn't handle non-finite values.
Results may differ from the reference program's by a relative error of at most 0.0095.
Values may be sent and summed in bfloat16 or wider, within the bound.
No kernel may reach another device: no remote copies, remote signals or barrier semaphores. Data moves between devices by JAX's collectives and lax.ppermute only.
A program may use at most 320 MiB of HBM per device.

```python
import jax
import jax.numpy as jnp
from jax import lax

D = 1024
HEADS = 16
HEAD_DIM = 64
ROT_DIM = 32
FF = 4096
SEQ_LEN = 1024
SEQ_GRP = 1
TOK_GRP = 1024
SEQS = 16
ROWS = 16384
N_DP = 16


def draw_lengths(key, part):
    first_key, second_key, third_key = jax.random.split(key, 3)
    span_width = SEQ_LEN - 30
    first_draw = jax.random.randint(first_key, (SEQS,), 0, span_width, dtype=jnp.int32)
    second_draw = jax.random.randint(second_key, (SEQS,), 0, span_width, dtype=jnp.int32)
    result = 30 + jnp.maximum(first_draw, second_draw)
    longest = jax.random.randint(third_key, (), 0, SEQS, dtype=jnp.int32)
    result = jnp.where(jnp.arange(SEQS, dtype=jnp.int32) == longest, jnp.int32(SEQ_LEN), result)
    return result.astype(jnp.int32)


def raised(entries, key, source, target, parts, factor):
    def block_of(dim):
        return (jnp.arange(entries.shape[dim]) // (entries.shape[dim] // parts)).reshape((-1,) + (1,) * (entries.ndim - 1 - dim))

    near = jax.random.permutation(key, parts)[block_of(target)]
    other_side = (block_of(target) + parts // 2) % parts
    return jnp.where((block_of(source) == near) | (block_of(source) == other_side), factor * entries, entries)


def block_levels(stream_key, shape, cuts, least, top_value):
    level, own = 1.0, jax.random.fold_in(stream_key, 6)
    for axis_at, blocks in cuts:
        steps = jnp.exp(jax.random.uniform(jax.random.fold_in(own, axis_at), (blocks,), jnp.float32, least / len(cuts), top_value / len(cuts)))
        level = level * jnp.repeat(steps, shape[axis_at] // blocks).reshape([-1 if axis == axis_at else 1 for axis in range(len(shape))])
    return level


def bell_draw(key, dims, deviation, bound, cuts=(), kind=jnp.bfloat16):
    values = deviation * jax.random.normal(key, dims, jnp.float32)
    if cuts:
        values = values * block_levels(key, dims, cuts, -0.22, 0.18)
    return jnp.clip(values, -bound, bound).astype(kind)


def gaussian_with(key, extent, scale, bound, cuts, heavy, held_as=jnp.bfloat16):
    array = scale * jax.random.normal(key, extent, jnp.float32)
    if cuts:
        array = array * block_levels(key, extent, cuts, -0.22, 0.18)
    return jnp.clip(raised(array, jax.random.fold_in(key, 3), *heavy), -bound, bound).astype(held_as)


def setup_inputs(seed: int = 0) -> dict:
    seeds = jax.random.split(jax.random.key(seed), 12)
    tokens = gaussian_with(seeds[0], (ROWS, D), 1.0, 6.0, ((0, 32),), (0, 1, 32, 2.75))
    lengths = draw_lengths(jax.random.fold_in(seeds[11], 71), 0)
    norm_gain = jnp.clip(1.0 + 0.1 * jax.random.normal(seeds[2], (D,), jnp.float32), 0.5, 1.5).astype(jnp.bfloat16)
    norm_shift = bell_draw(seeds[3], (D,), 0.5, 3.0)
    qkv_weight = bell_draw(seeds[4], (D, 3 * D), D ** -0.5, 0.1875)
    proj_weight = bell_draw(seeds[5], (D, D), (D // 128) ** -0.5, 2.0)
    up_weight = bell_draw(seeds[6], (D, FF), D ** -0.5, 0.1875)
    inner_bias = bell_draw(seeds[7], (FF,), 0.5, 3.0)
    down_weight = bell_draw(seeds[8], (FF, D), FF ** -0.5, 0.09375)
    outer_bias = bell_draw(seeds[9], (D,), 0.5, 3.0)
    cotangent = bell_draw(seeds[10], (ROWS, D), 1.0, 6.0, ((0, 32),))
    return {"tokens": tokens, "lengths": lengths, "norm_gain": norm_gain, "norm_shift": norm_shift, "qkv_weight": qkv_weight, "proj_weight": proj_weight, "up_weight": up_weight, "inner_bias": inner_bias, "down_weight": down_weight, "outer_bias": outer_bias, "cotangent": cotangent}


epsilon = 1e-05
negative = -1e+30
precise = lax.Precision.HIGHEST

@jax.custom_vjp
def low(v):
    return lax.optimization_barrier(v.astype(jnp.bfloat16)).astype(jnp.float32)

@jax.custom_vjp
def low_back(v):
    return v

def low_keep(v):
    return (low(v), None)

def low_pass(kept, grad):
    return (grad,)

def back_keep(v):
    return (v, None)

def back_low(kept, grad):
    return (low(grad),)
low.defvjp(low_keep, low_pass)
low_back.defvjp(back_keep, back_low)

def layer_norm(values, gain_value, shift_value):
    centred = values - lax.optimization_barrier(jnp.mean(values, axis=-1, keepdims=True))
    spread = lax.optimization_barrier(jnp.mean(centred * centred, axis=-1, keepdims=True))
    return centred * lax.rsqrt(spread + epsilon) * gain_value + shift_value

def rotary_tables(count):
    positions = (jnp.arange(count, dtype=jnp.int32) % SEQ_LEN).astype(jnp.float32)
    channel = jnp.arange(HEAD_DIM, dtype=jnp.int32)
    frequency = jnp.power(10000.0, -(2.0 * (channel // 2).astype(jnp.float32)) / ROT_DIM)
    angles = positions[:, None] * frequency[None, :]
    inside = (channel < ROT_DIM)[None, :]
    cosine_table = jnp.where(inside, jnp.cos(angles), jnp.float32(1.0))
    sine_table = jnp.where(inside, jnp.sin(angles), jnp.float32(0.0))
    return (cosine_table[:, None, :], sine_table[:, None, :])

def pair_swap(values):
    pairs = values.reshape(values.shape[:-1] + (HEAD_DIM // 2, 2))
    return jnp.stack([-pairs[..., 1], pairs[..., 0]], axis=-1).reshape(values.shape)

def split_heads(section):
    return section.reshape(TOK_GRP, HEADS, HEAD_DIM)

def group_forward(params, token_rows, group_lengths):
    gain_value, shift_value, qkv_weight, proj_weight, up_weight, inner_bias, down_weight, outer_bias = params
    normed = low(layer_norm(token_rows, gain_value, shift_value))
    mixed_proj = low_back(jnp.dot(normed, qkv_weight, precision=precise))
    cosine_table, sine_table = rotary_tables(TOK_GRP)
    raw_queries = split_heads(mixed_proj[:, :D])
    raw_keys = split_heads(mixed_proj[:, D:2 * D])
    queries = low(raw_queries * cosine_table + pair_swap(raw_queries) * sine_table)
    keys_rot = low(raw_keys * cosine_table + pair_swap(raw_keys) * sine_table)
    values = low(split_heads(mixed_proj[:, 2 * D:]))
    seq_shape = (SEQ_GRP, SEQ_LEN, HEADS, HEAD_DIM)
    scores = jnp.einsum('sqhd,skhd->shqk', queries.reshape(seq_shape), keys_rot.reshape(seq_shape), precision=precise) * HEAD_DIM ** (-0.5)
    position = jnp.arange(SEQ_LEN, dtype=jnp.int32)
    causal = (position[None, :] <= position[:, None])[None, :, :]
    allowed = causal & (position[None, None, :] < group_lengths[:, None, None])
    scores = low_back(jnp.where(allowed[:, None, :, :], scores, negative))
    weights = low(jax.nn.softmax(scores, axis=-1))
    context = jnp.einsum('shqk,skhd->sqhd', weights, values.reshape(seq_shape), precision=precise)
    context = low_back(low(context.reshape(TOK_GRP, D)))
    attended = low_back(low(jnp.dot(context, proj_weight, precision=precise)))
    before = low_back(jnp.dot(normed, up_weight, precision=precise) + inner_bias)
    hidden = low(jax.nn.gelu(before, approximate=True))
    expanded = low_back(low(jnp.dot(hidden, down_weight, precision=precise) + outer_bias))
    return token_rows + attended + expanded

def reference(tokens, lengths, norm_gain, norm_shift, qkv_weight, proj_weight, up_weight, inner_bias, down_weight, outer_bias, cotangent):
    params = tuple((member.astype(jnp.float32) for member in (norm_gain, norm_shift, qkv_weight, proj_weight, up_weight, inner_bias, down_weight, outer_bias)))
    token_rows = tokens.astype(jnp.float32).reshape(N_DP, TOK_GRP, D)
    group_lengths = lengths.astype(jnp.int32).reshape(N_DP, SEQ_GRP)
    position = jnp.arange(TOK_GRP, dtype=jnp.int32) % SEQ_LEN
    live_mask = position[None, :] < jnp.repeat(group_lengths, SEQ_LEN, axis=1)
    cotangents = jnp.where(live_mask[:, :, None], cotangent.astype(jnp.float32).reshape(N_DP, TOK_GRP, D), jnp.float32(0.0))

    def forward(param_set, all_rows):

        def scan_step(state_carry, inputs):
            return (state_carry, jax.checkpoint(group_forward)(param_set, inputs[0], inputs[1]))
        final_state, outputs = lax.scan(scan_step, jnp.zeros((), jnp.float32), (all_rows, group_lengths))
        return outputs
    outputs, pullback = jax.vjp(forward, params, token_rows)
    param_grads, row_grads = pullback(cotangents)
    return (outputs.reshape(ROWS, D).astype(jnp.bfloat16), row_grads.reshape(ROWS, D), param_grads[0], param_grads[1], param_grads[2], param_grads[3], param_grads[4], param_grads[5], param_grads[6], param_grads[7])
```

```python
import functools
import math

import jax
import jax.numpy as jnp
from jax import lax
from jax.experimental import pallas as pl
from jax.experimental.pallas import tpu as pltpu
from jax.sharding import PartitionSpec as P

D = 1024
HEADS = 16
HEAD_DIM = 64
ROT_DIM = 32
FF = 4096
SEQ_LEN = 1024
HALF = HEADS // 2 * HEAD_DIM
FF_HALF = FF // 2
LANES = 128
QB = 256
FB = 512
EPS = 1e-05
BF = jnp.bfloat16
F32 = jnp.float32


def params(mb=56):
    return pltpu.CompilerParams(vmem_limit_bytes=mb << 20)


def cost(flops, nbytes, trans=0):
    return pl.CostEstimate(flops=int(flops), bytes_accessed=int(nbytes), transcendentals=int(trans))


def dot_nn(a, b):
    return jnp.dot(a, b, preferred_element_type=F32)


def dot_nt(a, b):
    return lax.dot_general(a, b, (((1,), (1,)), ((), ())), preferred_element_type=F32)


def dot_tn(a, b):
    return lax.dot_general(a, b, (((0,), (0,)), ((), ())), preferred_element_type=F32)


def rotary_tables():
    position = jnp.arange(SEQ_LEN, dtype=jnp.int32).astype(F32)
    lane = jnp.arange(LANES, dtype=jnp.int32)
    channel = lane % HEAD_DIM
    frequency = jnp.power(10000.0, -(2.0 * (channel // 2).astype(F32)) / ROT_DIM)
    angles = position[:, None] * frequency[None, :]
    inside = (channel < ROT_DIM)[None, :]
    cosine = jnp.where(inside, jnp.cos(angles), 1.0)
    sine = jnp.where(inside, jnp.sin(angles), 0.0)
    even = (lane % 2 == 0)[None, :]
    return cosine, jnp.where(even, -sine, sine)


def rotate(x, cosine, sine):
    even = lax.broadcasted_iota(jnp.int32, x.shape, 1) % 2 == 0
    swapped = jnp.where(even, pltpu.roll(x, LANES - 1, 1), pltpu.roll(x, 1, 1))
    return x * cosine + swapped * sine


def unrotate(y, cosine, sine):
    even = lax.broadcasted_iota(jnp.int32, y.shape, 1) % 2 == 0
    swapped = jnp.where(even, pltpu.roll(y, LANES - 1, 1), pltpu.roll(y, 1, 1))
    return y * cosine - swapped * sine


def qkv_kernel(j_ref, x_ref, w_ref, cos_ref, sin_ref, o_ref):
    t = pl.program_id(0)
    mixed = dot_nn(x_ref[...], w_ref[...])

    @pl.when(t == 2)
    def _():
        o_ref[0] = mixed.astype(BF)

    @pl.when(t < 2)
    def _():
        scale = jnp.where(t == 0, HEAD_DIM**-0.5, 1.0)
        for c in range(0, HALF, LANES):
            turned = rotate(mixed[:, c : c + LANES], cos_ref[...], sin_ref[...])
            o_ref[0, :, c : c + LANES] = (turned * scale).astype(BF)


def qkv_call(branch, x, w, cosine, sine):
    rows = x.shape[0]
    return pl.pallas_call(
        qkv_kernel,
        grid_spec=pltpu.PrefetchScalarGridSpec(
            num_scalar_prefetch=1,
            grid=(3,),
            in_specs=[
                pl.BlockSpec((rows, D), lambda t, j: (0, 0)),
                pl.BlockSpec((D, HALF), lambda t, j: (0, 2 * t + j[0])),
                pl.BlockSpec((rows, LANES), lambda t, j: (0, 0)),
                pl.BlockSpec((rows, LANES), lambda t, j: (0, 0)),
            ],
            out_specs=pl.BlockSpec((1, rows, HALF), lambda t, j: (t, 0, 0)),
        ),
        out_shape=jax.ShapeDtypeStruct((3, rows, HALF), BF),
        compiler_params=params(),
        cost_estimate=cost(2 * rows * D * 3 * HALF, 2 * (rows * D + D * 3 * HALF + rows * 3 * HALF)),
        name="qkv",
    )(branch, x, w, cosine, sine)


def head_lanes(shape, head):
    lane = lax.broadcasted_iota(jnp.int32, shape, 1)
    own = (lane >= HEAD_DIM) if head else (lane < HEAD_DIM)
    spare = lane - (0 if head else HEAD_DIM)
    return own, spare


def keys_with_bias(k, head, length):
    own, spare = head_lanes(k.shape, head)
    row = lax.broadcasted_iota(jnp.int32, k.shape, 0)
    bias = jnp.where(row < length, 0.0, -1e30)
    extra = jnp.where(spare < 3, 1.0, jnp.where(spare == 3, bias, 0.0))
    return jnp.where(own, k.astype(F32), extra).astype(BF)


def attend_kernel(len_ref, q_ref, k_ref, v_ref, o_ref, qe_ref):
    length = len_ref[0]
    q = q_ref[0].astype(F32)
    k = k_ref[0]
    v = v_ref[0]
    tri = lax.broadcasted_iota(jnp.int32, (QB, QB), 0) >= lax.broadcasted_iota(jnp.int32, (QB, QB), 1)
    outs = []
    for head in range(2):
        own, spare = head_lanes((SEQ_LEN, LANES), head)
        ke = keys_with_bias(k, head, length)
        qe = jnp.where(own, q, jnp.where(spare == 3, 1.0, 0.0)).astype(BF)
        parts = []
        for b in range(SEQ_LEN // QB):
            lo, hi = b * QB, (b + 1) * QB
            s = dot_nt(qe[lo:hi], ke[:hi])
            diag = jnp.where(tri, s[:, lo:hi], -1e30)
            s = diag if b == 0 else jnp.concatenate([s[:, :lo], diag], axis=1)
            top = jnp.max(s, axis=1, keepdims=True)
            p = jnp.exp(s - top)
            total = jnp.sum(p, axis=1, keepdims=True)
            parts.append(dot_nn(p.astype(BF), v[:hi]) * (1.0 / total))
            lse = jnp.broadcast_to(top + jnp.log(total), (QB, LANES))
            first = lse.astype(BF).astype(F32)
            second = (lse - first).astype(BF).astype(F32)
            third = lse - first - second
            own_b, spare_b = head_lanes((QB, LANES), head)
            extra = jnp.where(
                spare_b == 0,
                -first,
                jnp.where(
                    spare_b == 1,
                    -second,
                    jnp.where(spare_b == 2, -third, jnp.where(spare_b == 3, 1.0, 0.0)),
                ),
            )
            qe_ref[head, lo:hi, :] = jnp.where(own_b, q[lo:hi], extra).astype(BF)
        outs.append(jnp.concatenate(parts, axis=0))
    own, _ = head_lanes((SEQ_LEN, LANES), 0)
    o_ref[...] = jnp.where(own, outs[0], outs[1]).astype(BF)


def attend_call(length, qkv):
    pairs = HALF // LANES
    spec = [pl.BlockSpec((1, SEQ_LEN, LANES), lambda p, n, t=t: (t, 0, p)) for t in range(3)]
    return pl.pallas_call(
        attend_kernel,
        grid_spec=pltpu.PrefetchScalarGridSpec(
            num_scalar_prefetch=1,
            grid=(pairs,),
            in_specs=spec,
            out_specs=[
                pl.BlockSpec((SEQ_LEN, LANES), lambda p, n: (0, p)),
                pl.BlockSpec((2, SEQ_LEN, LANES), lambda p, n: (p, 0, 0)),
            ],
        ),
        out_shape=[
            jax.ShapeDtypeStruct((SEQ_LEN, HALF), BF),
            jax.ShapeDtypeStruct((2 * pairs, SEQ_LEN, LANES), BF),
        ],
        compiler_params=params(),
        cost_estimate=cost(
            2 * pairs * 4 * SEQ_LEN * SEQ_LEN * LANES, 2 * SEQ_LEN * HALF * 6, 8 * SEQ_LEN * SEQ_LEN
        ),
        name="attend",
    )(length, qkv, qkv, qkv)


def attend_back_kernel(len_ref, qe_ref, k_ref, v_ref, o_ref, g_ref, cos_ref, sin_ref, d_ref, dk_ref, dv_ref):
    length = len_ref[0]
    k = k_ref[0]
    v = v_ref[0]
    g = g_ref[...].astype(F32)
    o = o_ref[...].astype(F32)
    tri = lax.broadcasted_iota(jnp.int32, (QB, QB), 0) >= lax.broadcasted_iota(jnp.int32, (QB, QB), 1)
    queries = []
    for head in range(2):
        own, spare = head_lanes((SEQ_LEN, LANES), head)
        ke = keys_with_bias(k, head, length)
        ve = jnp.where(own, v.astype(F32), jnp.where(spare < 3, 1.0, 0.0)).astype(BF)
        inner = jnp.sum(jnp.where(own, g * o, 0.0), axis=1, keepdims=True)
        inner = jnp.broadcast_to(inner, (SEQ_LEN, LANES))
        first = inner.astype(BF).astype(F32)
        second = (inner - first).astype(BF).astype(F32)
        third = inner - first - second
        extra = jnp.where(
            spare == 0,
            -first,
            jnp.where(spare == 1, -second, jnp.where(spare == 2, -third, 0.0)),
        )
        ge = jnp.where(own, g, extra).astype(BF)
        parts = []
        for b in range(SEQ_LEN // QB):
            lo, hi = b * QB, (b + 1) * QB
            qb = qe_ref[head, lo:hi, :]
            gb = ge[lo:hi]
            s = dot_nt(qb, ke[:hi])
            diag = jnp.where(tri, s[:, lo:hi], -1e30)
            s = diag if b == 0 else jnp.concatenate([s[:, :lo], diag], axis=1)
            p = jnp.exp(s)
            ds = (p * dot_nt(gb, ve[:hi])).astype(BF)
            parts.append(dot_nn(ds, k[:hi]))
            dk = dot_tn(ds, qb)
            dv = dot_tn(p.astype(BF), gb)
            if b > 0:
                dk_ref[head, :lo] += dk[:lo]
                dv_ref[head, :lo] += dv[:lo]
            dk_ref[head, lo:hi] = dk[lo:hi]
            dv_ref[head, lo:hi] = dv[lo:hi]
        queries.append(jnp.concatenate(parts, axis=0))
    own, _ = head_lanes((SEQ_LEN, LANES), 0)
    cosine, sine = cos_ref[...], sin_ref[...]
    dq = jnp.where(own, queries[0], queries[1]) * HEAD_DIM**-0.5
    d_ref[0] = unrotate(dq, cosine, sine).astype(BF)
    d_ref[1] = unrotate(jnp.where(own, dk_ref[0], dk_ref[1]), cosine, sine).astype(BF)
    d_ref[2] = jnp.where(own, dv_ref[0], dv_ref[1]).astype(BF)


def attend_back_call(length, qe, qkv, context, grad_context, cosine, sine):
    pairs = HALF // LANES
    return pl.pallas_call(
        attend_back_kernel,
        grid_spec=pltpu.PrefetchScalarGridSpec(
            num_scalar_prefetch=1,
            grid=(pairs,),
            in_specs=[
                pl.BlockSpec((2, SEQ_LEN, LANES), lambda p, n: (p, 0, 0)),
                pl.BlockSpec((1, SEQ_LEN, LANES), lambda p, n: (1, 0, p)),
                pl.BlockSpec((1, SEQ_LEN, LANES), lambda p, n: (2, 0, p)),
                pl.BlockSpec((SEQ_LEN, LANES), lambda p, n: (0, p)),
                pl.BlockSpec((SEQ_LEN, LANES), lambda p, n: (0, p)),
                pl.BlockSpec((SEQ_LEN, LANES), lambda p, n: (0, 0)),
                pl.BlockSpec((SEQ_LEN, LANES), lambda p, n: (0, 0)),
            ],
            out_specs=pl.BlockSpec((3, SEQ_LEN, LANES), lambda p, n: (0, 0, p)),
            scratch_shapes=[
                pltpu.VMEM((2, SEQ_LEN, LANES), F32),
                pltpu.VMEM((2, SEQ_LEN, LANES), F32),
            ],
        ),
        out_shape=jax.ShapeDtypeStruct((3, SEQ_LEN, HALF), BF),
        compiler_params=params(),
        cost_estimate=cost(
            2 * pairs * 10 * SEQ_LEN * SEQ_LEN * LANES, 2 * SEQ_LEN * HALF * 9, 8 * SEQ_LEN * SEQ_LEN
        ),
        name="attend_back",
    )(length, qe, qkv, qkv, context, grad_context, cosine, sine)


def gelu_parts(v):
    c = math.sqrt(2.0 / math.pi)
    square = v * v
    t = jnp.tanh(v * (c + (c * 0.044715) * square))
    half = 0.5 * (1.0 + t)
    slope = half + (0.5 * v) * (1.0 - t * t) * (c + (3.0 * c * 0.044715) * square)
    return v * half, slope


def mlp_kernel(splits, j_ref, x_ref, g_ref, *refs):
    ups, downs, biases = refs[:splits], refs[splits : 2 * splits], refs[2 * splits : 3 * splits]
    h_ref, gb_ref, e_ref, gn_ref = refs[3 * splits :]
    up = jnp.concatenate([r[...] for r in ups], axis=1) if splits > 1 else ups[0][...]
    down = jnp.concatenate([r[...] for r in downs], axis=0) if splits > 1 else downs[0][...]
    bias = jnp.concatenate([r[...] for r in biases], axis=1) if splits > 1 else biases[0][...]
    before = dot_nn(x_ref[...], up) + bias.astype(F32)
    hidden, slope = gelu_parts(before)
    hidden = hidden.astype(BF)
    grad_before = (dot_nt(g_ref[...], down) * slope).astype(BF)
    h_ref[...] = hidden
    gb_ref[...] = grad_before
    expanded = dot_nn(hidden, down)
    grad_normed = dot_nt(grad_before, up)

    @pl.when(pl.program_id(0) == 0)
    def _():
        e_ref[...] = expanded
        gn_ref[...] = grad_normed

    @pl.when(pl.program_id(0) > 0)
    def _():
        e_ref[...] += expanded
        gn_ref[...] += grad_normed


def mlp_call(branch, x, g, weights, splits):
    rows = x.shape[0]
    up, down, bias = weights
    wide = FB // splits
    pick = (lambda s, j, i: 2 * (splits * s + i) + j[0]) if splits > 1 else (lambda s, j, i: s)
    in_specs = [pl.BlockSpec((rows, D), lambda s, j: (0, 0))] * 2
    in_specs += [pl.BlockSpec((D, wide), lambda s, j, i=i: (0, pick(s, j, i))) for i in range(splits)]
    in_specs += [pl.BlockSpec((wide, D), lambda s, j, i=i: (pick(s, j, i), 0)) for i in range(splits)]
    in_specs += [pl.BlockSpec((1, wide), lambda s, j, i=i: (0, pick(s, j, i))) for i in range(splits)]
    return pl.pallas_call(
        functools.partial(mlp_kernel, splits),
        grid_spec=pltpu.PrefetchScalarGridSpec(
            num_scalar_prefetch=1,
            grid=(FF_HALF // FB,),
            in_specs=in_specs,
            out_specs=[pl.BlockSpec((rows, FB), lambda s, j: (0, s))] * 2
            + [pl.BlockSpec((rows, D), lambda s, j: (0, 0))] * 2,
        ),
        out_shape=[jax.ShapeDtypeStruct((rows, FF_HALF), BF)] * 2 + [jax.ShapeDtypeStruct((rows, D), F32)] * 2,
        compiler_params=params(),
        cost_estimate=cost(8 * rows * D * FF_HALF, 12 * rows * D + 4 * D * FF_HALF, rows * FF_HALF),
        name="mlp",
    )(branch, x, g, *([up] * splits), *([down] * splits), *([bias] * splits))


def weight_grad_kernel(slot_ref, a_ref, b_ref, keep_ref, send_ref):
    pieces, rows = 2 * keep_ref.shape[0], keep_ref.shape[1]
    b = b_ref[...].reshape(b_ref.shape[-2:])
    total = dot_tn(a_ref[...], b).astype(BF)
    for p in range(pieces):
        slot = slot_ref[p]
        piece = total[p * rows : (p + 1) * rows]

        @pl.when(slot < pieces // 2)
        def _(slot=slot, piece=piece):
            keep_ref[slot] = piece

        @pl.when(slot >= pieces // 2)
        def _(slot=slot, piece=piece):
            send_ref[slot - pieces // 2] = piece


def weight_grad(slots, order, a, b, tile):
    pieces = order.shape[0]
    m = a.shape[1]
    n = b.shape[-1] * (b.shape[0] if b.ndim == 3 else 1)
    k = a.shape[0]
    rows = m // pieces
    if rows % 16:
        if b.ndim == 3:
            b = jnp.concatenate([b[t] for t in range(b.shape[0])], axis=1)
        total = jnp.einsum("nd,nf->df", a, b, preferred_element_type=F32).astype(BF)
        total = jnp.take(total.reshape(pieces, rows, n), order, axis=0)
        return total[: pieces // 2], total[pieces // 2 :]
    if b.ndim == 3:
        b_spec = pl.BlockSpec((1, k, tile), lambda s, t: (s, 0, 0))
    else:
        b_spec = pl.BlockSpec((k, tile), lambda s, t: (0, s))
    return pl.pallas_call(
        weight_grad_kernel,
        grid_spec=pltpu.PrefetchScalarGridSpec(
            num_scalar_prefetch=1,
            grid=(n // tile,),
            in_specs=[pl.BlockSpec((k, m), lambda s, t: (0, 0)), b_spec],
            out_specs=[pl.BlockSpec((pieces // 2, rows, tile), lambda s, t: (0, 0, s))] * 2,
        ),
        out_shape=[jax.ShapeDtypeStruct((pieces // 2, rows, n), BF)] * 2,
        compiler_params=params(),
        cost_estimate=cost(2 * k * m * n, 2 * (k * m + k * n + m * n)),
        name="weight_grad",
    )(slots, a, b)


def grad_normed_kernel(j_ref, d_ref, wq_ref, wk_ref, wv_ref, base_ref, o_ref):
    total = base_ref[...]
    for t, w in enumerate((wq_ref, wk_ref, wv_ref)):
        total += dot_nt(d_ref[t], w[...])
    o_ref[...] = total


def grad_normed_call(branch, dmix, w, base):
    rows = base.shape[0]
    block = 256
    return pl.pallas_call(
        grad_normed_kernel,
        grid_spec=pltpu.PrefetchScalarGridSpec(
            num_scalar_prefetch=1,
            grid=(rows // block,),
            in_specs=[pl.BlockSpec((3, block, HALF), lambda r, j: (0, r, 0))]
            + [pl.BlockSpec((D, HALF), lambda r, j, t=t: (0, 2 * t + j[0])) for t in range(3)]
            + [pl.BlockSpec((block, D), lambda r, j: (r, 0))],
            out_specs=pl.BlockSpec((block, D), lambda r, j: (r, 0)),
        ),
        out_shape=jax.ShapeDtypeStruct((rows, D), F32),
        compiler_params=params(),
        cost_estimate=cost(2 * rows * D * 3 * HALF, 8 * rows * D + 6 * D * HALF + 6 * rows * HALF),
        name="grad_normed",
    )(branch, dmix, w, w, w, base)


def reduce_pieces(keep, send, n_dp):
    bit = 1
    while True:
        received = lax.ppermute(send, "dp", [(i, i ^ bit) for i in range(n_dp)])
        total = keep.astype(F32) + received.astype(F32)
        bit *= 2
        if bit == n_dp:
            return total[0]
        half = total.shape[0] // 2
        keep = total[:half].astype(send.dtype)
        send = total[half:].astype(send.dtype)


def on_device(n_dp, tokens, lengths, norm_gain, norm_shift, qkv_weight, proj_weight, up_weight, inner_bias,
              down_weight, outer_bias, cotangent):
    j = lax.axis_index("branch")
    me = lax.axis_index("dp")
    other = [(0, 1), (1, 0)]
    half_rows = tokens.shape[0]
    branch = j.astype(jnp.int32).reshape(1)
    length = lengths.astype(jnp.int32)

    bits = n_dp.bit_length() - 1
    reverse = [int(format(i, "b").zfill(bits)[::-1], 2) for i in range(n_dp)] if bits else [0]
    reverse_table = jnp.array(reverse, jnp.int32)
    every = jnp.arange(n_dp, dtype=jnp.int32)
    order = jnp.bitwise_xor(reverse_table, me)
    slots = jnp.zeros((n_dp,), jnp.int32)
    relative = jnp.bitwise_xor(every, me)
    for i in range(bits):
        slots = slots + (((relative >> i) & 1) << (bits - 1 - i))

    def in_order(mine, theirs):
        return jnp.where(j == 0, jnp.concatenate([mine, theirs], 0), jnp.concatenate([theirs, mine], 0))

    tokens_all = in_order(tokens, lax.ppermute(tokens, "branch", other)).astype(F32)
    grads_in = in_order(cotangent, lax.ppermute(cotangent, "branch", other))
    gain = norm_gain.astype(F32)
    shift = norm_shift.astype(F32)
    centred = tokens_all - jnp.mean(tokens_all, axis=1, keepdims=True)
    rstd = lax.rsqrt(jnp.mean(centred * centred, axis=1, keepdims=True) + EPS)
    normed = (centred * rstd * gain + shift).astype(BF)
    live = jnp.arange(SEQ_LEN, dtype=jnp.int32) < length[0]
    grads = jnp.where(live[:, None], grads_in, jnp.zeros_like(grads_in))

    cosine, sine = rotary_tables()
    ffb = FF_HALF // n_dp
    if ffb == LANES:
        splits = FB // LANES
        weights = (up_weight, down_weight, inner_bias.reshape(1, FF))
    else:
        splits = 1
        weights = (
            lax.dynamic_index_in_dim(up_weight.reshape(D, n_dp, 2, ffb), j, 2, False).reshape(D, FF_HALF),
            lax.dynamic_index_in_dim(down_weight.reshape(n_dp, 2, ffb, D), j, 1, False).reshape(FF_HALF, D),
            lax.dynamic_index_in_dim(inner_bias.reshape(n_dp, 2, ffb), j, 1, False).reshape(1, FF_HALF),
        )
    hidden, grad_before, expanded, grad_mlp = mlp_call(branch, normed, grads, weights, splits)
    down_keep, down_send = weight_grad(slots, order, hidden, grads, 256)
    up_keep, up_send = weight_grad(slots, order, normed, grad_before, 512)

    qkv = qkv_call(branch, normed, qkv_weight, cosine, sine)
    context, qe = attend_call(length, qkv)
    proj = lax.dynamic_slice_in_dim(proj_weight, j * HALF, HALF, 0)
    attended = jnp.dot(context, proj, preferred_element_type=F32)
    branch_out = attended + expanded
    mine = lax.dynamic_slice_in_dim(branch_out, j * half_rows, half_rows, 0)
    theirs = lax.dynamic_slice_in_dim(branch_out, (1 - j) * half_rows, half_rows, 0).astype(BF)
    theirs = lax.ppermute(theirs, "branch", other)
    layer_out = (tokens.astype(F32) + mine + theirs.astype(F32) + outer_bias.astype(F32)).astype(BF)

    proj_keep, proj_send = weight_grad(slots, order, context, grads, 512)
    grad_context = jnp.einsum("ne,de->nd", grads, proj, preferred_element_type=F32).astype(BF)
    dmix = attend_back_call(length, qe, qkv, context, grad_context, cosine, sine)
    qkv_keep, qkv_send = weight_grad(slots, order, normed, dmix, HALF)
    grad_normed = grad_normed_call(branch, dmix, qkv_weight, grad_mlp)

    mine = lax.dynamic_slice_in_dim(grad_normed, j * half_rows, half_rows, 0)
    theirs = lax.dynamic_slice_in_dim(grad_normed, (1 - j) * half_rows, half_rows, 0).astype(BF)
    mine = mine + lax.ppermute(theirs, "branch", other).astype(F32)
    own_centred = lax.dynamic_slice_in_dim(centred, j * half_rows, half_rows, 0)
    own_rstd = lax.dynamic_slice_in_dim(rstd, j * half_rows, half_rows, 0)
    own_grads = lax.dynamic_slice_in_dim(grads, j * half_rows, half_rows, 0).astype(F32)
    u = mine * gain
    own_hat = own_centred * own_rstd
    tokens_grad = own_grads + own_rstd * (
        u - jnp.mean(u, axis=1, keepdims=True) - own_hat * jnp.mean(u * own_hat, axis=1, keepdims=True)
    )

    small = D // n_dp
    vectors = jnp.concatenate(
        [
            jnp.sum(grad_normed * (centred * rstd), axis=0).reshape(n_dp, small),
            jnp.sum(grad_normed, axis=0).reshape(n_dp, small),
            jnp.sum(own_grads, axis=0).reshape(n_dp, small),
            jnp.sum(grad_before.astype(F32), axis=0).reshape(n_dp, ffb),
        ],
        axis=1,
    )
    vectors = jnp.take(vectors, order, axis=0)
    vector = reduce_pieces(vectors[: n_dp // 2], vectors[n_dp // 2 :], n_dp)
    triple = vector[: 3 * small].reshape(3, 2, small // 2)
    mine = lax.dynamic_index_in_dim(triple, j, 1, False)
    triple = mine + lax.ppermute(lax.dynamic_index_in_dim(triple, 1 - j, 1, False), "branch", other)

    def both_halves(piece, block):
        shard = piece.shape[0] // 2
        mine = lax.dynamic_slice_in_dim(piece, j * shard, shard, 0)
        theirs = lax.dynamic_slice_in_dim(piece, (1 - j) * shard, shard, 0).astype(BF)
        theirs = lax.ppermute(theirs, "branch", other).astype(F32)
        low = jnp.where(j == 0, mine, theirs).reshape(shard, -1, block)
        high = jnp.where(j == 0, theirs, mine).reshape(shard, -1, block)
        return jnp.stack([low, high], axis=2).reshape(shard, -1)

    down_grad = reduce_pieces(down_keep, down_send, n_dp)
    up_grad = both_halves(reduce_pieces(up_keep, up_send, n_dp), ffb)
    proj_piece = reduce_pieces(proj_keep, proj_send, n_dp).astype(BF)
    route = [(2 * p + h, n_dp * h + p) for h in range(2) for p in range(n_dp)]
    proj_grad = lax.ppermute(proj_piece, ("dp", "branch"), route).astype(F32)
    qkv_grad = both_halves(reduce_pieces(qkv_keep, qkv_send, n_dp), HALF)
    return (
        layer_out,
        tokens_grad,
        triple[0],
        triple[1],
        qkv_grad,
        proj_grad,
        up_grad,
        vector[3 * small :],
        down_grad,
        triple[2],
    )


def solution(mesh):
    rows = P(("dp", "branch"), None)
    flat = P(("dp", "branch"))
    return jax.shard_map(
        functools.partial(on_device, mesh.shape["dp"]),
        mesh=mesh,
        in_specs=(rows, P("dp"), P(), P(), P(), P(), P(), P(), P(), P(), rows),
        out_specs=(rows, rows, flat, flat, rows, rows, rows, flat, rows, flat),
        check_vma=False,
    )
```

```python
import functools
import math

import jax
import jax.numpy as jnp
from jax import lax
from jax.experimental import pallas as pl
from jax.experimental.pallas import tpu as pltpu
from jax.sharding import PartitionSpec as P

D = 1024
HEADS = 16
HEAD_DIM = 64
ROT_DIM = 32
FF = 4096
SEQ_LEN = 1024
HALF = HEADS // 2 * HEAD_DIM
FF_HALF = FF // 2
LANES = 128
QB = 256
FB = 512
EPS = 1e-05
BF = jnp.bfloat16
F32 = jnp.float32


def params(mb=56):
    return pltpu.CompilerParams(vmem_limit_bytes=mb << 20)


def cost(flops, nbytes, trans=0):
    return pl.CostEstimate(flops=int(flops), bytes_accessed=int(nbytes), transcendentals=int(trans))


def dot_nn(a, b):
    return jnp.dot(a, b, preferred_element_type=F32)


def dot_nt(a, b):
    return lax.dot_general(a, b, (((1,), (1,)), ((), ())), preferred_element_type=F32)


def dot_tn(a, b):
    return lax.dot_general(a, b, (((0,), (0,)), ((), ())), preferred_element_type=F32)


def rotary_tables():
    position = jnp.arange(SEQ_LEN, dtype=jnp.int32).astype(F32)
    lane = jnp.arange(LANES, dtype=jnp.int32)
    channel = lane % HEAD_DIM
    frequency = jnp.power(10000.0, -(2.0 * (channel // 2).astype(F32)) / ROT_DIM)
    angles = position[:, None] * frequency[None, :]
    inside = (channel < ROT_DIM)[None, :]
    cosine = jnp.where(inside, jnp.cos(angles), 1.0)
    sine = jnp.where(inside, jnp.sin(angles), 0.0)
    even = (lane % 2 == 0)[None, :]
    return cosine, jnp.where(even, -sine, sine)


def rotate(x, cosine, sine):
    even = lax.broadcasted_iota(jnp.int32, x.shape, 1) % 2 == 0
    swapped = jnp.where(even, pltpu.roll(x, LANES - 1, 1), pltpu.roll(x, 1, 1))
    return x * cosine + swapped * sine


def unrotate(y, cosine, sine):
    even = lax.broadcasted_iota(jnp.int32, y.shape, 1) % 2 == 0
    swapped = jnp.where(even, pltpu.roll(y, LANES - 1, 1), pltpu.roll(y, 1, 1))
    return y * cosine - swapped * sine


def head_lanes(shape, head):
    lane = lax.broadcasted_iota(jnp.int32, shape, 1)
    own = (lane >= HEAD_DIM) if head else (lane < HEAD_DIM)
    spare = lane - (0 if head else HEAD_DIM)
    return own, spare


def keys_with_bias(k, head, length):
    own, spare = head_lanes(k.shape, head)
    row = lax.broadcasted_iota(jnp.int32, k.shape, 0)
    bias = jnp.where(row < length, 0.0, -1e30)
    extra = jnp.where(spare < 3, 1.0, jnp.where(spare == 3, bias, 0.0))
    return jnp.where(own, k.astype(F32), extra).astype(BF)


def attend_kernel(skip, info_ref, q_ref, k_ref, v_ref, *refs):
    o_ref, qe_ref = refs[skip:]
    length = info_ref[1]
    q = q_ref[0].astype(F32)
    k = k_ref[0]
    v = v_ref[0]
    tri = lax.broadcasted_iota(jnp.int32, (QB, QB), 0) >= lax.broadcasted_iota(jnp.int32, (QB, QB), 1)
    outs = []
    for head in range(2):
        own, spare = head_lanes((SEQ_LEN, LANES), head)
        ke = keys_with_bias(k, head, length)
        qe = jnp.where(own, q, jnp.where(spare == 3, 1.0, 0.0)).astype(BF)
        parts = []
        for b in range(SEQ_LEN // QB):
            lo, hi = b * QB, (b + 1) * QB
            s = dot_nt(qe[lo:hi], ke[:hi])
            diag = jnp.where(tri, s[:, lo:hi], -1e30)
            s = diag if b == 0 else jnp.concatenate([s[:, :lo], diag], axis=1)
            top = jnp.max(s, axis=1, keepdims=True)
            p = jnp.exp(s - top)
            total = jnp.sum(p, axis=1, keepdims=True)
            parts.append(dot_nn(p.astype(BF), v[:hi]) * (1.0 / total))
            lse = jnp.broadcast_to(top + jnp.log(total), (QB, LANES))
            first = lse.astype(BF).astype(F32)
            second = (lse - first).astype(BF).astype(F32)
            third = lse - first - second
            own_b, spare_b = head_lanes((QB, LANES), head)
            extra = jnp.where(
                spare_b == 0,
                -first,
                jnp.where(
                    spare_b == 1,
                    -second,
                    jnp.where(spare_b == 2, -third, jnp.where(spare_b == 3, 1.0, 0.0)),
                ),
            )
            qe_ref[head, lo:hi, :] = jnp.where(own_b, q[lo:hi], extra).astype(BF)
        outs.append(jnp.concatenate(parts, axis=0))
    own, _ = head_lanes((SEQ_LEN, LANES), 0)
    o_ref[...] = jnp.where(own, outs[0], outs[1]).astype(BF)


def attend_call(info, part, qkv, earlier=()):
    pairs = HALF // LANES // 2
    first = part * pairs
    spec = [pl.BlockSpec((1, SEQ_LEN, LANES), lambda p, n, t=t: (t, 0, first + p)) for t in range(3)]
    return pl.pallas_call(
        functools.partial(attend_kernel, len(earlier)),
        grid_spec=pltpu.PrefetchScalarGridSpec(
            num_scalar_prefetch=1,
            grid=(pairs,),
            in_specs=spec + [pl.BlockSpec(memory_space=pl.ANY)] * len(earlier),
            out_specs=[
                pl.BlockSpec((SEQ_LEN, LANES), lambda p, n: (0, first + p)),
                pl.BlockSpec((2, SEQ_LEN, LANES), lambda p, n: (first + p, 0, 0)),
            ],
        ),
        out_shape=[
            jax.ShapeDtypeStruct((SEQ_LEN, HALF), BF),
            jax.ShapeDtypeStruct((HEADS // 2, SEQ_LEN, LANES), BF),
        ],
        input_output_aliases={4: 0, 5: 1} if earlier else {},
        compiler_params=params(),
        cost_estimate=cost(
            2 * pairs * 10 * SEQ_LEN * SEQ_LEN * LANES, 2 * SEQ_LEN * HALF * 3, 4 * SEQ_LEN * SEQ_LEN
        ),
        name="attend",
    )(info, qkv, qkv, qkv, *earlier)


def attend_back_kernel(info_ref, qe_ref, k_ref, v_ref, o_ref, g_ref, cos_ref, sin_ref, *refs):
    d_ref, dk_ref, dv_ref = refs[-3:]
    length = info_ref[1]
    k = k_ref[0]
    v = v_ref[0]
    g = g_ref[...].astype(F32)
    o = o_ref[...].astype(F32)
    tri = lax.broadcasted_iota(jnp.int32, (QB, QB), 0) >= lax.broadcasted_iota(jnp.int32, (QB, QB), 1)
    queries = []
    for head in range(2):
        own, spare = head_lanes((SEQ_LEN, LANES), head)
        ke = keys_with_bias(k, head, length)
        ve = jnp.where(own, v.astype(F32), jnp.where(spare < 3, 1.0, 0.0)).astype(BF)
        inner = jnp.sum(jnp.where(own, g * o, 0.0), axis=1, keepdims=True)
        inner = jnp.broadcast_to(inner, (SEQ_LEN, LANES))
        first = inner.astype(BF).astype(F32)
        second = (inner - first).astype(BF).astype(F32)
        third = inner - first - second
        extra = jnp.where(
            spare == 0,
            -first,
            jnp.where(spare == 1, -second, jnp.where(spare == 2, -third, 0.0)),
        )
        ge = jnp.where(own, g, extra).astype(BF)
        parts = []
        for b in range(SEQ_LEN // QB):
            lo, hi = b * QB, (b + 1) * QB
            qb = qe_ref[head, lo:hi, :]
            gb = ge[lo:hi]
            s = dot_nt(qb, ke[:hi])
            diag = jnp.where(tri, s[:, lo:hi], -1e30)
            s = diag if b == 0 else jnp.concatenate([s[:, :lo], diag], axis=1)
            p = jnp.exp(s)
            ds = (p * dot_nt(gb, ve[:hi])).astype(BF)
            parts.append(dot_nn(ds, k[:hi]))
            dk = dot_tn(ds, qb)
            dv = dot_tn(p.astype(BF), gb)
            if b > 0:
                dk_ref[head, :lo] += dk[:lo]
                dv_ref[head, :lo] += dv[:lo]
            dk_ref[head, lo:hi] = dk[lo:hi]
            dv_ref[head, lo:hi] = dv[lo:hi]
        queries.append(jnp.concatenate(parts, axis=0))
    own, _ = head_lanes((SEQ_LEN, LANES), 0)
    cosine, sine = cos_ref[...], sin_ref[...]
    dq = jnp.where(own, queries[0], queries[1]) * HEAD_DIM**-0.5
    d_ref[0] = unrotate(dq, cosine, sine).astype(BF)
    d_ref[1] = unrotate(jnp.where(own, dk_ref[0], dk_ref[1]), cosine, sine).astype(BF)
    d_ref[2] = jnp.where(own, dv_ref[0], dv_ref[1]).astype(BF)


def attend_back_call(info, part, qe, qkv, context, grad_context, cosine, sine, earlier=()):
    pairs = HALF // LANES // 2
    first = part * pairs
    table = pl.BlockSpec((SEQ_LEN, LANES), lambda p, n: (0, 0))
    return pl.pallas_call(
        attend_back_kernel,
        grid_spec=pltpu.PrefetchScalarGridSpec(
            num_scalar_prefetch=1,
            grid=(pairs,),
            in_specs=[
                pl.BlockSpec((2, SEQ_LEN, LANES), lambda p, n: (first + p, 0, 0)),
                pl.BlockSpec((1, SEQ_LEN, LANES), lambda p, n: (1, 0, first + p)),
                pl.BlockSpec((1, SEQ_LEN, LANES), lambda p, n: (2, 0, first + p)),
                pl.BlockSpec((SEQ_LEN, LANES), lambda p, n: (0, first + p)),
                pl.BlockSpec((SEQ_LEN, LANES), lambda p, n: (0, first + p)),
                table,
                table,
            ]
            + [pl.BlockSpec(memory_space=pl.ANY)] * len(earlier),
            out_specs=pl.BlockSpec((3, SEQ_LEN, LANES), lambda p, n: (0, 0, first + p)),
            scratch_shapes=[
                pltpu.VMEM((2, SEQ_LEN, LANES), F32),
                pltpu.VMEM((2, SEQ_LEN, LANES), F32),
            ],
        ),
        out_shape=jax.ShapeDtypeStruct((3, SEQ_LEN, HALF), BF),
        input_output_aliases={8: 0} if earlier else {},
        compiler_params=params(),
        cost_estimate=cost(
            2 * pairs * 12 * SEQ_LEN * SEQ_LEN * LANES, 2 * SEQ_LEN * HALF * 4, 4 * SEQ_LEN * SEQ_LEN
        ),
        name="attend_back",
    )(info, qe, qkv, qkv, context, grad_context, cosine, sine, *earlier)


def gelu_parts(v):
    c = math.sqrt(2.0 / math.pi)
    square = v * v
    t = jnp.tanh(v * (c + (c * 0.044715) * square))
    half = 0.5 * (1.0 + t)
    slope = half + (0.5 * v) * (1.0 - t * t) * (c + (3.0 * c * 0.044715) * square)
    return v * half, slope


def normalize(x):
    x = x.astype(F32)
    centred = x - jnp.mean(x, axis=1, keepdims=True)
    rstd = lax.rsqrt(jnp.mean(centred * centred, axis=1, keepdims=True) + EPS)
    return centred * rstd, rstd


def masked_rows(g, start, length):
    row = start + lax.broadcasted_iota(jnp.int32, g.shape, 0)
    return jnp.where(row < length, g.astype(F32), 0.0)


def joined(refs, axis):
    return refs[0][...] if len(refs) == 1 else jnp.concatenate([r[...] for r in refs], axis=axis)


def weight_specs(plan, rows_too=True):
    splits, wide, pick = plan["splits"], FB // plan["splits"], plan["pick"]
    specs = [pl.BlockSpec((D, wide), lambda s, *a, i=i: (0, pick(s, a, i))) for i in range(splits)]
    specs += [pl.BlockSpec((wide, D), lambda s, *a, i=i: (pick(s, a, i), 0)) for i in range(splits)]
    if rows_too:
        specs += [pl.BlockSpec((1, wide), lambda s, *a, i=i: (0, pick(s, a, i))) for i in range(splits)]
    return specs


def accumulate(ref, value):
    @pl.when(pl.program_id(0) == 0)
    def _():
        ref[...] = value

    @pl.when(pl.program_id(0) > 0)
    def _():
        ref[...] += value


def mlp_own_kernel(splits, info_ref, cls_ref, t_ref, c_ref, gain_ref, shift_ref, *refs):
    ups, downs, biases = refs[:splits], refs[splits : 2 * splits], refs[2 * splits : 3 * splits]
    x_ref, h_ref, g_ref, gb_ref, e_ref, gn_ref, outer_ref = refs[3 * splits :]

    @pl.when(pl.program_id(0) == 0)
    def _():
        hat, _ = normalize(t_ref[...])
        x_ref[...] = (hat * gain_ref[...].astype(F32) + shift_ref[...].astype(F32)).astype(BF)
        g = masked_rows(c_ref[...], info_ref[0] * c_ref.shape[0], info_ref[1])
        g_ref[...] = g.astype(BF)
        outer_ref[...] = jnp.sum(g, axis=0, keepdims=True)

    up, down, bias = joined(ups, 1), joined(downs, 0), joined(biases, 1)
    before = dot_nn(x_ref[...], up) + bias.astype(F32)
    hidden, slope = gelu_parts(before)
    hidden = hidden.astype(BF)
    grad_before = (dot_nt(g_ref[...], down) * slope).astype(BF)
    h_ref[...] = hidden
    gb_ref[...] = grad_before
    accumulate(e_ref, dot_nn(hidden, down))
    accumulate(gn_ref, dot_nt(grad_before, up))


def mlp_own_call(info, plan, tokens, cotangent, gain, shift):
    rows, splits = tokens.shape[0], plan["splits"]
    fixed = lambda s, *a: (0, 0)
    up, down, bias = plan["weights"]
    whole = pl.BlockSpec((rows, D), fixed)
    wide = pl.BlockSpec((rows, FB), lambda s, *a: (0, s))
    return pl.pallas_call(
        functools.partial(mlp_own_kernel, splits),
        grid_spec=pltpu.PrefetchScalarGridSpec(
            num_scalar_prefetch=2,
            grid=(FF_HALF // FB,),
            in_specs=[whole, whole, pl.BlockSpec((1, D), fixed), pl.BlockSpec((1, D), fixed)] + weight_specs(plan),
            out_specs=[whole, wide, whole, wide, whole, whole, pl.BlockSpec((1, D), fixed)],
        ),
        out_shape=[
            jax.ShapeDtypeStruct((2 * rows, D), BF),
            jax.ShapeDtypeStruct((2 * rows, FF_HALF), BF),
            jax.ShapeDtypeStruct((rows, D), BF),
            jax.ShapeDtypeStruct((rows, FF_HALF), BF),
            jax.ShapeDtypeStruct((rows, D), F32),
            jax.ShapeDtypeStruct((rows, D), F32),
            jax.ShapeDtypeStruct((1, D), F32),
        ],
        compiler_params=params(),
        cost_estimate=cost(8 * rows * D * FF_HALF, 12 * rows * D + 4 * D * FF_HALF, rows * FF_HALF),
        name="mlp_own",
    )(info, plan["classes"], tokens, cotangent, gain, shift, *([up] * splits), *([down] * splits), *([bias] * splits))


def mlp_forward_kernel(splits, info_ref, cls_ref, t_ref, gain_ref, shift_ref, *refs):
    ups, downs, biases = refs[:splits], refs[splits : 2 * splits], refs[2 * splits : 3 * splits]
    x_ref, h_ref, slope_ref, e_ref = refs[3 * splits + 2 :]

    @pl.when(pl.program_id(0) == 0)
    def _():
        hat, _ = normalize(t_ref[...])
        x_ref[...] = (hat * gain_ref[...].astype(F32) + shift_ref[...].astype(F32)).astype(BF)

    up, down, bias = joined(ups, 1), joined(downs, 0), joined(biases, 1)
    before = dot_nn(x_ref[...], up) + bias.astype(F32)
    hidden, slope = gelu_parts(before)
    hidden = hidden.astype(BF)
    h_ref[...] = hidden
    slope_ref[...] = slope.astype(BF)
    accumulate(e_ref, dot_nn(hidden, down))


def mlp_forward_call(info, plan, tokens, gain, shift, normed, hidden):
    rows, splits = tokens.shape[0], plan["splits"]
    fixed = lambda s, *a: (0, 0)
    up, down, bias = plan["weights"]
    whole = pl.BlockSpec((rows, D), fixed)
    anywhere = pl.BlockSpec(memory_space=pl.ANY)
    first = 5 + 3 * splits
    return pl.pallas_call(
        functools.partial(mlp_forward_kernel, splits),
        grid_spec=pltpu.PrefetchScalarGridSpec(
            num_scalar_prefetch=2,
            grid=(FF_HALF // FB,),
            in_specs=[whole, pl.BlockSpec((1, D), fixed), pl.BlockSpec((1, D), fixed)]
            + weight_specs(plan)
            + [anywhere, anywhere],
            out_specs=[
                pl.BlockSpec((rows, D), lambda s, *a: (1, 0)),
                pl.BlockSpec((rows, FB), lambda s, *a: (1, s)),
                pl.BlockSpec((rows, FB), lambda s, *a: (0, s)),
                whole,
            ],
        ),
        out_shape=[
            jax.ShapeDtypeStruct((2 * rows, D), BF),
            jax.ShapeDtypeStruct((2 * rows, FF_HALF), BF),
            jax.ShapeDtypeStruct((rows, FF_HALF), BF),
            jax.ShapeDtypeStruct((rows, D), F32),
        ],
        input_output_aliases={first: 0, first + 1: 1},
        compiler_params=params(),
        cost_estimate=cost(4 * rows * D * FF_HALF, 12 * rows * D + 4 * D * FF_HALF, rows * FF_HALF),
        name="mlp_forward",
    )(info, plan["classes"], tokens, gain, shift, *([up] * splits), *([down] * splits), *([bias] * splits), normed, hidden)


def down_grad_kernel(splits, pieces, info_ref, cls_ref, sub_ref, h_ref, go_ref, c_ref, g_ref, *grads):
    rows = c_ref.shape[0]
    step = pl.program_id(0)

    @pl.when(step == 0)
    def _():
        g_ref[:rows] = go_ref[...]
        g_ref[rows:] = masked_rows(c_ref[...], (1 - info_ref[0]) * rows, info_ref[1]).astype(BF)

    grad_down = dot_tn(h_ref[...], g_ref[...]).astype(BF)
    if not pieces:
        grads[0][...] = grad_down
        return
    down_keep, down_send = grads
    block = FB // splits

    @pl.when(step < 2)
    def _():
        for i in range(splits):
            down_send[sub_ref[i]] = grad_down[i * block : (i + 1) * block]

    @pl.when(step >= 2)
    def _():
        for i in range(splits):
            down_keep[sub_ref[i]] = grad_down[i * block : (i + 1) * block]


def down_grad_call(info, plan, hidden, grads_own, cotangent):
    rows, splits, pieces = cotangent.shape[0], plan["splits"], plan["pieces"]
    fixed = lambda s, *a: (0, 0)
    whole = pl.BlockSpec((rows, D), fixed)
    out_specs = [pl.BlockSpec((2 * rows, D), fixed)]
    out_shape = [jax.ShapeDtypeStruct((2 * rows, D), BF)]
    if pieces:
        half, down_rows = pieces // 2, FF_HALF // pieces
        out_specs += [
            pl.BlockSpec((splits, down_rows, D), lambda s, *a: (jnp.maximum(s - 2, 0), 0, 0)),
            pl.BlockSpec((splits, down_rows, D), lambda s, *a: (jnp.minimum(s, 1), 0, 0)),
        ]
        out_shape += [jax.ShapeDtypeStruct((half, down_rows, D), BF)] * 2
    else:
        out_specs += [pl.BlockSpec((FB, D), lambda s, *a: (s, 0))]
        out_shape += [jax.ShapeDtypeStruct((FF_HALF, D), BF)]
    return pl.pallas_call(
        functools.partial(down_grad_kernel, splits, pieces),
        grid_spec=pltpu.PrefetchScalarGridSpec(
            num_scalar_prefetch=3,
            grid=(FF_HALF // FB,),
            in_specs=[pl.BlockSpec((2 * rows, FB), lambda s, *a: (0, s)), whole, whole],
            out_specs=out_specs,
        ),
        out_shape=out_shape,
        compiler_params=params(),
        cost_estimate=cost(4 * rows * D * FF_HALF, 8 * rows * D + 2 * D * FF_HALF + 4 * rows * FF_HALF),
        name="down_grad",
    )(info, plan["classes"], plan["subs"], hidden, grads_own, cotangent)


def mlp_back_kernel(splits, pieces, info_ref, cls_ref, ord_ref, x_ref, slope_ref, g_ref, gb_ref, *refs):
    ups, downs = refs[:splits], refs[splits : 2 * splits]
    gn_ref, inner_ref, *grads = refs[2 * splits : -2 if pieces else -1]
    gball_ref = refs[-2 if pieces else -1]
    rows = g_ref.shape[0]
    up, down = joined(ups, 1), joined(downs, 0)
    grad_before = (dot_nt(g_ref[...], down) * slope_ref[...].astype(F32)).astype(BF)
    gball_ref[:rows] = gb_ref[...]
    gball_ref[rows:] = grad_before
    accumulate(gn_ref, dot_nt(grad_before, up))
    inner_ref[...] = jnp.sum(gball_ref[...].astype(F32), axis=0, keepdims=True)
    grad_up = dot_tn(x_ref[...], gball_ref[...]).astype(BF)
    if not pieces:
        grads[0][...] = grad_up
        return
    up_keep, up_send = grads
    upall_ref = refs[-1]
    upall_ref[...] = grad_up.reshape(upall_ref.shape)
    for q in range(pieces // 2):
        up_keep[q] = upall_ref[ord_ref[q]]
        up_send[q] = upall_ref[ord_ref[q + pieces // 2]]


def mlp_back_call(info, plan, normed, slope, grads, gb_own):
    rows, splits, pieces = gb_own.shape[0], plan["splits"], plan["pieces"]
    fixed = lambda s, *a: (0, 0)
    up, down, _ = plan["weights"]
    whole = pl.BlockSpec((rows, D), fixed)
    wide = pl.BlockSpec((rows, FB), lambda s, *a: (0, s))
    out_specs = [whole, pl.BlockSpec((1, FB), lambda s, i, cls, *a: (0, cls[s]))]
    out_shape = [jax.ShapeDtypeStruct((rows, D), F32), jax.ShapeDtypeStruct((1, FF_HALF), F32)]
    scratch = [pltpu.VMEM((2 * rows, FB), BF)]
    if pieces:
        shape = (pieces // 2, D // pieces, FB)
        out_specs += [pl.BlockSpec(shape, lambda s, i, cls, *a: (0, 0, cls[s]))] * 2
        out_shape += [jax.ShapeDtypeStruct(shape[:2] + (FF_HALF,), BF)] * 2
        scratch.append(pltpu.VMEM((pieces, D // pieces, FB), BF))
    else:
        out_specs += [pl.BlockSpec((D, FB), lambda s, *a: (0, s))]
        out_shape += [jax.ShapeDtypeStruct((D, FF_HALF), BF)]
    return pl.pallas_call(
        functools.partial(mlp_back_kernel, splits, pieces),
        grid_spec=pltpu.PrefetchScalarGridSpec(
            num_scalar_prefetch=3,
            grid=(FF_HALF // FB,),
            in_specs=[
                pl.BlockSpec((2 * rows, D), fixed),
                wide,
                pl.BlockSpec((rows, D), lambda s, *a: (1, 0)),
                wide,
            ]
            + weight_specs(plan, False),
            out_specs=out_specs,
            scratch_shapes=scratch,
        ),
        out_shape=out_shape,
        compiler_params=params(),
        cost_estimate=cost(8 * rows * D * FF_HALF, 12 * rows * D + 6 * D * FF_HALF + 4 * rows * FF_HALF),
        name="mlp_back",
    )(info, plan["classes"], plan["order"], normed, slope, grads, gb_own, *([up] * splits), *([down] * splits))


def qkv_half_kernel(place_ref, info_ref, x_ref, w_ref, cos_ref, sin_ref, *refs):
    o_ref = refs[-1]
    t = pl.program_id(0)
    chunk = 2 * LANES

    @pl.when(t == 2)
    def _():
        for c in range(0, HALF, chunk):
            o_ref[0, :, c : c + chunk] = dot_nn(x_ref[...], w_ref[:, c : c + chunk]).astype(BF)

    @pl.when(t < 2)
    def _():
        scale = jnp.where(t == 0, HEAD_DIM**-0.5, 1.0)
        cosine = cos_ref[...] * scale
        sine = sin_ref[...] * scale
        for c in range(0, HALF, chunk):
            mixed = dot_nn(x_ref[...], w_ref[:, c : c + chunk])
            for e in range(0, chunk, LANES):
                o_ref[0, :, c + e : c + e + LANES] = rotate(mixed[:, e : e + LANES], cosine, sine).astype(BF)


def qkv_half_call(place, info, half, normed, w, cosine, sine, qkv=None):
    rows = normed.shape[0] // 2
    table = pl.BlockSpec((rows, LANES), lambda t, p, i: (p[0], 0))
    more = [] if qkv is None else [qkv]
    return pl.pallas_call(
        qkv_half_kernel,
        grid_spec=pltpu.PrefetchScalarGridSpec(
            num_scalar_prefetch=2,
            grid=(3,),
            in_specs=[
                pl.BlockSpec((rows, D), lambda t, p, i: (half, 0)),
                pl.BlockSpec((D, HALF), lambda t, p, i: (0, 2 * t + i[0])),
                table,
                table,
            ]
            + [pl.BlockSpec(memory_space=pl.ANY)] * len(more),
            out_specs=pl.BlockSpec((1, rows, HALF), lambda t, p, i: (t, p[0], 0)),
        ),
        out_shape=jax.ShapeDtypeStruct((3, 2 * rows, HALF), BF),
        input_output_aliases={6: 0} if more else {},
        compiler_params=params(),
        cost_estimate=cost(2 * rows * D * 3 * HALF, 2 * (rows * D + D * 3 * HALF + rows * 3 * HALF)),
        name="qkv",
    )(place, info, normed, w, cosine, sine, *more)


def send_out_kernel(place_ref, info_ref, c_ref, w_ref, e_ref, o_ref):
    o_ref[...] = (dot_nn(c_ref[...], w_ref[...]) + e_ref[...]).astype(BF)


def finish_out_kernel(place_ref, info_ref, c_ref, w_ref, e_ref, t_ref, r_ref, bias_ref, o_ref):
    total = dot_nn(c_ref[...], w_ref[...]) + e_ref[...] + bias_ref[...].astype(F32)
    o_ref[...] = (total + t_ref[...].astype(F32) + r_ref[...].astype(F32)).astype(BF)


def out_call(place, info, context, proj, expanded, rest=()):
    rows, block = expanded.shape[0], 256
    steps = rows // block
    row = pl.BlockSpec((block, D), lambda s, p, i: (s, 0))
    return pl.pallas_call(
        finish_out_kernel if rest else send_out_kernel,
        grid_spec=pltpu.PrefetchScalarGridSpec(
            num_scalar_prefetch=2,
            grid=(steps,),
            in_specs=[
                pl.BlockSpec((block, HALF), lambda s, p, i: (p[0] * steps + s, 0)),
                pl.BlockSpec((HALF, D), lambda s, p, i: (i[0], 0)),
                row,
            ]
            + ([row, row, pl.BlockSpec((1, D), lambda s, p, i: (0, 0))] if rest else []),
            out_specs=row,
        ),
        out_shape=jax.ShapeDtypeStruct((rows, D), BF),
        compiler_params=params(),
        cost_estimate=cost(2 * rows * D * HALF, 8 * rows * D + 2 * HALF * D),
        name="finish_out" if rest else "send_out",
    )(place, info, context, proj, expanded, *rest)


def proj_back_kernel(info_ref, ord_ref, g_ref, c_ref, w_ref, gc_ref, *refs):
    acc_ref = refs[-2] if len(refs) > 2 else refs[-1]
    gc_ref[...] = dot_nt(g_ref[...], w_ref[...]).astype(BF)
    part = dot_tn(c_ref[...], g_ref[...])

    @pl.when(pl.program_id(0) == 0)
    def _():
        acc_ref[...] = part

    @pl.when(pl.program_id(0) == 1)
    def _():
        total = (acc_ref[...] + part).astype(BF)
        if len(refs) == 2:
            refs[0][...] = total
        else:
            keep, send, all_ref = refs[0], refs[1], refs[3]
            all_ref[...] = total.reshape(all_ref.shape)
            half = keep.shape[0]
            for q in range(half):
                keep[q] = all_ref[ord_ref[q]]
                send[q] = all_ref[ord_ref[q + half]]


def proj_back_call(info, plan, order, grads, context, proj):
    rows, pieces = grads.shape[0] // 2, plan["pieces"]
    scratch = [pltpu.VMEM((HALF, D), F32)]
    if pieces:
        shape = (pieces // 2, HALF // pieces, D)
        out_specs = [pl.BlockSpec(shape, lambda h, *a: (0, 0, 0))] * 2
        out_shape = [jax.ShapeDtypeStruct(shape, BF)] * 2
        scratch.append(pltpu.VMEM((pieces, HALF // pieces, D), BF))
    else:
        out_specs = [pl.BlockSpec((HALF, D), lambda h, *a: (0, 0))]
        out_shape = [jax.ShapeDtypeStruct((HALF, D), BF)]
    return pl.pallas_call(
        proj_back_kernel,
        grid_spec=pltpu.PrefetchScalarGridSpec(
            num_scalar_prefetch=2,
            grid=(2,),
            in_specs=[
                pl.BlockSpec((rows, D), lambda h, i, o: (h, 0)),
                pl.BlockSpec((rows, HALF), lambda h, i, o: (jnp.bitwise_xor(h, i[0]), 0)),
                pl.BlockSpec((HALF, D), lambda h, i, o: (i[0], 0)),
            ],
            out_specs=[pl.BlockSpec((rows, HALF), lambda h, i, o: (jnp.bitwise_xor(h, i[0]), 0))] + out_specs,
            scratch_shapes=scratch,
        ),
        out_shape=[jax.ShapeDtypeStruct((2 * rows, HALF), BF)] + out_shape,
        compiler_params=params(),
        cost_estimate=cost(8 * rows * D * HALF, 4 * rows * D + 8 * rows * HALF + 4 * HALF * D),
        name="proj_back",
    )(info, order, grads, context, proj)


def qkv_grad_kernel(info_ref, ord_ref, x_ref, own_ref, their_ref, *refs):
    d = jnp.concatenate([own_ref[0], their_ref[0]], axis=0)
    total = dot_tn(x_ref[...], d).astype(BF)
    if len(refs) == 1:
        refs[0][...] = total
        return
    keep, send, all_ref = refs
    all_ref[...] = total.reshape(all_ref.shape)
    half = keep.shape[0]
    for q in range(half):
        keep[q] = all_ref[ord_ref[q]]
        send[q] = all_ref[ord_ref[q + half]]


def qkv_grad_call(info, plan, order, normed, dmix, first, count):
    rows, pieces = normed.shape[0] // 2, plan["pieces"]
    scratch = []
    if pieces:
        shape = (pieces // 2, D // pieces, HALF)
        out_specs = [pl.BlockSpec(shape, lambda t, *a: (0, 0, t))] * 2
        out_shape = [jax.ShapeDtypeStruct(shape[:2] + (count * HALF,), BF)] * 2
        scratch = [pltpu.VMEM((pieces, D // pieces, HALF), BF)]
    else:
        out_specs = [pl.BlockSpec((D, HALF), lambda t, *a: (0, t))]
        out_shape = [jax.ShapeDtypeStruct((D, count * HALF), BF)]
    return pl.pallas_call(
        qkv_grad_kernel,
        grid_spec=pltpu.PrefetchScalarGridSpec(
            num_scalar_prefetch=2,
            grid=(count,),
            in_specs=[
                pl.BlockSpec((2 * rows, D), lambda t, i, o: (0, 0)),
                pl.BlockSpec((1, rows, HALF), lambda t, i, o: (first + t, i[0], 0)),
                pl.BlockSpec((1, rows, HALF), lambda t, i, o: (first + t, 1 - i[0], 0)),
            ],
            out_specs=out_specs,
            scratch_shapes=scratch,
        ),
        out_shape=out_shape,
        compiler_params=params(),
        cost_estimate=cost(4 * rows * D * count * HALF, 4 * rows * D + (4 * rows + 2 * D) * count * HALF),
        name="qkv_grad",
    )(info, order, normed, dmix, dmix)


def grad_normed_kernel(place_ref, info_ref, d_ref, wq_ref, wk_ref, wv_ref, base_ref, t_ref, o_ref, sum_ref):
    total = base_ref[...]
    for t, w in enumerate((wq_ref, wk_ref, wv_ref)):
        total += dot_nt(d_ref[t], w[...])
    o_ref[...] = total.astype(o_ref.dtype)
    hat, _ = normalize(t_ref[...])
    sums = jnp.concatenate([jnp.sum(total * hat, axis=0, keepdims=True), jnp.sum(total, axis=0, keepdims=True)], axis=0)
    accumulate(sum_ref, sums)


def grad_normed_call(place, info, dmix, w, base, tokens, kind):
    rows, block = base.shape[0], 256
    steps = rows // block
    row = pl.BlockSpec((block, D), lambda r, p, i: (r, 0))
    return pl.pallas_call(
        grad_normed_kernel,
        grid_spec=pltpu.PrefetchScalarGridSpec(
            num_scalar_prefetch=2,
            grid=(steps,),
            in_specs=[pl.BlockSpec((3, block, HALF), lambda r, p, i: (0, p[0] * steps + r, 0))]
            + [pl.BlockSpec((D, HALF), lambda r, p, i, t=t: (0, 2 * t + i[0])) for t in range(3)]
            + [row, row],
            out_specs=[row, pl.BlockSpec((2, D), lambda r, p, i: (0, 0))],
        ),
        out_shape=[jax.ShapeDtypeStruct((rows, D), kind), jax.ShapeDtypeStruct((2, D), F32)],
        compiler_params=params(),
        cost_estimate=cost(2 * rows * D * 3 * HALF, 8 * rows * D + 6 * D * HALF + 6 * rows * HALF),
        name="grad_normed",
    )(place, info, dmix, w, w, w, base, tokens)


def finish_grad_kernel(gn_ref, r_ref, t_ref, g_ref, gain_ref, o_ref):
    hat, rstd = normalize(t_ref[...])
    u = (gn_ref[...] + r_ref[...].astype(F32)) * gain_ref[...].astype(F32)
    inner = u - jnp.mean(u, axis=1, keepdims=True) - hat * jnp.mean(u * hat, axis=1, keepdims=True)
    o_ref[...] = g_ref[...].astype(F32) + inner * rstd


def finish_grad_call(grad_normed, received, tokens, grads, gain):
    rows, block = tokens.shape[0], 256
    row = pl.BlockSpec((block, D), lambda r: (r, 0))
    return pl.pallas_call(
        finish_grad_kernel,
        grid=(rows // block,),
        in_specs=[row, row, row, row, pl.BlockSpec((1, D), lambda r: (0, 0))],
        out_specs=row,
        out_shape=jax.ShapeDtypeStruct((rows, D), F32),
        compiler_params=params(),
        cost_estimate=cost(20 * rows * D, 14 * rows * D),
        name="finish_grad",
    )(grad_normed, received, tokens, grads, gain)


class Reduction:
    def __init__(self, pair, bits, n_dp):
        self.keep, self.send = pair
        self.bits, self.n_dp = list(bits), n_dp
        self.flying = None
        self.start()

    def start(self):
        bit = self.bits.pop(0)
        self.flying = lax.ppermute(self.send, "dp", [(i, i ^ bit) for i in range(self.n_dp)])

    def land(self):
        total = self.keep.astype(F32) + self.flying.astype(F32)
        if not self.bits:
            self.keep, self.send = total[0], None
            return (self.keep,)
        half = total.shape[0] // 2
        kind = self.send.dtype
        self.keep, self.send = total[:half].astype(kind), total[half:].astype(kind)
        done = (self.keep, self.send)
        self.start()
        return done

    def finish(self):
        while self.send is not None:
            self.land()
        return self.keep


def after(x, *done):
    return lax.optimization_barrier((x, *done))[0]


def send_order(bits, n_dp, me):
    table = []
    for slot in range(n_dp):
        table.append(sum(bit for place, bit in enumerate(reversed(bits)) if slot >> place & 1))
    return jnp.bitwise_xor(jnp.array(table, jnp.int32), me)


def on_device(n_dp, tokens, lengths, norm_gain, norm_shift, qkv_weight, proj_weight, up_weight, inner_bias,
              down_weight, outer_bias, cotangent):
    j = lax.axis_index("branch").astype(jnp.int32)
    me = lax.axis_index("dp").astype(jnp.int32)
    other = [(0, 1), (1, 0)]
    tokens_their = lax.ppermute(tokens, "branch", other)
    cotangent_their = lax.ppermute(cotangent, "branch", other)
    own, their = j.reshape(1), (1 - j).reshape(1)
    info = jnp.stack([j, lengths[0].astype(jnp.int32)])
    gain, shift = norm_gain.reshape(1, D), norm_shift.reshape(1, D)

    low_first = [1 << i for i in range(n_dp.bit_length() - 1)]
    high_first = low_first[:1] + low_first[2:] + low_first[1:2]
    order = send_order(low_first, n_dp, me)
    order_high = send_order(high_first, n_dp, me)
    ffb = FF_HALF // n_dp
    fast = ffb == LANES
    if fast:
        splits = FB // LANES
        high = jnp.arange(4, dtype=jnp.int32) ^ (me >> 2)
        plan = {
            "splits": splits,
            "pieces": n_dp,
            "pick": lambda s, a, i: 2 * (4 * i + a[1][s]) + a[0][0],
            "classes": jnp.array([1, 3, 0, 2], jnp.int32) ^ (me & 3),
            "subs": ((high & 1) << 1) | (high >> 1),
            "weights": (up_weight, down_weight, inner_bias.reshape(1, FF)),
        }
    else:
        plan = {
            "splits": 1,
            "pieces": 0,
            "pick": lambda s, a, i: s,
            "classes": jnp.arange(FF_HALF // FB, dtype=jnp.int32),
            "subs": jnp.zeros((1,), jnp.int32),
            "weights": (
                lax.dynamic_index_in_dim(up_weight.reshape(D, n_dp, 2, ffb), j, 2, False).reshape(D, FF_HALF),
                lax.dynamic_index_in_dim(down_weight.reshape(n_dp, 2, ffb, D), j, 1, False).reshape(FF_HALF, D),
                lax.dynamic_index_in_dim(inner_bias.reshape(n_dp, 2, ffb), j, 1, False).reshape(1, FF_HALF),
            ),
        }
    plan["order"] = order

    def pieces_of(grads, table):
        if len(grads) == 2:
            return grads
        whole = grads[0]
        ordered = jnp.take(whole.reshape(n_dp, whole.shape[0] // n_dp, whole.shape[1]), table, axis=0)
        return ordered[: n_dp // 2], ordered[n_dp // 2 :]

    cosine, sine = rotary_tables()
    normed, hidden, grads_own, gb_own, expanded_own, gn_own, outer = mlp_own_call(
        info, plan, tokens, cotangent, gain, shift
    )
    qkv = qkv_half_call(own, info, 0, normed, qkv_weight, cosine, sine)
    info = after(info, qkv)
    normed, hidden, slope, expanded_their = mlp_forward_call(info, plan, tokens_their, gain, shift, normed, hidden)
    qkv = qkv_half_call(their, info, 1, normed, qkv_weight, cosine, sine, qkv)
    attended = attend_call(info, 0, qkv)
    info = after(info, *attended)
    grads, *down = down_grad_call(info, plan, hidden, grads_own, cotangent_their)
    down = Reduction(pieces_of(down, order), low_first, n_dp)
    gn_their, inner, *up = mlp_back_call(info, plan, normed, slope, grads, gb_own)
    up = Reduction(pieces_of(up, order), low_first, n_dp)
    info = after(info, gn_their, *down.land())
    context, qe = attend_call(info, 1, qkv, attended)
    info = after(info, context, *up.land())
    out_their = out_call(their, info, context, proj_weight, expanded_their)
    out_received = lax.ppermute(out_their, "branch", other)
    info = after(info, out_their)
    grad_context, *proj = proj_back_call(info, plan, order_high, grads, context, proj_weight)
    proj = Reduction(pieces_of(proj, order_high), high_first, n_dp)
    dmix = attend_back_call(info, 0, qe, qkv, context, grad_context, cosine, sine)
    info = after(info, dmix, *proj.land())
    dmix = attend_back_call(info, 1, qe, qkv, context, grad_context, cosine, sine, (dmix,))
    info = after(info, dmix, *down.land(), *proj.land())
    gn_send, sums_their = grad_normed_call(their, info, dmix, qkv_weight, gn_their, tokens_their, BF)
    gn_received = lax.ppermute(gn_send, "branch", other)
    info = after(info, gn_send)
    value = Reduction(pieces_of(qkv_grad_call(info, plan, order_high, normed, dmix, 2, 1), order_high), high_first, n_dp)
    query_key = Reduction(pieces_of(qkv_grad_call(info, plan, order, normed, dmix, 0, 2), order), low_first, n_dp)
    info = after(info, value.send, query_key.send, *down.land())
    gn_own, sums_own = grad_normed_call(own, info, dmix, qkv_weight, gn_own, tokens, F32)
    info = after(info, gn_own, *value.land(), *query_key.land(), *up.land())
    layer_out = out_call(
        own, info, context, proj_weight, expanded_own, (tokens, out_received, outer_bias.reshape(1, D))
    )

    small = D // n_dp
    sums = sums_own + sums_their
    if fast:
        inner = inner.reshape(4, 4, ffb).transpose(1, 0, 2)
    vectors = jnp.concatenate(
        [
            sums[0].reshape(n_dp, small),
            sums[1].reshape(n_dp, small),
            outer.reshape(n_dp, small),
            inner.reshape(n_dp, ffb),
        ],
        axis=1,
    )
    vectors = jnp.take(vectors, order, axis=0)
    vector = Reduction((vectors[: n_dp // 2], vectors[n_dp // 2 :]), low_first, n_dp).finish()
    triple = vector[: 3 * small].reshape(3, 2, small // 2)
    mine = lax.dynamic_index_in_dim(triple, j, 1, False)
    triple = mine + lax.ppermute(lax.dynamic_index_in_dim(triple, 1 - j, 1, False), "branch", other)
    tokens_grad = finish_grad_call(gn_own, gn_received, tokens, grads_own, gain)

    def both_halves(piece):
        shard = piece.shape[0] // 2
        mine = lax.dynamic_slice_in_dim(piece, j * shard, shard, 0)
        theirs = lax.dynamic_slice_in_dim(piece, (1 - j) * shard, shard, 0).astype(BF)
        theirs = lax.ppermute(theirs, "branch", other).astype(F32)
        return jnp.where(j == 0, mine, theirs), jnp.where(j == 0, theirs, mine)

    down_grad = down.finish()
    low, high = both_halves(up.finish())
    shard = low.shape[0]
    if fast:
        low, high = (v.reshape(shard, 4, 4, ffb).swapaxes(1, 2) for v in (low, high))
    up_grad = jnp.stack([low.reshape(shard, n_dp, ffb), high.reshape(shard, n_dp, ffb)], axis=2).reshape(shard, FF)
    route = [(2 * p + h, n_dp * h + p) for h in range(2) for p in range(n_dp)]
    proj_grad = lax.ppermute(proj.finish().astype(BF), ("dp", "branch"), route).astype(F32)
    low, high = both_halves(jnp.concatenate([query_key.finish(), value.finish()], axis=1))
    qkv_grad = jnp.stack([low.reshape(shard, 3, HALF), high.reshape(shard, 3, HALF)], axis=2).reshape(shard, 3 * D)
    return (
        layer_out,
        tokens_grad,
        triple[0],
        triple[1],
        qkv_grad,
        proj_grad,
        up_grad,
        vector[3 * small :],
        down_grad,
        triple[2],
    )


def solution(mesh):
    rows = P(("dp", "branch"), None)
    flat = P(("dp", "branch"))
    return jax.shard_map(
        functools.partial(on_device, mesh.shape["dp"]),
        mesh=mesh,
        in_specs=(rows, P("dp"), P(), P(), P(), P(), P(), P(), P(), P(), rows),
        out_specs=(rows, rows, flat, flat, rows, rows, rows, flat, rows, flat),
        check_vma=False,
    )
```

```python
import functools
import math

import jax
import jax.numpy as jnp
from jax import lax
from jax.experimental import pallas as pl
from jax.experimental.pallas import tpu as pltpu
from jax.sharding import PartitionSpec as P

D = 1024
HEADS = 16
HEAD_DIM = 64
ROT_DIM = 32
FF = 4096
SEQ_LEN = 1024
HALF = HEADS // 2 * HEAD_DIM
FF_HALF = FF // 2
LANES = 128
QB = 256
FB = 512
EPS = 1e-05
BF = jnp.bfloat16
F32 = jnp.float32


def params(mb=24):
    return pltpu.CompilerParams(vmem_limit_bytes=mb << 20)


def cost(flops, nbytes, trans=0):
    return pl.CostEstimate(flops=int(flops) // 1000, bytes_accessed=int(nbytes) // 1000, transcendentals=0)


def in_hbm(shape, dtype):
    return pltpu.HBM(tuple(shape), dtype)


def dot_nn(a, b):
    return jnp.dot(a, b, preferred_element_type=F32)


def dot_nt(a, b):
    return lax.dot_general(a, b, (((1,), (1,)), ((), ())), preferred_element_type=F32)


def dot_tn(a, b):
    return lax.dot_general(a, b, (((0,), (0,)), ((), ())), preferred_element_type=F32)


def rotary_tables():
    position = jnp.arange(SEQ_LEN, dtype=jnp.int32).astype(F32)
    lane = jnp.arange(LANES, dtype=jnp.int32)
    channel = lane % HEAD_DIM
    frequency = jnp.power(10000.0, -(2.0 * (channel // 2).astype(F32)) / ROT_DIM)
    angles = position[:, None] * frequency[None, :]
    inside = (channel < ROT_DIM)[None, :]
    cosine = jnp.where(inside, jnp.cos(angles), 1.0)
    sine = jnp.where(inside, jnp.sin(angles), 0.0)
    even = (lane % 2 == 0)[None, :]
    return cosine, jnp.where(even, -sine, sine)


def rotate(x, cosine, sine):
    even = lax.broadcasted_iota(jnp.int32, x.shape, 1) % 2 == 0
    swapped = jnp.where(even, pltpu.roll(x, LANES - 1, 1), pltpu.roll(x, 1, 1))
    return x * cosine + swapped * sine


def unrotate(y, cosine, sine):
    even = lax.broadcasted_iota(jnp.int32, y.shape, 1) % 2 == 0
    swapped = jnp.where(even, pltpu.roll(y, LANES - 1, 1), pltpu.roll(y, 1, 1))
    return y * cosine - swapped * sine


def head_lanes(shape, head):
    lane = lax.broadcasted_iota(jnp.int32, shape, 1)
    own = (lane >= HEAD_DIM) if head else (lane < HEAD_DIM)
    spare = lane - (0 if head else HEAD_DIM)
    return own, spare


def keys_with_bias(k, head, length):
    own, spare = head_lanes(k.shape, head)
    row = lax.broadcasted_iota(jnp.int32, k.shape, 0)
    bias = jnp.where(row < length, 0.0, -1e30)
    extra = jnp.where(spare < 3, 1.0, jnp.where(spare == 3, bias, 0.0))
    return jnp.where(own, k.astype(F32), extra).astype(BF)


def attend_kernel(skip, info_ref, q_ref, k_ref, v_ref, *refs):
    o_ref, qe_ref = refs[skip:]
    length = info_ref[1]
    q = q_ref[0].astype(F32)
    k = k_ref[0]
    v = v_ref[0]
    tri = lax.broadcasted_iota(jnp.int32, (QB, QB), 0) >= lax.broadcasted_iota(jnp.int32, (QB, QB), 1)
    outs = []
    for head in range(2):
        own, spare = head_lanes((SEQ_LEN, LANES), head)
        ke = keys_with_bias(k, head, length)
        qe = jnp.where(own, q, jnp.where(spare == 3, 1.0, 0.0)).astype(BF)
        parts = []
        for b in range(SEQ_LEN // QB):
            lo, hi = b * QB, (b + 1) * QB
            s = dot_nt(qe[lo:hi], ke[:hi])
            diag = jnp.where(tri, s[:, lo:hi], -1e30)
            s = diag if b == 0 else jnp.concatenate([s[:, :lo], diag], axis=1)
            top = jnp.max(s, axis=1, keepdims=True)
            p = jnp.exp(s - top)
            total = jnp.sum(p, axis=1, keepdims=True)
            parts.append(dot_nn(p.astype(BF), v[:hi]) * (1.0 / total))
            lse = jnp.broadcast_to(top + jnp.log(total), (QB, LANES))
            first = lse.astype(BF).astype(F32)
            second = (lse - first).astype(BF).astype(F32)
            third = lse - first - second
            own_b, spare_b = head_lanes((QB, LANES), head)
            extra = jnp.where(
                spare_b == 0,
                -first,
                jnp.where(
                    spare_b == 1,
                    -second,
                    jnp.where(spare_b == 2, -third, jnp.where(spare_b == 3, 1.0, 0.0)),
                ),
            )
            qe_ref[head, lo:hi, :] = jnp.where(own_b, q[lo:hi], extra).astype(BF)
        outs.append(jnp.concatenate(parts, axis=0))
    own, _ = head_lanes((SEQ_LEN, LANES), 0)
    o_ref[...] = jnp.where(own, outs[0], outs[1]).astype(BF)


def attend_call(info, part, qkv, earlier=()):
    pairs = HALF // LANES // 2
    first = part * pairs
    spec = [pl.BlockSpec((1, SEQ_LEN, LANES), lambda p, n, t=t: (t, 0, first + p)) for t in range(3)]
    return pl.pallas_call(
        functools.partial(attend_kernel, len(earlier)),
        grid_spec=pltpu.PrefetchScalarGridSpec(
            num_scalar_prefetch=1,
            grid=(pairs,),
            in_specs=spec + [pl.BlockSpec(memory_space=pl.ANY)] * len(earlier),
            out_specs=[
                pl.BlockSpec((SEQ_LEN, LANES), lambda p, n: (0, first + p)),
                pl.BlockSpec((2, SEQ_LEN, LANES), lambda p, n: (first + p, 0, 0)),
            ],
        ),
        out_shape=[
            in_hbm((SEQ_LEN, HALF), BF),
            in_hbm((HEADS // 2, SEQ_LEN, LANES), BF),
        ],
        input_output_aliases={4: 0, 5: 1} if earlier else {},
        compiler_params=params(),
        cost_estimate=cost(
            2 * pairs * 10 * SEQ_LEN * SEQ_LEN * LANES, 2 * SEQ_LEN * HALF * 3, 4 * SEQ_LEN * SEQ_LEN
        ),
        name="attend",
    )(info, qkv, qkv, qkv, *earlier)


def attend_back_kernel(info_ref, qe_ref, k_ref, v_ref, o_ref, g_ref, cos_ref, sin_ref, *refs):
    d_ref, dk_ref, dv_ref = refs[-3:]
    length = info_ref[1]
    k = k_ref[0]
    v = v_ref[0]
    g = g_ref[...].astype(F32)
    o = o_ref[...].astype(F32)
    tri = lax.broadcasted_iota(jnp.int32, (QB, QB), 0) >= lax.broadcasted_iota(jnp.int32, (QB, QB), 1)
    queries = []
    for head in range(2):
        own, spare = head_lanes((SEQ_LEN, LANES), head)
        ke = keys_with_bias(k, head, length)
        ve = jnp.where(own, v.astype(F32), jnp.where(spare < 3, 1.0, 0.0)).astype(BF)
        inner = jnp.sum(jnp.where(own, g * o, 0.0), axis=1, keepdims=True)
        inner = jnp.broadcast_to(inner, (SEQ_LEN, LANES))
        first = inner.astype(BF).astype(F32)
        second = (inner - first).astype(BF).astype(F32)
        third = inner - first - second
        extra = jnp.where(
            spare == 0,
            -first,
            jnp.where(spare == 1, -second, jnp.where(spare == 2, -third, 0.0)),
        )
        ge = jnp.where(own, g, extra).astype(BF)
        parts = []
        for b in range(SEQ_LEN // QB):
            lo, hi = b * QB, (b + 1) * QB
            qb = qe_ref[head, lo:hi, :]
            gb = ge[lo:hi]
            s = dot_nt(qb, ke[:hi])
            diag = jnp.where(tri, s[:, lo:hi], -1e30)
            s = diag if b == 0 else jnp.concatenate([s[:, :lo], diag], axis=1)
            p = jnp.exp(s)
            ds = (p * dot_nt(gb, ve[:hi])).astype(BF)
            parts.append(dot_nn(ds, k[:hi]))
            dk = dot_tn(ds, qb)
            dv = dot_tn(p.astype(BF), gb)
            if b > 0:
                dk_ref[head, :lo] += dk[:lo]
                dv_ref[head, :lo] += dv[:lo]
            dk_ref[head, lo:hi] = dk[lo:hi]
            dv_ref[head, lo:hi] = dv[lo:hi]
        queries.append(jnp.concatenate(parts, axis=0))
    own, _ = head_lanes((SEQ_LEN, LANES), 0)
    cosine, sine = cos_ref[...], sin_ref[...]
    dq = jnp.where(own, queries[0], queries[1]) * HEAD_DIM**-0.5
    d_ref[0] = unrotate(dq, cosine, sine).astype(BF)
    d_ref[1] = unrotate(jnp.where(own, dk_ref[0], dk_ref[1]), cosine, sine).astype(BF)
    d_ref[2] = jnp.where(own, dv_ref[0], dv_ref[1]).astype(BF)


def attend_back_call(info, part, qe, qkv, context, grad_context, cosine, sine, earlier=()):
    pairs = HALF // LANES // 2
    first = part * pairs
    table = pl.BlockSpec((SEQ_LEN, LANES), lambda p, n: (0, 0))
    return pl.pallas_call(
        attend_back_kernel,
        grid_spec=pltpu.PrefetchScalarGridSpec(
            num_scalar_prefetch=1,
            grid=(pairs,),
            in_specs=[
                pl.BlockSpec((2, SEQ_LEN, LANES), lambda p, n: (first + p, 0, 0)),
                pl.BlockSpec((1, SEQ_LEN, LANES), lambda p, n: (1, 0, first + p)),
                pl.BlockSpec((1, SEQ_LEN, LANES), lambda p, n: (2, 0, first + p)),
                pl.BlockSpec((SEQ_LEN, LANES), lambda p, n: (0, first + p)),
                pl.BlockSpec((SEQ_LEN, LANES), lambda p, n: (0, first + p)),
                table,
                table,
            ]
            + [pl.BlockSpec(memory_space=pl.ANY)] * len(earlier),
            out_specs=pl.BlockSpec((3, SEQ_LEN, LANES), lambda p, n: (0, 0, first + p)),
            scratch_shapes=[
                pltpu.VMEM((2, SEQ_LEN, LANES), F32),
                pltpu.VMEM((2, SEQ_LEN, LANES), F32),
            ],
        ),
        out_shape=jax.ShapeDtypeStruct((3, SEQ_LEN, HALF), BF),
        input_output_aliases={8: 0} if earlier else {},
        compiler_params=params(),
        cost_estimate=cost(
            2 * pairs * 12 * SEQ_LEN * SEQ_LEN * LANES, 2 * SEQ_LEN * HALF * 4, 4 * SEQ_LEN * SEQ_LEN
        ),
        name="attend_back",
    )(info, qe, qkv, qkv, context, grad_context, cosine, sine, *earlier)


def gelu_parts(v):
    c = math.sqrt(2.0 / math.pi)
    square = v * v
    t = jnp.tanh(v * (c + (c * 0.044715) * square))
    half = 0.5 * (1.0 + t)
    slope = half + (0.5 * v) * (1.0 - t * t) * (c + (3.0 * c * 0.044715) * square)
    return v * half, slope


def normalize(x):
    x = x.astype(F32)
    centred = x - jnp.mean(x, axis=1, keepdims=True)
    rstd = lax.rsqrt(jnp.mean(centred * centred, axis=1, keepdims=True) + EPS)
    return centred * rstd, rstd


def masked_rows(g, start, length):
    row = start + lax.broadcasted_iota(jnp.int32, g.shape, 0)
    return jnp.where(row < length, g.astype(F32), 0.0)


def joined(refs, axis):
    return refs[0][...] if len(refs) == 1 else jnp.concatenate([r[...] for r in refs], axis=axis)


def weight_specs(plan, rows_too=True):
    splits, wide, pick = plan["splits"], FB // plan["splits"], plan["pick"]
    specs = [pl.BlockSpec((D, wide), lambda s, *a, i=i: (0, pick(s, a, i))) for i in range(splits)]
    specs += [pl.BlockSpec((wide, D), lambda s, *a, i=i: (pick(s, a, i), 0)) for i in range(splits)]
    if rows_too:
        specs += [pl.BlockSpec((1, wide), lambda s, *a, i=i: (0, pick(s, a, i))) for i in range(splits)]
    return specs


def accumulate(ref, value):
    @pl.when(pl.program_id(0) == 0)
    def _():
        ref[...] = value

    @pl.when(pl.program_id(0) > 0)
    def _():
        ref[...] += value


def mlp_own_kernel(splits, info_ref, cls_ref, t_ref, c_ref, gain_ref, shift_ref, *refs):
    ups, downs, biases = refs[:splits], refs[splits : 2 * splits], refs[2 * splits : 3 * splits]
    x_ref, h_ref, g_ref, gb_ref, e_ref, gn_ref, outer_ref = refs[3 * splits :]

    @pl.when(pl.program_id(0) == 0)
    def _():
        hat, _ = normalize(t_ref[...])
        x_ref[...] = (hat * gain_ref[...].astype(F32) + shift_ref[...].astype(F32)).astype(BF)
        g = masked_rows(c_ref[...], info_ref[0] * c_ref.shape[0], info_ref[1])
        g_ref[...] = g.astype(BF)
        outer_ref[...] = jnp.sum(g, axis=0, keepdims=True)

    up, down, bias = joined(ups, 1), joined(downs, 0), joined(biases, 1)
    before = dot_nn(x_ref[...], up) + bias.astype(F32)
    hidden, slope = gelu_parts(before)
    hidden = hidden.astype(BF)
    grad_before = (dot_nt(g_ref[...], down) * slope).astype(BF)
    h_ref[...] = hidden
    gb_ref[...] = grad_before
    accumulate(e_ref, dot_nn(hidden, down))
    accumulate(gn_ref, dot_nt(grad_before, up))


def mlp_own_call(info, plan, tokens, cotangent, gain, shift):
    rows, splits = tokens.shape[0], plan["splits"]
    fixed = lambda s, *a: (0, 0)
    up, down, bias = plan["weights"]
    whole = pl.BlockSpec((rows, D), fixed)
    wide = pl.BlockSpec((rows, FB), lambda s, *a: (0, s))
    return pl.pallas_call(
        functools.partial(mlp_own_kernel, splits),
        grid_spec=pltpu.PrefetchScalarGridSpec(
            num_scalar_prefetch=2,
            grid=(FF_HALF // FB,),
            in_specs=[whole, whole, pl.BlockSpec((1, D), fixed), pl.BlockSpec((1, D), fixed)] + weight_specs(plan),
            out_specs=[whole, wide, whole, wide, whole, whole, pl.BlockSpec((1, D), fixed)],
        ),
        out_shape=[
            jax.ShapeDtypeStruct((2 * rows, D), BF),
            in_hbm((2 * rows, FF_HALF), BF),
            in_hbm((rows, D), BF),
            in_hbm((rows, FF_HALF), BF),
            in_hbm((rows, D), F32),
            in_hbm((rows, D), F32),
            jax.ShapeDtypeStruct((1, D), F32),
        ],
        compiler_params=params(),
        cost_estimate=cost(8 * rows * D * FF_HALF, 12 * rows * D + 4 * D * FF_HALF, rows * FF_HALF),
        name="mlp_own",
    )(info, plan["classes"], tokens, cotangent, gain, shift, *([up] * splits), *([down] * splits), *([bias] * splits))


def mlp_forward_kernel(splits, info_ref, cls_ref, t_ref, gain_ref, shift_ref, *refs):
    ups, downs, biases = refs[:splits], refs[splits : 2 * splits], refs[2 * splits : 3 * splits]
    x_ref, h_ref, slope_ref, e_ref = refs[3 * splits + 2 :]

    @pl.when(pl.program_id(0) == 0)
    def _():
        hat, _ = normalize(t_ref[...])
        x_ref[...] = (hat * gain_ref[...].astype(F32) + shift_ref[...].astype(F32)).astype(BF)

    up, down, bias = joined(ups, 1), joined(downs, 0), joined(biases, 1)
    before = dot_nn(x_ref[...], up) + bias.astype(F32)
    hidden, slope = gelu_parts(before)
    hidden = hidden.astype(BF)
    h_ref[...] = hidden
    slope_ref[...] = slope.astype(BF)
    accumulate(e_ref, dot_nn(hidden, down))


def mlp_forward_call(info, plan, tokens, gain, shift, normed, hidden):
    rows, splits = tokens.shape[0], plan["splits"]
    fixed = lambda s, *a: (0, 0)
    up, down, bias = plan["weights"]
    whole = pl.BlockSpec((rows, D), fixed)
    anywhere = pl.BlockSpec(memory_space=pl.ANY)
    first = 5 + 3 * splits
    return pl.pallas_call(
        functools.partial(mlp_forward_kernel, splits),
        grid_spec=pltpu.PrefetchScalarGridSpec(
            num_scalar_prefetch=2,
            grid=(FF_HALF // FB,),
            in_specs=[whole, pl.BlockSpec((1, D), fixed), pl.BlockSpec((1, D), fixed)]
            + weight_specs(plan)
            + [anywhere, anywhere],
            out_specs=[
                pl.BlockSpec((rows, D), lambda s, *a: (1, 0)),
                pl.BlockSpec((rows, FB), lambda s, *a: (1, s)),
                pl.BlockSpec((rows, FB), lambda s, *a: (0, s)),
                whole,
            ],
        ),
        out_shape=[
            jax.ShapeDtypeStruct((2 * rows, D), BF),
            in_hbm((2 * rows, FF_HALF), BF),
            in_hbm((rows, FF_HALF), BF),
            in_hbm((rows, D), F32),
        ],
        input_output_aliases={first: 0, first + 1: 1},
        compiler_params=params(),
        cost_estimate=cost(4 * rows * D * FF_HALF, 12 * rows * D + 4 * D * FF_HALF, rows * FF_HALF),
        name="mlp_forward",
    )(info, plan["classes"], tokens, gain, shift, *([up] * splits), *([down] * splits), *([bias] * splits), normed, hidden)


def down_grad_kernel(splits, pieces, info_ref, cls_ref, sub_ref, h_ref, go_ref, c_ref, g_ref, *grads):
    rows = c_ref.shape[0]
    step = pl.program_id(0)

    @pl.when(step == 0)
    def _():
        g_ref[:rows] = go_ref[...]
        g_ref[rows:] = masked_rows(c_ref[...], (1 - info_ref[0]) * rows, info_ref[1]).astype(BF)

    grad_down = dot_tn(h_ref[...], g_ref[...]).astype(BF)
    if not pieces:
        grads[0][...] = grad_down
        return
    down_keep, down_send = grads
    block = FB // splits

    @pl.when(step < 2)
    def _():
        for i in range(splits):
            down_send[sub_ref[i]] = grad_down[i * block : (i + 1) * block]

    @pl.when(step >= 2)
    def _():
        for i in range(splits):
            down_keep[sub_ref[i]] = grad_down[i * block : (i + 1) * block]


def down_grad_call(info, plan, hidden, grads_own, cotangent):
    rows, splits, pieces = cotangent.shape[0], plan["splits"], plan["pieces"]
    fixed = lambda s, *a: (0, 0)
    whole = pl.BlockSpec((rows, D), fixed)
    out_specs = [pl.BlockSpec((2 * rows, D), fixed)]
    out_shape = [in_hbm((2 * rows, D), BF)]
    if pieces:
        half, down_rows = pieces // 2, FF_HALF // pieces
        out_specs += [
            pl.BlockSpec((splits, down_rows, D), lambda s, *a: (jnp.maximum(s - 2, 0), 0, 0)),
            pl.BlockSpec((splits, down_rows, D), lambda s, *a: (jnp.minimum(s, 1), 0, 0)),
        ]
        out_shape += [in_hbm((half, down_rows, D), BF)] * 2
    else:
        out_specs += [pl.BlockSpec((FB, D), lambda s, *a: (s, 0))]
        out_shape += [in_hbm((FF_HALF, D), BF)]
    return pl.pallas_call(
        functools.partial(down_grad_kernel, splits, pieces),
        grid_spec=pltpu.PrefetchScalarGridSpec(
            num_scalar_prefetch=3,
            grid=(FF_HALF // FB,),
            in_specs=[pl.BlockSpec((2 * rows, FB), lambda s, *a: (0, s)), whole, whole],
            out_specs=out_specs,
        ),
        out_shape=out_shape,
        compiler_params=params(),
        cost_estimate=cost(4 * rows * D * FF_HALF, 8 * rows * D + 2 * D * FF_HALF + 4 * rows * FF_HALF),
        name="down_grad",
    )(info, plan["classes"], plan["subs"], hidden, grads_own, cotangent)


def mlp_back_kernel(splits, pieces, info_ref, cls_ref, ord_ref, x_ref, slope_ref, g_ref, gb_ref, *refs):
    ups, downs = refs[:splits], refs[splits : 2 * splits]
    gn_ref, inner_ref, *grads = refs[2 * splits : -2 if pieces else -1]
    gball_ref = refs[-2 if pieces else -1]
    rows = g_ref.shape[0]
    up, down = joined(ups, 1), joined(downs, 0)
    grad_before = (dot_nt(g_ref[...], down) * slope_ref[...].astype(F32)).astype(BF)
    gball_ref[:rows] = gb_ref[...]
    gball_ref[rows:] = grad_before
    accumulate(gn_ref, dot_nt(grad_before, up))
    inner_ref[...] = jnp.sum(gball_ref[...].astype(F32), axis=0, keepdims=True)
    grad_up = dot_tn(x_ref[...], gball_ref[...]).astype(BF)
    if not pieces:
        grads[0][...] = grad_up
        return
    up_keep, up_send = grads
    upall_ref = refs[-1]
    upall_ref[...] = grad_up.reshape(upall_ref.shape)
    for q in range(pieces // 2):
        up_keep[q] = upall_ref[ord_ref[q]]
        up_send[q] = upall_ref[ord_ref[q + pieces // 2]]


def mlp_back_call(info, plan, normed, slope, grads, gb_own):
    rows, splits, pieces = gb_own.shape[0], plan["splits"], plan["pieces"]
    fixed = lambda s, *a: (0, 0)
    up, down, _ = plan["weights"]
    whole = pl.BlockSpec((rows, D), fixed)
    wide = pl.BlockSpec((rows, FB), lambda s, *a: (0, s))
    out_specs = [whole, pl.BlockSpec((1, FB), lambda s, i, cls, *a: (0, cls[s]))]
    out_shape = [in_hbm((rows, D), F32), jax.ShapeDtypeStruct((1, FF_HALF), F32)]
    scratch = [pltpu.VMEM((2 * rows, FB), BF)]
    if pieces:
        shape = (pieces // 2, D // pieces, FB)
        out_specs += [pl.BlockSpec(shape, lambda s, i, cls, *a: (0, 0, cls[s]))] * 2
        out_shape += [in_hbm(shape[:2] + (FF_HALF,), BF)] * 2
        scratch.append(pltpu.VMEM((pieces, D // pieces, FB), BF))
    else:
        out_specs += [pl.BlockSpec((D, FB), lambda s, *a: (0, s))]
        out_shape += [in_hbm((D, FF_HALF), BF)]
    return pl.pallas_call(
        functools.partial(mlp_back_kernel, splits, pieces),
        grid_spec=pltpu.PrefetchScalarGridSpec(
            num_scalar_prefetch=3,
            grid=(FF_HALF // FB,),
            in_specs=[
                pl.BlockSpec((2 * rows, D), fixed),
                wide,
                pl.BlockSpec((rows, D), lambda s, *a: (1, 0)),
                wide,
            ]
            + weight_specs(plan, False),
            out_specs=out_specs,
            scratch_shapes=scratch,
        ),
        out_shape=out_shape,
        compiler_params=params(),
        cost_estimate=cost(8 * rows * D * FF_HALF, 12 * rows * D + 6 * D * FF_HALF + 4 * rows * FF_HALF),
        name="mlp_back",
    )(info, plan["classes"], plan["order"], normed, slope, grads, gb_own, *([up] * splits), *([down] * splits))


def qkv_half_kernel(place_ref, info_ref, x_ref, w_ref, cos_ref, sin_ref, *refs):
    o_ref = refs[-1]
    t = pl.program_id(0)
    chunk = 2 * LANES

    @pl.when(t == 2)
    def _():
        for c in range(0, HALF, chunk):
            o_ref[0, :, c : c + chunk] = dot_nn(x_ref[...], w_ref[:, c : c + chunk]).astype(BF)

    @pl.when(t < 2)
    def _():
        scale = jnp.where(t == 0, HEAD_DIM**-0.5, 1.0)
        cosine = cos_ref[...] * scale
        sine = sin_ref[...] * scale
        for c in range(0, HALF, chunk):
            mixed = dot_nn(x_ref[...], w_ref[:, c : c + chunk])
            for e in range(0, chunk, LANES):
                o_ref[0, :, c + e : c + e + LANES] = rotate(mixed[:, e : e + LANES], cosine, sine).astype(BF)


def qkv_half_call(place, info, half, normed, w, cosine, sine, qkv=None):
    rows = normed.shape[0] // 2
    table = pl.BlockSpec((rows, LANES), lambda t, p, i: (p[0], 0))
    more = [] if qkv is None else [qkv]
    return pl.pallas_call(
        qkv_half_kernel,
        grid_spec=pltpu.PrefetchScalarGridSpec(
            num_scalar_prefetch=2,
            grid=(3,),
            in_specs=[
                pl.BlockSpec((rows, D), lambda t, p, i: (half, 0)),
                pl.BlockSpec((D, HALF), lambda t, p, i: (0, 2 * t + i[0])),
                table,
                table,
            ]
            + [pl.BlockSpec(memory_space=pl.ANY)] * len(more),
            out_specs=pl.BlockSpec((1, rows, HALF), lambda t, p, i: (t, p[0], 0)),
        ),
        out_shape=in_hbm((3, 2 * rows, HALF), BF),
        input_output_aliases={6: 0} if more else {},
        compiler_params=params(),
        cost_estimate=cost(2 * rows * D * 3 * HALF, 2 * (rows * D + D * 3 * HALF + rows * 3 * HALF)),
        name="qkv",
    )(place, info, normed, w, cosine, sine, *more)


def send_out_kernel(place_ref, info_ref, c_ref, w_ref, e_ref, o_ref):
    o_ref[...] = (dot_nn(c_ref[...], w_ref[...]) + e_ref[...]).astype(BF)


def finish_out_kernel(place_ref, info_ref, c_ref, w_ref, e_ref, t_ref, r_ref, bias_ref, o_ref):
    total = dot_nn(c_ref[...], w_ref[...]) + e_ref[...] + bias_ref[...].astype(F32)
    o_ref[...] = (total + t_ref[...].astype(F32) + r_ref[...].astype(F32)).astype(BF)


def out_call(place, info, context, proj, expanded, rest=()):
    rows, block = expanded.shape[0], 256
    steps = rows // block
    row = pl.BlockSpec((block, D), lambda s, p, i: (s, 0))
    return pl.pallas_call(
        finish_out_kernel if rest else send_out_kernel,
        grid_spec=pltpu.PrefetchScalarGridSpec(
            num_scalar_prefetch=2,
            grid=(steps,),
            in_specs=[
                pl.BlockSpec((block, HALF), lambda s, p, i: (p[0] * steps + s, 0)),
                pl.BlockSpec((HALF, D), lambda s, p, i: (i[0], 0)),
                row,
            ]
            + ([row, row, pl.BlockSpec((1, D), lambda s, p, i: (0, 0))] if rest else []),
            out_specs=row,
        ),
        out_shape=in_hbm((rows, D), BF),
        compiler_params=params(),
        cost_estimate=cost(2 * rows * D * HALF, 8 * rows * D + 2 * HALF * D),
        name="finish_out" if rest else "send_out",
    )(place, info, context, proj, expanded, *rest)


def proj_back_kernel(info_ref, ord_ref, g_ref, c_ref, w_ref, gc_ref, *refs):
    acc_ref = refs[-2] if len(refs) > 2 else refs[-1]
    gc_ref[...] = dot_nt(g_ref[...], w_ref[...]).astype(BF)
    part = dot_tn(c_ref[...], g_ref[...])

    @pl.when(pl.program_id(0) == 0)
    def _():
        acc_ref[...] = part

    @pl.when(pl.program_id(0) == 1)
    def _():
        total = (acc_ref[...] + part).astype(BF)
        if len(refs) == 2:
            refs[0][...] = total
        else:
            keep, send, all_ref = refs[0], refs[1], refs[3]
            all_ref[...] = total.reshape(all_ref.shape)
            half = keep.shape[0]
            for q in range(half):
                keep[q] = all_ref[ord_ref[q]]
                send[q] = all_ref[ord_ref[q + half]]


def proj_back_call(info, plan, order, grads, context, proj):
    rows, pieces = grads.shape[0] // 2, plan["pieces"]
    scratch = [pltpu.VMEM((HALF, D), F32)]
    if pieces:
        shape = (pieces // 2, HALF // pieces, D)
        out_specs = [pl.BlockSpec(shape, lambda h, *a: (0, 0, 0))] * 2
        out_shape = [in_hbm(shape, BF)] * 2
        scratch.append(pltpu.VMEM((pieces, HALF // pieces, D), BF))
    else:
        out_specs = [pl.BlockSpec((HALF, D), lambda h, *a: (0, 0))]
        out_shape = [in_hbm((HALF, D), BF)]
    return pl.pallas_call(
        proj_back_kernel,
        grid_spec=pltpu.PrefetchScalarGridSpec(
            num_scalar_prefetch=2,
            grid=(2,),
            in_specs=[
                pl.BlockSpec((rows, D), lambda h, i, o: (h, 0)),
                pl.BlockSpec((rows, HALF), lambda h, i, o: (jnp.bitwise_xor(h, i[0]), 0)),
                pl.BlockSpec((HALF, D), lambda h, i, o: (i[0], 0)),
            ],
            out_specs=[pl.BlockSpec((rows, HALF), lambda h, i, o: (jnp.bitwise_xor(h, i[0]), 0))] + out_specs,
            scratch_shapes=scratch,
        ),
        out_shape=[in_hbm((2 * rows, HALF), BF)] + out_shape,
        compiler_params=params(),
        cost_estimate=cost(8 * rows * D * HALF, 4 * rows * D + 8 * rows * HALF + 4 * HALF * D),
        name="proj_back",
    )(info, order, grads, context, proj)


def qkv_grad_kernel(info_ref, ord_ref, x_ref, own_ref, their_ref, *refs):
    d = jnp.concatenate([own_ref[0], their_ref[0]], axis=0)
    total = dot_tn(x_ref[...], d).astype(BF)
    if len(refs) == 1:
        refs[0][...] = total
        return
    keep, send, all_ref = refs
    all_ref[...] = total.reshape(all_ref.shape)
    half = keep.shape[0]
    for q in range(half):
        keep[q] = all_ref[ord_ref[q]]
        send[q] = all_ref[ord_ref[q + half]]


def qkv_grad_call(info, plan, order, normed, dmix, first, count):
    rows, pieces = normed.shape[0] // 2, plan["pieces"]
    scratch = []
    if pieces:
        shape = (pieces // 2, D // pieces, HALF)
        out_specs = [pl.BlockSpec(shape, lambda t, *a: (0, 0, t))] * 2
        out_shape = [in_hbm(shape[:2] + (count * HALF,), BF)] * 2
        scratch = [pltpu.VMEM((pieces, D // pieces, HALF), BF)]
    else:
        out_specs = [pl.BlockSpec((D, HALF), lambda t, *a: (0, t))]
        out_shape = [in_hbm((D, count * HALF), BF)]
    return pl.pallas_call(
        qkv_grad_kernel,
        grid_spec=pltpu.PrefetchScalarGridSpec(
            num_scalar_prefetch=2,
            grid=(count,),
            in_specs=[
                pl.BlockSpec((2 * rows, D), lambda t, i, o: (0, 0)),
                pl.BlockSpec((1, rows, HALF), lambda t, i, o: (first + t, i[0], 0)),
                pl.BlockSpec((1, rows, HALF), lambda t, i, o: (first + t, 1 - i[0], 0)),
            ],
            out_specs=out_specs,
            scratch_shapes=scratch,
        ),
        out_shape=out_shape,
        compiler_params=params(),
        cost_estimate=cost(4 * rows * D * count * HALF, 4 * rows * D + (4 * rows + 2 * D) * count * HALF),
        name="qkv_grad",
    )(info, order, normed, dmix, dmix)


def grad_normed_kernel(place_ref, info_ref, d_ref, wq_ref, wk_ref, wv_ref, base_ref, t_ref, o_ref, sum_ref):
    total = base_ref[...]
    for t, w in enumerate((wq_ref, wk_ref, wv_ref)):
        total += dot_nt(d_ref[t], w[...])
    o_ref[...] = total.astype(o_ref.dtype)
    hat, _ = normalize(t_ref[...])
    sums = jnp.concatenate([jnp.sum(total * hat, axis=0, keepdims=True), jnp.sum(total, axis=0, keepdims=True)], axis=0)
    accumulate(sum_ref, sums)


def grad_normed_call(place, info, dmix, w, base, tokens, kind):
    rows, block = base.shape[0], 256
    steps = rows // block
    row = pl.BlockSpec((block, D), lambda r, p, i: (r, 0))
    return pl.pallas_call(
        grad_normed_kernel,
        grid_spec=pltpu.PrefetchScalarGridSpec(
            num_scalar_prefetch=2,
            grid=(steps,),
            in_specs=[pl.BlockSpec((3, block, HALF), lambda r, p, i: (0, p[0] * steps + r, 0))]
            + [pl.BlockSpec((D, HALF), lambda r, p, i, t=t: (0, 2 * t + i[0])) for t in range(3)]
            + [row, row],
            out_specs=[row, pl.BlockSpec((2, D), lambda r, p, i: (0, 0))],
        ),
        out_shape=[in_hbm((rows, D), kind), jax.ShapeDtypeStruct((2, D), F32)],
        compiler_params=params(),
        cost_estimate=cost(2 * rows * D * 3 * HALF, 8 * rows * D + 6 * D * HALF + 6 * rows * HALF),
        name="grad_normed",
    )(place, info, dmix, w, w, w, base, tokens)


def finish_grad_kernel(gn_ref, r_ref, t_ref, g_ref, gain_ref, o_ref):
    hat, rstd = normalize(t_ref[...])
    u = (gn_ref[...] + r_ref[...].astype(F32)) * gain_ref[...].astype(F32)
    inner = u - jnp.mean(u, axis=1, keepdims=True) - hat * jnp.mean(u * hat, axis=1, keepdims=True)
    o_ref[...] = g_ref[...].astype(F32) + inner * rstd


def finish_grad_call(grad_normed, received, tokens, grads, gain):
    rows, block = tokens.shape[0], 256
    row = pl.BlockSpec((block, D), lambda r: (r, 0))
    return pl.pallas_call(
        finish_grad_kernel,
        grid=(rows // block,),
        in_specs=[row, row, row, row, pl.BlockSpec((1, D), lambda r: (0, 0))],
        out_specs=row,
        out_shape=in_hbm((rows, D), F32),
        compiler_params=params(),
        cost_estimate=cost(20 * rows * D, 14 * rows * D),
        name="finish_grad",
    )(grad_normed, received, tokens, grads, gain)


class Reduction:
    def __init__(self, keep, send, stages, n_dp):
        self.keep, self.sends, self.stages, self.n_dp = keep, [send], list(stages), n_dp
        self.start()

    def start(self):
        offsets = self.stages.pop(0)
        self.flying = [
            lax.ppermute(part, "dp", [(i, i ^ offset) for i in range(self.n_dp)])
            for part, offset in zip(self.sends, offsets, strict=True)
        ]

    def land(self):
        kind = self.flying[0].dtype
        total = self.keep.astype(F32)
        for part in self.flying:
            total = total + part.astype(F32)
        if not self.stages:
            self.keep, self.sends = total[0], []
            return (self.keep,)
        count = total.shape[0] // (len(self.stages[0]) + 1)
        parts = [total[i : i + count].astype(kind) for i in range(0, total.shape[0], count)]
        self.keep, self.sends = parts[0], parts[1:]
        self.start()
        return tuple(parts)

    def finish(self):
        while self.sends:
            self.land()
        return self.keep


def after(x, *done):
    return lax.optimization_barrier((x, *done))[0]


def send_order(stages, me):
    table = [0]
    for offsets in stages:
        table = [r ^ offset for r in table for offset in (0, *offsets)]
    return jnp.bitwise_xor(jnp.array(table, jnp.int32), me)


def pairs_of_bits(bits):
    stages = []
    for i in range(0, len(bits), 2):
        if i + 1 < len(bits):
            stages.append((bits[i], bits[i + 1], bits[i] ^ bits[i + 1]))
        else:
            stages.append((bits[i],))
    return stages


def on_device(n_dp, tokens, lengths, norm_gain, norm_shift, qkv_weight, proj_weight, up_weight, inner_bias,
              down_weight, outer_bias, cotangent):
    j = lax.axis_index("branch").astype(jnp.int32)
    me = lax.axis_index("dp").astype(jnp.int32)
    other = [(0, 1), (1, 0)]
    tokens_their = lax.ppermute(tokens, "branch", other)
    cotangent_their = lax.ppermute(cotangent, "branch", other)
    own, their = j.reshape(1), (1 - j).reshape(1)
    info = jnp.stack([j, lengths[0].astype(jnp.int32)])
    gain, shift = norm_gain.reshape(1, D), norm_shift.reshape(1, D)

    bits = [1 << i for i in range(n_dp.bit_length() - 1)]
    high_stages = pairs_of_bits(bits[2:])
    low_first = [(1,), (2,)] + high_stages
    high_first = [(1,)] + high_stages + [(2,)]
    order = send_order(low_first, me)
    order_high = send_order(high_first, me)
    ffb = FF_HALF // n_dp
    fast = ffb == LANES
    if fast:
        splits = FB // LANES
        plan = {
            "splits": splits,
            "pieces": n_dp,
            "pick": lambda s, a, i: 2 * (4 * i + a[1][s]) + a[0][0],
            "classes": jnp.array([1, 3, 0, 2], jnp.int32) ^ (me & 3),
            "subs": jnp.arange(4, dtype=jnp.int32) ^ (me >> 2),
            "weights": (up_weight, down_weight, inner_bias.reshape(1, FF)),
        }
    else:
        plan = {
            "splits": 1,
            "pieces": 0,
            "pick": lambda s, a, i: s,
            "classes": jnp.arange(FF_HALF // FB, dtype=jnp.int32),
            "subs": jnp.zeros((1,), jnp.int32),
            "weights": (
                lax.dynamic_index_in_dim(up_weight.reshape(D, n_dp, 2, ffb), j, 2, False).reshape(D, FF_HALF),
                lax.dynamic_index_in_dim(down_weight.reshape(n_dp, 2, ffb, D), j, 1, False).reshape(FF_HALF, D),
                lax.dynamic_index_in_dim(inner_bias.reshape(n_dp, 2, ffb), j, 1, False).reshape(1, FF_HALF),
            ),
        }
    plan["order"] = order

    def pieces_of(grads, table):
        if len(grads) == 2:
            return grads
        whole = grads[0]
        ordered = jnp.take(whole.reshape(n_dp, whole.shape[0] // n_dp, whole.shape[1]), table, axis=0)
        return ordered[: n_dp // 2], ordered[n_dp // 2 :]

    plan["weights"] = tuple(pltpu.with_memory_space_constraint(w, pltpu.HBM) for w in plan["weights"][:2]) + plan["weights"][2:]
    qkv_weight = pltpu.with_memory_space_constraint(qkv_weight, pltpu.HBM)
    proj_weight = pltpu.with_memory_space_constraint(proj_weight, pltpu.HBM)

    cosine, sine = rotary_tables()
    normed, hidden, grads_own, gb_own, expanded_own, gn_own, outer = mlp_own_call(
        info, plan, tokens, cotangent, gain, shift
    )
    qkv = qkv_half_call(own, info, 0, normed, qkv_weight, cosine, sine)
    info = after(info, qkv)
    normed, hidden, slope, expanded_their = mlp_forward_call(info, plan, tokens_their, gain, shift, normed, hidden)
    info = after(info, slope)
    grads, *down = down_grad_call(info, plan, hidden, grads_own, cotangent_their)
    down = Reduction(*pieces_of(down, order), low_first, n_dp)
    info = after(info, grads)
    gn_their, inner, *up = mlp_back_call(info, plan, normed, slope, grads, gb_own)

    info = after(info, gn_their, *down.land())
    up = Reduction(*pieces_of(up, order), low_first, n_dp)
    qkv = qkv_half_call(their, info, 1, normed, qkv_weight, cosine, sine, qkv)
    attended = attend_call(info, 0, qkv)
    context, qe = attend_call(info, 1, qkv, attended)
    out_their = out_call(their, info, context, proj_weight, expanded_their)

    info = after(info, out_their, *down.land(), *up.land())
    out_received = lax.ppermute(out_their, "branch", other)
    grad_context, *proj = proj_back_call(info, plan, order_high, grads, context, proj_weight)
    dmix = attend_back_call(info, 0, qe, qkv, context, grad_context, cosine, sine)
    dmix = attend_back_call(info, 1, qe, qkv, context, grad_context, cosine, sine, (dmix,))

    info = after(info, dmix, *up.land(), *down.land())
    proj = Reduction(*pieces_of(proj, order_high), high_first, n_dp)
    gn_send, sums_their = grad_normed_call(their, info, dmix, qkv_weight, gn_their, tokens_their, BF)
    info = after(info, gn_send)
    value = pieces_of(qkv_grad_call(info, plan, order_high, normed, dmix, 2, 1), order_high)
    query_key = pieces_of(qkv_grad_call(info, plan, order, normed, dmix, 0, 2), order)

    info = after(info, *value, *query_key, *proj.land())
    gn_received = lax.ppermute(gn_send, "branch", other)
    value = Reduction(*value, high_first, n_dp)
    query_key = Reduction(*query_key, low_first, n_dp)
    gn_own, sums_own = grad_normed_call(own, info, dmix, qkv_weight, gn_own, tokens, F32)

    info = after(info, gn_own, *value.land(), *query_key.land())
    small = D // n_dp
    sums = sums_own + sums_their
    if fast:
        inner = inner.reshape(4, 4, ffb).transpose(1, 0, 2)
    vectors = jnp.concatenate(
        [
            sums[0].reshape(n_dp, small),
            sums[1].reshape(n_dp, small),
            outer.reshape(n_dp, small),
            inner.reshape(n_dp, ffb),
        ],
        axis=1,
    )
    vectors = jnp.take(vectors, order_high, axis=0)
    vectors = Reduction(vectors[: n_dp // 2], vectors[n_dp // 2 :], high_first, n_dp)
    layer_out = out_call(
        own, info, context, proj_weight, expanded_own, (tokens, out_received, outer_bias.reshape(1, D))
    )
    vector = vectors.finish()
    triple = vector[: 3 * small].reshape(3, 2, small // 2)
    mine = lax.dynamic_index_in_dim(triple, j, 1, False)
    triple = mine + lax.ppermute(lax.dynamic_index_in_dim(triple, 1 - j, 1, False), "branch", other)
    tokens_grad = finish_grad_call(gn_own, gn_received, tokens, grads_own, gain)

    def both_halves(piece):
        shard = piece.shape[0] // 2
        mine = lax.dynamic_slice_in_dim(piece, j * shard, shard, 0)
        theirs = lax.dynamic_slice_in_dim(piece, (1 - j) * shard, shard, 0).astype(BF)
        theirs = lax.ppermute(theirs, "branch", other).astype(F32)
        return jnp.where(j == 0, mine, theirs), jnp.where(j == 0, theirs, mine)

    down_grad = down.finish()
    low, high = both_halves(up.finish())
    shard = low.shape[0]
    if fast:
        low, high = (v.reshape(shard, 4, 4, ffb).swapaxes(1, 2) for v in (low, high))
    up_grad = jnp.stack([low.reshape(shard, n_dp, ffb), high.reshape(shard, n_dp, ffb)], axis=2).reshape(shard, FF)
    route = [(2 * p + h, n_dp * h + p) for h in range(2) for p in range(n_dp)]
    proj_grad = lax.ppermute(proj.finish().astype(BF), ("dp", "branch"), route).astype(F32)
    low, high = both_halves(jnp.concatenate([query_key.finish(), value.finish()], axis=1))
    qkv_grad = jnp.stack([low.reshape(shard, 3, HALF), high.reshape(shard, 3, HALF)], axis=2).reshape(shard, 3 * D)
    return (
        layer_out,
        tokens_grad,
        triple[0],
        triple[1],
        qkv_grad,
        proj_grad,
        up_grad,
        vector[3 * small :],
        down_grad,
        triple[2],
    )


def solution(mesh):
    rows = P(("dp", "branch"), None)
    flat = P(("dp", "branch"))
    return jax.shard_map(
        functools.partial(on_device, mesh.shape["dp"]),
        mesh=mesh,
        in_specs=(rows, P("dp"), P(), P(), P(), P(), P(), P(), P(), P(), rows),
        out_specs=(rows, rows, flat, flat, rows, rows, rows, flat, rows, flat),
        check_vma=False,
    )
```

```python
import functools
import math

import jax
import jax.numpy as jnp
from jax import lax
from jax.experimental import pallas as pl
from jax.experimental.pallas import tpu as pltpu
from jax.sharding import PartitionSpec as P

D = 1024
HEADS = 16
HEAD_DIM = 64
ROT_DIM = 32
FF = 4096
SEQ_LEN = 1024
HALF = HEADS // 2 * HEAD_DIM
FF_HALF = FF // 2
LANES = 128
QB = 256
FB = 512
EPS = 1e-05
BF = jnp.bfloat16
F32 = jnp.float32


def params(mb=24):
    return pltpu.CompilerParams(vmem_limit_bytes=mb << 20)


def duration(us):
    return pl.CostEstimate(flops=int(us * 1e9), bytes_accessed=1, transcendentals=0)


def in_hbm(shape, dtype):
    return pltpu.HBM(tuple(shape), dtype)


def dot_nn(a, b):
    return jnp.dot(a, b, preferred_element_type=F32)


def dot_nt(a, b):
    return lax.dot_general(a, b, (((1,), (1,)), ((), ())), preferred_element_type=F32)


def dot_tn(a, b):
    return lax.dot_general(a, b, (((0,), (0,)), ((), ())), preferred_element_type=F32)


def rotary_tables():
    position = jnp.arange(SEQ_LEN, dtype=jnp.int32).astype(F32)
    lane = jnp.arange(LANES, dtype=jnp.int32)
    channel = lane % HEAD_DIM
    frequency = jnp.power(10000.0, -(2.0 * (channel // 2).astype(F32)) / ROT_DIM)
    angles = position[:, None] * frequency[None, :]
    inside = (channel < ROT_DIM)[None, :]
    cosine = jnp.where(inside, jnp.cos(angles), 1.0)
    sine = jnp.where(inside, jnp.sin(angles), 0.0)
    even = (lane % 2 == 0)[None, :]
    return cosine, jnp.where(even, -sine, sine)


def rotate(x, cosine, sine):
    even = lax.broadcasted_iota(jnp.int32, x.shape, 1) % 2 == 0
    swapped = jnp.where(even, pltpu.roll(x, LANES - 1, 1), pltpu.roll(x, 1, 1))
    return x * cosine + swapped * sine


def unrotate(y, cosine, sine):
    even = lax.broadcasted_iota(jnp.int32, y.shape, 1) % 2 == 0
    swapped = jnp.where(even, pltpu.roll(y, LANES - 1, 1), pltpu.roll(y, 1, 1))
    return y * cosine - swapped * sine


def head_lanes(shape, head):
    lane = lax.broadcasted_iota(jnp.int32, shape, 1)
    own = (lane >= HEAD_DIM) if head else (lane < HEAD_DIM)
    spare = lane - (0 if head else HEAD_DIM)
    return own, spare


def keys_with_bias(k, head, length):
    own, spare = head_lanes(k.shape, head)
    row = lax.broadcasted_iota(jnp.int32, k.shape, 0)
    bias = jnp.where(row < length, 0.0, -1e30)
    extra = jnp.where(spare < 3, 1.0, jnp.where(spare == 3, bias, 0.0))
    return jnp.where(own, k.astype(F32), extra).astype(BF)


def attend_kernel(info_ref, q_ref, k_ref, v_ref, o_ref, qe_ref):
    length = info_ref[1]
    q = q_ref[0].astype(F32)
    k = k_ref[0]
    v = v_ref[0]
    tri = lax.broadcasted_iota(jnp.int32, (QB, QB), 0) >= lax.broadcasted_iota(jnp.int32, (QB, QB), 1)
    outs = []
    for head in range(2):
        own, spare = head_lanes((SEQ_LEN, LANES), head)
        ke = keys_with_bias(k, head, length)
        qe = jnp.where(own, q, jnp.where(spare == 3, 1.0, 0.0)).astype(BF)
        parts = []
        for b in range(SEQ_LEN // QB):
            lo, hi = b * QB, (b + 1) * QB
            s = dot_nt(qe[lo:hi], ke[:hi])
            diag = jnp.where(tri, s[:, lo:hi], -1e30)
            s = diag if b == 0 else jnp.concatenate([s[:, :lo], diag], axis=1)
            top = jnp.max(s, axis=1, keepdims=True)
            p = jnp.exp(s - top)
            total = jnp.sum(p, axis=1, keepdims=True)
            parts.append(dot_nn(p.astype(BF), v[:hi]) * (1.0 / total))
            lse = jnp.broadcast_to(top + jnp.log(total), (QB, LANES))
            first = lse.astype(BF).astype(F32)
            second = (lse - first).astype(BF).astype(F32)
            third = lse - first - second
            own_b, spare_b = head_lanes((QB, LANES), head)
            extra = jnp.where(
                spare_b == 0,
                -first,
                jnp.where(
                    spare_b == 1,
                    -second,
                    jnp.where(spare_b == 2, -third, jnp.where(spare_b == 3, 1.0, 0.0)),
                ),
            )
            qe_ref[head, lo:hi, :] = jnp.where(own_b, q[lo:hi], extra).astype(BF)
        outs.append(jnp.concatenate(parts, axis=0))
    own, _ = head_lanes((SEQ_LEN, LANES), 0)
    o_ref[...] = jnp.where(own, outs[0], outs[1]).astype(BF)


def attend_call(info, qkv):
    pairs = HALF // LANES
    spec = [pl.BlockSpec((1, SEQ_LEN, LANES), lambda p, n, t=t: (t, 0, p)) for t in range(3)]
    return pl.pallas_call(
        attend_kernel,
        grid_spec=pltpu.PrefetchScalarGridSpec(
            num_scalar_prefetch=1,
            grid=(pairs,),
            in_specs=spec,
            out_specs=[
                pl.BlockSpec((SEQ_LEN, LANES), lambda p, n: (0, p)),
                pl.BlockSpec((2, SEQ_LEN, LANES), lambda p, n: (p, 0, 0)),
            ],
        ),
        out_shape=[
            in_hbm((SEQ_LEN, HALF), BF),
            in_hbm((HEADS // 2, SEQ_LEN, LANES), BF),
        ],
        compiler_params=params(),
        cost_estimate=duration(4.28),
        name="attend",
    )(info, qkv, qkv, qkv)


def attend_back_kernel(info_ref, qe_ref, k_ref, v_ref, o_ref, g_ref, cos_ref, sin_ref, d_ref, dk_ref, dv_ref):
    length = info_ref[1]
    k = k_ref[0]
    v = v_ref[0]
    g = g_ref[...].astype(F32)
    o = o_ref[...].astype(F32)
    tri = lax.broadcasted_iota(jnp.int32, (QB, QB), 0) >= lax.broadcasted_iota(jnp.int32, (QB, QB), 1)
    queries = []
    for head in range(2):
        own, spare = head_lanes((SEQ_LEN, LANES), head)
        ke = keys_with_bias(k, head, length)
        ve = jnp.where(own, v.astype(F32), jnp.where(spare < 3, 1.0, 0.0)).astype(BF)
        inner = jnp.sum(jnp.where(own, g * o, 0.0), axis=1, keepdims=True)
        inner = jnp.broadcast_to(inner, (SEQ_LEN, LANES))
        first = inner.astype(BF).astype(F32)
        second = (inner - first).astype(BF).astype(F32)
        third = inner - first - second
        extra = jnp.where(
            spare == 0,
            -first,
            jnp.where(spare == 1, -second, jnp.where(spare == 2, -third, 0.0)),
        )
        ge = jnp.where(own, g, extra).astype(BF)
        parts = []
        for b in range(SEQ_LEN // QB):
            lo, hi = b * QB, (b + 1) * QB
            qb = qe_ref[head, lo:hi, :]
            gb = ge[lo:hi]
            s = dot_nt(qb, ke[:hi])
            diag = jnp.where(tri, s[:, lo:hi], -1e30)
            s = diag if b == 0 else jnp.concatenate([s[:, :lo], diag], axis=1)
            p = jnp.exp(s)
            ds = (p * dot_nt(gb, ve[:hi])).astype(BF)
            parts.append(dot_nn(ds, k[:hi]))
            dk = dot_tn(ds, qb)
            dv = dot_tn(p.astype(BF), gb)
            if b > 0:
                dk_ref[head, :lo] += dk[:lo]
                dv_ref[head, :lo] += dv[:lo]
            dk_ref[head, lo:hi] = dk[lo:hi]
            dv_ref[head, lo:hi] = dv[lo:hi]
        queries.append(jnp.concatenate(parts, axis=0))
    own, _ = head_lanes((SEQ_LEN, LANES), 0)
    cosine, sine = cos_ref[...], sin_ref[...]
    dq = jnp.where(own, queries[0], queries[1]) * HEAD_DIM**-0.5
    d_ref[0] = unrotate(dq, cosine, sine).astype(BF)
    d_ref[1] = unrotate(jnp.where(own, dk_ref[0], dk_ref[1]), cosine, sine).astype(BF)
    d_ref[2] = jnp.where(own, dv_ref[0], dv_ref[1]).astype(BF)


def attend_back_call(info, qe, qkv, context, grad_context, cosine, sine):
    pairs = HALF // LANES
    table = pl.BlockSpec((SEQ_LEN, LANES), lambda p, n: (0, 0))
    return pl.pallas_call(
        attend_back_kernel,
        grid_spec=pltpu.PrefetchScalarGridSpec(
            num_scalar_prefetch=1,
            grid=(pairs,),
            in_specs=[
                pl.BlockSpec((2, SEQ_LEN, LANES), lambda p, n: (p, 0, 0)),
                pl.BlockSpec((1, SEQ_LEN, LANES), lambda p, n: (1, 0, p)),
                pl.BlockSpec((1, SEQ_LEN, LANES), lambda p, n: (2, 0, p)),
                pl.BlockSpec((SEQ_LEN, LANES), lambda p, n: (0, p)),
                pl.BlockSpec((SEQ_LEN, LANES), lambda p, n: (0, p)),
                table,
                table,
            ],
            out_specs=pl.BlockSpec((3, SEQ_LEN, LANES), lambda p, n: (0, 0, p)),
            scratch_shapes=[
                pltpu.VMEM((2, SEQ_LEN, LANES), F32),
                pltpu.VMEM((2, SEQ_LEN, LANES), F32),
            ],
        ),
        out_shape=jax.ShapeDtypeStruct((3, SEQ_LEN, HALF), BF),
        compiler_params=params(),
        cost_estimate=duration(4.80),
        name="attend_back",
    )(info, qe, qkv, qkv, context, grad_context, cosine, sine)


def gelu_parts(v):
    c = math.sqrt(2.0 / math.pi)
    square = v * v
    t = jnp.tanh(v * (c + (c * 0.044715) * square))
    half = 0.5 * (1.0 + t)
    slope = half + (0.5 * v) * (1.0 - t * t) * (c + (3.0 * c * 0.044715) * square)
    return v * half, slope


def normalize(x):
    x = x.astype(F32)
    centred = x - jnp.mean(x, axis=1, keepdims=True)
    rstd = lax.rsqrt(jnp.mean(centred * centred, axis=1, keepdims=True) + EPS)
    return centred * rstd, rstd


def masked_rows(g, start, length):
    row = start + lax.broadcasted_iota(jnp.int32, g.shape, 0)
    return jnp.where(row < length, g.astype(F32), 0.0)


def joined(refs, axis):
    return refs[0][...] if len(refs) == 1 else jnp.concatenate([r[...] for r in refs], axis=axis)


def weight_specs(plan, rows_too=True):
    splits, wide, pick = plan["splits"], FB // plan["splits"], plan["pick"]
    specs = [pl.BlockSpec((D, wide), lambda s, *a, i=i: (0, pick(s, a, i))) for i in range(splits)]
    specs += [pl.BlockSpec((wide, D), lambda s, *a, i=i: (pick(s, a, i), 0)) for i in range(splits)]
    if rows_too:
        specs += [pl.BlockSpec((1, wide), lambda s, *a, i=i: (0, pick(s, a, i))) for i in range(splits)]
    return specs


def accumulate(ref, value):
    @pl.when(pl.program_id(0) == 0)
    def _():
        ref[...] = value

    @pl.when(pl.program_id(0) > 0)
    def _():
        ref[...] += value


def mlp_own_kernel(splits, info_ref, cls_ref, t_ref, c_ref, gain_ref, shift_ref, *refs):
    ups, downs, biases = refs[:splits], refs[splits : 2 * splits], refs[2 * splits : 3 * splits]
    x_ref, h_ref, g_ref, gb_ref, e_ref, gn_ref, outer_ref = refs[3 * splits :]

    @pl.when(pl.program_id(0) == 0)
    def _():
        hat, _ = normalize(t_ref[...])
        x_ref[...] = (hat * gain_ref[...].astype(F32) + shift_ref[...].astype(F32)).astype(BF)
        g = masked_rows(c_ref[...], info_ref[0] * c_ref.shape[0], info_ref[1])
        g_ref[...] = g.astype(BF)
        outer_ref[...] = jnp.sum(g, axis=0, keepdims=True)

    up, down, bias = joined(ups, 1), joined(downs, 0), joined(biases, 1)
    before = dot_nn(x_ref[...], up) + bias.astype(F32)
    hidden, slope = gelu_parts(before)
    hidden = hidden.astype(BF)
    grad_before = (dot_nt(g_ref[...], down) * slope).astype(BF)
    h_ref[...] = hidden
    gb_ref[...] = grad_before
    accumulate(e_ref, dot_nn(hidden, down))
    accumulate(gn_ref, dot_nt(grad_before, up))


def mlp_own_call(info, plan, tokens, cotangent, gain, shift):
    rows, splits = tokens.shape[0], plan["splits"]
    fixed = lambda s, *a: (0, 0)
    up, down, bias = plan["weights"]
    whole = pl.BlockSpec((rows, D), fixed)
    wide = pl.BlockSpec((rows, FB), lambda s, *a: (0, s))
    return pl.pallas_call(
        functools.partial(mlp_own_kernel, splits),
        grid_spec=pltpu.PrefetchScalarGridSpec(
            num_scalar_prefetch=2,
            grid=(FF_HALF // FB,),
            in_specs=[whole, whole, pl.BlockSpec((1, D), fixed), pl.BlockSpec((1, D), fixed)] + weight_specs(plan),
            out_specs=[whole, wide, whole, wide, whole, whole, pl.BlockSpec((1, D), fixed)],
        ),
        out_shape=[
            jax.ShapeDtypeStruct((2 * rows, D), BF),
            in_hbm((2 * rows, FF_HALF), BF),
            in_hbm((rows, D), BF),
            in_hbm((rows, FF_HALF), BF),
            in_hbm((rows, D), F32),
            in_hbm((rows, D), F32),
            jax.ShapeDtypeStruct((1, D), F32),
        ],
        compiler_params=params(),
        cost_estimate=duration(4.75),
        name="mlp_own",
    )(info, plan["classes"], tokens, cotangent, gain, shift, *([up] * splits), *([down] * splits), *([bias] * splits))


def mlp_forward_kernel(splits, info_ref, cls_ref, t_ref, gain_ref, shift_ref, *refs):
    ups, downs, biases = refs[:splits], refs[splits : 2 * splits], refs[2 * splits : 3 * splits]
    x_ref, h_ref, slope_ref, e_ref = refs[3 * splits + 2 :]

    @pl.when(pl.program_id(0) == 0)
    def _():
        hat, _ = normalize(t_ref[...])
        x_ref[...] = (hat * gain_ref[...].astype(F32) + shift_ref[...].astype(F32)).astype(BF)

    up, down, bias = joined(ups, 1), joined(downs, 0), joined(biases, 1)
    before = dot_nn(x_ref[...], up) + bias.astype(F32)
    hidden, slope = gelu_parts(before)
    hidden = hidden.astype(BF)
    h_ref[...] = hidden
    slope_ref[...] = slope.astype(BF)
    accumulate(e_ref, dot_nn(hidden, down))


def mlp_forward_call(info, plan, tokens, gain, shift, normed, hidden):
    rows, splits = tokens.shape[0], plan["splits"]
    fixed = lambda s, *a: (0, 0)
    up, down, bias = plan["weights"]
    whole = pl.BlockSpec((rows, D), fixed)
    anywhere = pl.BlockSpec(memory_space=pl.ANY)
    first = 5 + 3 * splits
    return pl.pallas_call(
        functools.partial(mlp_forward_kernel, splits),
        grid_spec=pltpu.PrefetchScalarGridSpec(
            num_scalar_prefetch=2,
            grid=(FF_HALF // FB,),
            in_specs=[whole, pl.BlockSpec((1, D), fixed), pl.BlockSpec((1, D), fixed)]
            + weight_specs(plan)
            + [anywhere, anywhere],
            out_specs=[
                pl.BlockSpec((rows, D), lambda s, *a: (1, 0)),
                pl.BlockSpec((rows, FB), lambda s, *a: (1, s)),
                pl.BlockSpec((rows, FB), lambda s, *a: (0, s)),
                whole,
            ],
        ),
        out_shape=[
            jax.ShapeDtypeStruct((2 * rows, D), BF),
            in_hbm((2 * rows, FF_HALF), BF),
            in_hbm((rows, FF_HALF), BF),
            in_hbm((rows, D), F32),
        ],
        input_output_aliases={first: 0, first + 1: 1},
        compiler_params=params(),
        cost_estimate=duration(3.25),
        name="mlp_forward",
    )(info, plan["classes"], tokens, gain, shift, *([up] * splits), *([down] * splits), *([bias] * splits), normed, hidden)


def down_grad_kernel(splits, pieces, info_ref, cls_ref, sub_ref, h_ref, go_ref, c_ref, g_ref, *grads):
    rows = c_ref.shape[0]
    step = pl.program_id(0)

    @pl.when(step == 0)
    def _():
        g_ref[:rows] = go_ref[...]
        g_ref[rows:] = masked_rows(c_ref[...], (1 - info_ref[0]) * rows, info_ref[1]).astype(BF)

    grad_down = dot_tn(h_ref[...], g_ref[...]).astype(BF)
    if not pieces:
        grads[0][...] = grad_down
        return
    down_keep, down_send = grads
    block = FB // splits

    @pl.when(step < 2)
    def _():
        for i in range(splits):
            down_send[sub_ref[i]] = grad_down[i * block : (i + 1) * block]

    @pl.when(step >= 2)
    def _():
        for i in range(splits):
            down_keep[sub_ref[i]] = grad_down[i * block : (i + 1) * block]


def down_grad_call(info, plan, hidden, grads_own, cotangent):
    rows, splits, pieces = cotangent.shape[0], plan["splits"], plan["pieces"]
    fixed = lambda s, *a: (0, 0)
    whole = pl.BlockSpec((rows, D), fixed)
    out_specs = [pl.BlockSpec((2 * rows, D), fixed)]
    out_shape = [in_hbm((2 * rows, D), BF)]
    if pieces:
        half, down_rows = pieces // 2, FF_HALF // pieces
        out_specs += [
            pl.BlockSpec((splits, down_rows, D), lambda s, *a: (jnp.maximum(s - 2, 0), 0, 0)),
            pl.BlockSpec((splits, down_rows, D), lambda s, *a: (jnp.minimum(s, 1), 0, 0)),
        ]
        out_shape += [in_hbm((half, down_rows, D), BF)] * 2
    else:
        out_specs += [pl.BlockSpec((FB, D), lambda s, *a: (s, 0))]
        out_shape += [in_hbm((FF_HALF, D), BF)]
    return pl.pallas_call(
        functools.partial(down_grad_kernel, splits, pieces),
        grid_spec=pltpu.PrefetchScalarGridSpec(
            num_scalar_prefetch=3,
            grid=(FF_HALF // FB,),
            in_specs=[pl.BlockSpec((2 * rows, FB), lambda s, *a: (0, s)), whole, whole],
            out_specs=out_specs,
        ),
        out_shape=out_shape,
        compiler_params=params(),
        cost_estimate=duration(2.60),
        name="down_grad",
    )(info, plan["classes"], plan["subs"], hidden, grads_own, cotangent)


def mlp_back_kernel(splits, pieces, info_ref, cls_ref, ord_ref, x_ref, slope_ref, g_ref, gb_ref, *refs):
    ups, downs = refs[:splits], refs[splits : 2 * splits]
    gn_ref, inner_ref, *grads = refs[2 * splits : -2 if pieces else -1]
    gball_ref = refs[-2 if pieces else -1]
    rows = g_ref.shape[0]
    up, down = joined(ups, 1), joined(downs, 0)
    grad_before = (dot_nt(g_ref[...], down) * slope_ref[...].astype(F32)).astype(BF)
    gball_ref[:rows] = gb_ref[...]
    gball_ref[rows:] = grad_before
    accumulate(gn_ref, dot_nt(grad_before, up))
    inner_ref[...] = jnp.sum(gball_ref[...].astype(F32), axis=0, keepdims=True)
    grad_up = dot_tn(x_ref[...], gball_ref[...]).astype(BF)
    if not pieces:
        grads[0][...] = grad_up
        return
    up_keep, up_send = grads
    upall_ref = refs[-1]
    upall_ref[...] = grad_up.reshape(upall_ref.shape)
    for q in range(pieces // 2):
        up_keep[q] = upall_ref[ord_ref[q]]
        up_send[q] = upall_ref[ord_ref[q + pieces // 2]]


def mlp_back_call(info, plan, normed, slope, grads, gb_own):
    rows, splits, pieces = gb_own.shape[0], plan["splits"], plan["pieces"]
    fixed = lambda s, *a: (0, 0)
    up, down, _ = plan["weights"]
    whole = pl.BlockSpec((rows, D), fixed)
    wide = pl.BlockSpec((rows, FB), lambda s, *a: (0, s))
    out_specs = [whole, pl.BlockSpec((1, FB), lambda s, i, cls, *a: (0, cls[s]))]
    out_shape = [in_hbm((rows, D), F32), jax.ShapeDtypeStruct((1, FF_HALF), F32)]
    scratch = [pltpu.VMEM((2 * rows, FB), BF)]
    if pieces:
        shape = (pieces // 2, D // pieces, FB)
        out_specs += [pl.BlockSpec(shape, lambda s, i, cls, *a: (0, 0, cls[s]))] * 2
        out_shape += [in_hbm(shape[:2] + (FF_HALF,), BF)] * 2
        scratch.append(pltpu.VMEM((pieces, D // pieces, FB), BF))
    else:
        out_specs += [pl.BlockSpec((D, FB), lambda s, *a: (0, s))]
        out_shape += [in_hbm((D, FF_HALF), BF)]
    return pl.pallas_call(
        functools.partial(mlp_back_kernel, splits, pieces),
        grid_spec=pltpu.PrefetchScalarGridSpec(
            num_scalar_prefetch=3,
            grid=(FF_HALF // FB,),
            in_specs=[
                pl.BlockSpec((2 * rows, D), fixed),
                wide,
                pl.BlockSpec((rows, D), lambda s, *a: (1, 0)),
                wide,
            ]
            + weight_specs(plan, False),
            out_specs=out_specs,
            scratch_shapes=scratch,
        ),
        out_shape=out_shape,
        compiler_params=params(),
        cost_estimate=duration(3.92),
        name="mlp_back",
    )(info, plan["classes"], plan["order"], normed, slope, grads, gb_own, *([up] * splits), *([down] * splits))


def qkv_half_kernel(place_ref, info_ref, x_ref, w_ref, cos_ref, sin_ref, *refs):
    o_ref = refs[-1]
    t = pl.program_id(0)
    chunk = 2 * LANES

    @pl.when(t == 2)
    def _():
        for c in range(0, HALF, chunk):
            o_ref[0, :, c : c + chunk] = dot_nn(x_ref[...], w_ref[:, c : c + chunk]).astype(BF)

    @pl.when(t < 2)
    def _():
        scale = jnp.where(t == 0, HEAD_DIM**-0.5, 1.0)
        cosine = cos_ref[...] * scale
        sine = sin_ref[...] * scale
        for c in range(0, HALF, chunk):
            mixed = dot_nn(x_ref[...], w_ref[:, c : c + chunk])
            for e in range(0, chunk, LANES):
                o_ref[0, :, c + e : c + e + LANES] = rotate(mixed[:, e : e + LANES], cosine, sine).astype(BF)


def qkv_half_call(place, info, half, normed, w, cosine, sine, qkv=None):
    rows = normed.shape[0] // 2
    table = pl.BlockSpec((rows, LANES), lambda t, p, i: (p[0], 0))
    more = [] if qkv is None else [qkv]
    return pl.pallas_call(
        qkv_half_kernel,
        grid_spec=pltpu.PrefetchScalarGridSpec(
            num_scalar_prefetch=2,
            grid=(3,),
            in_specs=[
                pl.BlockSpec((rows, D), lambda t, p, i: (half, 0)),
                pl.BlockSpec((D, HALF), lambda t, p, i: (0, 2 * t + i[0])),
                table,
                table,
            ]
            + [pl.BlockSpec(memory_space=pl.ANY)] * len(more),
            out_specs=pl.BlockSpec((1, rows, HALF), lambda t, p, i: (t, p[0], 0)),
        ),
        out_shape=in_hbm((3, 2 * rows, HALF), BF),
        input_output_aliases={6: 0} if more else {},
        compiler_params=params(),
        cost_estimate=duration(1.50),
        name="qkv",
    )(place, info, normed, w, cosine, sine, *more)


def send_out_kernel(place_ref, info_ref, c_ref, w_ref, e_ref, o_ref):
    o_ref[...] = (dot_nn(c_ref[...], w_ref[...]) + e_ref[...]).astype(BF)


def finish_out_kernel(place_ref, info_ref, c_ref, w_ref, e_ref, t_ref, r_ref, bias_ref, o_ref):
    total = dot_nn(c_ref[...], w_ref[...]) + e_ref[...] + bias_ref[...].astype(F32)
    o_ref[...] = (total + t_ref[...].astype(F32) + r_ref[...].astype(F32)).astype(BF)


def out_call(place, info, context, proj, expanded, rest=()):
    rows, block = expanded.shape[0], 256
    steps = rows // block
    row = pl.BlockSpec((block, D), lambda s, p, i: (s, 0))
    return pl.pallas_call(
        finish_out_kernel if rest else send_out_kernel,
        grid_spec=pltpu.PrefetchScalarGridSpec(
            num_scalar_prefetch=2,
            grid=(steps,),
            in_specs=[
                pl.BlockSpec((block, HALF), lambda s, p, i: (p[0] * steps + s, 0)),
                pl.BlockSpec((HALF, D), lambda s, p, i: (i[0], 0)),
                row,
            ]
            + ([row, row, pl.BlockSpec((1, D), lambda s, p, i: (0, 0))] if rest else []),
            out_specs=row,
        ),
        out_shape=in_hbm((rows, D), BF),
        compiler_params=params(),
        cost_estimate=duration(0.90),
        name="finish_out" if rest else "send_out",
    )(place, info, context, proj, expanded, *rest)


def proj_back_kernel(info_ref, ord_ref, g_ref, c_ref, w_ref, gc_ref, *refs):
    acc_ref = refs[-2] if len(refs) > 2 else refs[-1]
    gc_ref[...] = dot_nt(g_ref[...], w_ref[...]).astype(BF)
    part = dot_tn(c_ref[...], g_ref[...])

    @pl.when(pl.program_id(0) == 0)
    def _():
        acc_ref[...] = part

    @pl.when(pl.program_id(0) == 1)
    def _():
        total = (acc_ref[...] + part).astype(BF)
        if len(refs) == 2:
            refs[0][...] = total
        else:
            keep, send, all_ref = refs[0], refs[1], refs[3]
            rows = all_ref.shape[1] // 2
            all_ref[:, :rows] = total[:, :HALF].reshape(all_ref.shape[0], rows, HALF)
            all_ref[:, rows:] = total[:, HALF:].reshape(all_ref.shape[0], rows, HALF)
            half = keep.shape[0]
            for q in range(half):
                keep[q] = all_ref[ord_ref[q]]
                send[q] = all_ref[ord_ref[q + half]]


def proj_back_call(info, plan, order, grads, context, proj):
    rows, pieces = grads.shape[0] // 2, plan["pieces"]
    scratch = [pltpu.VMEM((HALF, D), F32)]
    if pieces:
        shape = (pieces // 2, D // pieces, HALF)
        out_specs = [pl.BlockSpec(shape, lambda h, *a: (0, 0, 0))] * 2
        out_shape = [in_hbm(shape, BF)] * 2
        scratch.append(pltpu.VMEM((pieces, D // pieces, HALF), BF))
    else:
        out_specs = [pl.BlockSpec((HALF, D), lambda h, *a: (0, 0))]
        out_shape = [in_hbm((HALF, D), BF)]
    return pl.pallas_call(
        proj_back_kernel,
        grid_spec=pltpu.PrefetchScalarGridSpec(
            num_scalar_prefetch=2,
            grid=(2,),
            in_specs=[
                pl.BlockSpec((rows, D), lambda h, i, o: (h, 0)),
                pl.BlockSpec((rows, HALF), lambda h, i, o: (jnp.bitwise_xor(h, i[0]), 0)),
                pl.BlockSpec((HALF, D), lambda h, i, o: (i[0], 0)),
            ],
            out_specs=[pl.BlockSpec((rows, HALF), lambda h, i, o: (jnp.bitwise_xor(h, i[0]), 0))] + out_specs,
            scratch_shapes=scratch,
        ),
        out_shape=[in_hbm((2 * rows, HALF), BF)] + out_shape,
        compiler_params=params(),
        cost_estimate=duration(1.62),
        name="proj_back",
    )(info, order, grads, context, proj)


def qkv_grad_kernel(info_ref, ord_ref, x_ref, own_ref, their_ref, *refs):
    d = jnp.concatenate([own_ref[0], their_ref[0]], axis=0)
    total = dot_tn(x_ref[...], d).astype(BF)
    if len(refs) == 1:
        refs[0][...] = total
        return
    keep, send, all_ref = refs
    all_ref[...] = total.reshape(all_ref.shape)
    half = keep.shape[0]
    for q in range(half):
        keep[q] = all_ref[ord_ref[q]]
        send[q] = all_ref[ord_ref[q + half]]


def qkv_grad_call(info, plan, order, normed, dmix, first, count):
    rows, pieces = normed.shape[0] // 2, plan["pieces"]
    scratch = []
    if pieces:
        shape = (pieces // 2, D // pieces, HALF)
        out_specs = [pl.BlockSpec(shape, lambda t, *a: (0, 0, t))] * 2
        out_shape = [in_hbm(shape[:2] + (count * HALF,), BF)] * 2
        scratch = [pltpu.VMEM((pieces, D // pieces, HALF), BF)]
    else:
        out_specs = [pl.BlockSpec((D, HALF), lambda t, *a: (0, t))]
        out_shape = [in_hbm((D, count * HALF), BF)]
    return pl.pallas_call(
        qkv_grad_kernel,
        grid_spec=pltpu.PrefetchScalarGridSpec(
            num_scalar_prefetch=2,
            grid=(count,),
            in_specs=[
                pl.BlockSpec((2 * rows, D), lambda t, i, o: (0, 0)),
                pl.BlockSpec((1, rows, HALF), lambda t, i, o: (first + t, i[0], 0)),
                pl.BlockSpec((1, rows, HALF), lambda t, i, o: (first + t, 1 - i[0], 0)),
            ],
            out_specs=out_specs,
            scratch_shapes=scratch,
        ),
        out_shape=out_shape,
        compiler_params=params(),
        cost_estimate=duration(1.05),
        name="qkv_grad",
    )(info, order, normed, dmix, dmix)


def value_grad_kernel(info_ref, ord_ref, x_ref, own_ref, their_ref, pk_ref, ps_ref, so_ref, st_ref, outer_ref,
                      inner_ref, keep, send, all_ref):
    pieces, rows = all_ref.shape[0], x_ref.shape[1] // all_ref.shape[0]
    d = jnp.concatenate([own_ref[0], their_ref[0]], axis=0)
    all_ref[:, :rows] = dot_tn(x_ref[...], d).astype(BF).reshape(pieces, rows, HALF)
    sums = so_ref[...] + st_ref[...]
    outer = outer_ref[...]
    low = lax.broadcasted_iota(jnp.int32, (1, LANES), 1) < rows
    for p in range(pieces):
        at = p // 2 * LANES
        three = [v[:, at : at + LANES] for v in (sums[0:1], sums[1:2], outer)]
        turned = [pltpu.roll(v, rows, 1) for v in three]
        if p % 2:
            three, turned = turned, three
        inner = inner_ref[:, p % 4 * HALF + p // 4 * LANES : p % 4 * HALF + p // 4 * LANES + LANES]
        line = jnp.concatenate(
            [
                jnp.where(low, three[0], turned[1]),
                jnp.where(low, three[2], 0.0),
                inner,
                jnp.zeros((1, LANES), F32),
            ],
            axis=1,
        )
        all_ref[p, rows:] = jnp.broadcast_to(line, (16, HALF)).astype(BF)
    half = pieces // 2
    for q in range(half):
        for out, proj, at in ((keep, pk_ref, q), (send, ps_ref, q + half)):
            piece = all_ref[ord_ref[at]]
            out[q, :rows] = piece[:rows]
            out[q, rows : 2 * rows] = proj[q]
            out[q, 2 * rows :] = piece[rows:]


def value_grad_call(info, plan, order, normed, dmix, proj, vectors):
    rows, pieces = normed.shape[0] // 2, plan["pieces"]
    height = D // pieces
    shape = (pieces // 2, 2 * height + 16, HALF)
    whole = [pl.BlockSpec(v.shape, lambda t, i, o, n=v.ndim: (0,) * n) for v in (*proj, *vectors)]
    return pl.pallas_call(
        value_grad_kernel,
        grid_spec=pltpu.PrefetchScalarGridSpec(
            num_scalar_prefetch=2,
            grid=(1,),
            in_specs=[
                pl.BlockSpec((2 * rows, D), lambda t, i, o: (0, 0)),
                pl.BlockSpec((1, rows, HALF), lambda t, i, o: (2, i[0], 0)),
                pl.BlockSpec((1, rows, HALF), lambda t, i, o: (2, 1 - i[0], 0)),
            ]
            + whole,
            out_specs=[pl.BlockSpec(shape, lambda t, *a: (0, 0, 0))] * 2,
            scratch_shapes=[pltpu.VMEM((pieces, height + 16, HALF), BF)],
        ),
        out_shape=[in_hbm(shape, BF)] * 2,
        compiler_params=params(),
        cost_estimate=duration(0.82),
        name="value_grad",
    )(info, order, normed, dmix, dmix, *proj, *vectors)


def grad_normed_kernel(place_ref, info_ref, d_ref, wq_ref, wk_ref, wv_ref, base_ref, t_ref, o_ref, sum_ref):
    total = base_ref[...]
    for t, w in enumerate((wq_ref, wk_ref, wv_ref)):
        total += dot_nt(d_ref[t], w[...])
    o_ref[...] = total.astype(o_ref.dtype)
    hat, _ = normalize(t_ref[...])
    sums = jnp.concatenate([jnp.sum(total * hat, axis=0, keepdims=True), jnp.sum(total, axis=0, keepdims=True)], axis=0)
    accumulate(sum_ref, sums)


def grad_normed_call(place, info, dmix, w, base, tokens, kind):
    rows, block = base.shape[0], 256
    steps = rows // block
    row = pl.BlockSpec((block, D), lambda r, p, i: (r, 0))
    return pl.pallas_call(
        grad_normed_kernel,
        grid_spec=pltpu.PrefetchScalarGridSpec(
            num_scalar_prefetch=2,
            grid=(steps,),
            in_specs=[pl.BlockSpec((3, block, HALF), lambda r, p, i: (0, p[0] * steps + r, 0))]
            + [pl.BlockSpec((D, HALF), lambda r, p, i, t=t: (0, 2 * t + i[0])) for t in range(3)]
            + [row, row],
            out_specs=[row, pl.BlockSpec((2, D), lambda r, p, i: (0, 0))],
        ),
        out_shape=[in_hbm((rows, D), kind), jax.ShapeDtypeStruct((2, D), F32)],
        compiler_params=params(),
        cost_estimate=duration(1.45),
        name="grad_normed",
    )(place, info, dmix, w, w, w, base, tokens)


def finish_grad_kernel(gn_ref, r_ref, t_ref, g_ref, gain_ref, o_ref):
    hat, rstd = normalize(t_ref[...])
    u = (gn_ref[...] + r_ref[...].astype(F32)) * gain_ref[...].astype(F32)
    inner = u - jnp.mean(u, axis=1, keepdims=True) - hat * jnp.mean(u * hat, axis=1, keepdims=True)
    o_ref[...] = g_ref[...].astype(F32) + inner * rstd


def finish_grad_call(grad_normed, received, tokens, grads, gain):
    rows, block = tokens.shape[0], 256
    row = pl.BlockSpec((block, D), lambda r: (r, 0))
    return pl.pallas_call(
        finish_grad_kernel,
        grid=(rows // block,),
        in_specs=[row, row, row, row, pl.BlockSpec((1, D), lambda r: (0, 0))],
        out_specs=row,
        out_shape=in_hbm((rows, D), F32),
        compiler_params=params(),
        cost_estimate=duration(0.62),
        name="finish_grad",
    )(grad_normed, received, tokens, grads, gain)


class Reduction:
    def __init__(self, keep, send, stages, n_dp):
        self.keep, self.sends, self.stages, self.n_dp = keep, [send], list(stages), n_dp
        self.start()

    def start(self):
        offsets = self.stages.pop(0)
        self.flying = [
            lax.ppermute(part, "dp", [(i, i ^ offset) for i in range(self.n_dp)])
            for part, offset in zip(self.sends, offsets, strict=True)
        ]

    def land(self):
        kind = self.flying[0].dtype
        total = self.keep.astype(F32)
        for part in self.flying:
            total = total + part.astype(F32)
        if not self.stages:
            self.keep, self.sends = total[0], []
            return (self.keep,)
        count = total.shape[0] // (len(self.stages[0]) + 1)
        parts = [total[i : i + count].astype(kind) for i in range(0, total.shape[0], count)]
        self.keep, self.sends = parts[0], parts[1:]
        self.start()
        return tuple(parts)

    def finish(self):
        while self.sends:
            self.land()
        return self.keep


def after(x, *done):
    return lax.optimization_barrier((x, *done))[0]


def send_order(stages, me):
    table = [0]
    for offsets in stages:
        table = [r ^ offset for r in table for offset in (0, *offsets)]
    return jnp.bitwise_xor(jnp.array(table, jnp.int32), me)


def pairs_of_bits(bits):
    stages = []
    for i in range(0, len(bits), 2):
        if i + 1 < len(bits):
            stages.append((bits[i], bits[i + 1], bits[i] ^ bits[i + 1]))
        else:
            stages.append((bits[i],))
    return stages


def on_device(n_dp, tokens, lengths, norm_gain, norm_shift, qkv_weight, proj_weight, up_weight, inner_bias,
              down_weight, outer_bias, cotangent):
    j = lax.axis_index("branch").astype(jnp.int32)
    me = lax.axis_index("dp").astype(jnp.int32)
    other = [(0, 1), (1, 0)]
    tokens_their = lax.ppermute(tokens, "branch", other)
    cotangent_their = lax.ppermute(cotangent, "branch", other)
    own, their = j.reshape(1), (1 - j).reshape(1)
    info = jnp.stack([j, lengths[0].astype(jnp.int32)])
    gain, shift = norm_gain.reshape(1, D), norm_shift.reshape(1, D)

    bits = [1 << i for i in range(n_dp.bit_length() - 1)]
    high_stages = pairs_of_bits(bits[2:])
    low_first = [(1,), (2,)] + high_stages
    order = send_order(low_first, me)
    ffb = FF_HALF // n_dp
    fast = ffb == LANES
    if fast:
        splits = FB // LANES
        plan = {
            "splits": splits,
            "pieces": n_dp,
            "pick": lambda s, a, i: 2 * (4 * i + a[1][s]) + a[0][0],
            "classes": jnp.array([1, 3, 0, 2], jnp.int32) ^ (me & 3),
            "subs": jnp.arange(4, dtype=jnp.int32) ^ (me >> 2),
            "weights": (up_weight, down_weight, inner_bias.reshape(1, FF)),
        }
    else:
        plan = {
            "splits": 1,
            "pieces": 0,
            "pick": lambda s, a, i: s,
            "classes": jnp.arange(FF_HALF // FB, dtype=jnp.int32),
            "subs": jnp.zeros((1,), jnp.int32),
            "weights": (
                lax.dynamic_index_in_dim(up_weight.reshape(D, n_dp, 2, ffb), j, 2, False).reshape(D, FF_HALF),
                lax.dynamic_index_in_dim(down_weight.reshape(n_dp, 2, ffb, D), j, 1, False).reshape(FF_HALF, D),
                lax.dynamic_index_in_dim(inner_bias.reshape(n_dp, 2, ffb), j, 1, False).reshape(1, FF_HALF),
            ),
        }
    plan["order"] = order

    def pieces_of(grads, table):
        if len(grads) == 2:
            return grads
        whole = grads[0]
        ordered = jnp.take(whole.reshape(n_dp, whole.shape[0] // n_dp, whole.shape[1]), table, axis=0)
        return ordered[: n_dp // 2], ordered[n_dp // 2 :]

    plan["weights"] = tuple(pltpu.with_memory_space_constraint(w, pltpu.HBM) for w in plan["weights"][:2]) + plan["weights"][2:]
    qkv_weight = pltpu.with_memory_space_constraint(qkv_weight, pltpu.HBM)
    proj_weight = pltpu.with_memory_space_constraint(proj_weight, pltpu.HBM)

    cosine, sine = rotary_tables()
    normed, hidden, grads_own, gb_own, expanded_own, gn_own, outer = mlp_own_call(
        info, plan, tokens, cotangent, gain, shift
    )
    qkv = qkv_half_call(own, info, 0, normed, qkv_weight, cosine, sine)
    info = after(info, qkv)
    normed, hidden, slope, expanded_their = mlp_forward_call(info, plan, tokens_their, gain, shift, normed, hidden)
    info = after(info, slope)
    grads, *down = down_grad_call(info, plan, hidden, grads_own, cotangent_their)
    down = Reduction(*pieces_of(down, order), low_first, n_dp)
    info = after(info, grads)
    gn_their, inner, *up = mlp_back_call(info, plan, normed, slope, grads, gb_own)

    info = after(info, gn_their, *down.land())
    up = Reduction(*pieces_of(up, order), low_first, n_dp)
    qkv = qkv_half_call(their, info, 1, normed, qkv_weight, cosine, sine, qkv)
    context, qe = attend_call(info, qkv)
    out_their = out_call(their, info, context, proj_weight, expanded_their)

    info = after(info, out_their, *down.land(), *up.land())
    out_received = lax.ppermute(out_their, "branch", other)
    grad_context, *proj = proj_back_call(info, plan, order, grads, context, proj_weight)
    dmix = attend_back_call(info, qe, qkv, context, grad_context, cosine, sine)

    info = after(info, dmix, out_received, *up.land(), *down.land())
    query_key = pieces_of(qkv_grad_call(info, plan, order, normed, dmix, 0, 2), order)
    info = after(info, *query_key)
    query_key = Reduction(*query_key, low_first, n_dp)
    gn_send, sums_their = grad_normed_call(their, info, dmix, qkv_weight, gn_their, tokens_their, BF)

    info = after(info, gn_send, *query_key.land())
    gn_received = lax.ppermute(gn_send, "branch", other)
    gn_own, sums_own = grad_normed_call(own, info, dmix, qkv_weight, gn_own, tokens, F32)
    info = after(info, gn_own)
    small = D // n_dp
    if fast:
        value = value_grad_call(info, plan, order, normed, dmix, proj, (sums_own, sums_their, outer, inner))
    else:
        sums = sums_own + sums_their
        lines = jnp.concatenate([v.reshape(n_dp, small) for v in (sums[0], sums[1], outer)], axis=1)
        lines = jnp.concatenate(
            [jnp.pad(lines, ((0, 0), (0, 2 * LANES - 3 * small))), inner.reshape(n_dp, ffb)], axis=1
        )
        lines = jnp.pad(lines, ((0, 0), (0, HALF - lines.shape[1]))).astype(BF)
        grad_value = qkv_grad_call(info, plan, order, normed, dmix, 2, 1)[0].reshape(n_dp, small, HALF)
        proj = proj[0].reshape(n_dp, small // 2, 2, HALF).swapaxes(1, 2).reshape(n_dp, small, HALF)
        lines = jnp.broadcast_to(lines[:, None], (n_dp, 16, HALF))
        value = jnp.take(jnp.concatenate([grad_value, proj, lines], axis=1), order, axis=0)
        value = value[: n_dp // 2], value[n_dp // 2 :]
    info = after(info, *value, *query_key.land())
    value = Reduction(*value, low_first, n_dp)
    layer_out = out_call(
        own, info, context, proj_weight, expanded_own, (tokens, out_received, outer_bias.reshape(1, D))
    )
    info = after(info, layer_out, *value.land())

    def both_halves(piece):
        shard = piece.shape[0] // 2
        mine = lax.dynamic_slice_in_dim(piece, j * shard, shard, 0)
        theirs = lax.dynamic_slice_in_dim(piece, (1 - j) * shard, shard, 0).astype(BF)
        theirs = lax.ppermute(theirs, "branch", other).astype(F32)
        return jnp.where(j == 0, mine, theirs), jnp.where(j == 0, theirs, mine)

    low, high = both_halves(up.finish())
    shard = low.shape[0]
    if fast:
        low, high = (v.reshape(shard, 4, 4, ffb).swapaxes(1, 2) for v in (low, high))
    up_grad = jnp.stack([low.reshape(shard, n_dp, ffb), high.reshape(shard, n_dp, ffb)], axis=2).reshape(shard, FF)
    down_grad = down.finish()
    last = value.land()
    tokens_grad = finish_grad_call(gn_own, after(gn_received, *last), tokens, grads_own, gain)
    query_key, value = query_key.finish(), value.finish()
    proj_piece = jnp.concatenate([value[small : small + small // 2], value[small + small // 2 : 2 * small]], axis=1)
    route = [(2 * p + h, n_dp * h + p) for h in range(2) for p in range(n_dp)]
    proj_grad = lax.ppermute(proj_piece.astype(BF), ("dp", "branch"), route).astype(F32)
    piece = jnp.concatenate([query_key, value[:small]], axis=1)
    line = value[2 * small :]
    theirs = lax.dynamic_slice_in_dim(piece, (1 - j) * shard, shard, 0)
    theirs = jnp.concatenate([theirs, jnp.concatenate([line, line, line], axis=1)], axis=0).astype(BF)
    theirs = lax.ppermute(theirs, "branch", other).astype(F32)
    mine = lax.dynamic_slice_in_dim(piece, j * shard, shard, 0).reshape(shard, 3, HALF)
    triple = (line[0] + theirs[shard, :HALF])[: 3 * small].reshape(3, 2, shard)
    triple = lax.dynamic_index_in_dim(triple, j, 1, False)
    theirs = theirs[:shard].reshape(shard, 3, HALF)
    qkv_grad = jnp.stack([jnp.where(j == 0, mine, theirs), jnp.where(j == 0, theirs, mine)], axis=2)
    qkv_grad = qkv_grad.reshape(shard, 3 * D)
    return (
        layer_out,
        tokens_grad,
        triple[0],
        triple[1],
        qkv_grad,
        proj_grad,
        up_grad,
        line[0, 2 * LANES : 2 * LANES + ffb],
        down_grad,
        triple[2],
    )


def solution(mesh):
    rows = P(("dp", "branch"), None)
    flat = P(("dp", "branch"))
    return jax.shard_map(
        functools.partial(on_device, mesh.shape["dp"]),
        mesh=mesh,
        in_specs=(rows, P("dp"), P(), P(), P(), P(), P(), P(), P(), P(), rows),
        out_specs=(rows, rows, flat, flat, rows, rows, rows, flat, rows, flat),
        check_vma=False,
    )
```

```python
import functools
import math

import jax
import jax.numpy as jnp
from jax import lax
from jax.experimental import pallas as pl
from jax.experimental.pallas import tpu as pltpu
from jax.sharding import PartitionSpec as P

D = 1024
HEADS = 16
HEAD_DIM = 64
ROT_DIM = 32
FF = 4096
SEQ_LEN = 1024
HALF = HEADS // 2 * HEAD_DIM
FF_HALF = FF // 2
LANES = 128
QB = 256
FB = 512
EPS = 1e-05
BF = jnp.bfloat16
F32 = jnp.float32


def params(mb=24):
    return pltpu.CompilerParams(vmem_limit_bytes=mb << 20)


def cost(flops, nbytes, trans=0):
    return pl.CostEstimate(flops=int(flops) // 1000, bytes_accessed=int(nbytes) // 1000, transcendentals=0)


def in_hbm(shape, dtype):
    return pltpu.HBM(tuple(shape), dtype)


def dot_nn(a, b):
    return jnp.dot(a, b, preferred_element_type=F32)


def dot_nt(a, b):
    return lax.dot_general(a, b, (((1,), (1,)), ((), ())), preferred_element_type=F32)


def dot_tn(a, b):
    return lax.dot_general(a, b, (((0,), (0,)), ((), ())), preferred_element_type=F32)


def rotary_tables():
    position = jnp.arange(SEQ_LEN, dtype=jnp.int32).astype(F32)
    lane = jnp.arange(LANES, dtype=jnp.int32)
    channel = lane % HEAD_DIM
    frequency = jnp.power(10000.0, -(2.0 * (channel // 2).astype(F32)) / ROT_DIM)
    angles = position[:, None] * frequency[None, :]
    inside = (channel < ROT_DIM)[None, :]
    cosine = jnp.where(inside, jnp.cos(angles), 1.0)
    sine = jnp.where(inside, jnp.sin(angles), 0.0)
    even = (lane % 2 == 0)[None, :]
    return cosine, jnp.where(even, -sine, sine)


def rotate(x, cosine, sine):
    even = lax.broadcasted_iota(jnp.int32, x.shape, 1) % 2 == 0
    swapped = jnp.where(even, pltpu.roll(x, LANES - 1, 1), pltpu.roll(x, 1, 1))
    return x * cosine + swapped * sine


def unrotate(y, cosine, sine):
    even = lax.broadcasted_iota(jnp.int32, y.shape, 1) % 2 == 0
    swapped = jnp.where(even, pltpu.roll(y, LANES - 1, 1), pltpu.roll(y, 1, 1))
    return y * cosine - swapped * sine


def head_lanes(shape, head):
    lane = lax.broadcasted_iota(jnp.int32, shape, 1)
    own = (lane >= HEAD_DIM) if head else (lane < HEAD_DIM)
    spare = lane - (0 if head else HEAD_DIM)
    return own, spare


def keys_with_bias(k, head, length):
    own, spare = head_lanes(k.shape, head)
    row = lax.broadcasted_iota(jnp.int32, k.shape, 0)
    bias = jnp.where(row < length, 0.0, -1e30)
    extra = jnp.where(spare < 3, 1.0, jnp.where(spare == 3, bias, 0.0))
    return jnp.where(own, k.astype(F32), extra).astype(BF)


def attend_kernel(info_ref, q_ref, k_ref, v_ref, o_ref, qe_ref):
    length = info_ref[1]
    q = q_ref[0].astype(F32)
    k = k_ref[0]
    v = v_ref[0]
    tri = lax.broadcasted_iota(jnp.int32, (QB, QB), 0) >= lax.broadcasted_iota(jnp.int32, (QB, QB), 1)
    outs = []
    for head in range(2):
        own, spare = head_lanes((SEQ_LEN, LANES), head)
        ke = keys_with_bias(k, head, length)
        qe = jnp.where(own, q, jnp.where(spare == 3, 1.0, 0.0)).astype(BF)
        parts = []
        for b in range(SEQ_LEN // QB):
            lo, hi = b * QB, (b + 1) * QB
            s = dot_nt(qe[lo:hi], ke[:hi])
            diag = jnp.where(tri, s[:, lo:hi], -1e30)
            s = diag if b == 0 else jnp.concatenate([s[:, :lo], diag], axis=1)
            top = jnp.max(s, axis=1, keepdims=True)
            p = jnp.exp(s - top)
            total = jnp.sum(p, axis=1, keepdims=True)
            parts.append(dot_nn(p.astype(BF), v[:hi]) * (1.0 / total))
            lse = jnp.broadcast_to(top + jnp.log(total), (QB, LANES))
            first = lse.astype(BF).astype(F32)
            second = (lse - first).astype(BF).astype(F32)
            third = lse - first - second
            own_b, spare_b = head_lanes((QB, LANES), head)
            extra = jnp.where(
                spare_b == 0,
                -first,
                jnp.where(
                    spare_b == 1,
                    -second,
                    jnp.where(spare_b == 2, -third, jnp.where(spare_b == 3, 1.0, 0.0)),
                ),
            )
            qe_ref[head, lo:hi, :] = jnp.where(own_b, q[lo:hi], extra).astype(BF)
        outs.append(jnp.concatenate(parts, axis=0))
    own, _ = head_lanes((SEQ_LEN, LANES), 0)
    o_ref[...] = jnp.where(own, outs[0], outs[1]).astype(BF)


def attend_call(info, qkv):
    pairs = HALF // LANES
    spec = [pl.BlockSpec((1, SEQ_LEN, LANES), lambda p, n, t=t: (t, 0, p)) for t in range(3)]
    return pl.pallas_call(
        attend_kernel,
        grid_spec=pltpu.PrefetchScalarGridSpec(
            num_scalar_prefetch=1,
            grid=(pairs,),
            in_specs=spec,
            out_specs=[
                pl.BlockSpec((SEQ_LEN, LANES), lambda p, n: (0, p)),
                pl.BlockSpec((2, SEQ_LEN, LANES), lambda p, n: (p, 0, 0)),
            ],
        ),
        out_shape=[
            in_hbm((SEQ_LEN, HALF), BF),
            in_hbm((HEADS // 2, SEQ_LEN, LANES), BF),
        ],
        compiler_params=params(),
        cost_estimate=cost(
            2 * pairs * 10 * SEQ_LEN * SEQ_LEN * LANES, 2 * SEQ_LEN * HALF * 3, 4 * SEQ_LEN * SEQ_LEN
        ),
        name="attend",
    )(info, qkv, qkv, qkv)


def attend_back_kernel(info_ref, qe_ref, k_ref, v_ref, o_ref, g_ref, cos_ref, sin_ref, d_ref, dk_ref, dv_ref):
    length = info_ref[1]
    k = k_ref[0]
    v = v_ref[0]
    g = g_ref[...].astype(F32)
    o = o_ref[...].astype(F32)
    tri = lax.broadcasted_iota(jnp.int32, (QB, QB), 0) >= lax.broadcasted_iota(jnp.int32, (QB, QB), 1)
    queries = []
    for head in range(2):
        own, spare = head_lanes((SEQ_LEN, LANES), head)
        ke = keys_with_bias(k, head, length)
        ve = jnp.where(own, v.astype(F32), jnp.where(spare < 3, 1.0, 0.0)).astype(BF)
        inner = jnp.sum(jnp.where(own, g * o, 0.0), axis=1, keepdims=True)
        inner = jnp.broadcast_to(inner, (SEQ_LEN, LANES))
        first = inner.astype(BF).astype(F32)
        second = (inner - first).astype(BF).astype(F32)
        third = inner - first - second
        extra = jnp.where(
            spare == 0,
            -first,
            jnp.where(spare == 1, -second, jnp.where(spare == 2, -third, 0.0)),
        )
        ge = jnp.where(own, g, extra).astype(BF)
        parts = []
        for b in range(SEQ_LEN // QB):
            lo, hi = b * QB, (b + 1) * QB
            qb = qe_ref[head, lo:hi, :]
            gb = ge[lo:hi]
            s = dot_nt(qb, ke[:hi])
            diag = jnp.where(tri, s[:, lo:hi], -1e30)
            s = diag if b == 0 else jnp.concatenate([s[:, :lo], diag], axis=1)
            p = jnp.exp(s)
            ds = (p * dot_nt(gb, ve[:hi])).astype(BF)
            parts.append(dot_nn(ds, k[:hi]))
            dk = dot_tn(ds, qb)
            dv = dot_tn(p.astype(BF), gb)
            if b > 0:
                dk_ref[head, :lo] += dk[:lo]
                dv_ref[head, :lo] += dv[:lo]
            dk_ref[head, lo:hi] = dk[lo:hi]
            dv_ref[head, lo:hi] = dv[lo:hi]
        queries.append(jnp.concatenate(parts, axis=0))
    own, _ = head_lanes((SEQ_LEN, LANES), 0)
    cosine, sine = cos_ref[...], sin_ref[...]
    dq = jnp.where(own, queries[0], queries[1]) * HEAD_DIM**-0.5
    d_ref[0] = unrotate(dq, cosine, sine).astype(BF)
    d_ref[1] = unrotate(jnp.where(own, dk_ref[0], dk_ref[1]), cosine, sine).astype(BF)
    d_ref[2] = jnp.where(own, dv_ref[0], dv_ref[1]).astype(BF)


def attend_back_call(info, qe, qkv, context, grad_context, cosine, sine):
    pairs = HALF // LANES
    table = pl.BlockSpec((SEQ_LEN, LANES), lambda p, n: (0, 0))
    return pl.pallas_call(
        attend_back_kernel,
        grid_spec=pltpu.PrefetchScalarGridSpec(
            num_scalar_prefetch=1,
            grid=(pairs,),
            in_specs=[
                pl.BlockSpec((2, SEQ_LEN, LANES), lambda p, n: (p, 0, 0)),
                pl.BlockSpec((1, SEQ_LEN, LANES), lambda p, n: (1, 0, p)),
                pl.BlockSpec((1, SEQ_LEN, LANES), lambda p, n: (2, 0, p)),
                pl.BlockSpec((SEQ_LEN, LANES), lambda p, n: (0, p)),
                pl.BlockSpec((SEQ_LEN, LANES), lambda p, n: (0, p)),
                table,
                table,
            ],
            out_specs=pl.BlockSpec((3, SEQ_LEN, LANES), lambda p, n: (0, 0, p)),
            scratch_shapes=[
                pltpu.VMEM((2, SEQ_LEN, LANES), F32),
                pltpu.VMEM((2, SEQ_LEN, LANES), F32),
            ],
        ),
        out_shape=jax.ShapeDtypeStruct((3, SEQ_LEN, HALF), BF),
        compiler_params=params(),
        cost_estimate=cost(
            2 * pairs * 12 * SEQ_LEN * SEQ_LEN * LANES, 2 * SEQ_LEN * HALF * 4, 4 * SEQ_LEN * SEQ_LEN
        ),
        name="attend_back",
    )(info, qe, qkv, qkv, context, grad_context, cosine, sine)


def gelu_parts(v):
    c = math.sqrt(2.0 / math.pi)
    square = v * v
    half = 0.5 + 0.5 * jnp.tanh(v * (c + (c * 0.044715) * square))
    hidden = v * half
    slope = half * (1.0 + (v - hidden) * (2.0 * c + (6.0 * c * 0.044715) * square))
    return hidden, slope


def normalize(x):
    x = x.astype(F32)
    centred = x - jnp.mean(x, axis=1, keepdims=True)
    rstd = lax.rsqrt(jnp.mean(centred * centred, axis=1, keepdims=True) + EPS)
    return centred * rstd, rstd


def masked_rows(g, start, length):
    row = start + lax.broadcasted_iota(jnp.int32, g.shape, 0)
    return jnp.where(row < length, g.astype(F32), 0.0)


def joined(refs, axis):
    return refs[0][...] if len(refs) == 1 else jnp.concatenate([r[...] for r in refs], axis=axis)


def weight_specs(plan, rows_too=True):
    splits, wide, pick = plan["splits"], FB // plan["splits"], plan["pick"]
    specs = [pl.BlockSpec((D, wide), lambda s, *a, i=i: (0, pick(s, a, i))) for i in range(splits)]
    specs += [pl.BlockSpec((wide, D), lambda s, *a, i=i: (pick(s, a, i), 0)) for i in range(splits)]
    if rows_too:
        specs += [pl.BlockSpec((1, wide), lambda s, *a, i=i: (0, pick(s, a, i))) for i in range(splits)]
    return specs


def accumulate(ref, value):
    @pl.when(pl.program_id(0) == 0)
    def _():
        ref[...] = value

    @pl.when(pl.program_id(0) > 0)
    def _():
        ref[...] += value


def mlp_own_kernel(splits, info_ref, cls_ref, t_ref, c_ref, gain_ref, shift_ref, *refs):
    ups, downs, biases = refs[:splits], refs[splits : 2 * splits], refs[2 * splits : 3 * splits]
    x_ref, h_ref, g_ref, gb_ref, e_ref, gn_ref, outer_ref = refs[3 * splits :]

    @pl.when(pl.program_id(0) == 0)
    def _():
        hat, _ = normalize(t_ref[...])
        x_ref[...] = (hat * gain_ref[...].astype(F32) + shift_ref[...].astype(F32)).astype(BF)
        g = masked_rows(c_ref[...], info_ref[0] * c_ref.shape[0], info_ref[1])
        g_ref[...] = g.astype(BF)
        outer_ref[...] = jnp.sum(g, axis=0, keepdims=True)

    up, down, bias = joined(ups, 1), joined(downs, 0), joined(biases, 1)
    before = dot_nn(x_ref[...], up) + bias.astype(F32)
    hidden, slope = gelu_parts(before)
    hidden = hidden.astype(BF)
    grad_before = (dot_nt(g_ref[...], down) * slope).astype(BF)
    h_ref[...] = hidden
    gb_ref[...] = grad_before
    accumulate(e_ref, dot_nn(hidden, down))
    accumulate(gn_ref, dot_nt(grad_before, up))


def mlp_own_call(info, plan, tokens, cotangent, gain, shift):
    rows, splits = tokens.shape[0], plan["splits"]
    fixed = lambda s, *a: (0, 0)
    up, down, bias = plan["weights"]
    whole = pl.BlockSpec((rows, D), fixed)
    wide = pl.BlockSpec((rows, FB), lambda s, *a: (0, s))
    return pl.pallas_call(
        functools.partial(mlp_own_kernel, splits),
        grid_spec=pltpu.PrefetchScalarGridSpec(
            num_scalar_prefetch=2,
            grid=(FF_HALF // FB,),
            in_specs=[whole, whole, pl.BlockSpec((1, D), fixed), pl.BlockSpec((1, D), fixed)] + weight_specs(plan),
            out_specs=[whole, wide, whole, wide, whole, whole, pl.BlockSpec((1, D), fixed)],
        ),
        out_shape=[
            jax.ShapeDtypeStruct((2 * rows, D), BF),
            in_hbm((2 * rows, FF_HALF), BF),
            in_hbm((rows, D), BF),
            in_hbm((rows, FF_HALF), BF),
            in_hbm((rows, D), F32),
            in_hbm((rows, D), F32),
            jax.ShapeDtypeStruct((1, D), F32),
        ],
        compiler_params=params(),
        cost_estimate=cost(8 * rows * D * FF_HALF, 12 * rows * D + 4 * D * FF_HALF, rows * FF_HALF),
        name="mlp_own",
    )(info, plan["classes"], tokens, cotangent, gain, shift, *([up] * splits), *([down] * splits), *([bias] * splits))


def mlp_forward_kernel(splits, info_ref, cls_ref, t_ref, gain_ref, shift_ref, *refs):
    ups, downs, biases = refs[:splits], refs[splits : 2 * splits], refs[2 * splits : 3 * splits]
    x_ref, h_ref, slope_ref, e_ref = refs[3 * splits + 2 :]

    @pl.when(pl.program_id(0) == 0)
    def _():
        hat, _ = normalize(t_ref[...])
        x_ref[...] = (hat * gain_ref[...].astype(F32) + shift_ref[...].astype(F32)).astype(BF)

    up, down, bias = joined(ups, 1), joined(downs, 0), joined(biases, 1)
    before = dot_nn(x_ref[...], up) + bias.astype(F32)
    hidden, slope = gelu_parts(before)
    hidden = hidden.astype(BF)
    h_ref[...] = hidden
    slope_ref[...] = slope.astype(BF)
    accumulate(e_ref, dot_nn(hidden, down))


def mlp_forward_call(info, plan, tokens, gain, shift, normed, hidden):
    rows, splits = tokens.shape[0], plan["splits"]
    fixed = lambda s, *a: (0, 0)
    up, down, bias = plan["weights"]
    whole = pl.BlockSpec((rows, D), fixed)
    anywhere = pl.BlockSpec(memory_space=pl.ANY)
    first = 5 + 3 * splits
    return pl.pallas_call(
        functools.partial(mlp_forward_kernel, splits),
        grid_spec=pltpu.PrefetchScalarGridSpec(
            num_scalar_prefetch=2,
            grid=(FF_HALF // FB,),
            in_specs=[whole, pl.BlockSpec((1, D), fixed), pl.BlockSpec((1, D), fixed)]
            + weight_specs(plan)
            + [anywhere, anywhere],
            out_specs=[
                pl.BlockSpec((rows, D), lambda s, *a: (1, 0)),
                pl.BlockSpec((rows, FB), lambda s, *a: (1, s)),
                pl.BlockSpec((rows, FB), lambda s, *a: (0, s)),
                whole,
            ],
        ),
        out_shape=[
            jax.ShapeDtypeStruct((2 * rows, D), BF),
            in_hbm((2 * rows, FF_HALF), BF),
            in_hbm((rows, FF_HALF), BF),
            in_hbm((rows, D), F32),
        ],
        input_output_aliases={first: 0, first + 1: 1},
        compiler_params=params(),
        cost_estimate=cost(4 * rows * D * FF_HALF, 12 * rows * D + 4 * D * FF_HALF, rows * FF_HALF),
        name="mlp_forward",
    )(info, plan["classes"], tokens, gain, shift, *([up] * splits), *([down] * splits), *([bias] * splits), normed, hidden)


def down_grad_kernel(splits, pieces, info_ref, cls_ref, sub_ref, h_ref, go_ref, c_ref, g_ref, *grads):
    rows = c_ref.shape[0]
    step = pl.program_id(0)

    @pl.when(step == 0)
    def _():
        g_ref[:rows] = go_ref[...]
        g_ref[rows:] = masked_rows(c_ref[...], (1 - info_ref[0]) * rows, info_ref[1]).astype(BF)

    grad_down = dot_tn(h_ref[...], g_ref[...]).astype(BF)
    if not pieces:
        grads[0][...] = grad_down
        return
    down_keep, down_send = grads
    block = FB // splits

    @pl.when(step < 2)
    def _():
        for i in range(splits):
            down_send[sub_ref[i]] = grad_down[i * block : (i + 1) * block]

    @pl.when(step >= 2)
    def _():
        for i in range(splits):
            down_keep[sub_ref[i]] = grad_down[i * block : (i + 1) * block]


def down_grad_call(info, plan, hidden, grads_own, cotangent):
    rows, splits, pieces = cotangent.shape[0], plan["splits"], plan["pieces"]
    fixed = lambda s, *a: (0, 0)
    whole = pl.BlockSpec((rows, D), fixed)
    out_specs = [pl.BlockSpec((2 * rows, D), fixed)]
    out_shape = [in_hbm((2 * rows, D), BF)]
    if pieces:
        half, down_rows = pieces // 2, FF_HALF // pieces
        out_specs += [
            pl.BlockSpec((splits, down_rows, D), lambda s, *a: (jnp.maximum(s - 2, 0), 0, 0)),
            pl.BlockSpec((splits, down_rows, D), lambda s, *a: (jnp.minimum(s, 1), 0, 0)),
        ]
        out_shape += [in_hbm((half, down_rows, D), BF)] * 2
    else:
        out_specs += [pl.BlockSpec((FB, D), lambda s, *a: (s, 0))]
        out_shape += [in_hbm((FF_HALF, D), BF)]
    return pl.pallas_call(
        functools.partial(down_grad_kernel, splits, pieces),
        grid_spec=pltpu.PrefetchScalarGridSpec(
            num_scalar_prefetch=3,
            grid=(FF_HALF // FB,),
            in_specs=[pl.BlockSpec((2 * rows, FB), lambda s, *a: (0, s)), whole, whole],
            out_specs=out_specs,
        ),
        out_shape=out_shape,
        compiler_params=params(),
        cost_estimate=cost(4 * rows * D * FF_HALF, 8 * rows * D + 2 * D * FF_HALF + 4 * rows * FF_HALF),
        name="down_grad",
    )(info, plan["classes"], plan["subs"], hidden, grads_own, cotangent)


def mlp_back_kernel(splits, pieces, info_ref, cls_ref, ord_ref, x_ref, slope_ref, g_ref, gb_ref, *refs):
    ups, downs = refs[:splits], refs[splits : 2 * splits]
    gn_ref, inner_ref, *grads = refs[2 * splits : -2 if pieces else -1]
    gball_ref = refs[-2 if pieces else -1]
    rows = g_ref.shape[0]
    up, down = joined(ups, 1), joined(downs, 0)
    grad_before = (dot_nt(g_ref[...], down) * slope_ref[...].astype(F32)).astype(BF)
    gball_ref[:rows] = gb_ref[...]
    gball_ref[rows:] = grad_before
    accumulate(gn_ref, dot_nt(grad_before, up))
    inner_ref[...] = jnp.sum(gball_ref[...].astype(F32), axis=0, keepdims=True)
    grad_up = dot_tn(x_ref[...], gball_ref[...]).astype(BF)
    if not pieces:
        grads[0][...] = grad_up
        return
    up_keep, up_send = grads
    upall_ref = refs[-1]
    upall_ref[...] = grad_up.reshape(upall_ref.shape)
    for q in range(pieces // 2):
        up_keep[q] = upall_ref[ord_ref[q]]
        up_send[q] = upall_ref[ord_ref[q + pieces // 2]]


def mlp_back_call(info, plan, normed, slope, grads, gb_own):
    rows, splits, pieces = gb_own.shape[0], plan["splits"], plan["pieces"]
    fixed = lambda s, *a: (0, 0)
    up, down, _ = plan["weights"]
    whole = pl.BlockSpec((rows, D), fixed)
    wide = pl.BlockSpec((rows, FB), lambda s, *a: (0, s))
    out_specs = [whole, pl.BlockSpec((1, FB), lambda s, i, cls, *a: (0, cls[s]))]
    out_shape = [in_hbm((rows, D), F32), jax.ShapeDtypeStruct((1, FF_HALF), F32)]
    scratch = [pltpu.VMEM((2 * rows, FB), BF)]
    if pieces:
        shape = (pieces // 2, D // pieces, FB)
        out_specs += [pl.BlockSpec(shape, lambda s, i, cls, *a: (0, 0, cls[s]))] * 2
        out_shape += [in_hbm(shape[:2] + (FF_HALF,), BF)] * 2
        scratch.append(pltpu.VMEM((pieces, D // pieces, FB), BF))
    else:
        out_specs += [pl.BlockSpec((D, FB), lambda s, *a: (0, s))]
        out_shape += [in_hbm((D, FF_HALF), BF)]
    return pl.pallas_call(
        functools.partial(mlp_back_kernel, splits, pieces),
        grid_spec=pltpu.PrefetchScalarGridSpec(
            num_scalar_prefetch=3,
            grid=(FF_HALF // FB,),
            in_specs=[
                pl.BlockSpec((2 * rows, D), fixed),
                wide,
                pl.BlockSpec((rows, D), lambda s, *a: (1, 0)),
                wide,
            ]
            + weight_specs(plan, False),
            out_specs=out_specs,
            scratch_shapes=scratch,
        ),
        out_shape=out_shape,
        compiler_params=params(),
        cost_estimate=cost(8 * rows * D * FF_HALF, 12 * rows * D + 6 * D * FF_HALF + 4 * rows * FF_HALF),
        name="mlp_back",
    )(info, plan["classes"], plan["order"], normed, slope, grads, gb_own, *([up] * splits), *([down] * splits))


def qkv_half_kernel(place_ref, info_ref, x_ref, w_ref, cos_ref, sin_ref, *refs):
    o_ref = refs[-1]
    t = pl.program_id(0)
    chunk = 2 * LANES

    @pl.when(t == 2)
    def _():
        for c in range(0, HALF, chunk):
            o_ref[0, :, c : c + chunk] = dot_nn(x_ref[...], w_ref[:, c : c + chunk]).astype(BF)

    @pl.when(t < 2)
    def _():
        scale = jnp.where(t == 0, HEAD_DIM**-0.5, 1.0)
        cosine = cos_ref[...] * scale
        sine = sin_ref[...] * scale
        for c in range(0, HALF, chunk):
            mixed = dot_nn(x_ref[...], w_ref[:, c : c + chunk])
            for e in range(0, chunk, LANES):
                o_ref[0, :, c + e : c + e + LANES] = rotate(mixed[:, e : e + LANES], cosine, sine).astype(BF)


def qkv_half_call(place, info, half, normed, w, cosine, sine, qkv=None):
    rows = normed.shape[0] // 2
    table = pl.BlockSpec((rows, LANES), lambda t, p, i: (p[0], 0))
    more = [] if qkv is None else [qkv]
    return pl.pallas_call(
        qkv_half_kernel,
        grid_spec=pltpu.PrefetchScalarGridSpec(
            num_scalar_prefetch=2,
            grid=(3,),
            in_specs=[
                pl.BlockSpec((rows, D), lambda t, p, i: (half, 0)),
                pl.BlockSpec((D, HALF), lambda t, p, i: (0, 2 * t + i[0])),
                table,
                table,
            ]
            + [pl.BlockSpec(memory_space=pl.ANY)] * len(more),
            out_specs=pl.BlockSpec((1, rows, HALF), lambda t, p, i: (t, p[0], 0)),
        ),
        out_shape=in_hbm((3, 2 * rows, HALF), BF),
        input_output_aliases={6: 0} if more else {},
        compiler_params=params(),
        cost_estimate=cost(2 * rows * D * 3 * HALF, 2 * (rows * D + D * 3 * HALF + rows * 3 * HALF)),
        name="qkv",
    )(place, info, normed, w, cosine, sine, *more)


def send_out_kernel(place_ref, info_ref, c_ref, w_ref, e_ref, o_ref):
    o_ref[...] = (dot_nn(c_ref[...], w_ref[...]) + e_ref[...]).astype(BF)


def finish_out_kernel(place_ref, info_ref, c_ref, w_ref, e_ref, t_ref, r_ref, bias_ref, o_ref):
    total = dot_nn(c_ref[...], w_ref[...]) + e_ref[...] + bias_ref[...].astype(F32)
    o_ref[...] = (total + t_ref[...].astype(F32) + r_ref[...].astype(F32)).astype(BF)


def out_call(place, info, context, proj, expanded, rest=()):
    rows, block = expanded.shape[0], 256
    steps = rows // block
    row = pl.BlockSpec((block, D), lambda s, p, i: (s, 0))
    return pl.pallas_call(
        finish_out_kernel if rest else send_out_kernel,
        grid_spec=pltpu.PrefetchScalarGridSpec(
            num_scalar_prefetch=2,
            grid=(steps,),
            in_specs=[
                pl.BlockSpec((block, HALF), lambda s, p, i: (p[0] * steps + s, 0)),
                pl.BlockSpec((HALF, D), lambda s, p, i: (i[0], 0)),
                row,
            ]
            + ([row, row, pl.BlockSpec((1, D), lambda s, p, i: (0, 0))] if rest else []),
            out_specs=row,
        ),
        out_shape=in_hbm((rows, D), BF),
        compiler_params=params(),
        cost_estimate=cost(2 * rows * D * HALF, 8 * rows * D + 2 * HALF * D),
        name="finish_out" if rest else "send_out",
    )(place, info, context, proj, expanded, *rest)


def proj_back_kernel(info_ref, ord_ref, g_ref, c_ref, w_ref, gc_ref, *refs):
    acc_ref = refs[-2] if len(refs) > 2 else refs[-1]
    gc_ref[...] = dot_nt(g_ref[...], w_ref[...]).astype(BF)
    part = dot_tn(c_ref[...], g_ref[...])

    @pl.when(pl.program_id(0) == 0)
    def _():
        acc_ref[...] = part

    @pl.when(pl.program_id(0) == 1)
    def _():
        total = (acc_ref[...] + part).astype(BF)
        if len(refs) == 2:
            refs[0][...] = total
        else:
            keep, send, all_ref = refs[0], refs[1], refs[3]
            all_ref[...] = total.reshape(all_ref.shape)
            half = keep.shape[0]
            for q in range(half):
                keep[q] = all_ref[ord_ref[q]]
                send[q] = all_ref[ord_ref[q + half]]


def proj_back_call(info, plan, order, grads, context, proj):
    rows, pieces = grads.shape[0] // 2, plan["pieces"]
    scratch = [pltpu.VMEM((HALF, D), F32)]
    if pieces:
        shape = (pieces // 2, HALF // pieces, D)
        out_specs = [pl.BlockSpec(shape, lambda h, *a: (0, 0, 0))] * 2
        out_shape = [in_hbm(shape, BF)] * 2
        scratch.append(pltpu.VMEM((pieces, HALF // pieces, D), BF))
    else:
        out_specs = [pl.BlockSpec((HALF, D), lambda h, *a: (0, 0))]
        out_shape = [in_hbm((HALF, D), BF)]
    return pl.pallas_call(
        proj_back_kernel,
        grid_spec=pltpu.PrefetchScalarGridSpec(
            num_scalar_prefetch=2,
            grid=(2,),
            in_specs=[
                pl.BlockSpec((rows, D), lambda h, i, o: (h, 0)),
                pl.BlockSpec((rows, HALF), lambda h, i, o: (jnp.bitwise_xor(h, i[0]), 0)),
                pl.BlockSpec((HALF, D), lambda h, i, o: (i[0], 0)),
            ],
            out_specs=[pl.BlockSpec((rows, HALF), lambda h, i, o: (jnp.bitwise_xor(h, i[0]), 0))] + out_specs,
            scratch_shapes=scratch,
        ),
        out_shape=[in_hbm((2 * rows, HALF), BF)] + out_shape,
        compiler_params=params(),
        cost_estimate=cost(8 * rows * D * HALF, 4 * rows * D + 8 * rows * HALF + 4 * HALF * D),
        name="proj_back",
    )(info, order, grads, context, proj)


def line_of(p, rows, sums, outer, inner_ref):
    low = lax.broadcasted_iota(jnp.int32, (1, LANES), 1) < rows
    at = p // 2 * LANES
    three = [v[:, at : at + LANES] for v in (sums[0:1], sums[1:2], outer)]
    turned = [pltpu.roll(v, rows, 1) for v in three]
    if p % 2:
        three, turned = turned, three
    at = p % 4 * HALF + p // 4 * LANES
    parts = [jnp.where(low, three[0], turned[1]), jnp.where(low, three[2], 0.0), inner_ref[:, at : at + LANES]]
    return jnp.concatenate(parts + [jnp.zeros((1, LANES), F32)], axis=1)


def pair_grad_kernel(info_ref, ord_ref, x_ref, own_ref, their_ref, *refs):
    d = jnp.concatenate([own_ref[0], their_ref[0]], axis=0)
    total = dot_tn(x_ref[...], d).astype(BF)
    if len(refs) == 1:
        refs[0][...] = total
        return
    pk_ref, ps_ref, keep, send, all_ref = refs
    half, rows = keep.shape[0], all_ref.shape[1]
    all_ref[...] = total.reshape(all_ref.shape)
    for q in range(half):
        for out, proj, at in ((keep, pk_ref, q), (send, ps_ref, q + half)):
            out[q, :rows] = all_ref[ord_ref[at]]
            out[q, rows:] = proj[q]


def value_grad_kernel(info_ref, ord_ref, x_ref, own_ref, their_ref, so_ref, st_ref, outer_ref, inner_ref, keep, send,
                      all_ref):
    pieces, rows = all_ref.shape[0], x_ref.shape[1] // all_ref.shape[0]
    half = pieces // 2
    d = jnp.concatenate([own_ref[0], their_ref[0]], axis=0)
    all_ref[:, :rows] = dot_tn(x_ref[...], d).astype(BF).reshape(pieces, rows, HALF)
    sums = so_ref[...] + st_ref[...]
    outer = outer_ref[...]
    for p in range(pieces):
        line = line_of(p, rows, sums, outer, inner_ref)
        all_ref[p, rows:] = jnp.broadcast_to(line, (all_ref.shape[1] - rows, HALF)).astype(BF)
    for q in range(half):
        keep[q] = all_ref[ord_ref[q]]
        send[q] = all_ref[ord_ref[q + half]]


def qkv_grad_call(info, plan, normed, dmix, first, count, extra=()):
    rows, pieces = normed.shape[0] // 2, plan["pieces"]
    in_specs, scratch, kernel = [], [], pair_grad_kernel
    if not pieces:
        extra = ()
        out_specs = [pl.BlockSpec((D, HALF), lambda t, *a: (0, t))]
        out_shape = [in_hbm((D, count * HALF), BF)]
    else:
        height = D // pieces
        if count == 2:
            shape = (pieces // 2, height + HALF // pieces, HALF)
            in_specs = [pl.BlockSpec((pieces // 2, HALF // pieces, HALF), lambda t, *a: (0, 0, t))] * 2
            scratch = [pltpu.VMEM((pieces, height, HALF), BF)]
        else:
            kernel = value_grad_kernel
            shape = (pieces // 2, height + 16, HALF)
            in_specs = [pl.BlockSpec(v.shape, lambda t, *a: (0, 0)) for v in extra]
            scratch = [pltpu.VMEM((pieces, height + 16, HALF), BF)]
        out_specs = [pl.BlockSpec(shape, lambda t, *a: (0, 0, t))] * 2
        out_shape = [in_hbm(shape[:2] + (count * HALF,), BF)] * 2
    return pl.pallas_call(
        kernel,
        grid_spec=pltpu.PrefetchScalarGridSpec(
            num_scalar_prefetch=2,
            grid=(count,),
            in_specs=[
                pl.BlockSpec((2 * rows, D), lambda t, *a: (0, 0)),
                pl.BlockSpec((1, rows, HALF), lambda t, i, *a: (first + t, i[0], 0)),
                pl.BlockSpec((1, rows, HALF), lambda t, i, *a: (first + t, 1 - i[0], 0)),
            ]
            + in_specs,
            out_specs=out_specs,
            scratch_shapes=scratch,
        ),
        out_shape=out_shape,
        compiler_params=params(),
        cost_estimate=cost(4 * rows * D * count * HALF, 4 * rows * D + (4 * rows + 2 * D) * count * HALF),
        name="qkv_grad",
    )(info, plan["order"], normed, dmix, dmix, *extra)


def grad_normed_kernel(place_ref, info_ref, d_ref, wq_ref, wk_ref, wv_ref, base_ref, t_ref, *refs):
    outs, sum_ref = refs[:-1], refs[-1]
    total = base_ref[...]
    for t, w in enumerate((wq_ref, wk_ref, wv_ref)):
        total += dot_nt(d_ref[t], w[...])
    if len(outs) == 1:
        outs[0][...] = total.astype(outs[0].dtype)
    else:
        for r, o_ref in enumerate(outs):

            @pl.when(pl.program_id(0) == r)
            def _(o_ref=o_ref):
                o_ref[...] = total.astype(o_ref.dtype)

    hat, _ = normalize(t_ref[...])
    sums = jnp.concatenate([jnp.sum(total * hat, axis=0, keepdims=True), jnp.sum(total, axis=0, keepdims=True)], axis=0)
    accumulate(sum_ref, sums)


def grad_normed_call(place, info, dmix, w, base, tokens, parts):
    rows, block = base.shape[0], 256
    steps = rows // block
    row = pl.BlockSpec((block, D), lambda r, p, i: (r, 0))
    kind = BF if parts else F32
    count = parts or 1
    return pl.pallas_call(
        grad_normed_kernel,
        grid_spec=pltpu.PrefetchScalarGridSpec(
            num_scalar_prefetch=2,
            grid=(steps,),
            in_specs=[pl.BlockSpec((3, block, HALF), lambda r, p, i: (0, p[0] * steps + r, 0))]
            + [pl.BlockSpec((D, HALF), lambda r, p, i, t=t: (0, 2 * t + i[0])) for t in range(3)]
            + [row, row],
            out_specs=([row] if count == 1 else [pl.BlockSpec((block, D), lambda r, p, i: (0, 0))] * count)
            + [pl.BlockSpec((2, D), lambda r, p, i: (0, 0))],
        ),
        out_shape=[in_hbm((rows // count, D), kind)] * count + [jax.ShapeDtypeStruct((2, D), F32)],
        compiler_params=params(),
        cost_estimate=cost(2 * rows * D * 3 * HALF, 8 * rows * D + 6 * D * HALF + 6 * rows * HALF),
        name="grad_normed",
    )(place, info, dmix, w, w, w, base, tokens)


def finish_grad_kernel(gn_ref, r_ref, t_ref, g_ref, gain_ref, o_ref):
    hat, rstd = normalize(t_ref[...])
    u = (gn_ref[...] + r_ref[...].astype(F32)) * gain_ref[...].astype(F32)
    inner = u - jnp.mean(u, axis=1, keepdims=True) - hat * jnp.mean(u * hat, axis=1, keepdims=True)
    o_ref[...] = g_ref[...].astype(F32) + inner * rstd


def finish_grad_call(grad_normed, received, tokens, grads, gain):
    rows, block = tokens.shape[0], 256
    row = pl.BlockSpec((block, D), lambda r: (r, 0))
    return pl.pallas_call(
        finish_grad_kernel,
        grid=(rows // block,),
        in_specs=[row, row, row, row, pl.BlockSpec((1, D), lambda r: (0, 0))],
        out_specs=row,
        out_shape=in_hbm((rows, D), F32),
        compiler_params=params(),
        cost_estimate=cost(20 * rows * D, 14 * rows * D),
        name="finish_grad",
    )(grad_normed, received, tokens, grads, gain)


class Reduction:
    def __init__(self, keep, send, stages, n_dp):
        self.keep, self.sends, self.stages, self.n_dp = keep, [send], list(stages), n_dp
        self.start()

    def start(self):
        offsets = self.stages.pop(0)
        self.flying = [
            lax.ppermute(part, "dp", [(i, i ^ offset) for i in range(self.n_dp)])
            for part, offset in zip(self.sends, offsets, strict=True)
        ]

    def land(self, *first):
        if first:
            self.keep = after(self.keep, *first)
        kind = self.flying[0].dtype
        pieces = self.keep.shape[0]
        count = pieces // (len(self.stages[0]) + 1) if self.stages else pieces
        parts = []
        for i in range(0, pieces, count):
            total = self.keep[i : i + count].astype(F32)
            for part in self.flying:
                total = total + part[i : i + count].astype(F32)
            parts.append(total)
        if not self.stages:
            self.keep, self.sends = parts[0][0], []
            return (self.keep,)
        parts = [part.astype(kind) for part in parts]
        self.keep, self.sends = parts[0], parts[1:]
        self.start()
        return tuple(parts)

    def finish(self, *first):
        self.land(*first)
        while self.sends:
            self.land()
        return self.keep


def after(x, *done):
    return lax.optimization_barrier((x, *done))[0]


def send_order(stages, me):
    table = [0]
    for offsets in stages:
        table = [r ^ offset for r in table for offset in (0, *offsets)]
    return jnp.bitwise_xor(jnp.array(table, jnp.int32), me)


def pairs_of_bits(bits):
    stages = []
    for i in range(0, len(bits), 2):
        if i + 1 < len(bits):
            stages.append((bits[i], bits[i + 1], bits[i] ^ bits[i + 1]))
        else:
            stages.append((bits[i],))
    return stages


def on_device(n_dp, tokens, lengths, norm_gain, norm_shift, qkv_weight, proj_weight, up_weight, inner_bias,
              down_weight, outer_bias, cotangent):
    j = lax.axis_index("branch").astype(jnp.int32)
    me = lax.axis_index("dp").astype(jnp.int32)
    other = [(0, 1), (1, 0)]
    tokens_their = lax.ppermute(tokens, "branch", other)
    cotangent_their = lax.ppermute(cotangent, "branch", other)
    own, their = j.reshape(1), (1 - j).reshape(1)
    info = jnp.stack([j, lengths[0].astype(jnp.int32)])
    gain, shift = norm_gain.reshape(1, D), norm_shift.reshape(1, D)

    bits = [1 << i for i in range(n_dp.bit_length() - 1)]
    high_stages = pairs_of_bits(bits[2:])
    low_first = [(1,), (2,)] + high_stages
    order = send_order(low_first, me)
    ffb = FF_HALF // n_dp
    fast = ffb == LANES
    if fast:
        splits = FB // LANES
        plan = {
            "splits": splits,
            "pieces": n_dp,
            "pick": lambda s, a, i: 2 * (4 * i + a[1][s]) + a[0][0],
            "classes": jnp.array([1, 3, 0, 2], jnp.int32) ^ (me & 3),
            "subs": jnp.arange(4, dtype=jnp.int32) ^ (me >> 2),
            "weights": (up_weight, down_weight, inner_bias.reshape(1, FF)),
        }
    else:
        plan = {
            "splits": 1,
            "pieces": 0,
            "pick": lambda s, a, i: s,
            "classes": jnp.arange(FF_HALF // FB, dtype=jnp.int32),
            "subs": jnp.zeros((1,), jnp.int32),
            "weights": (
                lax.dynamic_index_in_dim(up_weight.reshape(D, n_dp, 2, ffb), j, 2, False).reshape(D, FF_HALF),
                lax.dynamic_index_in_dim(down_weight.reshape(n_dp, 2, ffb, D), j, 1, False).reshape(FF_HALF, D),
                lax.dynamic_index_in_dim(inner_bias.reshape(n_dp, 2, ffb), j, 1, False).reshape(1, FF_HALF),
            ),
        }
    plan["order"] = order

    def pieces_of(grads, table):
        if len(grads) == 2:
            return grads
        whole = grads[0]
        ordered = jnp.take(whole.reshape(n_dp, whole.shape[0] // n_dp, whole.shape[1]), table, axis=0)
        return ordered[: n_dp // 2], ordered[n_dp // 2 :]

    plan["weights"] = tuple(pltpu.with_memory_space_constraint(w, pltpu.HBM) for w in plan["weights"][:2]) + plan["weights"][2:]
    qkv_weight = pltpu.with_memory_space_constraint(qkv_weight, pltpu.HBM)
    proj_weight = pltpu.with_memory_space_constraint(proj_weight, pltpu.HBM)

    cosine, sine = rotary_tables()
    normed, hidden, grads_own, gb_own, expanded_own, gn_own, outer = mlp_own_call(
        info, plan, tokens, cotangent, gain, shift
    )
    qkv = qkv_half_call(own, info, 0, normed, qkv_weight, cosine, sine)
    info = after(info, qkv)
    normed, hidden, slope, expanded_their = mlp_forward_call(info, plan, tokens_their, gain, shift, normed, hidden)
    info = after(info, slope)
    grads, *down = down_grad_call(info, plan, hidden, grads_own, cotangent_their)
    down = Reduction(*pieces_of(down, order), low_first, n_dp)
    info = after(info, grads)
    gn_their, inner, *up = mlp_back_call(info, plan, normed, slope, grads, gb_own)

    up = Reduction(*pieces_of(up, order), low_first, n_dp)
    info = after(info, *down.land(gn_their), *up.land(gn_their))
    qkv = qkv_half_call(their, info, 1, normed, qkv_weight, cosine, sine, qkv)
    context, qe = attend_call(info, qkv)
    out_their = out_call(their, info, context, proj_weight, expanded_their)

    info = after(info, *down.land(out_their))
    out_received = lax.ppermute(out_their, "branch", other)
    grad_context, *proj = proj_back_call(info, plan, order, grads, context, proj_weight)
    info = after(info, *up.land(grad_context))
    dmix = attend_back_call(info, qe, qkv, context, grad_context, cosine, sine)

    down_grad = down.finish(dmix)
    info = after(info, out_received, down_grad)
    small = D // n_dp
    shard = small // 2
    first = qkv_grad_call(info, plan, normed, dmix, 0, 2, proj)
    if not fast:
        first = jnp.concatenate([first[0].reshape(n_dp, small, D), proj[0].reshape(n_dp, shard, D)], axis=1)
        first = jnp.take(first, order, axis=0)
        first = first[: n_dp // 2], first[n_dp // 2 :]
    info = after(info, *first)
    first = Reduction(*first, low_first, n_dp)
    *gn_send, sums_their = grad_normed_call(their, info, dmix, qkv_weight, gn_their, tokens_their, 1)

    info = after(info, *first.land(*gn_send))
    gn_first = lax.ppermute(gn_send[0], "branch", other)
    gn_own, sums_own = grad_normed_call(own, info, dmix, qkv_weight, gn_own, tokens, 0)
    info = after(info, gn_own)
    layer_out = out_call(
        own, info, context, proj_weight, expanded_own, (tokens, out_received, outer_bias.reshape(1, D))
    )
    info = after(info, layer_out)
    if fast:
        value = qkv_grad_call(info, plan, normed, dmix, 2, 1, (sums_own, sums_their, outer, inner))
    else:
        sums = sums_own + sums_their
        lines = jnp.concatenate([v.reshape(n_dp, small) for v in (sums[0], sums[1], outer)], axis=1)
        lines = jnp.concatenate(
            [jnp.pad(lines, ((0, 0), (0, 2 * LANES - 3 * small))), inner.reshape(n_dp, ffb)], axis=1
        )
        lines = jnp.pad(lines, ((0, 0), (0, HALF - lines.shape[1]))).astype(BF)
        lines = jnp.broadcast_to(lines[:, None], (n_dp, 16, HALF))
        value = qkv_grad_call(info, plan, normed, dmix, 2, 1)[0].reshape(n_dp, small, HALF)
        value = jnp.take(jnp.concatenate([value, lines], axis=1), order, axis=0)
        value = value[: n_dp // 2], value[n_dp // 2 :]
    up.finish(*value)
    landed = first.land(*value)
    value, up.keep, _ = lax.optimization_barrier((tuple(value), up.keep, (*landed, gn_first)))
    value = Reduction(*value, low_first, n_dp)
    up_mine = lax.dynamic_slice_in_dim(up.keep, j * shard, shard, 0)
    up_their = lax.dynamic_slice_in_dim(up.keep, (1 - j) * shard, shard, 0).astype(BF)
    up_their = lax.ppermute(up_their, "branch", other)
    landed = value.land()
    tokens_grad = finish_grad_call(gn_own, after(gn_first, *landed), tokens, grads_own, gain)
    up_mine, up_their, tokens_grad = lax.optimization_barrier((up_mine, up_their.astype(F32), tokens_grad))
    low, high = jnp.where(j == 0, up_mine, up_their), jnp.where(j == 0, up_their, up_mine)
    if fast:
        low, high = (v.reshape(shard, 4, 4, ffb).swapaxes(1, 2) for v in (low, high))
    up_grad = jnp.stack([low.reshape(shard, n_dp, ffb), high.reshape(shard, n_dp, ffb)], axis=2).reshape(shard, FF)
    first = first.finish(up_grad)
    value.land(first)
    value = value.finish()
    query_key, proj_piece = first[:small], first[small:]
    piece = jnp.concatenate([query_key, value[:small]], axis=1)
    line = value[small:]
    theirs = lax.dynamic_slice_in_dim(piece, (1 - j) * shard, shard, 0)
    theirs = jnp.concatenate([theirs, jnp.concatenate([line, line, line], axis=1)], axis=0).astype(BF)
    route = [(2 * p + h, n_dp * h + p) for h in range(2) for p in range(n_dp)]
    proj_grad = lax.ppermute(after(proj_piece.astype(BF), theirs), ("dp", "branch"), route).astype(F32)
    theirs = lax.ppermute(theirs, "branch", other).astype(F32)
    mine = lax.dynamic_slice_in_dim(piece, j * shard, shard, 0).reshape(shard, 3, HALF)
    triple = (line[0] + theirs[shard, :HALF])[: 3 * small].reshape(3, 2, shard)
    triple = lax.dynamic_index_in_dim(triple, j, 1, False)
    theirs = theirs[:shard].reshape(shard, 3, HALF)
    qkv_grad = jnp.stack([jnp.where(j == 0, mine, theirs), jnp.where(j == 0, theirs, mine)], axis=2)
    qkv_grad = qkv_grad.reshape(shard, 3 * D)
    return (
        layer_out,
        tokens_grad,
        triple[0],
        triple[1],
        qkv_grad,
        proj_grad,
        up_grad,
        line[0, 2 * LANES : 2 * LANES + ffb],
        down_grad,
        triple[2],
    )


def solution(mesh):
    rows = P(("dp", "branch"), None)
    flat = P(("dp", "branch"))
    return jax.shard_map(
        functools.partial(on_device, mesh.shape["dp"]),
        mesh=mesh,
        in_specs=(rows, P("dp"), P(), P(), P(), P(), P(), P(), P(), P(), rows),
        out_specs=(rows, rows, flat, flat, rows, rows, rows, flat, rows, flat),
        check_vma=False,
    )
```

```python
import functools
import math

import jax
import jax.numpy as jnp
from jax import lax
from jax.experimental import pallas as pl
from jax.experimental.pallas import tpu as pltpu
from jax.sharding import PartitionSpec as P

D = 1024
HEADS = 16
HEAD_DIM = 64
ROT_DIM = 32
FF = 4096
SEQ_LEN = 1024
HALF = HEADS // 2 * HEAD_DIM
FF_HALF = FF // 2
LANES = 128
QB = 256
ROWS = 128
FB = 512
EPS = 1e-05
BF = jnp.bfloat16
F32 = jnp.float32


def params(mb=24):
    return pltpu.CompilerParams(vmem_limit_bytes=mb << 20)


def cost(flops, nbytes, trans=0):
    return pl.CostEstimate(flops=int(flops) // 1000, bytes_accessed=int(nbytes) // 1000, transcendentals=0)


def in_hbm(shape, dtype):
    return pltpu.HBM(tuple(shape), dtype)


def dot_nn(a, b):
    return jnp.dot(a, b, preferred_element_type=F32)


def dot_nt(a, b):
    return lax.dot_general(a, b, (((1,), (1,)), ((), ())), preferred_element_type=F32)


def dot_tn(a, b):
    return lax.dot_general(a, b, (((0,), (0,)), ((), ())), preferred_element_type=F32)


def rotary_tables():
    lane = jnp.arange(LANES, dtype=jnp.int32)
    channel = lane % HEAD_DIM
    frequency = jnp.power(10000.0, -(2.0 * (channel // 2).astype(F32)) / ROT_DIM)
    frequency = jnp.where(channel < ROT_DIM, frequency, 0.0)
    step = 32
    index = jnp.arange(2 * step, dtype=jnp.int32)
    position = jnp.where(index < step, index * (SEQ_LEN // step), index - step).astype(F32)
    angles = position[:, None] * frequency[None, :]
    cosine, sine = lax.optimization_barrier((jnp.cos(angles), jnp.sin(angles)))
    high_cosine, high_sine = cosine[:step, None], sine[:step, None]
    low_cosine, low_sine = cosine[None, step:], sine[None, step:]
    even = (lane % 2 == 0)[None, None, :]
    sine = high_sine * low_cosine + high_cosine * low_sine
    cosine = high_cosine * low_cosine - high_sine * low_sine
    return cosine.reshape(SEQ_LEN, LANES), jnp.where(even, -sine, sine).reshape(SEQ_LEN, LANES)


def rotate(x, cosine, sine):
    even = lax.broadcasted_iota(jnp.int32, x.shape, 1) % 2 == 0
    swapped = jnp.where(even, pltpu.roll(x, LANES - 1, 1), pltpu.roll(x, 1, 1))
    return x * cosine + swapped * sine


def unrotate(y, cosine, sine):
    even = lax.broadcasted_iota(jnp.int32, y.shape, 1) % 2 == 0
    swapped = jnp.where(even, pltpu.roll(y, LANES - 1, 1), pltpu.roll(y, 1, 1))
    return y * cosine - swapped * sine


def head_lanes(shape, head):
    lane = lax.broadcasted_iota(jnp.int32, shape, 1)
    own = (lane >= HEAD_DIM) if head else (lane < HEAD_DIM)
    spare = lane - (0 if head else HEAD_DIM)
    return own, spare


def keys_with_bias(k, head, length):
    own, spare = head_lanes(k.shape, head)
    row = lax.broadcasted_iota(jnp.int32, k.shape, 0)
    bias = jnp.where(row < length, 0.0, -1e30)
    extra = jnp.where(spare < 3, 1.0, jnp.where(spare == 3, bias, 0.0))
    return jnp.where(own, k.astype(F32), extra).astype(BF)


def attend_kernel(info_ref, q_ref, k_ref, v_ref, o_ref, qe_ref):
    length = info_ref[1]
    q = q_ref[0].astype(F32)
    k = k_ref[0]
    v = v_ref[0]
    tri = lax.broadcasted_iota(jnp.int32, (QB, QB), 0) >= lax.broadcasted_iota(jnp.int32, (QB, QB), 1)
    outs = []
    for head in range(2):
        own, spare = head_lanes((SEQ_LEN, LANES), head)
        ke = keys_with_bias(k, head, length)
        qe = jnp.where(own, q, jnp.where(spare == 3, 1.0, 0.0)).astype(BF)
        parts = []
        for b in range(SEQ_LEN // QB):
            lo, hi = b * QB, (b + 1) * QB
            s = dot_nt(qe[lo:hi], ke[:hi])
            diag = jnp.where(tri, s[:, lo:hi], -1e30)
            s = diag if b == 0 else jnp.concatenate([s[:, :lo], diag], axis=1)
            top = jnp.max(s, axis=1, keepdims=True)
            p = jnp.exp(s - top)
            total = jnp.sum(p, axis=1, keepdims=True)
            parts.append(dot_nn(p.astype(BF), v[:hi]) * (1.0 / total))
            lse = jnp.broadcast_to(top + jnp.log(total), (QB, LANES))
            first = lse.astype(BF).astype(F32)
            second = (lse - first).astype(BF).astype(F32)
            third = lse - first - second
            own_b, spare_b = head_lanes((QB, LANES), head)
            extra = jnp.where(
                spare_b == 0,
                -first,
                jnp.where(
                    spare_b == 1,
                    -second,
                    jnp.where(spare_b == 2, -third, jnp.where(spare_b == 3, 1.0, 0.0)),
                ),
            )
            qe_ref[head, lo:hi, :] = jnp.where(own_b, q[lo:hi], extra).astype(BF)
        outs.append(jnp.concatenate(parts, axis=0))
    own, _ = head_lanes((SEQ_LEN, LANES), 0)
    o_ref[...] = jnp.where(own, outs[0], outs[1]).astype(BF)


def attend_call(info, qkv):
    pairs = HALF // LANES
    spec = [pl.BlockSpec((1, SEQ_LEN, LANES), lambda p, n, t=t: (t, 0, p)) for t in range(3)]
    return pl.pallas_call(
        attend_kernel,
        grid_spec=pltpu.PrefetchScalarGridSpec(
            num_scalar_prefetch=1,
            grid=(pairs,),
            in_specs=spec,
            out_specs=[
                pl.BlockSpec((SEQ_LEN, LANES), lambda p, n: (0, p)),
                pl.BlockSpec((2, SEQ_LEN, LANES), lambda p, n: (p, 0, 0)),
            ],
        ),
        out_shape=[
            in_hbm((SEQ_LEN, HALF), BF),
            in_hbm((HEADS // 2, SEQ_LEN, LANES), BF),
        ],
        compiler_params=params(),
        cost_estimate=cost(
            2 * pairs * 10 * SEQ_LEN * SEQ_LEN * LANES, 2 * SEQ_LEN * HALF * 3, 4 * SEQ_LEN * SEQ_LEN
        ),
        name="attend",
    )(info, qkv, qkv, qkv)


def attend_back_kernel(info_ref, qe_ref, k_ref, v_ref, o_ref, g_ref, cos_ref, sin_ref, d_ref, dk_ref, dv_ref):
    length = info_ref[1]
    k = k_ref[0]
    v = v_ref[0]
    g = g_ref[...].astype(F32)
    o = o_ref[...].astype(F32)
    tri = lax.broadcasted_iota(jnp.int32, (QB, QB), 0) >= lax.broadcasted_iota(jnp.int32, (QB, QB), 1)
    queries = []
    for head in range(2):
        own, spare = head_lanes((SEQ_LEN, LANES), head)
        ke = keys_with_bias(k, head, length)
        ve = jnp.where(own, v.astype(F32), jnp.where(spare < 3, 1.0, 0.0)).astype(BF)
        inner = jnp.sum(jnp.where(own, g * o, 0.0), axis=1, keepdims=True)
        inner = jnp.broadcast_to(inner, (SEQ_LEN, LANES))
        first = inner.astype(BF).astype(F32)
        second = (inner - first).astype(BF).astype(F32)
        third = inner - first - second
        extra = jnp.where(
            spare == 0,
            -first,
            jnp.where(spare == 1, -second, jnp.where(spare == 2, -third, 0.0)),
        )
        ge = jnp.where(own, g, extra).astype(BF)
        parts = []
        for b in range(SEQ_LEN // QB):
            lo, hi = b * QB, (b + 1) * QB
            qb = qe_ref[head, lo:hi, :]
            gb = ge[lo:hi]
            s = dot_nt(qb, ke[:hi])
            diag = jnp.where(tri, s[:, lo:hi], -1e30)
            s = diag if b == 0 else jnp.concatenate([s[:, :lo], diag], axis=1)
            p = jnp.exp(s)
            ds = (p * dot_nt(gb, ve[:hi])).astype(BF)
            parts.append(dot_nn(ds, k[:hi]))
            dk = dot_tn(ds, qb)
            dv = dot_tn(p.astype(BF), gb)
            if b > 0:
                dk_ref[head, :lo] += dk[:lo]
                dv_ref[head, :lo] += dv[:lo]
            dk_ref[head, lo:hi] = dk[lo:hi]
            dv_ref[head, lo:hi] = dv[lo:hi]
        queries.append(jnp.concatenate(parts, axis=0))
    own, _ = head_lanes((SEQ_LEN, LANES), 0)
    cosine, sine = cos_ref[...], sin_ref[...]
    dq = jnp.where(own, queries[0], queries[1]) * HEAD_DIM**-0.5
    d_ref[0] = unrotate(dq, cosine, sine).astype(BF)
    d_ref[1] = unrotate(jnp.where(own, dk_ref[0], dk_ref[1]), cosine, sine).astype(BF)
    d_ref[2] = jnp.where(own, dv_ref[0], dv_ref[1]).astype(BF)


def attend_back_call(info, qe, qkv, context, grad_context, cosine, sine):
    pairs = HALF // LANES
    table = pl.BlockSpec((SEQ_LEN, LANES), lambda p, n: (0, 0))
    return pl.pallas_call(
        attend_back_kernel,
        grid_spec=pltpu.PrefetchScalarGridSpec(
            num_scalar_prefetch=1,
            grid=(pairs,),
            in_specs=[
                pl.BlockSpec((2, SEQ_LEN, LANES), lambda p, n: (p, 0, 0)),
                pl.BlockSpec((1, SEQ_LEN, LANES), lambda p, n: (1, 0, p)),
                pl.BlockSpec((1, SEQ_LEN, LANES), lambda p, n: (2, 0, p)),
                pl.BlockSpec((SEQ_LEN, LANES), lambda p, n: (0, p)),
                pl.BlockSpec((SEQ_LEN, LANES), lambda p, n: (0, p)),
                table,
                table,
            ],
            out_specs=pl.BlockSpec((3, SEQ_LEN, LANES), lambda p, n: (0, 0, p)),
            scratch_shapes=[
                pltpu.VMEM((2, SEQ_LEN, LANES), F32),
                pltpu.VMEM((2, SEQ_LEN, LANES), F32),
            ],
        ),
        out_shape=jax.ShapeDtypeStruct((3, SEQ_LEN, HALF), BF),
        compiler_params=params(),
        cost_estimate=cost(
            2 * pairs * 12 * SEQ_LEN * SEQ_LEN * LANES, 2 * SEQ_LEN * HALF * 4, 4 * SEQ_LEN * SEQ_LEN
        ),
        name="attend_back",
    )(info, qe, qkv, qkv, context, grad_context, cosine, sine)


def gelu_parts(v):
    c = math.sqrt(2.0 / math.pi)
    square = v * v
    half = 0.5 + 0.5 * jnp.tanh(v * (c + (c * 0.044715) * square))
    hidden = v * half
    slope = half * (1.0 + (v - hidden) * (2.0 * c + (6.0 * c * 0.044715) * square))
    return hidden, slope


def normalize(x):
    x = x.astype(F32)
    centred = x - jnp.mean(x, axis=1, keepdims=True)
    rstd = lax.rsqrt(jnp.mean(centred * centred, axis=1, keepdims=True) + EPS)
    return centred * rstd, rstd


def masked_rows(g, start, length):
    row = start + lax.broadcasted_iota(jnp.int32, g.shape, 0)
    return jnp.where(row < length, g.astype(F32), 0.0)


def joined(refs, axis):
    return refs[0][...] if len(refs) == 1 else jnp.concatenate([r[...] for r in refs], axis=axis)


def weight_specs(plan, rows_too=True):
    splits, wide, pick = plan["splits"], FB // plan["splits"], plan["pick"]
    specs = [pl.BlockSpec((D, wide), lambda s, *a, i=i: (0, pick(s, a, i))) for i in range(splits)]
    specs += [pl.BlockSpec((wide, D), lambda s, *a, i=i: (pick(s, a, i), 0)) for i in range(splits)]
    if rows_too:
        specs += [pl.BlockSpec((1, wide), lambda s, *a, i=i: (0, pick(s, a, i))) for i in range(splits)]
    return specs


def accumulate(ref, value):
    @pl.when(pl.program_id(0) == 0)
    def _():
        ref[...] = value

    @pl.when(pl.program_id(0) > 0)
    def _():
        ref[...] += value


def mlp_own_kernel(splits, info_ref, cls_ref, t_ref, c_ref, gain_ref, shift_ref, *refs):
    ups, downs, biases = refs[:splits], refs[splits : 2 * splits], refs[2 * splits : 3 * splits]
    x_ref, h_ref, g_ref, gb_ref, e_ref, gn_ref, outer_ref = refs[3 * splits :]

    @pl.when(pl.program_id(0) == 0)
    def _():
        outer_ref[...] = jnp.zeros_like(outer_ref)

        @pl.loop(0, t_ref.shape[0] // ROWS)
        def _(r):
            at = pl.ds(pl.multiple_of(r * ROWS, ROWS), ROWS)
            hat, _ = normalize(t_ref[at, :])
            x_ref[at, :] = (hat * gain_ref[...].astype(F32) + shift_ref[...].astype(F32)).astype(BF)
            g = masked_rows(c_ref[at, :], info_ref[0] * c_ref.shape[0] + r * ROWS, info_ref[1])
            g_ref[at, :] = g.astype(BF)
            outer_ref[...] += jnp.sum(g, axis=0, keepdims=True)

    up, down, bias = joined(ups, 1), joined(downs, 0), joined(biases, 1)
    before = dot_nn(x_ref[...], up) + bias.astype(F32)
    hidden, slope = gelu_parts(before)
    hidden = hidden.astype(BF)
    grad_before = (dot_nt(g_ref[...], down) * slope).astype(BF)
    h_ref[...] = hidden
    gb_ref[...] = grad_before
    accumulate(e_ref, dot_nn(hidden, down))
    accumulate(gn_ref, dot_nt(grad_before, up))


def mlp_own_call(info, plan, tokens, cotangent, gain, shift):
    rows, splits = tokens.shape[0], plan["splits"]
    fixed = lambda s, *a: (0, 0)
    up, down, bias = plan["weights"]
    whole = pl.BlockSpec((rows, D), fixed)
    wide = pl.BlockSpec((rows, FB), lambda s, *a: (0, s))
    return pl.pallas_call(
        functools.partial(mlp_own_kernel, splits),
        grid_spec=pltpu.PrefetchScalarGridSpec(
            num_scalar_prefetch=2,
            grid=(FF_HALF // FB,),
            in_specs=[whole, whole, pl.BlockSpec((1, D), fixed), pl.BlockSpec((1, D), fixed)] + weight_specs(plan),
            out_specs=[whole, wide, whole, wide, whole, whole, pl.BlockSpec((1, D), fixed)],
        ),
        out_shape=[
            jax.ShapeDtypeStruct((2 * rows, D), BF),
            in_hbm((2 * rows, FF_HALF), BF),
            in_hbm((rows, D), BF),
            in_hbm((rows, FF_HALF), BF),
            in_hbm((rows, D), F32),
            in_hbm((rows, D), F32),
            jax.ShapeDtypeStruct((1, D), F32),
        ],
        compiler_params=params(),
        cost_estimate=cost(8 * rows * D * FF_HALF, 12 * rows * D + 4 * D * FF_HALF, rows * FF_HALF),
        name="mlp_own",
    )(info, plan["classes"], tokens, cotangent, gain, shift, *([up] * splits), *([down] * splits), *([bias] * splits))


def mlp_forward_kernel(splits, info_ref, cls_ref, t_ref, gain_ref, shift_ref, *refs):
    ups, downs, biases = refs[:splits], refs[splits : 2 * splits], refs[2 * splits : 3 * splits]
    x_ref, h_ref, slope_ref, e_ref = refs[3 * splits + 2 :]

    @pl.when(pl.program_id(0) == 0)
    def _():
        @pl.loop(0, t_ref.shape[0] // ROWS)
        def _(r):
            at = pl.ds(pl.multiple_of(r * ROWS, ROWS), ROWS)
            hat, _ = normalize(t_ref[at, :])
            x_ref[at, :] = (hat * gain_ref[...].astype(F32) + shift_ref[...].astype(F32)).astype(BF)

    up, down, bias = joined(ups, 1), joined(downs, 0), joined(biases, 1)
    before = dot_nn(x_ref[...], up) + bias.astype(F32)
    hidden, slope = gelu_parts(before)
    hidden = hidden.astype(BF)
    h_ref[...] = hidden
    slope_ref[...] = slope.astype(BF)
    accumulate(e_ref, dot_nn(hidden, down))


def mlp_forward_call(info, plan, tokens, gain, shift, normed, hidden):
    rows, splits = tokens.shape[0], plan["splits"]
    fixed = lambda s, *a: (0, 0)
    up, down, bias = plan["weights"]
    whole = pl.BlockSpec((rows, D), fixed)
    anywhere = pl.BlockSpec(memory_space=pl.ANY)
    first = 5 + 3 * splits
    return pl.pallas_call(
        functools.partial(mlp_forward_kernel, splits),
        grid_spec=pltpu.PrefetchScalarGridSpec(
            num_scalar_prefetch=2,
            grid=(FF_HALF // FB,),
            in_specs=[whole, pl.BlockSpec((1, D), fixed), pl.BlockSpec((1, D), fixed)]
            + weight_specs(plan)
            + [anywhere, anywhere],
            out_specs=[
                pl.BlockSpec((rows, D), lambda s, *a: (1, 0)),
                pl.BlockSpec((rows, FB), lambda s, *a: (1, s)),
                pl.BlockSpec((rows, FB), lambda s, *a: (0, s)),
                whole,
            ],
        ),
        out_shape=[
            jax.ShapeDtypeStruct((2 * rows, D), BF),
            in_hbm((2 * rows, FF_HALF), BF),
            in_hbm((rows, FF_HALF), BF),
            in_hbm((rows, D), F32),
        ],
        input_output_aliases={first: 0, first + 1: 1},
        compiler_params=params(),
        cost_estimate=cost(4 * rows * D * FF_HALF, 12 * rows * D + 4 * D * FF_HALF, rows * FF_HALF),
        name="mlp_forward",
    )(info, plan["classes"], tokens, gain, shift, *([up] * splits), *([down] * splits), *([bias] * splits), normed, hidden)


def down_grad_kernel(splits, pieces, info_ref, cls_ref, sub_ref, h_ref, go_ref, c_ref, g_ref, *grads):
    rows = c_ref.shape[0]
    step = pl.program_id(0)

    @pl.when(step == 0)
    def _():
        g_ref[:rows] = go_ref[...]
        g_ref[rows:] = masked_rows(c_ref[...], (1 - info_ref[0]) * rows, info_ref[1]).astype(BF)

    grad_down = dot_tn(h_ref[...], g_ref[...]).astype(BF)
    if not pieces:
        grads[0][...] = grad_down
        return
    down_keep, down_send = grads
    block = FB // splits

    @pl.when(step < 2)
    def _():
        for i in range(splits):
            down_send[sub_ref[i]] = grad_down[i * block : (i + 1) * block]

    @pl.when(step >= 2)
    def _():
        for i in range(splits):
            down_keep[sub_ref[i]] = grad_down[i * block : (i + 1) * block]


def down_grad_call(info, plan, hidden, grads_own, cotangent):
    rows, splits, pieces = cotangent.shape[0], plan["splits"], plan["pieces"]
    fixed = lambda s, *a: (0, 0)
    whole = pl.BlockSpec((rows, D), fixed)
    out_specs = [pl.BlockSpec((2 * rows, D), fixed)]
    out_shape = [in_hbm((2 * rows, D), BF)]
    if pieces:
        half, down_rows = pieces // 2, FF_HALF // pieces
        out_specs += [
            pl.BlockSpec((splits, down_rows, D), lambda s, *a: (jnp.maximum(s - 2, 0), 0, 0)),
            pl.BlockSpec((splits, down_rows, D), lambda s, *a: (jnp.minimum(s, 1), 0, 0)),
        ]
        out_shape += [in_hbm((half, down_rows, D), BF)] * 2
    else:
        out_specs += [pl.BlockSpec((FB, D), lambda s, *a: (s, 0))]
        out_shape += [in_hbm((FF_HALF, D), BF)]
    return pl.pallas_call(
        functools.partial(down_grad_kernel, splits, pieces),
        grid_spec=pltpu.PrefetchScalarGridSpec(
            num_scalar_prefetch=3,
            grid=(FF_HALF // FB,),
            in_specs=[pl.BlockSpec((2 * rows, FB), lambda s, *a: (0, s)), whole, whole],
            out_specs=out_specs,
        ),
        out_shape=out_shape,
        compiler_params=params(),
        cost_estimate=cost(4 * rows * D * FF_HALF, 8 * rows * D + 2 * D * FF_HALF + 4 * rows * FF_HALF),
        name="down_grad",
    )(info, plan["classes"], plan["subs"], hidden, grads_own, cotangent)


def mlp_back_kernel(splits, pieces, info_ref, cls_ref, ord_ref, x_ref, slope_ref, g_ref, gb_ref, *refs):
    ups, downs = refs[:splits], refs[splits : 2 * splits]
    gn_ref, inner_ref, *grads = refs[2 * splits : -2 if pieces else -1]
    gball_ref = refs[-2 if pieces else -1]
    rows = g_ref.shape[0]
    up, down = joined(ups, 1), joined(downs, 0)
    grad_before = (dot_nt(g_ref[...], down) * slope_ref[...].astype(F32)).astype(BF)
    gball_ref[:rows] = gb_ref[...]
    gball_ref[rows:] = grad_before
    accumulate(gn_ref, dot_nt(grad_before, up))
    inner_ref[...] = jnp.sum(gball_ref[...].astype(F32), axis=0, keepdims=True)
    grad_up = dot_tn(x_ref[...], gball_ref[...]).astype(BF)
    if not pieces:
        grads[0][...] = grad_up
        return
    up_keep, up_send = grads
    upall_ref = refs[-1]
    upall_ref[...] = grad_up.reshape(upall_ref.shape)
    for q in range(pieces // 2):
        up_keep[q] = upall_ref[ord_ref[q]]
        up_send[q] = upall_ref[ord_ref[q + pieces // 2]]


def mlp_back_call(info, plan, normed, slope, grads, gb_own):
    rows, splits, pieces = gb_own.shape[0], plan["splits"], plan["pieces"]
    fixed = lambda s, *a: (0, 0)
    up, down, _ = plan["weights"]
    whole = pl.BlockSpec((rows, D), fixed)
    wide = pl.BlockSpec((rows, FB), lambda s, *a: (0, s))
    out_specs = [whole, pl.BlockSpec((1, FB), lambda s, i, cls, *a: (0, cls[s]))]
    out_shape = [in_hbm((rows, D), F32), jax.ShapeDtypeStruct((1, FF_HALF), F32)]
    scratch = [pltpu.VMEM((2 * rows, FB), BF)]
    if pieces:
        shape = (pieces // 2, D // pieces, FB)
        out_specs += [pl.BlockSpec(shape, lambda s, i, cls, *a: (0, 0, cls[s]))] * 2
        out_shape += [in_hbm(shape[:2] + (FF_HALF,), BF)] * 2
        scratch.append(pltpu.VMEM((pieces, D // pieces, FB), BF))
    else:
        out_specs += [pl.BlockSpec((D, FB), lambda s, *a: (0, s))]
        out_shape += [in_hbm((D, FF_HALF), BF)]
    return pl.pallas_call(
        functools.partial(mlp_back_kernel, splits, pieces),
        grid_spec=pltpu.PrefetchScalarGridSpec(
            num_scalar_prefetch=3,
            grid=(FF_HALF // FB,),
            in_specs=[
                pl.BlockSpec((2 * rows, D), fixed),
                wide,
                pl.BlockSpec((rows, D), lambda s, *a: (1, 0)),
                wide,
            ]
            + weight_specs(plan, False),
            out_specs=out_specs,
            scratch_shapes=scratch,
        ),
        out_shape=out_shape,
        compiler_params=params(),
        cost_estimate=cost(8 * rows * D * FF_HALF, 12 * rows * D + 6 * D * FF_HALF + 4 * rows * FF_HALF),
        name="mlp_back",
    )(info, plan["classes"], plan["order"], normed, slope, grads, gb_own, *([up] * splits), *([down] * splits))


def qkv_half_kernel(place_ref, info_ref, x_ref, w_ref, cos_ref, sin_ref, *refs):
    o_ref = refs[-1]
    t = pl.program_id(0)
    chunk = 2 * LANES

    @pl.when(t == 2)
    def _():
        for c in range(0, HALF, chunk):
            o_ref[0, :, c : c + chunk] = dot_nn(x_ref[...], w_ref[:, c : c + chunk]).astype(BF)

    @pl.when(t < 2)
    def _():
        scale = jnp.where(t == 0, HEAD_DIM**-0.5, 1.0)
        cosine = cos_ref[...] * scale
        sine = sin_ref[...] * scale
        for c in range(0, HALF, chunk):
            mixed = dot_nn(x_ref[...], w_ref[:, c : c + chunk])
            for e in range(0, chunk, LANES):
                o_ref[0, :, c + e : c + e + LANES] = rotate(mixed[:, e : e + LANES], cosine, sine).astype(BF)


def qkv_half_call(place, info, half, normed, w, cosine, sine, qkv=None):
    rows = normed.shape[0] // 2
    table = pl.BlockSpec((rows, LANES), lambda t, p, i: (p[0], 0))
    more = [] if qkv is None else [qkv]
    return pl.pallas_call(
        qkv_half_kernel,
        grid_spec=pltpu.PrefetchScalarGridSpec(
            num_scalar_prefetch=2,
            grid=(3,),
            in_specs=[
                pl.BlockSpec((rows, D), lambda t, p, i: (half, 0)),
                pl.BlockSpec((D, HALF), lambda t, p, i: (0, 2 * t + i[0])),
                table,
                table,
            ]
            + [pl.BlockSpec(memory_space=pl.ANY)] * len(more),
            out_specs=pl.BlockSpec((1, rows, HALF), lambda t, p, i: (t, p[0], 0)),
        ),
        out_shape=in_hbm((3, 2 * rows, HALF), BF),
        input_output_aliases={6: 0} if more else {},
        compiler_params=params(),
        cost_estimate=cost(2 * rows * D * 3 * HALF, 2 * (rows * D + D * 3 * HALF + rows * 3 * HALF)),
        name="qkv",
    )(place, info, normed, w, cosine, sine, *more)


def send_out_kernel(place_ref, info_ref, c_ref, w_ref, e_ref, o_ref):
    o_ref[...] = (dot_nn(c_ref[...], w_ref[...]) + e_ref[...]).astype(BF)


def finish_out_kernel(place_ref, info_ref, c_ref, w_ref, e_ref, t_ref, r_ref, bias_ref, o_ref):
    total = dot_nn(c_ref[...], w_ref[...]) + e_ref[...] + bias_ref[...].astype(F32)
    o_ref[...] = (total + t_ref[...].astype(F32) + r_ref[...].astype(F32)).astype(BF)


def out_call(place, info, context, proj, expanded, rest=()):
    rows, block = expanded.shape[0], 256
    steps = rows // block
    row = pl.BlockSpec((block, D), lambda s, p, i: (s, 0))
    return pl.pallas_call(
        finish_out_kernel if rest else send_out_kernel,
        grid_spec=pltpu.PrefetchScalarGridSpec(
            num_scalar_prefetch=2,
            grid=(steps,),
            in_specs=[
                pl.BlockSpec((block, HALF), lambda s, p, i: (p[0] * steps + s, 0)),
                pl.BlockSpec((HALF, D), lambda s, p, i: (i[0], 0)),
                row,
            ]
            + ([row, row, pl.BlockSpec((1, D), lambda s, p, i: (0, 0))] if rest else []),
            out_specs=row,
        ),
        out_shape=in_hbm((rows, D), BF),
        compiler_params=params(),
        cost_estimate=cost(2 * rows * D * HALF, 8 * rows * D + 2 * HALF * D),
        name="finish_out" if rest else "send_out",
    )(place, info, context, proj, expanded, *rest)


def proj_back_kernel(info_ref, ord_ref, g_ref, c_ref, w_ref, gc_ref, *refs):
    acc_ref = refs[-2] if len(refs) > 2 else refs[-1]
    gc_ref[...] = dot_nt(g_ref[...], w_ref[...]).astype(BF)
    part = dot_tn(c_ref[...], g_ref[...])

    @pl.when(pl.program_id(0) == 0)
    def _():
        acc_ref[...] = part

    @pl.when(pl.program_id(0) == 1)
    def _():
        total = (acc_ref[...] + part).astype(BF)
        if len(refs) == 2:
            refs[0][...] = total
        else:
            keep, send, all_ref = refs[0], refs[1], refs[3]
            all_ref[...] = total.reshape(all_ref.shape)
            half = keep.shape[0]
            for q in range(half):
                keep[q] = all_ref[ord_ref[q]]
                send[q] = all_ref[ord_ref[q + half]]


def proj_back_call(info, plan, order, grads, context, proj):
    rows, pieces = grads.shape[0] // 2, plan["pieces"]
    scratch = [pltpu.VMEM((HALF, D), F32)]
    if pieces:
        shape = (pieces // 2, HALF // pieces, D)
        out_specs = [pl.BlockSpec(shape, lambda h, *a: (0, 0, 0))] * 2
        out_shape = [in_hbm(shape, BF)] * 2
        scratch.append(pltpu.VMEM((pieces, HALF // pieces, D), BF))
    else:
        out_specs = [pl.BlockSpec((HALF, D), lambda h, *a: (0, 0))]
        out_shape = [in_hbm((HALF, D), BF)]
    return pl.pallas_call(
        proj_back_kernel,
        grid_spec=pltpu.PrefetchScalarGridSpec(
            num_scalar_prefetch=2,
            grid=(2,),
            in_specs=[
                pl.BlockSpec((rows, D), lambda h, i, o: (h, 0)),
                pl.BlockSpec((rows, HALF), lambda h, i, o: (jnp.bitwise_xor(h, i[0]), 0)),
                pl.BlockSpec((HALF, D), lambda h, i, o: (i[0], 0)),
            ],
            out_specs=[pl.BlockSpec((rows, HALF), lambda h, i, o: (jnp.bitwise_xor(h, i[0]), 0))] + out_specs,
            scratch_shapes=scratch,
        ),
        out_shape=[in_hbm((2 * rows, HALF), BF)] + out_shape,
        compiler_params=params(),
        cost_estimate=cost(8 * rows * D * HALF, 4 * rows * D + 8 * rows * HALF + 4 * HALF * D),
        name="proj_back",
    )(info, order, grads, context, proj)


def line_of(p, rows, sums, outer, inner_ref):
    low = lax.broadcasted_iota(jnp.int32, (1, LANES), 1) < rows
    at = p // 2 * LANES
    three = [v[:, at : at + LANES] for v in (sums[0:1], sums[1:2], outer)]
    turned = [pltpu.roll(v, rows, 1) for v in three]
    if p % 2:
        three, turned = turned, three
    at = p % 4 * HALF + p // 4 * LANES
    parts = [jnp.where(low, three[0], turned[1]), jnp.where(low, three[2], 0.0), inner_ref[:, at : at + LANES]]
    return jnp.concatenate(parts + [jnp.zeros((1, LANES), F32)], axis=1)


def pair_grad_kernel(info_ref, ord_ref, x_ref, own_ref, their_ref, *refs):
    d = jnp.concatenate([own_ref[0], their_ref[0]], axis=0)
    total = dot_tn(x_ref[...], d).astype(BF)
    if len(refs) == 1:
        refs[0][...] = total
        return
    pk_ref, ps_ref, keep, send, all_ref = refs
    half, rows = keep.shape[0], all_ref.shape[1]
    all_ref[...] = total.reshape(all_ref.shape)
    for q in range(half):
        for out, proj, at in ((keep, pk_ref, q), (send, ps_ref, q + half)):
            out[q, :rows] = all_ref[ord_ref[at]]
            out[q, rows:] = proj[q]


def value_grad_kernel(info_ref, ord_ref, x_ref, own_ref, their_ref, so_ref, st_ref, outer_ref, inner_ref, keep, send,
                      all_ref):
    pieces, rows = all_ref.shape[0], x_ref.shape[1] // all_ref.shape[0]
    half = pieces // 2
    d = jnp.concatenate([own_ref[0], their_ref[0]], axis=0)
    all_ref[:, :rows] = dot_tn(x_ref[...], d).astype(BF).reshape(pieces, rows, HALF)
    sums = so_ref[...] + st_ref[...]
    outer = outer_ref[...]
    for p in range(pieces):
        line = line_of(p, rows, sums, outer, inner_ref)
        all_ref[p, rows:] = jnp.broadcast_to(line, (all_ref.shape[1] - rows, HALF)).astype(BF)
    for q in range(half):
        keep[q] = all_ref[ord_ref[q]]
        send[q] = all_ref[ord_ref[q + half]]


def qkv_grad_call(info, plan, normed, dmix, first, count, extra=()):
    rows, pieces = normed.shape[0] // 2, plan["pieces"]
    in_specs, scratch, kernel = [], [], pair_grad_kernel
    if not pieces:
        extra = ()
        out_specs = [pl.BlockSpec((D, HALF), lambda t, *a: (0, t))]
        out_shape = [in_hbm((D, count * HALF), BF)]
    else:
        height = D // pieces
        if count == 2:
            shape = (pieces // 2, height + HALF // pieces, HALF)
            in_specs = [pl.BlockSpec((pieces // 2, HALF // pieces, HALF), lambda t, *a: (0, 0, t))] * 2
            scratch = [pltpu.VMEM((pieces, height, HALF), BF)]
        else:
            kernel = value_grad_kernel
            shape = (pieces // 2, height + 16, HALF)
            in_specs = [pl.BlockSpec(v.shape, lambda t, *a: (0, 0)) for v in extra]
            scratch = [pltpu.VMEM((pieces, height + 16, HALF), BF)]
        out_specs = [pl.BlockSpec(shape, lambda t, *a: (0, 0, t))] * 2
        out_shape = [in_hbm(shape[:2] + (count * HALF,), BF)] * 2
    return pl.pallas_call(
        kernel,
        grid_spec=pltpu.PrefetchScalarGridSpec(
            num_scalar_prefetch=2,
            grid=(count,),
            in_specs=[
                pl.BlockSpec((2 * rows, D), lambda t, *a: (0, 0)),
                pl.BlockSpec((1, rows, HALF), lambda t, i, *a: (first + t, i[0], 0)),
                pl.BlockSpec((1, rows, HALF), lambda t, i, *a: (first + t, 1 - i[0], 0)),
            ]
            + in_specs,
            out_specs=out_specs,
            scratch_shapes=scratch,
        ),
        out_shape=out_shape,
        compiler_params=params(),
        cost_estimate=cost(4 * rows * D * count * HALF, 4 * rows * D + (4 * rows + 2 * D) * count * HALF),
        name="qkv_grad",
    )(info, plan["order"], normed, dmix, dmix, *extra)


def grad_normed_kernel(place_ref, info_ref, d_ref, wq_ref, wk_ref, wv_ref, base_ref, t_ref, *refs):
    outs, sum_ref = refs[:-1], refs[-1]
    total = base_ref[...]
    for t, w in enumerate((wq_ref, wk_ref, wv_ref)):
        total += dot_nt(d_ref[t], w[...])
    if len(outs) == 1:
        outs[0][...] = total.astype(outs[0].dtype)
    else:
        for r, o_ref in enumerate(outs):

            @pl.when(pl.program_id(0) == r)
            def _(o_ref=o_ref):
                o_ref[...] = total.astype(o_ref.dtype)

    hat, _ = normalize(t_ref[...])
    sums = jnp.concatenate([jnp.sum(total * hat, axis=0, keepdims=True), jnp.sum(total, axis=0, keepdims=True)], axis=0)
    accumulate(sum_ref, sums)


def grad_normed_call(place, info, dmix, w, base, tokens, parts):
    rows, block = base.shape[0], 256
    steps = rows // block
    row = pl.BlockSpec((block, D), lambda r, p, i: (r, 0))
    kind = BF if parts else F32
    count = parts or 1
    return pl.pallas_call(
        grad_normed_kernel,
        grid_spec=pltpu.PrefetchScalarGridSpec(
            num_scalar_prefetch=2,
            grid=(steps,),
            in_specs=[pl.BlockSpec((3, block, HALF), lambda r, p, i: (0, p[0] * steps + r, 0))]
            + [pl.BlockSpec((D, HALF), lambda r, p, i, t=t: (0, 2 * t + i[0])) for t in range(3)]
            + [row, row],
            out_specs=([row] if count == 1 else [pl.BlockSpec((block, D), lambda r, p, i: (0, 0))] * count)
            + [pl.BlockSpec((2, D), lambda r, p, i: (0, 0))],
        ),
        out_shape=[in_hbm((rows // count, D), kind)] * count + [jax.ShapeDtypeStruct((2, D), F32)],
        compiler_params=params(),
        cost_estimate=cost(2 * rows * D * 3 * HALF, 8 * rows * D + 6 * D * HALF + 6 * rows * HALF),
        name="grad_normed",
    )(place, info, dmix, w, w, w, base, tokens)


def assemble_kernel(sources, width, info_ref, mine_ref, their_ref, o_ref):
    first = info_ref[0] == 0
    rows = o_ref.shape[0]
    for k, at in enumerate(sources):
        mine = mine_ref[:, at : at + width]
        theirs = their_ref[:rows, at : at + width].astype(F32)
        o_ref[:, 2 * k * width : (2 * k + 1) * width] = jnp.where(first, mine, theirs)
        o_ref[:, (2 * k + 1) * width : (2 * k + 2) * width] = jnp.where(first, theirs, mine)


def assemble_call(info, mine, theirs, sources, width):
    whole = lambda v: pl.BlockSpec(v.shape, lambda s, i: (0, 0))
    shape = (mine.shape[0], 2 * width * len(sources))
    return pl.pallas_call(
        functools.partial(assemble_kernel, sources, width),
        grid_spec=pltpu.PrefetchScalarGridSpec(
            num_scalar_prefetch=1,
            grid=(1,),
            in_specs=[whole(mine), whole(theirs)],
            out_specs=pl.BlockSpec(shape, lambda s, i: (0, 0)),
        ),
        out_shape=in_hbm(shape, F32),
        compiler_params=params(),
        cost_estimate=cost(1000, 1000),
        name="assemble",
    )(info, mine, theirs)


def finish_grad_kernel(gn_ref, r_ref, t_ref, g_ref, gain_ref, o_ref):
    hat, rstd = normalize(t_ref[...])
    u = (gn_ref[...] + r_ref[...].astype(F32)) * gain_ref[...].astype(F32)
    inner = u - jnp.mean(u, axis=1, keepdims=True) - hat * jnp.mean(u * hat, axis=1, keepdims=True)
    o_ref[...] = g_ref[...].astype(F32) + inner * rstd


def finish_grad_call(grad_normed, received, tokens, grads, gain):
    rows, block = tokens.shape[0], 256
    row = pl.BlockSpec((block, D), lambda r: (r, 0))
    return pl.pallas_call(
        finish_grad_kernel,
        grid=(rows // block,),
        in_specs=[row, row, row, row, pl.BlockSpec((1, D), lambda r: (0, 0))],
        out_specs=row,
        out_shape=in_hbm((rows, D), F32),
        compiler_params=params(),
        cost_estimate=cost(20 * rows * D, 14 * rows * D),
        name="finish_grad",
    )(grad_normed, received, tokens, grads, gain)


class Reduction:
    def __init__(self, keep, send, stages, n_dp):
        self.keep, self.sends, self.stages, self.n_dp = keep, [send], list(stages), n_dp
        self.start()

    def start(self):
        offsets = self.stages.pop(0)
        self.flying = [
            lax.ppermute(part, "dp", [(i, i ^ offset) for i in range(self.n_dp)])
            for part, offset in zip(self.sends, offsets, strict=True)
        ]

    def land(self, *first):
        if first:
            self.keep = after(self.keep, *first)
        kind = self.flying[0].dtype
        pieces = self.keep.shape[0]
        count = pieces // (len(self.stages[0]) + 1) if self.stages else pieces
        parts = []
        for i in range(0, pieces, count):
            total = self.keep[i : i + count].astype(F32)
            for part in self.flying:
                total = total + part[i : i + count].astype(F32)
            parts.append(total)
        if not self.stages:
            self.keep, self.sends = parts[0][0], []
            return (self.keep,)
        parts = [part.astype(kind) for part in parts]
        self.keep, self.sends = parts[0], parts[1:]
        self.start()
        return tuple(parts)

    def finish(self, *first):
        self.land(*first)
        while self.sends:
            self.land()
        return self.keep


def after(x, *done):
    return lax.optimization_barrier((x, *done))[0]


def send_order(stages, me):
    table = [0]
    for offsets in stages:
        table = [r ^ offset for r in table for offset in (0, *offsets)]
    return jnp.bitwise_xor(jnp.array(table, jnp.int32), me)


def pairs_of_bits(bits):
    stages = []
    for i in range(0, len(bits), 2):
        if i + 1 < len(bits):
            stages.append((bits[i], bits[i + 1], bits[i] ^ bits[i + 1]))
        else:
            stages.append((bits[i],))
    return stages


def on_device(n_dp, tokens, lengths, norm_gain, norm_shift, qkv_weight, proj_weight, up_weight, inner_bias,
              down_weight, outer_bias, cotangent):
    j = lax.axis_index("branch").astype(jnp.int32)
    me = lax.axis_index("dp").astype(jnp.int32)
    other = [(0, 1), (1, 0)]
    tokens_their = lax.ppermute(tokens, "branch", other)
    cotangent_their = lax.ppermute(cotangent, "branch", other)
    own, their = j.reshape(1), (1 - j).reshape(1)
    info = jnp.stack([j, lengths[0].astype(jnp.int32)])
    gain, shift = norm_gain.reshape(1, D), norm_shift.reshape(1, D)

    bits = [1 << i for i in range(n_dp.bit_length() - 1)]
    high_stages = pairs_of_bits(bits[2:])
    low_first = [(1,), (2,)] + high_stages
    order = send_order(low_first, me)
    ffb = FF_HALF // n_dp
    fast = ffb == LANES
    if fast:
        splits = FB // LANES
        plan = {
            "splits": splits,
            "pieces": n_dp,
            "pick": lambda s, a, i: 2 * (4 * i + a[1][s]) + a[0][0],
            "classes": jnp.array([1, 3, 0, 2], jnp.int32) ^ (me & 3),
            "subs": jnp.arange(4, dtype=jnp.int32) ^ (me >> 2),
            "weights": (up_weight, down_weight, inner_bias.reshape(1, FF)),
        }
    else:
        plan = {
            "splits": 1,
            "pieces": 0,
            "pick": lambda s, a, i: s,
            "classes": jnp.arange(FF_HALF // FB, dtype=jnp.int32),
            "subs": jnp.zeros((1,), jnp.int32),
            "weights": (
                lax.dynamic_index_in_dim(up_weight.reshape(D, n_dp, 2, ffb), j, 2, False).reshape(D, FF_HALF),
                lax.dynamic_index_in_dim(down_weight.reshape(n_dp, 2, ffb, D), j, 1, False).reshape(FF_HALF, D),
                lax.dynamic_index_in_dim(inner_bias.reshape(n_dp, 2, ffb), j, 1, False).reshape(1, FF_HALF),
            ),
        }
    plan["order"] = order

    def pieces_of(grads, table):
        if len(grads) == 2:
            return grads
        whole = grads[0]
        ordered = jnp.take(whole.reshape(n_dp, whole.shape[0] // n_dp, whole.shape[1]), table, axis=0)
        return ordered[: n_dp // 2], ordered[n_dp // 2 :]

    plan["weights"] = tuple(pltpu.with_memory_space_constraint(w, pltpu.HBM) for w in plan["weights"][:2]) + plan["weights"][2:]
    qkv_weight = pltpu.with_memory_space_constraint(qkv_weight, pltpu.HBM)
    proj_weight = pltpu.with_memory_space_constraint(proj_weight, pltpu.HBM)

    cosine, sine = rotary_tables()
    normed, hidden, grads_own, gb_own, expanded_own, gn_own, outer = mlp_own_call(
        info, plan, tokens, cotangent, gain, shift
    )
    qkv = qkv_half_call(own, info, 0, normed, qkv_weight, cosine, sine)
    info = after(info, qkv)
    normed, hidden, slope, expanded_their = mlp_forward_call(info, plan, tokens_their, gain, shift, normed, hidden)
    info = after(info, slope)
    grads, *down = down_grad_call(info, plan, hidden, grads_own, cotangent_their)
    down = Reduction(*pieces_of(down, order), low_first, n_dp)
    info = after(info, grads)
    gn_their, inner, *up = mlp_back_call(info, plan, normed, slope, grads, gb_own)

    up = Reduction(*pieces_of(up, order), low_first, n_dp)
    info = after(info, *down.land(gn_their), *up.land(gn_their))
    qkv = qkv_half_call(their, info, 1, normed, qkv_weight, cosine, sine, qkv)
    context, qe = attend_call(info, qkv)
    out_their = out_call(their, info, context, proj_weight, expanded_their)

    info = after(info, *down.land(out_their))
    out_received = lax.ppermute(out_their, "branch", other)
    grad_context, *proj = proj_back_call(info, plan, order, grads, context, proj_weight)
    info = after(info, *up.land(grad_context))
    dmix = attend_back_call(info, qe, qkv, context, grad_context, cosine, sine)

    down_grad = down.finish(dmix)
    info = after(info, out_received, down_grad)
    small = D // n_dp
    shard = small // 2
    first = qkv_grad_call(info, plan, normed, dmix, 0, 2, proj)
    if not fast:
        first = jnp.concatenate([first[0].reshape(n_dp, small, D), proj[0].reshape(n_dp, shard, D)], axis=1)
        first = jnp.take(first, order, axis=0)
        first = first[: n_dp // 2], first[n_dp // 2 :]
    info = after(info, *first)
    first = Reduction(*first, low_first, n_dp)
    *gn_send, sums_their = grad_normed_call(their, info, dmix, qkv_weight, gn_their, tokens_their, 1)

    info = after(info, *first.land(*gn_send))
    gn_first = lax.ppermute(gn_send[0], "branch", other)
    gn_own, sums_own = grad_normed_call(own, info, dmix, qkv_weight, gn_own, tokens, 0)
    info = after(info, gn_own)
    layer_out = out_call(
        own, info, context, proj_weight, expanded_own, (tokens, out_received, outer_bias.reshape(1, D))
    )
    info = after(info, layer_out)
    if fast:
        value = qkv_grad_call(info, plan, normed, dmix, 2, 1, (sums_own, sums_their, outer, inner))
    else:
        sums = sums_own + sums_their
        lines = jnp.concatenate([v.reshape(n_dp, small) for v in (sums[0], sums[1], outer)], axis=1)
        lines = jnp.concatenate(
            [jnp.pad(lines, ((0, 0), (0, 2 * LANES - 3 * small))), inner.reshape(n_dp, ffb)], axis=1
        )
        lines = jnp.pad(lines, ((0, 0), (0, HALF - lines.shape[1]))).astype(BF)
        lines = jnp.broadcast_to(lines[:, None], (n_dp, 16, HALF))
        value = qkv_grad_call(info, plan, normed, dmix, 2, 1)[0].reshape(n_dp, small, HALF)
        value = jnp.take(jnp.concatenate([value, lines], axis=1), order, axis=0)
        value = value[: n_dp // 2], value[n_dp // 2 :]
    up.finish(*value)
    landed = first.land(*value)
    value, up.keep, _ = lax.optimization_barrier((tuple(value), up.keep, (*landed, gn_first)))
    value = Reduction(*value, low_first, n_dp)
    up_mine = lax.dynamic_slice_in_dim(up.keep, j * shard, shard, 0)
    up_their = lax.dynamic_slice_in_dim(up.keep, (1 - j) * shard, shard, 0).astype(BF)
    up_their = lax.ppermute(up_their, "branch", other)
    landed = value.land()
    tokens_grad = finish_grad_call(gn_own, after(gn_first, *landed), tokens, grads_own, gain)
    up_mine, up_their, tokens_grad = lax.optimization_barrier((up_mine, up_their, tokens_grad))
    if fast:
        sources = tuple(p % 4 * HALF + p // 4 * LANES for p in range(n_dp))
        up_grad = assemble_call(info, up_mine, up_their, sources, LANES)
    else:
        up_their = up_their.astype(F32)
        low, high = jnp.where(j == 0, up_mine, up_their), jnp.where(j == 0, up_their, up_mine)
        up_grad = jnp.stack([low.reshape(shard, n_dp, ffb), high.reshape(shard, n_dp, ffb)], axis=2).reshape(shard, FF)
    first = first.finish(up_grad)
    value.land(first)
    value = value.finish()
    query_key, proj_piece = first[:small], first[small:]
    piece = jnp.concatenate([query_key, value[:small]], axis=1)
    line = value[small:]
    theirs = lax.dynamic_slice_in_dim(piece, (1 - j) * shard, shard, 0)
    theirs = jnp.concatenate([theirs, jnp.concatenate([line, line, line], axis=1)], axis=0).astype(BF)
    route = [(2 * p + h, n_dp * h + p) for h in range(2) for p in range(n_dp)]
    proj_grad = lax.ppermute(after(proj_piece.astype(BF), theirs), ("dp", "branch"), route).astype(F32)
    theirs = lax.ppermute(theirs, "branch", other)
    mine = lax.dynamic_slice_in_dim(piece, j * shard, shard, 0)
    qkv_grad = assemble_call(info, mine, theirs, (0, HALF, 2 * HALF), HALF) if fast else None
    triple = (line[0] + theirs[shard, :HALF].astype(F32))[: 3 * small].reshape(3, 2, shard)
    triple = lax.dynamic_index_in_dim(triple, j, 1, False)
    if not fast:
        mine = mine.reshape(shard, 3, HALF)
        theirs = theirs[:shard].astype(F32).reshape(shard, 3, HALF)
        qkv_grad = jnp.stack([jnp.where(j == 0, mine, theirs), jnp.where(j == 0, theirs, mine)], axis=2)
        qkv_grad = qkv_grad.reshape(shard, 3 * D)
    return (
        layer_out,
        tokens_grad,
        triple[0],
        triple[1],
        qkv_grad,
        proj_grad,
        up_grad,
        line[0, 2 * LANES : 2 * LANES + ffb],
        down_grad,
        triple[2],
    )


def solution(mesh):
    rows = P(("dp", "branch"), None)
    flat = P(("dp", "branch"))
    return jax.shard_map(
        functools.partial(on_device, mesh.shape["dp"]),
        mesh=mesh,
        in_specs=(rows, P("dp"), P(), P(), P(), P(), P(), P(), P(), P(), rows),
        out_specs=(rows, rows, flat, flat, rows, rows, rows, flat, rows, flat),
        check_vma=False,
    )
```

```python
import functools
import math

import jax
import jax.numpy as jnp
from jax import lax
from jax.experimental import pallas as pl
from jax.experimental.pallas import tpu as pltpu
from jax.sharding import PartitionSpec as P

D = 1024
HEADS = 16
HEAD_DIM = 64
ROT_DIM = 32
FF = 4096
SEQ_LEN = 1024
HALF = HEADS // 2 * HEAD_DIM
FF_HALF = FF // 2
LANES = 128
QB = 256
ROWS = 128
FB = 512
EPS = 1e-05
BF = jnp.bfloat16
F32 = jnp.float32


def params(mb=24):
    return pltpu.CompilerParams(vmem_limit_bytes=mb << 20)


def cost(flops, nbytes, trans=0):
    return pl.CostEstimate(flops=int(flops) // 1000, bytes_accessed=int(nbytes) // 1000, transcendentals=0)


def in_hbm(shape, dtype):
    return pltpu.HBM(tuple(shape), dtype)


def dot_nn(a, b):
    return jnp.dot(a, b, preferred_element_type=F32)


def dot_nt(a, b):
    return lax.dot_general(a, b, (((1,), (1,)), ((), ())), preferred_element_type=F32)


def dot_tn(a, b):
    return lax.dot_general(a, b, (((0,), (0,)), ((), ())), preferred_element_type=F32)


def rotary_tables():
    lane = jnp.arange(LANES, dtype=jnp.int32)
    channel = lane % HEAD_DIM
    frequency = jnp.power(10000.0, -(2.0 * (channel // 2).astype(F32)) / ROT_DIM)
    frequency = jnp.where(channel < ROT_DIM, frequency, 0.0)
    step = 32
    index = jnp.arange(2 * step, dtype=jnp.int32)
    position = jnp.where(index < step, index * (SEQ_LEN // step), index - step).astype(F32)
    angles = position[:, None] * frequency[None, :]
    cosine, sine = lax.optimization_barrier((jnp.cos(angles), jnp.sin(angles)))
    high_cosine, high_sine = cosine[:step, None], sine[:step, None]
    low_cosine, low_sine = cosine[None, step:], sine[None, step:]
    even = (lane % 2 == 0)[None, None, :]
    sine = high_sine * low_cosine + high_cosine * low_sine
    cosine = high_cosine * low_cosine - high_sine * low_sine
    return cosine.reshape(SEQ_LEN, LANES), jnp.where(even, -sine, sine).reshape(SEQ_LEN, LANES)


def rotate(x, cosine, sine):
    even = lax.broadcasted_iota(jnp.int32, x.shape, 1) % 2 == 0
    swapped = jnp.where(even, pltpu.roll(x, LANES - 1, 1), pltpu.roll(x, 1, 1))
    return x * cosine + swapped * sine


def unrotate(y, cosine, sine):
    even = lax.broadcasted_iota(jnp.int32, y.shape, 1) % 2 == 0
    swapped = jnp.where(even, pltpu.roll(y, LANES - 1, 1), pltpu.roll(y, 1, 1))
    return y * cosine - swapped * sine


def head_lanes(shape, head):
    lane = lax.broadcasted_iota(jnp.int32, shape, 1)
    own = (lane >= HEAD_DIM) if head else (lane < HEAD_DIM)
    spare = lane - (0 if head else HEAD_DIM)
    return own, spare


def keys_with_bias(k, head, length):
    own, spare = head_lanes(k.shape, head)
    row = lax.broadcasted_iota(jnp.int32, k.shape, 0)
    bias = jnp.where(row < length, 0.0, -1e30)
    extra = jnp.where(spare < 3, 1.0, jnp.where(spare == 3, bias, 0.0))
    return jnp.where(own, k.astype(F32), extra).astype(BF)


def attend_kernel(info_ref, q_ref, k_ref, v_ref, o_ref, qe_ref):
    length = info_ref[1]
    q = q_ref[0].astype(F32)
    k = k_ref[0]
    v = v_ref[0]
    tri = lax.broadcasted_iota(jnp.int32, (QB, QB), 0) >= lax.broadcasted_iota(jnp.int32, (QB, QB), 1)
    outs = []
    for head in range(2):
        own, spare = head_lanes((SEQ_LEN, LANES), head)
        ke = keys_with_bias(k, head, length)
        qe = jnp.where(own, q, jnp.where(spare == 3, 1.0, 0.0)).astype(BF)
        parts = []
        for b in range(SEQ_LEN // QB):
            lo, hi = b * QB, (b + 1) * QB
            s = dot_nt(qe[lo:hi], ke[:hi])
            diag = jnp.where(tri, s[:, lo:hi], -1e30)
            s = diag if b == 0 else jnp.concatenate([s[:, :lo], diag], axis=1)
            top = jnp.max(s, axis=1, keepdims=True)
            p = jnp.exp(s - top)
            total = jnp.sum(p, axis=1, keepdims=True)
            parts.append(dot_nn(p.astype(BF), v[:hi]) * (1.0 / total))
            lse = jnp.broadcast_to(top + jnp.log(total), (QB, LANES))
            first = lse.astype(BF).astype(F32)
            second = (lse - first).astype(BF).astype(F32)
            third = lse - first - second
            own_b, spare_b = head_lanes((QB, LANES), head)
            extra = jnp.where(
                spare_b == 0,
                -first,
                jnp.where(
                    spare_b == 1,
                    -second,
                    jnp.where(spare_b == 2, -third, jnp.where(spare_b == 3, 1.0, 0.0)),
                ),
            )
            qe_ref[head, lo:hi, :] = jnp.where(own_b, q[lo:hi], extra).astype(BF)
        outs.append(jnp.concatenate(parts, axis=0))
    own, _ = head_lanes((SEQ_LEN, LANES), 0)
    o_ref[...] = jnp.where(own, outs[0], outs[1]).astype(BF)


def attend_call(info, qkv):
    pairs = HALF // LANES
    spec = [pl.BlockSpec((1, SEQ_LEN, LANES), lambda p, n, t=t: (t, 0, p)) for t in range(3)]
    return pl.pallas_call(
        attend_kernel,
        grid_spec=pltpu.PrefetchScalarGridSpec(
            num_scalar_prefetch=1,
            grid=(pairs,),
            in_specs=spec,
            out_specs=[
                pl.BlockSpec((SEQ_LEN, LANES), lambda p, n: (0, p)),
                pl.BlockSpec((2, SEQ_LEN, LANES), lambda p, n: (p, 0, 0)),
            ],
        ),
        out_shape=[
            in_hbm((SEQ_LEN, HALF), BF),
            in_hbm((HEADS // 2, SEQ_LEN, LANES), BF),
        ],
        compiler_params=params(),
        cost_estimate=cost(
            2 * pairs * 10 * SEQ_LEN * SEQ_LEN * LANES, 2 * SEQ_LEN * HALF * 3, 4 * SEQ_LEN * SEQ_LEN
        ),
        name="attend",
    )(info, qkv, qkv, qkv)


def attend_back_kernel(info_ref, qe_ref, k_ref, v_ref, o_ref, g_ref, cos_ref, sin_ref, d_ref, dk_ref, dv_ref):
    length = info_ref[1]
    k = k_ref[0]
    v = v_ref[0]
    g = g_ref[...].astype(F32)
    o = o_ref[...].astype(F32)
    tri = lax.broadcasted_iota(jnp.int32, (QB, QB), 0) >= lax.broadcasted_iota(jnp.int32, (QB, QB), 1)
    queries = []
    for head in range(2):
        own, spare = head_lanes((SEQ_LEN, LANES), head)
        ke = keys_with_bias(k, head, length)
        ve = jnp.where(own, v.astype(F32), jnp.where(spare < 3, 1.0, 0.0)).astype(BF)
        inner = jnp.sum(jnp.where(own, g * o, 0.0), axis=1, keepdims=True)
        inner = jnp.broadcast_to(inner, (SEQ_LEN, LANES))
        first = inner.astype(BF).astype(F32)
        second = (inner - first).astype(BF).astype(F32)
        third = inner - first - second
        extra = jnp.where(
            spare == 0,
            -first,
            jnp.where(spare == 1, -second, jnp.where(spare == 2, -third, 0.0)),
        )
        ge = jnp.where(own, g, extra).astype(BF)
        parts = []
        for b in range(SEQ_LEN // QB):
            lo, hi = b * QB, (b + 1) * QB
            qb = qe_ref[head, lo:hi, :]
            gb = ge[lo:hi]
            s = dot_nt(qb, ke[:hi])
            diag = jnp.where(tri, s[:, lo:hi], -1e30)
            s = diag if b == 0 else jnp.concatenate([s[:, :lo], diag], axis=1)
            p = jnp.exp(s)
            ds = (p * dot_nt(gb, ve[:hi])).astype(BF)
            parts.append(dot_nn(ds, k[:hi]))
            dk = dot_tn(ds, qb)
            dv = dot_tn(p.astype(BF), gb)
            if b > 0:
                dk_ref[head, :lo] += dk[:lo]
                dv_ref[head, :lo] += dv[:lo]
            dk_ref[head, lo:hi] = dk[lo:hi]
            dv_ref[head, lo:hi] = dv[lo:hi]
        queries.append(jnp.concatenate(parts, axis=0))
    own, _ = head_lanes((SEQ_LEN, LANES), 0)
    cosine, sine = cos_ref[...], sin_ref[...]
    dq = jnp.where(own, queries[0], queries[1]) * HEAD_DIM**-0.5
    d_ref[0] = unrotate(dq, cosine, sine).astype(BF)
    d_ref[1] = unrotate(jnp.where(own, dk_ref[0], dk_ref[1]), cosine, sine).astype(BF)
    d_ref[2] = jnp.where(own, dv_ref[0], dv_ref[1]).astype(BF)


def attend_back_call(info, qe, qkv, context, grad_context, cosine, sine):
    pairs = HALF // LANES
    table = pl.BlockSpec((SEQ_LEN, LANES), lambda p, n: (0, 0))
    return pl.pallas_call(
        attend_back_kernel,
        grid_spec=pltpu.PrefetchScalarGridSpec(
            num_scalar_prefetch=1,
            grid=(pairs,),
            in_specs=[
                pl.BlockSpec((2, SEQ_LEN, LANES), lambda p, n: (p, 0, 0)),
                pl.BlockSpec((1, SEQ_LEN, LANES), lambda p, n: (1, 0, p)),
                pl.BlockSpec((1, SEQ_LEN, LANES), lambda p, n: (2, 0, p)),
                pl.BlockSpec((SEQ_LEN, LANES), lambda p, n: (0, p)),
                pl.BlockSpec((SEQ_LEN, LANES), lambda p, n: (0, p)),
                table,
                table,
            ],
            out_specs=pl.BlockSpec((3, SEQ_LEN, LANES), lambda p, n: (0, 0, p)),
            scratch_shapes=[
                pltpu.VMEM((2, SEQ_LEN, LANES), F32),
                pltpu.VMEM((2, SEQ_LEN, LANES), F32),
            ],
        ),
        out_shape=jax.ShapeDtypeStruct((3, SEQ_LEN, HALF), BF),
        compiler_params=params(),
        cost_estimate=cost(
            2 * pairs * 12 * SEQ_LEN * SEQ_LEN * LANES, 2 * SEQ_LEN * HALF * 4, 4 * SEQ_LEN * SEQ_LEN
        ),
        name="attend_back",
    )(info, qe, qkv, qkv, context, grad_context, cosine, sine)


def gelu_parts(v):
    c = math.sqrt(2.0 / math.pi)
    square = v * v
    half = 0.5 + 0.5 * jnp.tanh(v * (c + (c * 0.044715) * square))
    hidden = v * half
    slope = half * (1.0 + (v - hidden) * (2.0 * c + (6.0 * c * 0.044715) * square))
    return hidden, slope


def normalize(x):
    x = x.astype(F32)
    centred = x - jnp.mean(x, axis=1, keepdims=True)
    rstd = lax.rsqrt(jnp.mean(centred * centred, axis=1, keepdims=True) + EPS)
    return centred * rstd, rstd


def masked_rows(g, start, length):
    row = start + lax.broadcasted_iota(jnp.int32, g.shape, 0)
    return jnp.where(row < length, g.astype(F32), 0.0)


def joined(refs, axis):
    return refs[0][...] if len(refs) == 1 else jnp.concatenate([r[...] for r in refs], axis=axis)


def weight_specs(plan, rows_too=True):
    splits, wide, pick = plan["splits"], FB // plan["splits"], plan["pick"]
    specs = [pl.BlockSpec((D, wide), lambda s, *a, i=i: (0, pick(s, a, i))) for i in range(splits)]
    specs += [pl.BlockSpec((wide, D), lambda s, *a, i=i: (pick(s, a, i), 0)) for i in range(splits)]
    if rows_too:
        specs += [pl.BlockSpec((1, wide), lambda s, *a, i=i: (0, pick(s, a, i))) for i in range(splits)]
    return specs


def accumulate(ref, value):
    @pl.when(pl.program_id(0) == 0)
    def _():
        ref[...] = value

    @pl.when(pl.program_id(0) > 0)
    def _():
        ref[...] += value


def mlp_own_kernel(splits, info_ref, cls_ref, t_ref, c_ref, gain_ref, shift_ref, *refs):
    ups, downs, biases = refs[:splits], refs[splits : 2 * splits], refs[2 * splits : 3 * splits]
    x_ref, h_ref, g_ref, gb_ref, e_ref, gn_ref, outer_ref = refs[3 * splits :]

    @pl.when(pl.program_id(0) == 0)
    def _():
        outer_ref[...] = jnp.zeros_like(outer_ref)

        @pl.loop(0, t_ref.shape[0] // ROWS)
        def _(r):
            at = pl.ds(pl.multiple_of(r * ROWS, ROWS), ROWS)
            hat, _ = normalize(t_ref[at, :])
            x_ref[at, :] = (hat * gain_ref[...].astype(F32) + shift_ref[...].astype(F32)).astype(BF)
            g = masked_rows(c_ref[at, :], info_ref[0] * c_ref.shape[0] + r * ROWS, info_ref[1])
            g_ref[at, :] = g.astype(BF)
            outer_ref[...] += jnp.sum(g, axis=0, keepdims=True)

    up, down, bias = joined(ups, 1), joined(downs, 0), joined(biases, 1)
    before = dot_nn(x_ref[...], up) + bias.astype(F32)
    hidden, slope = gelu_parts(before)
    hidden = hidden.astype(BF)
    grad_before = (dot_nt(g_ref[...], down) * slope).astype(BF)
    h_ref[...] = hidden
    gb_ref[...] = grad_before
    accumulate(e_ref, dot_nn(hidden, down))
    accumulate(gn_ref, dot_nt(grad_before, up))


def mlp_own_call(info, plan, tokens, cotangent, gain, shift):
    rows, splits = tokens.shape[0], plan["splits"]
    fixed = lambda s, *a: (0, 0)
    up, down, bias = plan["weights"]
    whole = pl.BlockSpec((rows, D), fixed)
    wide = pl.BlockSpec((rows, FB), lambda s, *a: (0, s))
    return pl.pallas_call(
        functools.partial(mlp_own_kernel, splits),
        grid_spec=pltpu.PrefetchScalarGridSpec(
            num_scalar_prefetch=2,
            grid=(FF_HALF // FB,),
            in_specs=[whole, whole, pl.BlockSpec((1, D), fixed), pl.BlockSpec((1, D), fixed)] + weight_specs(plan),
            out_specs=[whole, wide, whole, wide, whole, whole, pl.BlockSpec((1, D), fixed)],
        ),
        out_shape=[
            jax.ShapeDtypeStruct((2 * rows, D), BF),
            in_hbm((2 * rows, FF_HALF), BF),
            in_hbm((rows, D), BF),
            in_hbm((rows, FF_HALF), BF),
            in_hbm((rows, D), F32),
            in_hbm((rows, D), F32),
            jax.ShapeDtypeStruct((1, D), F32),
        ],
        compiler_params=params(),
        cost_estimate=cost(8 * rows * D * FF_HALF, 12 * rows * D + 4 * D * FF_HALF, rows * FF_HALF),
        name="mlp_own",
    )(info, plan["classes"], tokens, cotangent, gain, shift, *([up] * splits), *([down] * splits), *([bias] * splits))


def mlp_forward_kernel(splits, info_ref, cls_ref, t_ref, gain_ref, shift_ref, *refs):
    ups, downs, biases = refs[:splits], refs[splits : 2 * splits], refs[2 * splits : 3 * splits]
    x_ref, h_ref, slope_ref, e_ref = refs[3 * splits + 2 :]

    @pl.when(pl.program_id(0) == 0)
    def _():
        @pl.loop(0, t_ref.shape[0] // ROWS)
        def _(r):
            at = pl.ds(pl.multiple_of(r * ROWS, ROWS), ROWS)
            hat, _ = normalize(t_ref[at, :])
            x_ref[at, :] = (hat * gain_ref[...].astype(F32) + shift_ref[...].astype(F32)).astype(BF)

    up, down, bias = joined(ups, 1), joined(downs, 0), joined(biases, 1)
    before = dot_nn(x_ref[...], up) + bias.astype(F32)
    hidden, slope = gelu_parts(before)
    hidden = hidden.astype(BF)
    h_ref[...] = hidden
    slope_ref[...] = slope.astype(BF)
    accumulate(e_ref, dot_nn(hidden, down))


def mlp_forward_call(info, plan, tokens, gain, shift, normed, hidden):
    rows, splits = tokens.shape[0], plan["splits"]
    fixed = lambda s, *a: (0, 0)
    up, down, bias = plan["weights"]
    whole = pl.BlockSpec((rows, D), fixed)
    anywhere = pl.BlockSpec(memory_space=pl.ANY)
    first = 5 + 3 * splits
    return pl.pallas_call(
        functools.partial(mlp_forward_kernel, splits),
        grid_spec=pltpu.PrefetchScalarGridSpec(
            num_scalar_prefetch=2,
            grid=(FF_HALF // FB,),
            in_specs=[whole, pl.BlockSpec((1, D), fixed), pl.BlockSpec((1, D), fixed)]
            + weight_specs(plan)
            + [anywhere, anywhere],
            out_specs=[
                pl.BlockSpec((rows, D), lambda s, *a: (1, 0)),
                pl.BlockSpec((rows, FB), lambda s, *a: (1, s)),
                pl.BlockSpec((rows, FB), lambda s, *a: (0, s)),
                whole,
            ],
        ),
        out_shape=[
            jax.ShapeDtypeStruct((2 * rows, D), BF),
            in_hbm((2 * rows, FF_HALF), BF),
            in_hbm((rows, FF_HALF), BF),
            in_hbm((rows, D), F32),
        ],
        input_output_aliases={first: 0, first + 1: 1},
        compiler_params=params(),
        cost_estimate=cost(4 * rows * D * FF_HALF, 12 * rows * D + 4 * D * FF_HALF, rows * FF_HALF),
        name="mlp_forward",
    )(info, plan["classes"], tokens, gain, shift, *([up] * splits), *([down] * splits), *([bias] * splits), normed, hidden)


def down_grad_kernel(splits, pieces, info_ref, cls_ref, sub_ref, h_ref, go_ref, c_ref, g_ref, *grads):
    rows = c_ref.shape[0]
    step = pl.program_id(0)

    @pl.when(step == 0)
    def _():
        g_ref[:rows] = go_ref[...]
        g_ref[rows:] = masked_rows(c_ref[...], (1 - info_ref[0]) * rows, info_ref[1]).astype(BF)

    grad_down = dot_tn(h_ref[...], g_ref[...]).astype(BF)
    if not pieces:
        grads[0][...] = grad_down
        return
    down_keep, down_send = grads
    block = FB // splits

    @pl.when(step < 2)
    def _():
        for i in range(splits):
            down_send[sub_ref[i]] = grad_down[i * block : (i + 1) * block]

    @pl.when(step >= 2)
    def _():
        for i in range(splits):
            down_keep[sub_ref[i]] = grad_down[i * block : (i + 1) * block]


def down_grad_call(info, plan, hidden, grads_own, cotangent):
    rows, splits, pieces = cotangent.shape[0], plan["splits"], plan["pieces"]
    fixed = lambda s, *a: (0, 0)
    whole = pl.BlockSpec((rows, D), fixed)
    out_specs = [pl.BlockSpec((2 * rows, D), fixed)]
    out_shape = [in_hbm((2 * rows, D), BF)]
    if pieces:
        half, down_rows = pieces // 2, FF_HALF // pieces
        out_specs += [
            pl.BlockSpec((splits, down_rows, D), lambda s, *a: (jnp.maximum(s - 2, 0), 0, 0)),
            pl.BlockSpec((splits, down_rows, D), lambda s, *a: (jnp.minimum(s, 1), 0, 0)),
        ]
        out_shape += [in_hbm((half, down_rows, D), BF)] * 2
    else:
        out_specs += [pl.BlockSpec((FB, D), lambda s, *a: (s, 0))]
        out_shape += [in_hbm((FF_HALF, D), BF)]
    return pl.pallas_call(
        functools.partial(down_grad_kernel, splits, pieces),
        grid_spec=pltpu.PrefetchScalarGridSpec(
            num_scalar_prefetch=3,
            grid=(FF_HALF // FB,),
            in_specs=[pl.BlockSpec((2 * rows, FB), lambda s, *a: (0, s)), whole, whole],
            out_specs=out_specs,
        ),
        out_shape=out_shape,
        compiler_params=params(),
        cost_estimate=cost(4 * rows * D * FF_HALF, 8 * rows * D + 2 * D * FF_HALF + 4 * rows * FF_HALF),
        name="down_grad",
    )(info, plan["classes"], plan["subs"], hidden, grads_own, cotangent)


def mlp_back_kernel(splits, pieces, info_ref, cls_ref, ord_ref, x_ref, slope_ref, g_ref, gb_ref, *refs):
    ups, downs = refs[:splits], refs[splits : 2 * splits]
    gn_ref, inner_ref, *grads = refs[2 * splits : -2 if pieces else -1]
    gball_ref = refs[-2 if pieces else -1]
    rows = g_ref.shape[0]
    up, down = joined(ups, 1), joined(downs, 0)
    grad_before = (dot_nt(g_ref[...], down) * slope_ref[...].astype(F32)).astype(BF)
    gball_ref[:rows] = gb_ref[...]
    gball_ref[rows:] = grad_before
    accumulate(gn_ref, dot_nt(grad_before, up))
    inner_ref[...] = jnp.sum(gball_ref[...].astype(F32), axis=0, keepdims=True)
    grad_up = dot_tn(x_ref[...], gball_ref[...]).astype(BF)
    if not pieces:
        grads[0][...] = grad_up
        return
    up_keep, up_send = grads
    upall_ref = refs[-1]
    upall_ref[...] = grad_up.reshape(upall_ref.shape)
    for q in range(pieces // 2):
        up_keep[q] = upall_ref[ord_ref[q]]
        up_send[q] = upall_ref[ord_ref[q + pieces // 2]]


def mlp_back_call(info, plan, normed, slope, grads, gb_own):
    rows, splits, pieces = gb_own.shape[0], plan["splits"], plan["pieces"]
    fixed = lambda s, *a: (0, 0)
    up, down, _ = plan["weights"]
    whole = pl.BlockSpec((rows, D), fixed)
    wide = pl.BlockSpec((rows, FB), lambda s, *a: (0, s))
    out_specs = [whole, pl.BlockSpec((1, FB), lambda s, i, cls, *a: (0, cls[s]))]
    out_shape = [in_hbm((rows, D), F32), jax.ShapeDtypeStruct((1, FF_HALF), F32)]
    scratch = [pltpu.VMEM((2 * rows, FB), BF)]
    if pieces:
        shape = (pieces // 2, D // pieces, FB)
        out_specs += [pl.BlockSpec(shape, lambda s, i, cls, *a: (0, 0, cls[s]))] * 2
        out_shape += [in_hbm(shape[:2] + (FF_HALF,), BF)] * 2
        scratch.append(pltpu.VMEM((pieces, D // pieces, FB), BF))
    else:
        out_specs += [pl.BlockSpec((D, FB), lambda s, *a: (0, s))]
        out_shape += [in_hbm((D, FF_HALF), BF)]
    return pl.pallas_call(
        functools.partial(mlp_back_kernel, splits, pieces),
        grid_spec=pltpu.PrefetchScalarGridSpec(
            num_scalar_prefetch=3,
            grid=(FF_HALF // FB,),
            in_specs=[
                pl.BlockSpec((2 * rows, D), fixed),
                wide,
                pl.BlockSpec((rows, D), lambda s, *a: (1, 0)),
                wide,
            ]
            + weight_specs(plan, False),
            out_specs=out_specs,
            scratch_shapes=scratch,
        ),
        out_shape=out_shape,
        compiler_params=params(),
        cost_estimate=cost(8 * rows * D * FF_HALF, 12 * rows * D + 6 * D * FF_HALF + 4 * rows * FF_HALF),
        name="mlp_back",
    )(info, plan["classes"], plan["halved"], normed, slope, grads, gb_own, *([up] * splits), *([down] * splits))


def qkv_half_kernel(place_ref, info_ref, x_ref, w_ref, cos_ref, sin_ref, *refs):
    o_ref = refs[-1]
    t = pl.program_id(0)
    chunk = 2 * LANES

    @pl.when(t == 2)
    def _():
        for c in range(0, HALF, chunk):
            o_ref[0, :, c : c + chunk] = dot_nn(x_ref[...], w_ref[:, c : c + chunk]).astype(BF)

    @pl.when(t < 2)
    def _():
        scale = jnp.where(t == 0, HEAD_DIM**-0.5, 1.0)
        cosine = cos_ref[...] * scale
        sine = sin_ref[...] * scale
        for c in range(0, HALF, chunk):
            mixed = dot_nn(x_ref[...], w_ref[:, c : c + chunk])
            for e in range(0, chunk, LANES):
                o_ref[0, :, c + e : c + e + LANES] = rotate(mixed[:, e : e + LANES], cosine, sine).astype(BF)


def qkv_half_call(place, info, half, normed, w, cosine, sine, qkv=None):
    rows = normed.shape[0] // 2
    table = pl.BlockSpec((rows, LANES), lambda t, p, i: (p[0], 0))
    more = [] if qkv is None else [qkv]
    return pl.pallas_call(
        qkv_half_kernel,
        grid_spec=pltpu.PrefetchScalarGridSpec(
            num_scalar_prefetch=2,
            grid=(3,),
            in_specs=[
                pl.BlockSpec((rows, D), lambda t, p, i: (half, 0)),
                pl.BlockSpec((D, HALF), lambda t, p, i: (0, 2 * t + i[0])),
                table,
                table,
            ]
            + [pl.BlockSpec(memory_space=pl.ANY)] * len(more),
            out_specs=pl.BlockSpec((1, rows, HALF), lambda t, p, i: (t, p[0], 0)),
        ),
        out_shape=in_hbm((3, 2 * rows, HALF), BF),
        input_output_aliases={6: 0} if more else {},
        compiler_params=params(),
        cost_estimate=cost(2 * rows * D * 3 * HALF, 2 * (rows * D + D * 3 * HALF + rows * 3 * HALF)),
        name="qkv",
    )(place, info, normed, w, cosine, sine, *more)


def send_out_kernel(place_ref, info_ref, c_ref, w_ref, e_ref, o_ref):
    o_ref[...] = (dot_nn(c_ref[...], w_ref[...]) + e_ref[...]).astype(BF)


def finish_out_kernel(place_ref, info_ref, c_ref, w_ref, e_ref, t_ref, r_ref, bias_ref, o_ref):
    total = dot_nn(c_ref[...], w_ref[...]) + e_ref[...] + bias_ref[...].astype(F32)
    o_ref[...] = (total + t_ref[...].astype(F32) + r_ref[...].astype(F32)).astype(BF)


def out_call(place, info, context, proj, expanded, rest=()):
    rows, block = expanded.shape[0], 256
    steps = rows // block
    row = pl.BlockSpec((block, D), lambda s, p, i: (s, 0))
    return pl.pallas_call(
        finish_out_kernel if rest else send_out_kernel,
        grid_spec=pltpu.PrefetchScalarGridSpec(
            num_scalar_prefetch=2,
            grid=(steps,),
            in_specs=[
                pl.BlockSpec((block, HALF), lambda s, p, i: (p[0] * steps + s, 0)),
                pl.BlockSpec((HALF, D), lambda s, p, i: (i[0], 0)),
                row,
            ]
            + ([row, row, pl.BlockSpec((1, D), lambda s, p, i: (0, 0))] if rest else []),
            out_specs=row,
        ),
        out_shape=in_hbm((rows, D), BF),
        compiler_params=params(),
        cost_estimate=cost(2 * rows * D * HALF, 8 * rows * D + 2 * HALF * D),
        name="finish_out" if rest else "send_out",
    )(place, info, context, proj, expanded, *rest)


def proj_back_kernel(info_ref, ord_ref, g_ref, c_ref, w_ref, gc_ref, *refs):
    acc_ref = refs[-2] if len(refs) > 2 else refs[-1]
    gc_ref[...] = dot_nt(g_ref[...], w_ref[...]).astype(BF)
    part = dot_tn(c_ref[...], g_ref[...])

    @pl.when(pl.program_id(0) == 0)
    def _():
        acc_ref[...] = part

    @pl.when(pl.program_id(0) == 1)
    def _():
        total = (acc_ref[...] + part).astype(BF)
        if len(refs) == 2:
            refs[0][...] = total
        else:
            keep, send, all_ref = refs[0], refs[1], refs[3]
            all_ref[...] = total.reshape(all_ref.shape)
            half = keep.shape[0]
            for q in range(half):
                keep[q] = all_ref[ord_ref[q]]
                send[q] = all_ref[ord_ref[q + half]]


def proj_back_call(info, plan, order, grads, context, proj):
    rows, pieces = grads.shape[0] // 2, plan["pieces"]
    scratch = [pltpu.VMEM((HALF, D), F32)]
    if pieces:
        shape = (pieces // 2, HALF // pieces, D)
        out_specs = [pl.BlockSpec(shape, lambda h, *a: (0, 0, 0))] * 2
        out_shape = [in_hbm(shape, BF)] * 2
        scratch.append(pltpu.VMEM((pieces, HALF // pieces, D), BF))
    else:
        out_specs = [pl.BlockSpec((HALF, D), lambda h, *a: (0, 0))]
        out_shape = [in_hbm((HALF, D), BF)]
    return pl.pallas_call(
        proj_back_kernel,
        grid_spec=pltpu.PrefetchScalarGridSpec(
            num_scalar_prefetch=2,
            grid=(2,),
            in_specs=[
                pl.BlockSpec((rows, D), lambda h, i, o: (h, 0)),
                pl.BlockSpec((rows, HALF), lambda h, i, o: (jnp.bitwise_xor(h, i[0]), 0)),
                pl.BlockSpec((HALF, D), lambda h, i, o: (i[0], 0)),
            ],
            out_specs=[pl.BlockSpec((rows, HALF), lambda h, i, o: (jnp.bitwise_xor(h, i[0]), 0))] + out_specs,
            scratch_shapes=scratch,
        ),
        out_shape=[in_hbm((2 * rows, HALF), BF)] + out_shape,
        compiler_params=params(),
        cost_estimate=cost(8 * rows * D * HALF, 4 * rows * D + 8 * rows * HALF + 4 * HALF * D),
        name="proj_back",
    )(info, order, grads, context, proj)


def line_of(p, rows, sums, outer, inner_ref):
    low = lax.broadcasted_iota(jnp.int32, (1, LANES), 1) < rows
    at = p // 2 * LANES
    three = [v[:, at : at + LANES] for v in (sums[0:1], sums[1:2], outer)]
    turned = [pltpu.roll(v, rows, 1) for v in three]
    if p % 2:
        three, turned = turned, three
    at = p % 4 * HALF + p // 4 * LANES
    parts = [jnp.where(low, three[0], turned[1]), jnp.where(low, three[2], 0.0), inner_ref[:, at : at + LANES]]
    return jnp.concatenate(parts + [jnp.zeros((1, LANES), F32)], axis=1)


def pair_grad_kernel(info_ref, ord_ref, x_ref, own_ref, their_ref, *refs):
    d = jnp.concatenate([own_ref[0], their_ref[0]], axis=0)
    total = dot_tn(x_ref[...], d).astype(BF)
    if len(refs) == 1:
        refs[0][...] = total
        return
    pk_ref, ps_ref, keep, send, all_ref = refs
    half, rows = keep.shape[0], all_ref.shape[1]
    all_ref[...] = total.reshape(all_ref.shape)
    for q in range(half):
        for out, proj, at in ((keep, pk_ref, q), (send, ps_ref, q + half)):
            out[q, :rows] = all_ref[ord_ref[at]]
            out[q, rows:] = proj[q]


def value_grad_kernel(info_ref, ord_ref, x_ref, own_ref, their_ref, so_ref, st_ref, outer_ref, inner_ref, keep, send,
                      all_ref):
    pieces, rows = all_ref.shape[0], x_ref.shape[1] // all_ref.shape[0]
    half = pieces // 2
    d = jnp.concatenate([own_ref[0], their_ref[0]], axis=0)
    all_ref[:, :rows] = dot_tn(x_ref[...], d).astype(BF).reshape(pieces, rows, HALF)
    sums = so_ref[...] + st_ref[...]
    outer = outer_ref[...]
    for p in range(pieces):
        line = line_of(p, rows, sums, outer, inner_ref)
        all_ref[p, rows:] = jnp.broadcast_to(line, (all_ref.shape[1] - rows, HALF)).astype(BF)
    for q in range(half):
        keep[q] = all_ref[ord_ref[q]]
        send[q] = all_ref[ord_ref[q + half]]


def qkv_grad_call(info, plan, normed, dmix, first, count, extra=()):
    rows, pieces = normed.shape[0] // 2, plan["pieces"]
    in_specs, scratch, kernel = [], [], pair_grad_kernel
    if not pieces:
        extra = ()
        out_specs = [pl.BlockSpec((D, HALF), lambda t, *a: (0, t))]
        out_shape = [in_hbm((D, count * HALF), BF)]
    else:
        height = D // pieces
        if count == 2:
            shape = (pieces // 2, height + HALF // pieces, HALF)
            in_specs = [pl.BlockSpec((pieces // 2, HALF // pieces, HALF), lambda t, *a: (0, 0, t))] * 2
            scratch = [pltpu.VMEM((pieces, height, HALF), BF)]
        else:
            kernel = value_grad_kernel
            shape = (pieces // 2, height + 16, HALF)
            in_specs = [pl.BlockSpec(v.shape, lambda t, *a: (0, 0)) for v in extra]
            scratch = [pltpu.VMEM((pieces, height + 16, HALF), BF)]
        out_specs = [pl.BlockSpec(shape, lambda t, *a: (0, 0, t))] * 2
        out_shape = [in_hbm(shape[:2] + (count * HALF,), BF)] * 2
    return pl.pallas_call(
        kernel,
        grid_spec=pltpu.PrefetchScalarGridSpec(
            num_scalar_prefetch=2,
            grid=(count,),
            in_specs=[
                pl.BlockSpec((2 * rows, D), lambda t, *a: (0, 0)),
                pl.BlockSpec((1, rows, HALF), lambda t, i, *a: (first + t, i[0], 0)),
                pl.BlockSpec((1, rows, HALF), lambda t, i, *a: (first + t, 1 - i[0], 0)),
            ]
            + in_specs,
            out_specs=out_specs,
            scratch_shapes=scratch,
        ),
        out_shape=out_shape,
        compiler_params=params(),
        cost_estimate=cost(4 * rows * D * count * HALF, 4 * rows * D + (4 * rows + 2 * D) * count * HALF),
        name="qkv_grad",
    )(info, plan["order"], normed, dmix, dmix, *extra)


def grad_normed_kernel(place_ref, info_ref, d_ref, wq_ref, wk_ref, wv_ref, base_ref, t_ref, *refs):
    outs, sum_ref = refs[:-1], refs[-1]
    total = base_ref[...]
    for t, w in enumerate((wq_ref, wk_ref, wv_ref)):
        total += dot_nt(d_ref[t], w[...])
    if len(outs) == 1:
        outs[0][...] = total.astype(outs[0].dtype)
    else:
        for r, o_ref in enumerate(outs):

            @pl.when(pl.program_id(0) == r)
            def _(o_ref=o_ref):
                o_ref[...] = total.astype(o_ref.dtype)

    hat, _ = normalize(t_ref[...])
    sums = jnp.concatenate([jnp.sum(total * hat, axis=0, keepdims=True), jnp.sum(total, axis=0, keepdims=True)], axis=0)
    accumulate(sum_ref, sums)


def grad_normed_call(place, info, dmix, w, base, tokens, parts):
    rows, block = base.shape[0], 256
    steps = rows // block
    row = pl.BlockSpec((block, D), lambda r, p, i: (r, 0))
    kind = BF if parts else F32
    count = parts or 1
    return pl.pallas_call(
        grad_normed_kernel,
        grid_spec=pltpu.PrefetchScalarGridSpec(
            num_scalar_prefetch=2,
            grid=(steps,),
            in_specs=[pl.BlockSpec((3, block, HALF), lambda r, p, i: (0, p[0] * steps + r, 0))]
            + [pl.BlockSpec((D, HALF), lambda r, p, i, t=t: (0, 2 * t + i[0])) for t in range(3)]
            + [row, row],
            out_specs=([row] if count == 1 else [pl.BlockSpec((block, D), lambda r, p, i: (0, 0))] * count)
            + [pl.BlockSpec((2, D), lambda r, p, i: (0, 0))],
        ),
        out_shape=[in_hbm((rows // count, D), kind)] * count + [jax.ShapeDtypeStruct((2, D), F32)],
        compiler_params=params(),
        cost_estimate=cost(2 * rows * D * 3 * HALF, 8 * rows * D + 6 * D * HALF + 6 * rows * HALF),
        name="grad_normed",
    )(place, info, dmix, w, w, w, base, tokens)


def assemble_kernel(sources, width, info_ref, mine_ref, their_ref, o_ref):
    first = info_ref[0] == 0
    rows = o_ref.shape[0]
    for k, at in enumerate(sources):
        mine = mine_ref[:, at : at + width]
        theirs = their_ref[:rows, at : at + width].astype(F32)
        o_ref[:, 2 * k * width : (2 * k + 1) * width] = jnp.where(first, mine, theirs)
        o_ref[:, (2 * k + 1) * width : (2 * k + 2) * width] = jnp.where(first, theirs, mine)


def assemble_call(info, mine, theirs, sources, width):
    whole = lambda v: pl.BlockSpec(v.shape, lambda s, i: (0, 0))
    shape = (mine.shape[0], 2 * width * len(sources))
    return pl.pallas_call(
        functools.partial(assemble_kernel, sources, width),
        grid_spec=pltpu.PrefetchScalarGridSpec(
            num_scalar_prefetch=1,
            grid=(1,),
            in_specs=[whole(mine), whole(theirs)],
            out_specs=pl.BlockSpec(shape, lambda s, i: (0, 0)),
        ),
        out_shape=in_hbm(shape, F32),
        compiler_params=params(),
        cost_estimate=cost(1000, 1000),
        name="assemble",
    )(info, mine, theirs)


def finish_grad_kernel(gn_ref, r_ref, t_ref, g_ref, gain_ref, o_ref):
    hat, rstd = normalize(t_ref[...])
    u = (gn_ref[...] + r_ref[...].astype(F32)) * gain_ref[...].astype(F32)
    inner = u - jnp.mean(u, axis=1, keepdims=True) - hat * jnp.mean(u * hat, axis=1, keepdims=True)
    o_ref[...] = g_ref[...].astype(F32) + inner * rstd


def finish_grad_call(grad_normed, received, tokens, grads, gain):
    rows, block = tokens.shape[0], 256
    row = pl.BlockSpec((block, D), lambda r: (r, 0))
    return pl.pallas_call(
        finish_grad_kernel,
        grid=(rows // block,),
        in_specs=[row, row, row, row, pl.BlockSpec((1, D), lambda r: (0, 0))],
        out_specs=row,
        out_shape=in_hbm((rows, D), F32),
        compiler_params=params(),
        cost_estimate=cost(20 * rows * D, 14 * rows * D),
        name="finish_grad",
    )(grad_normed, received, tokens, grads, gain)


class Reduction:
    def __init__(self, keep, send, stages, n_dp):
        self.keep, self.sends, self.stages, self.n_dp = keep, [send], list(stages), n_dp
        self.start()

    def start(self):
        offsets = self.stages.pop(0)
        self.flying = [
            lax.ppermute(part, "dp", [(i, i ^ offset) for i in range(self.n_dp)])
            for part, offset in zip(self.sends, offsets, strict=True)
        ]

    def land(self, *first):
        if first:
            self.keep = after(self.keep, *first)
        kind = self.flying[0].dtype
        pieces = self.keep.shape[0]
        count = pieces // (len(self.stages[0]) + 1) if self.stages else pieces
        parts = []
        for i in range(0, pieces, count):
            total = self.keep[i : i + count].astype(F32)
            for part in self.flying:
                total = total + part[i : i + count].astype(F32)
            parts.append(total)
        if not self.stages:
            self.keep, self.sends = parts[0][0], []
            return (self.keep,)
        parts = [part.astype(kind) for part in parts]
        self.keep, self.sends = parts[0], parts[1:]
        self.start()
        return tuple(parts)

    def finish(self, *first):
        self.land(*first)
        while self.sends:
            self.land()
        return self.keep


def after(x, *done):
    return lax.optimization_barrier((x, *done))[0]


def send_order(stages, me):
    table = [0]
    for offsets in stages:
        table = [r ^ offset for r in table for offset in (0, *offsets)]
    return jnp.bitwise_xor(jnp.array(table, jnp.int32), me)


def pairs_of_bits(bits):
    stages = []
    for i in range(0, len(bits), 2):
        if i + 1 < len(bits):
            stages.append((bits[i], bits[i + 1], bits[i] ^ bits[i + 1]))
        else:
            stages.append((bits[i],))
    return stages


def on_device(n_dp, tokens, lengths, norm_gain, norm_shift, qkv_weight, proj_weight, up_weight, inner_bias,
              down_weight, outer_bias, cotangent):
    j = lax.axis_index("branch").astype(jnp.int32)
    me = lax.axis_index("dp").astype(jnp.int32)
    other = [(0, 1), (1, 0)]
    tokens_their = lax.ppermute(tokens, "branch", other)
    cotangent_their = lax.ppermute(cotangent, "branch", other)
    own, their = j.reshape(1), (1 - j).reshape(1)
    info = jnp.stack([j, lengths[0].astype(jnp.int32)])
    gain, shift = norm_gain.reshape(1, D), norm_shift.reshape(1, D)

    bits = [1 << i for i in range(n_dp.bit_length() - 1)]
    high_stages = pairs_of_bits(bits[2:])
    low_first = [(1,), (2,)] + high_stages
    halvings = [(bit,) for bit in bits]
    order = send_order(low_first, me)
    ffb = FF_HALF // n_dp
    fast = ffb == LANES
    if fast:
        splits = FB // LANES
        plan = {
            "splits": splits,
            "pieces": n_dp,
            "pick": lambda s, a, i: 2 * (4 * i + a[1][s]) + a[0][0],
            "classes": jnp.array([1, 3, 0, 2], jnp.int32) ^ (me & 3),
            "subs": jnp.arange(4, dtype=jnp.int32) ^ (me >> 2),
            "weights": (up_weight, down_weight, inner_bias.reshape(1, FF)),
        }
    else:
        plan = {
            "splits": 1,
            "pieces": 0,
            "pick": lambda s, a, i: s,
            "classes": jnp.arange(FF_HALF // FB, dtype=jnp.int32),
            "subs": jnp.zeros((1,), jnp.int32),
            "weights": (
                lax.dynamic_index_in_dim(up_weight.reshape(D, n_dp, 2, ffb), j, 2, False).reshape(D, FF_HALF),
                lax.dynamic_index_in_dim(down_weight.reshape(n_dp, 2, ffb, D), j, 1, False).reshape(FF_HALF, D),
                lax.dynamic_index_in_dim(inner_bias.reshape(n_dp, 2, ffb), j, 1, False).reshape(1, FF_HALF),
            ),
        }
    plan["order"], plan["halved"] = order, send_order(halvings, me)

    def pieces_of(grads, table):
        if len(grads) == 2:
            return grads
        whole = grads[0]
        ordered = jnp.take(whole.reshape(n_dp, whole.shape[0] // n_dp, whole.shape[1]), table, axis=0)
        return ordered[: n_dp // 2], ordered[n_dp // 2 :]

    plan["weights"] = tuple(pltpu.with_memory_space_constraint(w, pltpu.HBM) for w in plan["weights"][:2]) + plan["weights"][2:]
    qkv_weight = pltpu.with_memory_space_constraint(qkv_weight, pltpu.HBM)
    proj_weight = pltpu.with_memory_space_constraint(proj_weight, pltpu.HBM)

    cosine, sine = rotary_tables()
    normed, hidden, grads_own, gb_own, expanded_own, gn_own, outer = mlp_own_call(
        info, plan, tokens, cotangent, gain, shift
    )
    qkv = qkv_half_call(own, info, 0, normed, qkv_weight, cosine, sine)
    info = after(info, qkv)
    normed, hidden, slope, expanded_their = mlp_forward_call(info, plan, tokens_their, gain, shift, normed, hidden)
    info = after(info, slope)
    grads, *down = down_grad_call(info, plan, hidden, grads_own, cotangent_their)
    down = Reduction(*pieces_of(down, order), low_first, n_dp)
    info = after(info, grads)
    gn_their, inner, *up = mlp_back_call(info, plan, normed, slope, grads, gb_own)

    up = Reduction(*pieces_of(up, plan["halved"]), halvings, n_dp)
    info = after(info, *down.land(gn_their), *up.land(gn_their))
    qkv = qkv_half_call(their, info, 1, normed, qkv_weight, cosine, sine, qkv)
    context, qe = attend_call(info, qkv)
    out_their = out_call(their, info, context, proj_weight, expanded_their)

    info = after(info, *down.land(out_their))
    out_received = lax.ppermute(out_their, "branch", other)
    grad_context, *proj = proj_back_call(info, plan, order, grads, context, proj_weight)
    info = after(info, *up.land(grad_context))
    dmix = attend_back_call(info, qe, qkv, context, grad_context, cosine, sine)

    down_grad = down.finish(dmix)
    info = after(info, out_received, down_grad, *up.land(dmix))
    small = D // n_dp
    shard = small // 2
    first = qkv_grad_call(info, plan, normed, dmix, 0, 2, proj)
    if not fast:
        first = jnp.concatenate([first[0].reshape(n_dp, small, D), proj[0].reshape(n_dp, shard, D)], axis=1)
        first = jnp.take(first, order, axis=0)
        first = first[: n_dp // 2], first[n_dp // 2 :]
    info = after(info, *first)
    first = Reduction(*first, low_first, n_dp)
    *gn_send, sums_their = grad_normed_call(their, info, dmix, qkv_weight, gn_their, tokens_their, 1)

    info = after(info, *first.land(*gn_send))
    gn_first = lax.ppermute(gn_send[0], "branch", other)
    gn_own, sums_own = grad_normed_call(own, info, dmix, qkv_weight, gn_own, tokens, 0)
    info = after(info, gn_own)
    layer_out = out_call(
        own, info, context, proj_weight, expanded_own, (tokens, out_received, outer_bias.reshape(1, D))
    )
    info = after(info, layer_out)
    if fast:
        value = qkv_grad_call(info, plan, normed, dmix, 2, 1, (sums_own, sums_their, outer, inner))
    else:
        sums = sums_own + sums_their
        lines = jnp.concatenate([v.reshape(n_dp, small) for v in (sums[0], sums[1], outer)], axis=1)
        lines = jnp.concatenate(
            [jnp.pad(lines, ((0, 0), (0, 2 * LANES - 3 * small))), inner.reshape(n_dp, ffb)], axis=1
        )
        lines = jnp.pad(lines, ((0, 0), (0, HALF - lines.shape[1]))).astype(BF)
        lines = jnp.broadcast_to(lines[:, None], (n_dp, 16, HALF))
        value = qkv_grad_call(info, plan, normed, dmix, 2, 1)[0].reshape(n_dp, small, HALF)
        value = jnp.take(jnp.concatenate([value, lines], axis=1), order, axis=0)
        value = value[: n_dp // 2], value[n_dp // 2 :]
    up.finish(*value)
    landed = first.land(*value)
    value, up.keep, _ = lax.optimization_barrier((tuple(value), up.keep, landed))
    value = Reduction(*value, low_first, n_dp)
    up_mine = lax.dynamic_slice_in_dim(up.keep, j * shard, shard, 0)
    up_their = lax.dynamic_slice_in_dim(up.keep, (1 - j) * shard, shard, 0).astype(BF)
    up_their = lax.ppermute(up_their, "branch", other)
    value.keep, gn_first = lax.optimization_barrier((value.keep, gn_first))
    landed = value.land()
    tokens_grad = finish_grad_call(gn_own, after(gn_first, *landed), tokens, grads_own, gain)
    up_mine, up_their, tokens_grad = lax.optimization_barrier((up_mine, up_their, tokens_grad))
    if fast:
        sources = tuple(p % 4 * HALF + p // 4 * LANES for p in range(n_dp))
        up_grad = assemble_call(info, up_mine, up_their, sources, LANES)
    else:
        up_their = up_their.astype(F32)
        low, high = jnp.where(j == 0, up_mine, up_their), jnp.where(j == 0, up_their, up_mine)
        up_grad = jnp.stack([low.reshape(shard, n_dp, ffb), high.reshape(shard, n_dp, ffb)], axis=2).reshape(shard, FF)
    first = first.finish(up_grad)
    value.land(first)
    value = value.finish()
    query_key, proj_piece = first[:small], first[small:]
    piece = jnp.concatenate([query_key, value[:small]], axis=1)
    line = value[small:]
    theirs = lax.dynamic_slice_in_dim(piece, (1 - j) * shard, shard, 0)
    theirs = jnp.concatenate([theirs, jnp.concatenate([line, line, line], axis=1)], axis=0).astype(BF)
    route = [(2 * p + h, n_dp * h + p) for h in range(2) for p in range(n_dp)]
    proj_grad = lax.ppermute(after(proj_piece.astype(BF), theirs), ("dp", "branch"), route).astype(F32)
    theirs = lax.ppermute(theirs, "branch", other)
    mine = lax.dynamic_slice_in_dim(piece, j * shard, shard, 0)
    qkv_grad = assemble_call(info, mine, theirs, (0, HALF, 2 * HALF), HALF) if fast else None
    triple = (line[0] + theirs[shard, :HALF].astype(F32))[: 3 * small].reshape(3, 2, shard)
    triple = lax.dynamic_index_in_dim(triple, j, 1, False)
    if not fast:
        mine = mine.reshape(shard, 3, HALF)
        theirs = theirs[:shard].astype(F32).reshape(shard, 3, HALF)
        qkv_grad = jnp.stack([jnp.where(j == 0, mine, theirs), jnp.where(j == 0, theirs, mine)], axis=2)
        qkv_grad = qkv_grad.reshape(shard, 3 * D)
    return (
        layer_out,
        tokens_grad,
        triple[0],
        triple[1],
        qkv_grad,
        proj_grad,
        up_grad,
        line[0, 2 * LANES : 2 * LANES + ffb],
        down_grad,
        triple[2],
    )


def solution(mesh):
    rows = P(("dp", "branch"), None)
    flat = P(("dp", "branch"))
    return jax.shard_map(
        functools.partial(on_device, mesh.shape["dp"]),
        mesh=mesh,
        in_specs=(rows, P("dp"), P(), P(), P(), P(), P(), P(), P(), P(), rows),
        out_specs=(rows, rows, flat, flat, rows, rows, rows, flat, rows, flat),
        check_vma=False,
    )
```

```python
import functools
import math

import jax
import jax.numpy as jnp
from jax import lax
from jax.experimental import pallas as pl
from jax.experimental.pallas import tpu as pltpu
from jax.sharding import PartitionSpec as P

D = 1024
HEADS = 16
HEAD_DIM = 64
ROT_DIM = 32
FF = 4096
SEQ_LEN = 1024
HALF = HEADS // 2 * HEAD_DIM
FF_HALF = FF // 2
LANES = 128
QB = 256
ROWS = 128
FB = 512
EPS = 1e-05
BF = jnp.bfloat16
F32 = jnp.float32


def params(mb=24):
    return pltpu.CompilerParams(vmem_limit_bytes=mb << 20)


def cost(flops, nbytes, trans=0):
    return pl.CostEstimate(flops=int(flops) // 1000, bytes_accessed=int(nbytes) // 1000, transcendentals=0)


def in_hbm(shape, dtype):
    return pltpu.HBM(tuple(shape), dtype)


def stay(x):
    return pltpu.with_memory_space_constraint(x, pltpu.HBM)


def dot_nn(a, b):
    return jnp.dot(a, b, preferred_element_type=F32)


def dot_nt(a, b):
    return lax.dot_general(a, b, (((1,), (1,)), ((), ())), preferred_element_type=F32)


def dot_tn(a, b):
    return lax.dot_general(a, b, (((0,), (0,)), ((), ())), preferred_element_type=F32)


def rotary_tables():
    lane = jnp.arange(LANES, dtype=jnp.int32)
    channel = lane % HEAD_DIM
    frequency = jnp.power(10000.0, -(2.0 * (channel // 2).astype(F32)) / ROT_DIM)
    frequency = jnp.where(channel < ROT_DIM, frequency, 0.0)
    step = 32
    index = jnp.arange(2 * step, dtype=jnp.int32)
    position = jnp.where(index < step, index * (SEQ_LEN // step), index - step).astype(F32)
    angles = position[:, None] * frequency[None, :]
    cosine, sine = lax.optimization_barrier((jnp.cos(angles), jnp.sin(angles)))
    high_cosine, high_sine = cosine[:step, None], sine[:step, None]
    low_cosine, low_sine = cosine[None, step:], sine[None, step:]
    even = (lane % 2 == 0)[None, None, :]
    sine = high_sine * low_cosine + high_cosine * low_sine
    cosine = high_cosine * low_cosine - high_sine * low_sine
    return cosine.reshape(SEQ_LEN, LANES), jnp.where(even, -sine, sine).reshape(SEQ_LEN, LANES)


def rotate(x, cosine, sine):
    even = lax.broadcasted_iota(jnp.int32, x.shape, 1) % 2 == 0
    swapped = jnp.where(even, pltpu.roll(x, LANES - 1, 1), pltpu.roll(x, 1, 1))
    return x * cosine + swapped * sine


def unrotate(y, cosine, sine):
    even = lax.broadcasted_iota(jnp.int32, y.shape, 1) % 2 == 0
    swapped = jnp.where(even, pltpu.roll(y, LANES - 1, 1), pltpu.roll(y, 1, 1))
    return y * cosine - swapped * sine


def head_lanes(shape, head):
    lane = lax.broadcasted_iota(jnp.int32, shape, 1)
    own = (lane >= HEAD_DIM) if head else (lane < HEAD_DIM)
    spare = lane - (0 if head else HEAD_DIM)
    return own, spare


def keys_with_bias(k, head, length):
    own, spare = head_lanes(k.shape, head)
    row = lax.broadcasted_iota(jnp.int32, k.shape, 0)
    bias = jnp.where(row < length, 0.0, -1e30)
    extra = jnp.where(spare < 3, 1.0, jnp.where(spare == 3, bias, 0.0))
    return jnp.where(own, k.astype(F32), extra).astype(BF)


def attend_kernel(info_ref, q_ref, k_ref, v_ref, o_ref, qe_ref):
    length = info_ref[1]
    q = q_ref[0].astype(F32)
    k = k_ref[0]
    v = v_ref[0]
    tri = lax.broadcasted_iota(jnp.int32, (QB, QB), 0) >= lax.broadcasted_iota(jnp.int32, (QB, QB), 1)
    outs = []
    for head in range(2):
        own, spare = head_lanes((SEQ_LEN, LANES), head)
        ke = keys_with_bias(k, head, length)
        qe = jnp.where(own, q, jnp.where(spare == 3, 1.0, 0.0)).astype(BF)
        parts = []
        for b in range(SEQ_LEN // QB):
            lo, hi = b * QB, (b + 1) * QB
            s = dot_nt(qe[lo:hi], ke[:hi])
            diag = jnp.where(tri, s[:, lo:hi], -1e30)
            s = diag if b == 0 else jnp.concatenate([s[:, :lo], diag], axis=1)
            top = jnp.max(s, axis=1, keepdims=True)
            p = jnp.exp(s - top)
            total = jnp.sum(p, axis=1, keepdims=True)
            parts.append(dot_nn(p.astype(BF), v[:hi]) * (1.0 / total))
            lse = jnp.broadcast_to(top + jnp.log(total), (QB, LANES))
            first = lse.astype(BF).astype(F32)
            second = (lse - first).astype(BF).astype(F32)
            third = lse - first - second
            own_b, spare_b = head_lanes((QB, LANES), head)
            extra = jnp.where(
                spare_b == 0,
                -first,
                jnp.where(
                    spare_b == 1,
                    -second,
                    jnp.where(spare_b == 2, -third, jnp.where(spare_b == 3, 1.0, 0.0)),
                ),
            )
            qe_ref[head, lo:hi, :] = jnp.where(own_b, q[lo:hi], extra).astype(BF)
        outs.append(jnp.concatenate(parts, axis=0))
    own, _ = head_lanes((SEQ_LEN, LANES), 0)
    o_ref[...] = jnp.where(own, outs[0], outs[1]).astype(BF)


def attend_call(info, qkv):
    pairs = HALF // LANES
    spec = [pl.BlockSpec((1, SEQ_LEN, LANES), lambda p, n, t=t: (t, 0, p)) for t in range(3)]
    return pl.pallas_call(
        attend_kernel,
        grid_spec=pltpu.PrefetchScalarGridSpec(
            num_scalar_prefetch=1,
            grid=(pairs,),
            in_specs=spec,
            out_specs=[
                pl.BlockSpec((SEQ_LEN, LANES), lambda p, n: (0, p)),
                pl.BlockSpec((2, SEQ_LEN, LANES), lambda p, n: (p, 0, 0)),
            ],
        ),
        out_shape=[
            in_hbm((SEQ_LEN, HALF), BF),
            in_hbm((HEADS // 2, SEQ_LEN, LANES), BF),
        ],
        compiler_params=params(),
        cost_estimate=cost(
            2 * pairs * 10 * SEQ_LEN * SEQ_LEN * LANES, 2 * SEQ_LEN * HALF * 3, 4 * SEQ_LEN * SEQ_LEN
        ),
        name="attend",
    )(info, qkv, qkv, qkv)


def attend_back_kernel(info_ref, qe_ref, k_ref, v_ref, o_ref, g_ref, cos_ref, sin_ref, d_ref, dk_ref, dv_ref):
    length = info_ref[1]
    k = k_ref[0]
    v = v_ref[0]
    g = g_ref[...].astype(F32)
    o = o_ref[...].astype(F32)
    tri = lax.broadcasted_iota(jnp.int32, (QB, QB), 0) >= lax.broadcasted_iota(jnp.int32, (QB, QB), 1)
    queries = []
    for head in range(2):
        own, spare = head_lanes((SEQ_LEN, LANES), head)
        ke = keys_with_bias(k, head, length)
        ve = jnp.where(own, v.astype(F32), jnp.where(spare < 3, 1.0, 0.0)).astype(BF)
        inner = jnp.sum(jnp.where(own, g * o, 0.0), axis=1, keepdims=True)
        inner = jnp.broadcast_to(inner, (SEQ_LEN, LANES))
        first = inner.astype(BF).astype(F32)
        second = (inner - first).astype(BF).astype(F32)
        third = inner - first - second
        extra = jnp.where(
            spare == 0,
            -first,
            jnp.where(spare == 1, -second, jnp.where(spare == 2, -third, 0.0)),
        )
        ge = jnp.where(own, g, extra).astype(BF)
        parts = []
        for b in range(SEQ_LEN // QB):
            lo, hi = b * QB, (b + 1) * QB
            qb = qe_ref[head, lo:hi, :]
            gb = ge[lo:hi]
            s = dot_nt(qb, ke[:hi])
            diag = jnp.where(tri, s[:, lo:hi], -1e30)
            s = diag if b == 0 else jnp.concatenate([s[:, :lo], diag], axis=1)
            p = jnp.exp(s)
            ds = (p * dot_nt(gb, ve[:hi])).astype(BF)
            parts.append(dot_nn(ds, k[:hi]))
            dk = dot_tn(ds, qb)
            dv = dot_tn(p.astype(BF), gb)
            if b > 0:
                dk_ref[head, :lo] += dk[:lo]
                dv_ref[head, :lo] += dv[:lo]
            dk_ref[head, lo:hi] = dk[lo:hi]
            dv_ref[head, lo:hi] = dv[lo:hi]
        queries.append(jnp.concatenate(parts, axis=0))
    own, _ = head_lanes((SEQ_LEN, LANES), 0)
    cosine, sine = cos_ref[...], sin_ref[...]
    dq = jnp.where(own, queries[0], queries[1]) * HEAD_DIM**-0.5
    d_ref[0] = unrotate(dq, cosine, sine).astype(BF)
    d_ref[1] = unrotate(jnp.where(own, dk_ref[0], dk_ref[1]), cosine, sine).astype(BF)
    d_ref[2] = jnp.where(own, dv_ref[0], dv_ref[1]).astype(BF)


def attend_back_call(info, qe, qkv, context, grad_context, cosine, sine):
    pairs = HALF // LANES
    table = pl.BlockSpec((SEQ_LEN, LANES), lambda p, n: (0, 0))
    return pl.pallas_call(
        attend_back_kernel,
        grid_spec=pltpu.PrefetchScalarGridSpec(
            num_scalar_prefetch=1,
            grid=(pairs,),
            in_specs=[
                pl.BlockSpec((2, SEQ_LEN, LANES), lambda p, n: (p, 0, 0)),
                pl.BlockSpec((1, SEQ_LEN, LANES), lambda p, n: (1, 0, p)),
                pl.BlockSpec((1, SEQ_LEN, LANES), lambda p, n: (2, 0, p)),
                pl.BlockSpec((SEQ_LEN, LANES), lambda p, n: (0, p)),
                pl.BlockSpec((SEQ_LEN, LANES), lambda p, n: (0, p)),
                table,
                table,
            ],
            out_specs=pl.BlockSpec((3, SEQ_LEN, LANES), lambda p, n: (0, 0, p)),
            scratch_shapes=[
                pltpu.VMEM((2, SEQ_LEN, LANES), F32),
                pltpu.VMEM((2, SEQ_LEN, LANES), F32),
            ],
        ),
        out_shape=jax.ShapeDtypeStruct((3, SEQ_LEN, HALF), BF),
        compiler_params=params(),
        cost_estimate=cost(
            2 * pairs * 12 * SEQ_LEN * SEQ_LEN * LANES, 2 * SEQ_LEN * HALF * 4, 4 * SEQ_LEN * SEQ_LEN
        ),
        name="attend_back",
    )(info, qe, qkv, qkv, context, grad_context, cosine, sine)


def gelu_parts(v):
    c = math.sqrt(2.0 / math.pi)
    square = v * v
    half = 0.5 + 0.5 * jnp.tanh(v * (c + (c * 0.044715) * square))
    hidden = v * half
    slope = half * (1.0 + (v - hidden) * (2.0 * c + (6.0 * c * 0.044715) * square))
    return hidden, slope


def normalize(x):
    x = x.astype(F32)
    centred = x - jnp.mean(x, axis=1, keepdims=True)
    rstd = lax.rsqrt(jnp.mean(centred * centred, axis=1, keepdims=True) + EPS)
    return centred * rstd, rstd


def masked_rows(g, start, length):
    row = start + lax.broadcasted_iota(jnp.int32, g.shape, 0)
    return jnp.where(row < length, g.astype(F32), 0.0)


def joined(refs, axis):
    return refs[0][...] if len(refs) == 1 else jnp.concatenate([r[...] for r in refs], axis=axis)


def weight_specs(plan, rows_too=True):
    splits, wide, pick = plan["splits"], FB // plan["splits"], plan["pick"]
    specs = [pl.BlockSpec((D, wide), lambda s, *a, i=i: (0, pick(s, a, i))) for i in range(splits)]
    specs += [pl.BlockSpec((wide, D), lambda s, *a, i=i: (pick(s, a, i), 0)) for i in range(splits)]
    if rows_too:
        specs += [pl.BlockSpec((1, wide), lambda s, *a, i=i: (0, pick(s, a, i))) for i in range(splits)]
    return specs


def accumulate(ref, value):
    @pl.when(pl.program_id(0) == 0)
    def _():
        ref[...] = value

    @pl.when(pl.program_id(0) > 0)
    def _():
        ref[...] += value


def mlp_own_kernel(splits, info_ref, cls_ref, t_ref, c_ref, gain_ref, shift_ref, *refs):
    ups, downs, biases = refs[:splits], refs[splits : 2 * splits], refs[2 * splits : 3 * splits]
    x_ref, h_ref, g_ref, gb_ref, e_ref, gn_ref, outer_ref = refs[3 * splits :]

    @pl.when(pl.program_id(0) == 0)
    def _():
        outer_ref[...] = jnp.zeros_like(outer_ref)

        @pl.loop(0, t_ref.shape[0] // ROWS)
        def _(r):
            at = pl.ds(pl.multiple_of(r * ROWS, ROWS), ROWS)
            hat, _ = normalize(t_ref[at, :])
            x_ref[at, :] = (hat * gain_ref[...].astype(F32) + shift_ref[...].astype(F32)).astype(BF)
            g = masked_rows(c_ref[at, :], info_ref[0] * c_ref.shape[0] + r * ROWS, info_ref[1])
            g_ref[at, :] = g.astype(BF)
            outer_ref[...] += jnp.sum(g, axis=0, keepdims=True)

    up, down, bias = joined(ups, 1), joined(downs, 0), joined(biases, 1)
    before = dot_nn(x_ref[...], up) + bias.astype(F32)
    hidden, slope = gelu_parts(before)
    hidden = hidden.astype(BF)
    grad_before = (dot_nt(g_ref[...], down) * slope).astype(BF)
    h_ref[...] = hidden
    gb_ref[...] = grad_before
    accumulate(e_ref, dot_nn(hidden, down))
    accumulate(gn_ref, dot_nt(grad_before, up))


def mlp_own_call(info, plan, tokens, cotangent, gain, shift):
    rows, splits = tokens.shape[0], plan["splits"]
    fixed = lambda s, *a: (0, 0)
    up, down, bias = plan["weights"]
    whole = pl.BlockSpec((rows, D), fixed)
    wide = pl.BlockSpec((rows, FB), lambda s, *a: (0, s))
    return pl.pallas_call(
        functools.partial(mlp_own_kernel, splits),
        grid_spec=pltpu.PrefetchScalarGridSpec(
            num_scalar_prefetch=2,
            grid=(FF_HALF // FB,),
            in_specs=[whole, whole, pl.BlockSpec((1, D), fixed), pl.BlockSpec((1, D), fixed)] + weight_specs(plan),
            out_specs=[whole, wide, whole, wide, whole, whole, pl.BlockSpec((1, D), fixed)],
        ),
        out_shape=[
            jax.ShapeDtypeStruct((2 * rows, D), BF),
            in_hbm((2 * rows, FF_HALF), BF),
            in_hbm((rows, D), BF),
            in_hbm((rows, FF_HALF), BF),
            in_hbm((rows, D), F32),
            in_hbm((rows, D), F32),
            jax.ShapeDtypeStruct((1, D), F32),
        ],
        compiler_params=params(),
        cost_estimate=cost(8 * rows * D * FF_HALF, 12 * rows * D + 4 * D * FF_HALF, rows * FF_HALF),
        name="mlp_own",
    )(info, plan["classes"], tokens, cotangent, gain, shift, *([up] * splits), *([down] * splits), *([bias] * splits))


def mlp_forward_kernel(splits, info_ref, cls_ref, t_ref, gain_ref, shift_ref, *refs):
    ups, downs, biases = refs[:splits], refs[splits : 2 * splits], refs[2 * splits : 3 * splits]
    x_ref, h_ref, slope_ref, e_ref = refs[3 * splits + 2 :]

    @pl.when(pl.program_id(0) == 0)
    def _():
        @pl.loop(0, t_ref.shape[0] // ROWS)
        def _(r):
            at = pl.ds(pl.multiple_of(r * ROWS, ROWS), ROWS)
            hat, _ = normalize(t_ref[at, :])
            x_ref[at, :] = (hat * gain_ref[...].astype(F32) + shift_ref[...].astype(F32)).astype(BF)

    up, down, bias = joined(ups, 1), joined(downs, 0), joined(biases, 1)
    before = dot_nn(x_ref[...], up) + bias.astype(F32)
    hidden, slope = gelu_parts(before)
    hidden = hidden.astype(BF)
    h_ref[...] = hidden
    slope_ref[...] = slope.astype(BF)
    accumulate(e_ref, dot_nn(hidden, down))


def mlp_forward_call(info, plan, tokens, gain, shift, normed, hidden):
    rows, splits = tokens.shape[0], plan["splits"]
    fixed = lambda s, *a: (0, 0)
    up, down, bias = plan["weights"]
    whole = pl.BlockSpec((rows, D), fixed)
    anywhere = pl.BlockSpec(memory_space=pl.ANY)
    first = 5 + 3 * splits
    return pl.pallas_call(
        functools.partial(mlp_forward_kernel, splits),
        grid_spec=pltpu.PrefetchScalarGridSpec(
            num_scalar_prefetch=2,
            grid=(FF_HALF // FB,),
            in_specs=[whole, pl.BlockSpec((1, D), fixed), pl.BlockSpec((1, D), fixed)]
            + weight_specs(plan)
            + [anywhere, anywhere],
            out_specs=[
                pl.BlockSpec((rows, D), lambda s, *a: (1, 0)),
                pl.BlockSpec((rows, FB), lambda s, *a: (1, s)),
                pl.BlockSpec((rows, FB), lambda s, *a: (0, s)),
                whole,
            ],
        ),
        out_shape=[
            jax.ShapeDtypeStruct((2 * rows, D), BF),
            in_hbm((2 * rows, FF_HALF), BF),
            in_hbm((rows, FF_HALF), BF),
            in_hbm((rows, D), F32),
        ],
        input_output_aliases={first: 0, first + 1: 1},
        compiler_params=params(),
        cost_estimate=cost(4 * rows * D * FF_HALF, 12 * rows * D + 4 * D * FF_HALF, rows * FF_HALF),
        name="mlp_forward",
    )(info, plan["classes"], tokens, gain, shift, *([up] * splits), *([down] * splits), *([bias] * splits), normed, hidden)


def down_grad_kernel(splits, pieces, info_ref, cls_ref, sub_ref, h_ref, go_ref, c_ref, g_ref, *grads):
    rows = c_ref.shape[0]
    step = pl.program_id(0)

    @pl.when(step == 0)
    def _():
        g_ref[:rows] = go_ref[...]
        g_ref[rows:] = masked_rows(c_ref[...], (1 - info_ref[0]) * rows, info_ref[1]).astype(BF)

    grad_down = dot_tn(h_ref[...], g_ref[...]).astype(BF)
    if not pieces:
        grads[0][...] = grad_down
        return
    down_keep, down_send = grads
    block = FB // splits

    @pl.when(step < 2)
    def _():
        for i in range(splits):
            down_send[sub_ref[i]] = grad_down[i * block : (i + 1) * block]

    @pl.when(step >= 2)
    def _():
        for i in range(splits):
            down_keep[sub_ref[i]] = grad_down[i * block : (i + 1) * block]


def down_grad_call(info, plan, hidden, grads_own, cotangent):
    rows, splits, pieces = cotangent.shape[0], plan["splits"], plan["pieces"]
    fixed = lambda s, *a: (0, 0)
    whole = pl.BlockSpec((rows, D), fixed)
    out_specs = [pl.BlockSpec((2 * rows, D), fixed)]
    out_shape = [in_hbm((2 * rows, D), BF)]
    if pieces:
        half, down_rows = pieces // 2, FF_HALF // pieces
        out_specs += [
            pl.BlockSpec((splits, down_rows, D), lambda s, *a: (jnp.maximum(s - 2, 0), 0, 0)),
            pl.BlockSpec((splits, down_rows, D), lambda s, *a: (jnp.minimum(s, 1), 0, 0)),
        ]
        out_shape += [in_hbm((half, down_rows, D), BF)] * 2
    else:
        out_specs += [pl.BlockSpec((FB, D), lambda s, *a: (s, 0))]
        out_shape += [in_hbm((FF_HALF, D), BF)]
    return pl.pallas_call(
        functools.partial(down_grad_kernel, splits, pieces),
        grid_spec=pltpu.PrefetchScalarGridSpec(
            num_scalar_prefetch=3,
            grid=(FF_HALF // FB,),
            in_specs=[pl.BlockSpec((2 * rows, FB), lambda s, *a: (0, s)), whole, whole],
            out_specs=out_specs,
        ),
        out_shape=out_shape,
        compiler_params=params(),
        cost_estimate=cost(4 * rows * D * FF_HALF, 8 * rows * D + 2 * D * FF_HALF + 4 * rows * FF_HALF),
        name="down_grad",
    )(info, plan["classes"], plan["subs"], hidden, grads_own, cotangent)


def mlp_back_kernel(splits, pieces, info_ref, cls_ref, ord_ref, x_ref, slope_ref, g_ref, gb_ref, *refs):
    ups, downs = refs[:splits], refs[splits : 2 * splits]
    gn_ref, inner_ref, *grads = refs[2 * splits : -2 if pieces else -1]
    gball_ref = refs[-2 if pieces else -1]
    rows = g_ref.shape[0]
    up, down = joined(ups, 1), joined(downs, 0)
    grad_before = (dot_nt(g_ref[...], down) * slope_ref[...].astype(F32)).astype(BF)
    gball_ref[:rows] = gb_ref[...]
    gball_ref[rows:] = grad_before
    accumulate(gn_ref, dot_nt(grad_before, up))
    inner_ref[...] = jnp.sum(gball_ref[...].astype(F32), axis=0, keepdims=True)
    grad_up = dot_tn(x_ref[...], gball_ref[...]).astype(BF)
    if not pieces:
        grads[0][...] = grad_up
        return
    up_keep, up_send = grads
    upall_ref = refs[-1]
    upall_ref[...] = grad_up.reshape(upall_ref.shape)
    for q in range(pieces // 2):
        up_keep[q] = upall_ref[ord_ref[q]]
        up_send[q] = upall_ref[ord_ref[q + pieces // 2]]


def mlp_back_call(info, plan, normed, slope, grads, gb_own):
    rows, splits, pieces = gb_own.shape[0], plan["splits"], plan["pieces"]
    fixed = lambda s, *a: (0, 0)
    up, down, _ = plan["weights"]
    whole = pl.BlockSpec((rows, D), fixed)
    wide = pl.BlockSpec((rows, FB), lambda s, *a: (0, s))
    out_specs = [whole, pl.BlockSpec((1, FB), lambda s, i, cls, *a: (0, cls[s]))]
    out_shape = [in_hbm((rows, D), F32), jax.ShapeDtypeStruct((1, FF_HALF), F32)]
    scratch = [pltpu.VMEM((2 * rows, FB), BF)]
    if pieces:
        shape = (pieces // 2, D // pieces, FB)
        out_specs += [pl.BlockSpec(shape, lambda s, i, cls, *a: (0, 0, cls[s]))] * 2
        out_shape += [in_hbm(shape[:2] + (FF_HALF,), BF)] * 2
        scratch.append(pltpu.VMEM((pieces, D // pieces, FB), BF))
    else:
        out_specs += [pl.BlockSpec((D, FB), lambda s, *a: (0, s))]
        out_shape += [in_hbm((D, FF_HALF), BF)]
    return pl.pallas_call(
        functools.partial(mlp_back_kernel, splits, pieces),
        grid_spec=pltpu.PrefetchScalarGridSpec(
            num_scalar_prefetch=3,
            grid=(FF_HALF // FB,),
            in_specs=[
                pl.BlockSpec((2 * rows, D), fixed),
                wide,
                pl.BlockSpec((rows, D), lambda s, *a: (1, 0)),
                wide,
            ]
            + weight_specs(plan, False),
            out_specs=out_specs,
            scratch_shapes=scratch,
        ),
        out_shape=out_shape,
        compiler_params=params(),
        cost_estimate=cost(8 * rows * D * FF_HALF, 12 * rows * D + 6 * D * FF_HALF + 4 * rows * FF_HALF),
        name="mlp_back",
    )(info, plan["classes"], plan["halved"], normed, slope, grads, gb_own, *([up] * splits), *([down] * splits))


def qkv_half_kernel(place_ref, info_ref, x_ref, w_ref, cos_ref, sin_ref, *refs):
    o_ref = refs[-1]
    t = pl.program_id(0)
    chunk = 2 * LANES

    @pl.when(t == 2)
    def _():
        for c in range(0, HALF, chunk):
            o_ref[0, :, c : c + chunk] = dot_nn(x_ref[...], w_ref[:, c : c + chunk]).astype(BF)

    @pl.when(t < 2)
    def _():
        scale = jnp.where(t == 0, HEAD_DIM**-0.5, 1.0)
        cosine = cos_ref[...] * scale
        sine = sin_ref[...] * scale
        for c in range(0, HALF, chunk):
            mixed = dot_nn(x_ref[...], w_ref[:, c : c + chunk])
            for e in range(0, chunk, LANES):
                o_ref[0, :, c + e : c + e + LANES] = rotate(mixed[:, e : e + LANES], cosine, sine).astype(BF)


def qkv_half_call(place, info, half, normed, w, cosine, sine, qkv=None):
    rows = normed.shape[0] // 2
    table = pl.BlockSpec((rows, LANES), lambda t, p, i: (p[0], 0))
    more = [] if qkv is None else [qkv]
    return pl.pallas_call(
        qkv_half_kernel,
        grid_spec=pltpu.PrefetchScalarGridSpec(
            num_scalar_prefetch=2,
            grid=(3,),
            in_specs=[
                pl.BlockSpec((rows, D), lambda t, p, i: (half, 0)),
                pl.BlockSpec((D, HALF), lambda t, p, i: (0, 2 * t + i[0])),
                table,
                table,
            ]
            + [pl.BlockSpec(memory_space=pl.ANY)] * len(more),
            out_specs=pl.BlockSpec((1, rows, HALF), lambda t, p, i: (t, p[0], 0)),
        ),
        out_shape=in_hbm((3, 2 * rows, HALF), BF),
        input_output_aliases={6: 0} if more else {},
        compiler_params=params(),
        cost_estimate=cost(2 * rows * D * 3 * HALF, 2 * (rows * D + D * 3 * HALF + rows * 3 * HALF)),
        name="qkv",
    )(place, info, normed, w, cosine, sine, *more)


def send_out_kernel(place_ref, info_ref, c_ref, w_ref, e_ref, o_ref):
    o_ref[...] = (dot_nn(c_ref[...], w_ref[...]) + e_ref[...]).astype(BF)


def finish_out_kernel(place_ref, info_ref, c_ref, w_ref, e_ref, t_ref, r_ref, bias_ref, o_ref):
    total = dot_nn(c_ref[...], w_ref[...]) + e_ref[...] + bias_ref[...].astype(F32)
    o_ref[...] = (total + t_ref[...].astype(F32) + r_ref[...].astype(F32)).astype(BF)


def out_call(place, info, context, proj, expanded, rest=()):
    rows, block = expanded.shape[0], 256
    steps = rows // block
    row = pl.BlockSpec((block, D), lambda s, p, i: (s, 0))
    return pl.pallas_call(
        finish_out_kernel if rest else send_out_kernel,
        grid_spec=pltpu.PrefetchScalarGridSpec(
            num_scalar_prefetch=2,
            grid=(steps,),
            in_specs=[
                pl.BlockSpec((block, HALF), lambda s, p, i: (p[0] * steps + s, 0)),
                pl.BlockSpec((HALF, D), lambda s, p, i: (i[0], 0)),
                row,
            ]
            + ([row, row, pl.BlockSpec((1, D), lambda s, p, i: (0, 0))] if rest else []),
            out_specs=row,
        ),
        out_shape=in_hbm((rows, D), BF),
        compiler_params=params(),
        cost_estimate=cost(2 * rows * D * HALF, 8 * rows * D + 2 * HALF * D),
        name="finish_out" if rest else "send_out",
    )(place, info, context, proj, expanded, *rest)


def proj_back_kernel(info_ref, ord_ref, g_ref, c_ref, w_ref, gc_ref, *refs):
    acc_ref = refs[-2] if len(refs) > 2 else refs[-1]
    gc_ref[...] = dot_nt(g_ref[...], w_ref[...]).astype(BF)
    part = dot_tn(c_ref[...], g_ref[...])

    @pl.when(pl.program_id(0) == 0)
    def _():
        acc_ref[...] = part

    @pl.when(pl.program_id(0) == 1)
    def _():
        total = (acc_ref[...] + part).astype(BF)
        if len(refs) == 2:
            refs[0][...] = total
        else:
            keep, send, all_ref = refs[0], refs[1], refs[3]
            all_ref[...] = total.reshape(all_ref.shape)
            half = keep.shape[0]
            for q in range(half):
                keep[q] = all_ref[ord_ref[q]]
                send[q] = all_ref[ord_ref[q + half]]


def proj_back_call(info, plan, order, grads, context, proj):
    rows, pieces = grads.shape[0] // 2, plan["pieces"]
    scratch = [pltpu.VMEM((HALF, D), F32)]
    if pieces:
        shape = (pieces // 2, HALF // pieces, D)
        out_specs = [pl.BlockSpec(shape, lambda h, *a: (0, 0, 0))] * 2
        out_shape = [in_hbm(shape, BF)] * 2
        scratch.append(pltpu.VMEM((pieces, HALF // pieces, D), BF))
    else:
        out_specs = [pl.BlockSpec((HALF, D), lambda h, *a: (0, 0))]
        out_shape = [in_hbm((HALF, D), BF)]
    return pl.pallas_call(
        proj_back_kernel,
        grid_spec=pltpu.PrefetchScalarGridSpec(
            num_scalar_prefetch=2,
            grid=(2,),
            in_specs=[
                pl.BlockSpec((rows, D), lambda h, i, o: (h, 0)),
                pl.BlockSpec((rows, HALF), lambda h, i, o: (jnp.bitwise_xor(h, i[0]), 0)),
                pl.BlockSpec((HALF, D), lambda h, i, o: (i[0], 0)),
            ],
            out_specs=[pl.BlockSpec((rows, HALF), lambda h, i, o: (jnp.bitwise_xor(h, i[0]), 0))] + out_specs,
            scratch_shapes=scratch,
        ),
        out_shape=[in_hbm((2 * rows, HALF), BF)] + out_shape,
        compiler_params=params(),
        cost_estimate=cost(8 * rows * D * HALF, 4 * rows * D + 8 * rows * HALF + 4 * HALF * D),
        name="proj_back",
    )(info, order, grads, context, proj)


def line_of(p, rows, sums, outer, inner_ref):
    low = lax.broadcasted_iota(jnp.int32, (1, LANES), 1) < rows
    at = p // 2 * LANES
    three = [v[:, at : at + LANES] for v in (sums[0:1], sums[1:2], outer)]
    turned = [pltpu.roll(v, rows, 1) for v in three]
    if p % 2:
        three, turned = turned, three
    at = p % 4 * HALF + p // 4 * LANES
    parts = [jnp.where(low, three[0], turned[1]), jnp.where(low, three[2], 0.0), inner_ref[:, at : at + LANES]]
    return jnp.concatenate(parts + [jnp.zeros((1, LANES), F32)], axis=1)


def pair_grad_kernel(info_ref, ord_ref, x_ref, own_ref, their_ref, *refs):
    d = jnp.concatenate([own_ref[0], their_ref[0]], axis=0)
    total = dot_tn(x_ref[...], d).astype(BF)
    if len(refs) == 1:
        refs[0][...] = total
        return
    pk_ref, ps_ref, keep, send, all_ref = refs
    half, rows = keep.shape[0], all_ref.shape[1]
    all_ref[...] = total.reshape(all_ref.shape)
    for q in range(half):
        for out, proj, at in ((keep, pk_ref, q), (send, ps_ref, q + half)):
            out[q, :rows] = all_ref[ord_ref[at]]
            out[q, rows:] = proj[q]


def value_grad_kernel(info_ref, ord_ref, x_ref, own_ref, their_ref, so_ref, st_ref, outer_ref, inner_ref, keep, send,
                      all_ref):
    pieces, rows = all_ref.shape[0], x_ref.shape[1] // all_ref.shape[0]
    half = pieces // 2
    d = jnp.concatenate([own_ref[0], their_ref[0]], axis=0)
    all_ref[:, :rows] = dot_tn(x_ref[...], d).astype(BF).reshape(pieces, rows, HALF)
    sums = so_ref[...] + st_ref[...]
    outer = outer_ref[...]
    for p in range(pieces):
        line = line_of(p, rows, sums, outer, inner_ref)
        all_ref[p, rows:] = jnp.broadcast_to(line, (all_ref.shape[1] - rows, HALF)).astype(BF)
    for q in range(half):
        keep[q] = all_ref[ord_ref[q]]
        send[q] = all_ref[ord_ref[q + half]]


def qkv_grad_call(info, plan, normed, dmix, first, count, extra=()):
    rows, pieces = normed.shape[0] // 2, plan["pieces"]
    in_specs, scratch, kernel = [], [], pair_grad_kernel
    if not pieces:
        extra = ()
        out_specs = [pl.BlockSpec((D, HALF), lambda t, *a: (0, t))]
        out_shape = [in_hbm((D, count * HALF), BF)]
    else:
        height = D // pieces
        if count == 2:
            shape = (pieces // 2, height + HALF // pieces, HALF)
            in_specs = [pl.BlockSpec((pieces // 2, HALF // pieces, HALF), lambda t, *a: (0, 0, t))] * 2
            scratch = [pltpu.VMEM((pieces, height, HALF), BF)]
        else:
            kernel = value_grad_kernel
            shape = (pieces // 2, height + 16, HALF)
            in_specs = [pl.BlockSpec(v.shape, lambda t, *a: (0, 0)) for v in extra]
            scratch = [pltpu.VMEM((pieces, height + 16, HALF), BF)]
        out_specs = [pl.BlockSpec(shape, lambda t, *a: (0, 0, t))] * 2
        out_shape = [in_hbm(shape[:2] + (count * HALF,), BF)] * 2
    return pl.pallas_call(
        kernel,
        grid_spec=pltpu.PrefetchScalarGridSpec(
            num_scalar_prefetch=2,
            grid=(count,),
            in_specs=[
                pl.BlockSpec((2 * rows, D), lambda t, *a: (0, 0)),
                pl.BlockSpec((1, rows, HALF), lambda t, i, *a: (first + t, i[0], 0)),
                pl.BlockSpec((1, rows, HALF), lambda t, i, *a: (first + t, 1 - i[0], 0)),
            ]
            + in_specs,
            out_specs=out_specs,
            scratch_shapes=scratch,
        ),
        out_shape=out_shape,
        compiler_params=params(),
        cost_estimate=cost(4 * rows * D * count * HALF, 4 * rows * D + (4 * rows + 2 * D) * count * HALF),
        name="qkv_grad",
    )(info, plan["order"], normed, dmix, dmix, *extra)


def grad_normed_kernel(place_ref, info_ref, d_ref, wq_ref, wk_ref, wv_ref, base_ref, t_ref, *refs):
    outs, sum_ref = refs[:-1], refs[-1]
    total = base_ref[...]
    for t, w in enumerate((wq_ref, wk_ref, wv_ref)):
        total += dot_nt(d_ref[t], w[...])
    if len(outs) == 1:
        outs[0][...] = total.astype(outs[0].dtype)
    else:
        for r, o_ref in enumerate(outs):

            @pl.when(pl.program_id(0) == r)
            def _(o_ref=o_ref):
                o_ref[...] = total.astype(o_ref.dtype)

    hat, _ = normalize(t_ref[...])
    sums = jnp.concatenate([jnp.sum(total * hat, axis=0, keepdims=True), jnp.sum(total, axis=0, keepdims=True)], axis=0)
    accumulate(sum_ref, sums)


def grad_normed_call(place, info, dmix, w, base, tokens, parts):
    rows, block = base.shape[0], 256
    steps = rows // block
    row = pl.BlockSpec((block, D), lambda r, p, i: (r, 0))
    kind = BF if parts else F32
    count = parts or 1
    return pl.pallas_call(
        grad_normed_kernel,
        grid_spec=pltpu.PrefetchScalarGridSpec(
            num_scalar_prefetch=2,
            grid=(steps,),
            in_specs=[pl.BlockSpec((3, block, HALF), lambda r, p, i: (0, p[0] * steps + r, 0))]
            + [pl.BlockSpec((D, HALF), lambda r, p, i, t=t: (0, 2 * t + i[0])) for t in range(3)]
            + [row, row],
            out_specs=([row] if count == 1 else [pl.BlockSpec((block, D), lambda r, p, i: (0, 0))] * count)
            + [pl.BlockSpec((2, D), lambda r, p, i: (0, 0))],
        ),
        out_shape=[in_hbm((rows // count, D), kind)] * count + [jax.ShapeDtypeStruct((2, D), F32)],
        compiler_params=params(),
        cost_estimate=cost(2 * rows * D * 3 * HALF, 8 * rows * D + 6 * D * HALF + 6 * rows * HALF),
        name="grad_normed",
    )(place, info, dmix, w, w, w, base, tokens)


def assemble_kernel(sources, width, info_ref, mine_ref, their_ref, o_ref):
    first = info_ref[0] == 0
    rows = o_ref.shape[0]
    for k, at in enumerate(sources):
        mine = mine_ref[:, at : at + width]
        theirs = their_ref[:rows, at : at + width].astype(F32)
        o_ref[:, 2 * k * width : (2 * k + 1) * width] = jnp.where(first, mine, theirs)
        o_ref[:, (2 * k + 1) * width : (2 * k + 2) * width] = jnp.where(first, theirs, mine)


def assemble_call(info, mine, theirs, sources, width):
    whole = lambda v: pl.BlockSpec(v.shape, lambda s, i: (0, 0))
    shape = (mine.shape[0], 2 * width * len(sources))
    return pl.pallas_call(
        functools.partial(assemble_kernel, sources, width),
        grid_spec=pltpu.PrefetchScalarGridSpec(
            num_scalar_prefetch=1,
            grid=(1,),
            in_specs=[whole(mine), whole(theirs)],
            out_specs=pl.BlockSpec(shape, lambda s, i: (0, 0)),
        ),
        out_shape=in_hbm(shape, F32),
        compiler_params=params(),
        cost_estimate=cost(1000, 1000),
        name="assemble",
    )(info, mine, theirs)


def finish_grad_kernel(gn_ref, r_ref, t_ref, g_ref, gain_ref, o_ref):
    hat, rstd = normalize(t_ref[...])
    u = (gn_ref[...] + r_ref[...].astype(F32)) * gain_ref[...].astype(F32)
    inner = u - jnp.mean(u, axis=1, keepdims=True) - hat * jnp.mean(u * hat, axis=1, keepdims=True)
    o_ref[...] = g_ref[...].astype(F32) + inner * rstd


def finish_grad_call(grad_normed, received, tokens, grads, gain):
    rows, block = tokens.shape[0], 256
    row = pl.BlockSpec((block, D), lambda r: (r, 0))
    return pl.pallas_call(
        finish_grad_kernel,
        grid=(rows // block,),
        in_specs=[row, row, row, row, pl.BlockSpec((1, D), lambda r: (0, 0))],
        out_specs=row,
        out_shape=in_hbm((rows, D), F32),
        compiler_params=params(),
        cost_estimate=cost(20 * rows * D, 14 * rows * D),
        name="finish_grad",
    )(grad_normed, received, tokens, grads, gain)


class Reduction:
    def __init__(self, keep, send, stages, n_dp):
        self.keep, self.sends, self.stages, self.n_dp = keep, [send], list(stages), n_dp
        self.start()

    def start(self):
        offsets = self.stages.pop(0)
        self.flying = [
            lax.ppermute(part, "dp", [(i, i ^ offset) for i in range(self.n_dp)])
            for part, offset in zip(self.sends, offsets, strict=True)
        ]

    def land(self, *first):
        if first:
            self.keep = after(self.keep, *first)
        kind = self.flying[0].dtype
        pieces = self.keep.shape[0]
        count = pieces // (len(self.stages[0]) + 1) if self.stages else pieces
        parts = []
        for i in range(0, pieces, count):
            total = self.keep[i : i + count].astype(F32)
            for part in self.flying:
                total = total + part[i : i + count].astype(F32)
            parts.append(total)
        if not self.stages:
            self.keep, self.sends = parts[0][0], []
            return (self.keep,)
        parts = [part.astype(kind) for part in parts]
        self.keep, self.sends = parts[0], parts[1:]
        self.start()
        return tuple(parts)

    def finish(self, *first):
        self.land(*first)
        while self.sends:
            self.land()
        return self.keep


def after(x, *done):
    return lax.optimization_barrier((x, *done))[0]


def send_order(stages, me):
    table = [0]
    for offsets in stages:
        table = [r ^ offset for r in table for offset in (0, *offsets)]
    return jnp.bitwise_xor(jnp.array(table, jnp.int32), me)


def pairs_of_bits(bits):
    stages = []
    for i in range(0, len(bits), 2):
        if i + 1 < len(bits):
            stages.append((bits[i], bits[i + 1], bits[i] ^ bits[i + 1]))
        else:
            stages.append((bits[i],))
    return stages


def on_device(n_dp, tokens, lengths, norm_gain, norm_shift, qkv_weight, proj_weight, up_weight, inner_bias,
              down_weight, outer_bias, cotangent):
    j = lax.axis_index("branch").astype(jnp.int32)
    me = lax.axis_index("dp").astype(jnp.int32)
    other = [(0, 1), (1, 0)]
    tokens_their = lax.ppermute(tokens, "branch", other)
    cotangent_their = lax.ppermute(cotangent, "branch", other)
    own, their = j.reshape(1), (1 - j).reshape(1)
    info = jnp.stack([j, lengths[0].astype(jnp.int32)])
    gain, shift = norm_gain.reshape(1, D), norm_shift.reshape(1, D)

    bits = [1 << i for i in range(n_dp.bit_length() - 1)]
    high_stages = pairs_of_bits(bits[2:])
    low_first = [(1,), (2,)] + high_stages
    halvings = [(bit,) for bit in bits]
    order = send_order(low_first, me)
    ffb = FF_HALF // n_dp
    fast = ffb == LANES
    if fast:
        splits = FB // LANES
        plan = {
            "splits": splits,
            "pieces": n_dp,
            "pick": lambda s, a, i: 2 * (4 * i + a[1][s]) + a[0][0],
            "classes": jnp.array([1, 3, 0, 2], jnp.int32) ^ (me & 3),
            "subs": jnp.arange(4, dtype=jnp.int32) ^ (me >> 2),
            "weights": (up_weight, down_weight, inner_bias.reshape(1, FF)),
        }
    else:
        plan = {
            "splits": 1,
            "pieces": 0,
            "pick": lambda s, a, i: s,
            "classes": jnp.arange(FF_HALF // FB, dtype=jnp.int32),
            "subs": jnp.zeros((1,), jnp.int32),
            "weights": (
                lax.dynamic_index_in_dim(up_weight.reshape(D, n_dp, 2, ffb), j, 2, False).reshape(D, FF_HALF),
                lax.dynamic_index_in_dim(down_weight.reshape(n_dp, 2, ffb, D), j, 1, False).reshape(FF_HALF, D),
                lax.dynamic_index_in_dim(inner_bias.reshape(n_dp, 2, ffb), j, 1, False).reshape(1, FF_HALF),
            ),
        }
    plan["order"], plan["halved"] = order, send_order(halvings, me)

    def pieces_of(grads, table):
        if len(grads) == 2:
            return grads
        whole = grads[0]
        ordered = jnp.take(whole.reshape(n_dp, whole.shape[0] // n_dp, whole.shape[1]), table, axis=0)
        return ordered[: n_dp // 2], ordered[n_dp // 2 :]

    plan["weights"] = tuple(pltpu.with_memory_space_constraint(w, pltpu.HBM) for w in plan["weights"][:2]) + plan["weights"][2:]
    qkv_weight = pltpu.with_memory_space_constraint(qkv_weight, pltpu.HBM)
    proj_weight = pltpu.with_memory_space_constraint(proj_weight, pltpu.HBM)

    cosine, sine = rotary_tables()
    normed, hidden, grads_own, gb_own, expanded_own, gn_own, outer = mlp_own_call(
        info, plan, tokens, cotangent, gain, shift
    )
    qkv = qkv_half_call(own, info, 0, normed, qkv_weight, cosine, sine)
    info = after(info, qkv)
    normed, hidden, slope, expanded_their = mlp_forward_call(info, plan, tokens_their, gain, shift, normed, hidden)
    info = after(info, slope)
    grads, *down = down_grad_call(info, plan, stay(hidden), grads_own, cotangent_their)
    down = Reduction(*pieces_of(down, order), low_first, n_dp)
    info = after(info, grads)
    gn_their, inner, *up = mlp_back_call(info, plan, normed, stay(slope), grads, stay(gb_own))

    up = Reduction(*pieces_of(up, plan["halved"]), halvings, n_dp)
    info = after(info, *down.land(gn_their), *up.land(gn_their))
    qkv = qkv_half_call(their, info, 1, normed, qkv_weight, cosine, sine, qkv)
    context, qe = attend_call(info, stay(qkv))
    out_their = out_call(their, info, context, proj_weight, expanded_their)

    info = after(info, *down.land(out_their))
    out_received = lax.ppermute(out_their, "branch", other)
    grad_context, *proj = proj_back_call(info, plan, order, grads, context, proj_weight)
    info = after(info, *up.land(grad_context))
    dmix = attend_back_call(info, qe, qkv, context, grad_context, cosine, sine)

    down_grad = down.finish(dmix)
    info = after(info, out_received, down_grad, *up.land(dmix))
    small = D // n_dp
    shard = small // 2
    first = qkv_grad_call(info, plan, normed, dmix, 0, 2, proj)
    if not fast:
        first = jnp.concatenate([first[0].reshape(n_dp, small, D), proj[0].reshape(n_dp, shard, D)], axis=1)
        first = jnp.take(first, order, axis=0)
        first = first[: n_dp // 2], first[n_dp // 2 :]
    info = after(info, *first)
    first = Reduction(*first, low_first, n_dp)
    *gn_send, sums_their = grad_normed_call(their, info, dmix, qkv_weight, gn_their, tokens_their, 1)

    info = after(info, *first.land(*gn_send))
    gn_first = lax.ppermute(gn_send[0], "branch", other)
    gn_own, sums_own = grad_normed_call(own, info, dmix, qkv_weight, gn_own, tokens, 0)
    info = after(info, gn_own)
    layer_out = out_call(
        own, info, context, proj_weight, expanded_own, (tokens, out_received, outer_bias.reshape(1, D))
    )
    info = after(info, layer_out)
    if fast:
        value = qkv_grad_call(info, plan, normed, dmix, 2, 1, (sums_own, sums_their, outer, inner))
    else:
        sums = sums_own + sums_their
        lines = jnp.concatenate([v.reshape(n_dp, small) for v in (sums[0], sums[1], outer)], axis=1)
        lines = jnp.concatenate(
            [jnp.pad(lines, ((0, 0), (0, 2 * LANES - 3 * small))), inner.reshape(n_dp, ffb)], axis=1
        )
        lines = jnp.pad(lines, ((0, 0), (0, HALF - lines.shape[1]))).astype(BF)
        lines = jnp.broadcast_to(lines[:, None], (n_dp, 16, HALF))
        value = qkv_grad_call(info, plan, normed, dmix, 2, 1)[0].reshape(n_dp, small, HALF)
        value = jnp.take(jnp.concatenate([value, lines], axis=1), order, axis=0)
        value = value[: n_dp // 2], value[n_dp // 2 :]
    up.finish(*value)
    landed = first.land(*value)
    value, up.keep, _ = lax.optimization_barrier((tuple(value), up.keep, landed))
    value = Reduction(*value, low_first, n_dp)
    up_mine = lax.dynamic_slice_in_dim(up.keep, j * shard, shard, 0)
    up_their = lax.dynamic_slice_in_dim(up.keep, (1 - j) * shard, shard, 0).astype(BF)
    up_their = lax.ppermute(up_their, "branch", other)
    value.keep, gn_first = lax.optimization_barrier((value.keep, gn_first))
    landed = value.land()
    tokens_grad = finish_grad_call(gn_own, after(gn_first, *landed), tokens, grads_own, gain)
    up_mine, up_their, tokens_grad = lax.optimization_barrier((up_mine, up_their, tokens_grad))
    if fast:
        sources = tuple(p % 4 * HALF + p // 4 * LANES for p in range(n_dp))
        up_grad = assemble_call(info, up_mine, up_their, sources, LANES)
    else:
        up_their = up_their.astype(F32)
        low, high = jnp.where(j == 0, up_mine, up_their), jnp.where(j == 0, up_their, up_mine)
        up_grad = jnp.stack([low.reshape(shard, n_dp, ffb), high.reshape(shard, n_dp, ffb)], axis=2).reshape(shard, FF)
    first = first.finish(up_grad)
    value.land(first)
    value = value.finish()
    query_key, proj_piece = first[:small], first[small:]
    piece = jnp.concatenate([query_key, value[:small]], axis=1)
    line = value[small:]
    theirs = lax.dynamic_slice_in_dim(piece, (1 - j) * shard, shard, 0)
    theirs = jnp.concatenate([theirs, jnp.concatenate([line, line, line], axis=1)], axis=0).astype(BF)
    route = [(2 * p + h, n_dp * h + p) for h in range(2) for p in range(n_dp)]
    proj_grad = lax.ppermute(after(proj_piece.astype(BF), theirs), ("dp", "branch"), route).astype(F32)
    theirs = lax.ppermute(theirs, "branch", other)
    mine = lax.dynamic_slice_in_dim(piece, j * shard, shard, 0)
    qkv_grad = assemble_call(info, mine, theirs, (0, HALF, 2 * HALF), HALF) if fast else None
    triple = (line[0] + theirs[shard, :HALF].astype(F32))[: 3 * small].reshape(3, 2, shard)
    triple = lax.dynamic_index_in_dim(triple, j, 1, False)
    if not fast:
        mine = mine.reshape(shard, 3, HALF)
        theirs = theirs[:shard].astype(F32).reshape(shard, 3, HALF)
        qkv_grad = jnp.stack([jnp.where(j == 0, mine, theirs), jnp.where(j == 0, theirs, mine)], axis=2)
        qkv_grad = qkv_grad.reshape(shard, 3 * D)
    return (
        layer_out,
        tokens_grad,
        triple[0],
        triple[1],
        qkv_grad,
        proj_grad,
        up_grad,
        line[0, 2 * LANES : 2 * LANES + ffb],
        down_grad,
        triple[2],
    )


def solution(mesh):
    rows = P(("dp", "branch"), None)
    flat = P(("dp", "branch"))
    return jax.shard_map(
        functools.partial(on_device, mesh.shape["dp"]),
        mesh=mesh,
        in_specs=(rows, P("dp"), P(), P(), P(), P(), P(), P(), P(), P(), rows),
        out_specs=(rows, rows, flat, flat, rows, rows, rows, flat, rows, flat),
        check_vma=False,
    )
```

```python
import functools
import math

import jax
import jax.numpy as jnp
from jax import lax
from jax.experimental import pallas as pl
from jax.experimental.pallas import tpu as pltpu
from jax.sharding import PartitionSpec as P

D = 1024
HEADS = 16
HEAD_DIM = 64
ROT_DIM = 32
FF = 4096
SEQ_LEN = 1024
HALF = HEADS // 2 * HEAD_DIM
FF_HALF = FF // 2
LANES = 128
QB = 256
ROWS = 128
FB = 512
EPS = 1e-05
BF = jnp.bfloat16
F32 = jnp.float32


def params(mb=24):
    return pltpu.CompilerParams(vmem_limit_bytes=mb << 20)


def cost(flops, nbytes, trans=0):
    return pl.CostEstimate(flops=int(flops) // 1000, bytes_accessed=int(nbytes) // 1000, transcendentals=0)


def in_hbm(shape, dtype):
    return pltpu.HBM(tuple(shape), dtype)


def stay(x):
    return pltpu.with_memory_space_constraint(x, pltpu.HBM)


def dot_nn(a, b):
    return jnp.dot(a, b, preferred_element_type=F32)


def dot_nt(a, b):
    return lax.dot_general(a, b, (((1,), (1,)), ((), ())), preferred_element_type=F32)


def dot_tn(a, b):
    return lax.dot_general(a, b, (((0,), (0,)), ((), ())), preferred_element_type=F32)


def rotary_tables():
    lane = jnp.arange(LANES, dtype=jnp.int32)
    channel = lane % HEAD_DIM
    frequency = jnp.power(10000.0, -(2.0 * (channel // 2).astype(F32)) / ROT_DIM)
    frequency = jnp.where(channel < ROT_DIM, frequency, 0.0)
    step = 32
    index = jnp.arange(2 * step, dtype=jnp.int32)
    position = jnp.where(index < step, index * (SEQ_LEN // step), index - step).astype(F32)
    angles = position[:, None] * frequency[None, :]
    cosine, sine = lax.optimization_barrier((jnp.cos(angles), jnp.sin(angles)))
    high_cosine, high_sine = cosine[:step, None], sine[:step, None]
    low_cosine, low_sine = cosine[None, step:], sine[None, step:]
    even = (lane % 2 == 0)[None, None, :]
    sine = high_sine * low_cosine + high_cosine * low_sine
    cosine = high_cosine * low_cosine - high_sine * low_sine
    return cosine.reshape(SEQ_LEN, LANES), jnp.where(even, -sine, sine).reshape(SEQ_LEN, LANES)


def rotate(x, cosine, sine):
    even = lax.broadcasted_iota(jnp.int32, x.shape, 1) % 2 == 0
    swapped = jnp.where(even, pltpu.roll(x, LANES - 1, 1), pltpu.roll(x, 1, 1))
    return x * cosine + swapped * sine


def unrotate(y, cosine, sine):
    even = lax.broadcasted_iota(jnp.int32, y.shape, 1) % 2 == 0
    swapped = jnp.where(even, pltpu.roll(y, LANES - 1, 1), pltpu.roll(y, 1, 1))
    return y * cosine - swapped * sine


def head_lanes(shape, head):
    lane = lax.broadcasted_iota(jnp.int32, shape, 1)
    own = (lane >= HEAD_DIM) if head else (lane < HEAD_DIM)
    spare = lane - (0 if head else HEAD_DIM)
    return own, spare


def keys_with_bias(k, head, length):
    own, spare = head_lanes(k.shape, head)
    row = lax.broadcasted_iota(jnp.int32, k.shape, 0)
    bias = jnp.where(row < length, 0.0, -1e30)
    extra = jnp.where(spare < 3, 1.0, jnp.where(spare == 3, bias, 0.0))
    return jnp.where(own, k.astype(F32), extra).astype(BF)


def attend_kernel(info_ref, q_ref, k_ref, v_ref, o_ref, qe_ref):
    length = info_ref[1]
    q = q_ref[0].astype(F32)
    k = k_ref[0]
    v = v_ref[0]
    tri = lax.broadcasted_iota(jnp.int32, (QB, QB), 0) >= lax.broadcasted_iota(jnp.int32, (QB, QB), 1)
    outs = []
    for head in range(2):
        own, spare = head_lanes((SEQ_LEN, LANES), head)
        ke = keys_with_bias(k, head, length)
        qe = jnp.where(own, q, jnp.where(spare == 3, 1.0, 0.0)).astype(BF)
        parts = []
        for b in range(SEQ_LEN // QB):
            lo, hi = b * QB, (b + 1) * QB
            s = dot_nt(qe[lo:hi], ke[:hi])
            diag = jnp.where(tri, s[:, lo:hi], -1e30)
            s = diag if b == 0 else jnp.concatenate([s[:, :lo], diag], axis=1)
            top = jnp.max(s, axis=1, keepdims=True)
            p = jnp.exp(s - top)
            total = jnp.sum(p, axis=1, keepdims=True)
            parts.append(dot_nn(p.astype(BF), v[:hi]) * (1.0 / total))
            lse = jnp.broadcast_to(top + jnp.log(total), (QB, LANES))
            first = lse.astype(BF).astype(F32)
            second = (lse - first).astype(BF).astype(F32)
            third = lse - first - second
            own_b, spare_b = head_lanes((QB, LANES), head)
            extra = jnp.where(
                spare_b == 0,
                -first,
                jnp.where(
                    spare_b == 1,
                    -second,
                    jnp.where(spare_b == 2, -third, jnp.where(spare_b == 3, 1.0, 0.0)),
                ),
            )
            qe_ref[head, lo:hi, :] = jnp.where(own_b, q[lo:hi], extra).astype(BF)
        outs.append(jnp.concatenate(parts, axis=0))
    own, _ = head_lanes((SEQ_LEN, LANES), 0)
    o_ref[...] = jnp.where(own, outs[0], outs[1]).astype(BF)


def attend_call(info, qkv):
    pairs = HALF // LANES
    spec = [pl.BlockSpec((1, SEQ_LEN, LANES), lambda p, n, t=t: (t, 0, p)) for t in range(3)]
    return pl.pallas_call(
        attend_kernel,
        grid_spec=pltpu.PrefetchScalarGridSpec(
            num_scalar_prefetch=1,
            grid=(pairs,),
            in_specs=spec,
            out_specs=[
                pl.BlockSpec((SEQ_LEN, LANES), lambda p, n: (0, p)),
                pl.BlockSpec((2, SEQ_LEN, LANES), lambda p, n: (p, 0, 0)),
            ],
        ),
        out_shape=[
            in_hbm((SEQ_LEN, HALF), BF),
            in_hbm((HEADS // 2, SEQ_LEN, LANES), BF),
        ],
        compiler_params=params(),
        cost_estimate=cost(
            2 * pairs * 10 * SEQ_LEN * SEQ_LEN * LANES, 2 * SEQ_LEN * HALF * 3, 4 * SEQ_LEN * SEQ_LEN
        ),
        name="attend",
    )(info, qkv, qkv, qkv)


def attend_back_kernel(info_ref, qe_ref, k_ref, v_ref, o_ref, g_ref, cos_ref, sin_ref, d_ref, dk_ref, dv_ref):
    length = info_ref[1]
    k = k_ref[0]
    v = v_ref[0]
    g = g_ref[...].astype(F32)
    o = o_ref[...].astype(F32)
    tri = lax.broadcasted_iota(jnp.int32, (QB, QB), 0) >= lax.broadcasted_iota(jnp.int32, (QB, QB), 1)
    queries = []
    for head in range(2):
        own, spare = head_lanes((SEQ_LEN, LANES), head)
        ke = keys_with_bias(k, head, length)
        ve = jnp.where(own, v.astype(F32), jnp.where(spare < 3, 1.0, 0.0)).astype(BF)
        inner = jnp.sum(jnp.where(own, g * o, 0.0), axis=1, keepdims=True)
        inner = jnp.broadcast_to(inner, (SEQ_LEN, LANES))
        first = inner.astype(BF).astype(F32)
        second = (inner - first).astype(BF).astype(F32)
        third = inner - first - second
        extra = jnp.where(
            spare == 0,
            -first,
            jnp.where(spare == 1, -second, jnp.where(spare == 2, -third, 0.0)),
        )
        ge = jnp.where(own, g, extra).astype(BF)
        parts = []
        for b in range(SEQ_LEN // QB):
            lo, hi = b * QB, (b + 1) * QB
            qb = qe_ref[head, lo:hi, :]
            gb = ge[lo:hi]
            s = dot_nt(qb, ke[:hi])
            diag = jnp.where(tri, s[:, lo:hi], -1e30)
            s = diag if b == 0 else jnp.concatenate([s[:, :lo], diag], axis=1)
            p = jnp.exp(s)
            ds = (p * dot_nt(gb, ve[:hi])).astype(BF)
            parts.append(dot_nn(ds, k[:hi]))
            dk = dot_tn(ds, qb)
            dv = dot_tn(p.astype(BF), gb)
            if b > 0:
                dk_ref[head, :lo] += dk[:lo]
                dv_ref[head, :lo] += dv[:lo]
            dk_ref[head, lo:hi] = dk[lo:hi]
            dv_ref[head, lo:hi] = dv[lo:hi]
        queries.append(jnp.concatenate(parts, axis=0))
    own, _ = head_lanes((SEQ_LEN, LANES), 0)
    cosine, sine = cos_ref[...], sin_ref[...]
    dq = jnp.where(own, queries[0], queries[1]) * HEAD_DIM**-0.5
    d_ref[0] = unrotate(dq, cosine, sine).astype(BF)
    d_ref[1] = unrotate(jnp.where(own, dk_ref[0], dk_ref[1]), cosine, sine).astype(BF)
    d_ref[2] = jnp.where(own, dv_ref[0], dv_ref[1]).astype(BF)


def attend_back_call(info, qe, qkv, context, grad_context, cosine, sine):
    pairs = HALF // LANES
    table = pl.BlockSpec((SEQ_LEN, LANES), lambda p, n: (0, 0))
    return pl.pallas_call(
        attend_back_kernel,
        grid_spec=pltpu.PrefetchScalarGridSpec(
            num_scalar_prefetch=1,
            grid=(pairs,),
            in_specs=[
                pl.BlockSpec((2, SEQ_LEN, LANES), lambda p, n: (p, 0, 0)),
                pl.BlockSpec((1, SEQ_LEN, LANES), lambda p, n: (1, 0, p)),
                pl.BlockSpec((1, SEQ_LEN, LANES), lambda p, n: (2, 0, p)),
                pl.BlockSpec((SEQ_LEN, LANES), lambda p, n: (0, p)),
                pl.BlockSpec((SEQ_LEN, LANES), lambda p, n: (0, p)),
                table,
                table,
            ],
            out_specs=pl.BlockSpec((3, SEQ_LEN, LANES), lambda p, n: (0, 0, p)),
            scratch_shapes=[
                pltpu.VMEM((2, SEQ_LEN, LANES), F32),
                pltpu.VMEM((2, SEQ_LEN, LANES), F32),
            ],
        ),
        out_shape=jax.ShapeDtypeStruct((3, SEQ_LEN, HALF), BF),
        compiler_params=params(),
        cost_estimate=cost(
            2 * pairs * 12 * SEQ_LEN * SEQ_LEN * LANES, 2 * SEQ_LEN * HALF * 4, 4 * SEQ_LEN * SEQ_LEN
        ),
        name="attend_back",
    )(info, qe, qkv, qkv, context, grad_context, cosine, sine)


def gelu_parts(v):
    c = math.sqrt(2.0 / math.pi)
    square = v * v
    half = 0.5 + 0.5 * jnp.tanh(v * (c + (c * 0.044715) * square))
    hidden = v * half
    slope = half * (1.0 + (v - hidden) * (2.0 * c + (6.0 * c * 0.044715) * square))
    return hidden, slope


def normalize(x):
    x = x.astype(F32)
    centred = x - jnp.mean(x, axis=1, keepdims=True)
    rstd = lax.rsqrt(jnp.mean(centred * centred, axis=1, keepdims=True) + EPS)
    return centred * rstd, rstd


def masked_rows(g, start, length):
    row = start + lax.broadcasted_iota(jnp.int32, g.shape, 0)
    return jnp.where(row < length, g.astype(F32), 0.0)


def joined(refs, axis):
    return refs[0][...] if len(refs) == 1 else jnp.concatenate([r[...] for r in refs], axis=axis)


def weight_specs(plan, rows_too=True):
    splits, wide, pick = plan["splits"], FB // plan["splits"], plan["pick"]
    specs = [pl.BlockSpec((D, wide), lambda s, *a, i=i: (0, pick(s, a, i))) for i in range(splits)]
    specs += [pl.BlockSpec((wide, D), lambda s, *a, i=i: (pick(s, a, i), 0)) for i in range(splits)]
    if rows_too:
        specs += [pl.BlockSpec((1, wide), lambda s, *a, i=i: (0, pick(s, a, i))) for i in range(splits)]
    return specs


def accumulate(ref, value):
    @pl.when(pl.program_id(0) == 0)
    def _():
        ref[...] = value

    @pl.when(pl.program_id(0) > 0)
    def _():
        ref[...] += value


def mlp_own_kernel(splits, info_ref, cls_ref, t_ref, c_ref, gain_ref, shift_ref, *refs):
    ups, downs, biases = refs[:splits], refs[splits : 2 * splits], refs[2 * splits : 3 * splits]
    x_ref, h_ref, g_ref, gb_ref, e_ref, gn_ref, outer_ref = refs[3 * splits :]

    @pl.when(pl.program_id(0) == 0)
    def _():
        outer_ref[...] = jnp.zeros_like(outer_ref)

        @pl.loop(0, t_ref.shape[0] // ROWS)
        def _(r):
            at = pl.ds(pl.multiple_of(r * ROWS, ROWS), ROWS)
            hat, _ = normalize(t_ref[at, :])
            x_ref[at, :] = (hat * gain_ref[...].astype(F32) + shift_ref[...].astype(F32)).astype(BF)
            g = masked_rows(c_ref[at, :], info_ref[0] * c_ref.shape[0] + r * ROWS, info_ref[1])
            g_ref[at, :] = g.astype(BF)
            outer_ref[...] += jnp.sum(g, axis=0, keepdims=True)

    up, down, bias = joined(ups, 1), joined(downs, 0), joined(biases, 1)
    before = dot_nn(x_ref[...], up) + bias.astype(F32)
    hidden, slope = gelu_parts(before)
    hidden = hidden.astype(BF)
    grad_before = (dot_nt(g_ref[...], down) * slope).astype(BF)
    h_ref[...] = hidden
    gb_ref[...] = grad_before
    accumulate(e_ref, dot_nn(hidden, down))
    accumulate(gn_ref, dot_nt(grad_before, up))


def mlp_own_call(info, plan, tokens, cotangent, gain, shift):
    rows, splits = tokens.shape[0], plan["splits"]
    fixed = lambda s, *a: (0, 0)
    up, down, bias = plan["weights"]
    whole = pl.BlockSpec((rows, D), fixed)
    wide = pl.BlockSpec((rows, FB), lambda s, *a: (0, s))
    return pl.pallas_call(
        functools.partial(mlp_own_kernel, splits),
        grid_spec=pltpu.PrefetchScalarGridSpec(
            num_scalar_prefetch=2,
            grid=(FF_HALF // FB,),
            in_specs=[whole, whole, pl.BlockSpec((1, D), fixed), pl.BlockSpec((1, D), fixed)] + weight_specs(plan),
            out_specs=[whole, wide, whole, wide, whole, whole, pl.BlockSpec((1, D), fixed)],
        ),
        out_shape=[
            jax.ShapeDtypeStruct((2 * rows, D), BF),
            in_hbm((2 * rows, FF_HALF), BF),
            in_hbm((rows, D), BF),
            in_hbm((rows, FF_HALF), BF),
            in_hbm((rows, D), F32),
            in_hbm((rows, D), F32),
            jax.ShapeDtypeStruct((1, D), F32),
        ],
        compiler_params=params(),
        cost_estimate=cost(8 * rows * D * FF_HALF, 12 * rows * D + 4 * D * FF_HALF, rows * FF_HALF),
        name="mlp_own",
    )(info, plan["classes"], tokens, cotangent, gain, shift, *([up] * splits), *([down] * splits), *([bias] * splits))


def mlp_forward_kernel(splits, info_ref, cls_ref, t_ref, gain_ref, shift_ref, *refs):
    ups, downs, biases = refs[:splits], refs[splits : 2 * splits], refs[2 * splits : 3 * splits]
    x_ref, h_ref, slope_ref, e_ref = refs[3 * splits + 2 :]

    @pl.when(pl.program_id(0) == 0)
    def _():
        @pl.loop(0, t_ref.shape[0] // ROWS)
        def _(r):
            at = pl.ds(pl.multiple_of(r * ROWS, ROWS), ROWS)
            hat, _ = normalize(t_ref[at, :])
            x_ref[at, :] = (hat * gain_ref[...].astype(F32) + shift_ref[...].astype(F32)).astype(BF)

    up, down, bias = joined(ups, 1), joined(downs, 0), joined(biases, 1)
    before = dot_nn(x_ref[...], up) + bias.astype(F32)
    hidden, slope = gelu_parts(before)
    hidden = hidden.astype(BF)
    h_ref[...] = hidden
    slope_ref[...] = slope.astype(BF)
    accumulate(e_ref, dot_nn(hidden, down))


def mlp_forward_call(info, plan, tokens, gain, shift, normed, hidden):
    rows, splits = tokens.shape[0], plan["splits"]
    fixed = lambda s, *a: (0, 0)
    up, down, bias = plan["weights"]
    whole = pl.BlockSpec((rows, D), fixed)
    anywhere = pl.BlockSpec(memory_space=pl.ANY)
    first = 5 + 3 * splits
    return pl.pallas_call(
        functools.partial(mlp_forward_kernel, splits),
        grid_spec=pltpu.PrefetchScalarGridSpec(
            num_scalar_prefetch=2,
            grid=(FF_HALF // FB,),
            in_specs=[whole, pl.BlockSpec((1, D), fixed), pl.BlockSpec((1, D), fixed)]
            + weight_specs(plan)
            + [anywhere, anywhere],
            out_specs=[
                pl.BlockSpec((rows, D), lambda s, *a: (1, 0)),
                pl.BlockSpec((rows, FB), lambda s, *a: (1, s)),
                pl.BlockSpec((rows, FB), lambda s, *a: (0, s)),
                whole,
            ],
        ),
        out_shape=[
            jax.ShapeDtypeStruct((2 * rows, D), BF),
            in_hbm((2 * rows, FF_HALF), BF),
            in_hbm((rows, FF_HALF), BF),
            in_hbm((rows, D), F32),
        ],
        input_output_aliases={first: 0, first + 1: 1},
        compiler_params=params(),
        cost_estimate=cost(4 * rows * D * FF_HALF, 12 * rows * D + 4 * D * FF_HALF, rows * FF_HALF),
        name="mlp_forward",
    )(info, plan["classes"], tokens, gain, shift, *([up] * splits), *([down] * splits), *([bias] * splits), normed, hidden)


def down_grad_kernel(splits, pieces, info_ref, cls_ref, sub_ref, h_ref, go_ref, c_ref, g_ref, *grads):
    rows = c_ref.shape[0]
    step = pl.program_id(0)

    @pl.when(step == 0)
    def _():
        g_ref[:rows] = go_ref[...]
        g_ref[rows:] = masked_rows(c_ref[...], (1 - info_ref[0]) * rows, info_ref[1]).astype(BF)

    grad_down = dot_tn(h_ref[...], g_ref[...]).astype(BF)
    if not pieces:
        grads[0][...] = grad_down
        return
    down_keep, down_send = grads
    block = FB // splits

    @pl.when(step < 2)
    def _():
        for i in range(splits):
            down_send[sub_ref[i]] = grad_down[i * block : (i + 1) * block]

    @pl.when(step >= 2)
    def _():
        for i in range(splits):
            down_keep[sub_ref[i]] = grad_down[i * block : (i + 1) * block]


def down_grad_call(info, plan, hidden, grads_own, cotangent):
    rows, splits, pieces = cotangent.shape[0], plan["splits"], plan["pieces"]
    fixed = lambda s, *a: (0, 0)
    whole = pl.BlockSpec((rows, D), fixed)
    out_specs = [pl.BlockSpec((2 * rows, D), fixed)]
    out_shape = [in_hbm((2 * rows, D), BF)]
    if pieces:
        half, down_rows = pieces // 2, FF_HALF // pieces
        out_specs += [
            pl.BlockSpec((splits, down_rows, D), lambda s, *a: (jnp.maximum(s - 2, 0), 0, 0)),
            pl.BlockSpec((splits, down_rows, D), lambda s, *a: (jnp.minimum(s, 1), 0, 0)),
        ]
        out_shape += [in_hbm((half, down_rows, D), BF)] * 2
    else:
        out_specs += [pl.BlockSpec((FB, D), lambda s, *a: (s, 0))]
        out_shape += [in_hbm((FF_HALF, D), BF)]
    return pl.pallas_call(
        functools.partial(down_grad_kernel, splits, pieces),
        grid_spec=pltpu.PrefetchScalarGridSpec(
            num_scalar_prefetch=3,
            grid=(FF_HALF // FB,),
            in_specs=[pl.BlockSpec((2 * rows, FB), lambda s, *a: (0, s)), whole, whole],
            out_specs=out_specs,
        ),
        out_shape=out_shape,
        compiler_params=params(),
        cost_estimate=cost(4 * rows * D * FF_HALF, 8 * rows * D + 2 * D * FF_HALF + 4 * rows * FF_HALF),
        name="down_grad",
    )(info, plan["classes"], plan["subs"], hidden, grads_own, cotangent)


def mlp_back_kernel(splits, pieces, info_ref, cls_ref, ord_ref, x_ref, slope_ref, g_ref, gb_ref, *refs):
    ups, downs = refs[:splits], refs[splits : 2 * splits]
    gn_ref, inner_ref, *grads = refs[2 * splits : -2 if pieces else -1]
    gball_ref = refs[-2 if pieces else -1]
    rows = g_ref.shape[0]
    up, down = joined(ups, 1), joined(downs, 0)
    grad_before = (dot_nt(g_ref[...], down) * slope_ref[...].astype(F32)).astype(BF)
    gball_ref[:rows] = gb_ref[...]
    gball_ref[rows:] = grad_before
    accumulate(gn_ref, dot_nt(grad_before, up))
    inner_ref[...] = jnp.sum(gball_ref[...].astype(F32), axis=0, keepdims=True)
    grad_up = dot_tn(x_ref[...], gball_ref[...]).astype(BF)
    if not pieces:
        grads[0][...] = grad_up
        return
    up_keep, up_send = grads
    upall_ref = refs[-1]
    upall_ref[...] = grad_up.reshape(upall_ref.shape)
    for q in range(pieces // 2):
        up_keep[q] = upall_ref[ord_ref[q]]
        up_send[q] = upall_ref[ord_ref[q + pieces // 2]]


def mlp_back_call(info, plan, normed, slope, grads, gb_own):
    rows, splits, pieces = gb_own.shape[0], plan["splits"], plan["pieces"]
    fixed = lambda s, *a: (0, 0)
    up, down, _ = plan["weights"]
    whole = pl.BlockSpec((rows, D), fixed)
    wide = pl.BlockSpec((rows, FB), lambda s, *a: (0, s))
    out_specs = [whole, pl.BlockSpec((1, FB), lambda s, i, cls, *a: (0, cls[s]))]
    out_shape = [in_hbm((rows, D), F32), jax.ShapeDtypeStruct((1, FF_HALF), F32)]
    scratch = [pltpu.VMEM((2 * rows, FB), BF)]
    if pieces:
        shape = (pieces // 2, D // pieces, FB)
        out_specs += [pl.BlockSpec(shape, lambda s, i, cls, *a: (0, 0, cls[s]))] * 2
        out_shape += [in_hbm(shape[:2] + (FF_HALF,), BF)] * 2
        scratch.append(pltpu.VMEM((pieces, D // pieces, FB), BF))
    else:
        out_specs += [pl.BlockSpec((D, FB), lambda s, *a: (0, s))]
        out_shape += [in_hbm((D, FF_HALF), BF)]
    return pl.pallas_call(
        functools.partial(mlp_back_kernel, splits, pieces),
        grid_spec=pltpu.PrefetchScalarGridSpec(
            num_scalar_prefetch=3,
            grid=(FF_HALF // FB,),
            in_specs=[
                pl.BlockSpec((2 * rows, D), fixed),
                wide,
                pl.BlockSpec((rows, D), lambda s, *a: (1, 0)),
                wide,
            ]
            + weight_specs(plan, False),
            out_specs=out_specs,
            scratch_shapes=scratch,
        ),
        out_shape=out_shape,
        compiler_params=params(),
        cost_estimate=cost(8 * rows * D * FF_HALF, 12 * rows * D + 6 * D * FF_HALF + 4 * rows * FF_HALF),
        name="mlp_back",
    )(info, plan["classes"], plan["halved"], normed, slope, grads, gb_own, *([up] * splits), *([down] * splits))


def qkv_half_kernel(place_ref, info_ref, x_ref, w_ref, cos_ref, sin_ref, *refs):
    o_ref = refs[-1]
    t = pl.program_id(0)
    chunk = 2 * LANES

    @pl.when(t == 2)
    def _():
        for c in range(0, HALF, chunk):
            o_ref[0, :, c : c + chunk] = dot_nn(x_ref[...], w_ref[:, c : c + chunk]).astype(BF)

    @pl.when(t < 2)
    def _():
        scale = jnp.where(t == 0, HEAD_DIM**-0.5, 1.0)
        cosine = cos_ref[...] * scale
        sine = sin_ref[...] * scale
        for c in range(0, HALF, chunk):
            mixed = dot_nn(x_ref[...], w_ref[:, c : c + chunk])
            for e in range(0, chunk, LANES):
                o_ref[0, :, c + e : c + e + LANES] = rotate(mixed[:, e : e + LANES], cosine, sine).astype(BF)


def qkv_half_call(place, info, half, normed, w, cosine, sine, qkv=None):
    rows = normed.shape[0] // 2
    table = pl.BlockSpec((rows, LANES), lambda t, p, i: (p[0], 0))
    more = [] if qkv is None else [qkv]
    return pl.pallas_call(
        qkv_half_kernel,
        grid_spec=pltpu.PrefetchScalarGridSpec(
            num_scalar_prefetch=2,
            grid=(3,),
            in_specs=[
                pl.BlockSpec((rows, D), lambda t, p, i: (half, 0)),
                pl.BlockSpec((D, HALF), lambda t, p, i: (0, 2 * t + i[0])),
                table,
                table,
            ]
            + [pl.BlockSpec(memory_space=pl.ANY)] * len(more),
            out_specs=pl.BlockSpec((1, rows, HALF), lambda t, p, i: (t, p[0], 0)),
        ),
        out_shape=in_hbm((3, 2 * rows, HALF), BF),
        input_output_aliases={6: 0} if more else {},
        compiler_params=params(),
        cost_estimate=cost(2 * rows * D * 3 * HALF, 2 * (rows * D + D * 3 * HALF + rows * 3 * HALF)),
        name="qkv",
    )(place, info, normed, w, cosine, sine, *more)


def send_out_kernel(place_ref, info_ref, c_ref, w_ref, e_ref, o_ref):
    o_ref[...] = (dot_nn(c_ref[...], w_ref[...]) + e_ref[...]).astype(BF)


def finish_out_kernel(place_ref, info_ref, c_ref, w_ref, e_ref, t_ref, r_ref, bias_ref, o_ref):
    total = dot_nn(c_ref[...], w_ref[...]) + e_ref[...] + bias_ref[...].astype(F32)
    o_ref[...] = (total + t_ref[...].astype(F32) + r_ref[...].astype(F32)).astype(BF)


def out_call(place, info, context, proj, expanded, rest=()):
    rows, block = expanded.shape[0], 256
    steps = rows // block
    row = pl.BlockSpec((block, D), lambda s, p, i: (s, 0))
    return pl.pallas_call(
        finish_out_kernel if rest else send_out_kernel,
        grid_spec=pltpu.PrefetchScalarGridSpec(
            num_scalar_prefetch=2,
            grid=(steps,),
            in_specs=[
                pl.BlockSpec((block, HALF), lambda s, p, i: (p[0] * steps + s, 0)),
                pl.BlockSpec((HALF, D), lambda s, p, i: (i[0], 0)),
                row,
            ]
            + ([row, row, pl.BlockSpec((1, D), lambda s, p, i: (0, 0))] if rest else []),
            out_specs=row,
        ),
        out_shape=in_hbm((rows, D), BF),
        compiler_params=params(),
        cost_estimate=cost(2 * rows * D * HALF, 8 * rows * D + 2 * HALF * D),
        name="finish_out" if rest else "send_out",
    )(place, info, context, proj, expanded, *rest)


def proj_back_kernel(info_ref, ord_ref, g_ref, c_ref, w_ref, gc_ref, *refs):
    acc_ref = refs[-2] if len(refs) > 2 else refs[-1]
    gc_ref[...] = dot_nt(g_ref[...], w_ref[...]).astype(BF)
    part = dot_tn(c_ref[...], g_ref[...])

    @pl.when(pl.program_id(0) == 0)
    def _():
        acc_ref[...] = part

    @pl.when(pl.program_id(0) == 1)
    def _():
        total = (acc_ref[...] + part).astype(BF)
        if len(refs) == 2:
            refs[0][...] = total
        else:
            keep, send, all_ref = refs[0], refs[1], refs[3]
            all_ref[...] = total.reshape(all_ref.shape)
            half = keep.shape[0]
            for q in range(half):
                keep[q] = all_ref[ord_ref[q]]
                send[q] = all_ref[ord_ref[q + half]]


def proj_back_call(info, plan, order, grads, context, proj):
    rows, pieces = grads.shape[0] // 2, plan["pieces"]
    scratch = [pltpu.VMEM((HALF, D), F32)]
    if pieces:
        shape = (pieces // 2, HALF // pieces, D)
        out_specs = [pl.BlockSpec(shape, lambda h, *a: (0, 0, 0))] * 2
        out_shape = [in_hbm(shape, BF)] * 2
        scratch.append(pltpu.VMEM((pieces, HALF // pieces, D), BF))
    else:
        out_specs = [pl.BlockSpec((HALF, D), lambda h, *a: (0, 0))]
        out_shape = [in_hbm((HALF, D), BF)]
    return pl.pallas_call(
        proj_back_kernel,
        grid_spec=pltpu.PrefetchScalarGridSpec(
            num_scalar_prefetch=2,
            grid=(2,),
            in_specs=[
                pl.BlockSpec((rows, D), lambda h, i, o: (h, 0)),
                pl.BlockSpec((rows, HALF), lambda h, i, o: (jnp.bitwise_xor(h, i[0]), 0)),
                pl.BlockSpec((HALF, D), lambda h, i, o: (i[0], 0)),
            ],
            out_specs=[pl.BlockSpec((rows, HALF), lambda h, i, o: (jnp.bitwise_xor(h, i[0]), 0))] + out_specs,
            scratch_shapes=scratch,
        ),
        out_shape=[in_hbm((2 * rows, HALF), BF)] + out_shape,
        compiler_params=params(),
        cost_estimate=cost(8 * rows * D * HALF, 4 * rows * D + 8 * rows * HALF + 4 * HALF * D),
        name="proj_back",
    )(info, order, grads, context, proj)


def line_of(p, rows, sums, outer, inner_ref):
    low = lax.broadcasted_iota(jnp.int32, (1, LANES), 1) < rows
    at = p // 2 * LANES
    three = [v[:, at : at + LANES] for v in (sums[0:1], sums[1:2], outer)]
    turned = [pltpu.roll(v, rows, 1) for v in three]
    if p % 2:
        three, turned = turned, three
    at = p % 4 * HALF + p // 4 * LANES
    parts = [jnp.where(low, three[0], turned[1]), jnp.where(low, three[2], 0.0), inner_ref[:, at : at + LANES]]
    return jnp.concatenate(parts + [jnp.zeros((1, LANES), F32)], axis=1)


def pair_grad_kernel(info_ref, ord_ref, x_ref, own_ref, their_ref, *refs):
    d = jnp.concatenate([own_ref[0], their_ref[0]], axis=0)
    total = dot_tn(x_ref[...], d).astype(BF)
    if len(refs) == 1:
        refs[0][...] = total
        return
    pk_ref, ps_ref, keep, send, all_ref = refs
    half, rows = keep.shape[0], all_ref.shape[1]
    all_ref[...] = total.reshape(all_ref.shape)
    for q in range(half):
        for out, proj, at in ((keep, pk_ref, q), (send, ps_ref, q + half)):
            out[q, :rows] = all_ref[ord_ref[at]]
            out[q, rows:] = proj[q]


def value_grad_kernel(info_ref, ord_ref, x_ref, own_ref, their_ref, so_ref, st_ref, outer_ref, inner_ref, keep, send,
                      all_ref):
    pieces, rows = all_ref.shape[0], x_ref.shape[1] // all_ref.shape[0]
    half = pieces // 2
    d = jnp.concatenate([own_ref[0], their_ref[0]], axis=0)
    all_ref[:, :rows] = dot_tn(x_ref[...], d).astype(BF).reshape(pieces, rows, HALF)
    sums = so_ref[...] + st_ref[...]
    outer = outer_ref[...]
    for p in range(pieces):
        line = line_of(p, rows, sums, outer, inner_ref)
        all_ref[p, rows:] = jnp.broadcast_to(line, (all_ref.shape[1] - rows, HALF)).astype(BF)
    for q in range(half):
        keep[q] = all_ref[ord_ref[q]]
        send[q] = all_ref[ord_ref[q + half]]


def qkv_grad_call(info, plan, normed, dmix, first, count, extra=()):
    rows, pieces = normed.shape[0] // 2, plan["pieces"]
    in_specs, scratch, kernel = [], [], pair_grad_kernel
    if not pieces:
        extra = ()
        out_specs = [pl.BlockSpec((D, HALF), lambda t, *a: (0, t))]
        out_shape = [in_hbm((D, count * HALF), BF)]
    else:
        height = D // pieces
        if count == 2:
            shape = (pieces // 2, height + HALF // pieces, HALF)
            in_specs = [pl.BlockSpec((pieces // 2, HALF // pieces, HALF), lambda t, *a: (0, 0, t))] * 2
            scratch = [pltpu.VMEM((pieces, height, HALF), BF)]
        else:
            kernel = value_grad_kernel
            shape = (pieces // 2, height + 16, HALF)
            in_specs = [pl.BlockSpec(v.shape, lambda t, *a: (0, 0)) for v in extra]
            scratch = [pltpu.VMEM((pieces, height + 16, HALF), BF)]
        out_specs = [pl.BlockSpec(shape, lambda t, *a: (0, 0, t))] * 2
        out_shape = [in_hbm(shape[:2] + (count * HALF,), BF)] * 2
    return pl.pallas_call(
        kernel,
        grid_spec=pltpu.PrefetchScalarGridSpec(
            num_scalar_prefetch=2,
            grid=(count,),
            in_specs=[
                pl.BlockSpec((2 * rows, D), lambda t, *a: (0, 0)),
                pl.BlockSpec((1, rows, HALF), lambda t, i, *a: (first + t, i[0], 0)),
                pl.BlockSpec((1, rows, HALF), lambda t, i, *a: (first + t, 1 - i[0], 0)),
            ]
            + in_specs,
            out_specs=out_specs,
            scratch_shapes=scratch,
        ),
        out_shape=out_shape,
        compiler_params=params(),
        cost_estimate=cost(4 * rows * D * count * HALF, 4 * rows * D + (4 * rows + 2 * D) * count * HALF),
        name="qkv_grad",
    )(info, plan["order"], normed, dmix, dmix, *extra)


def grad_normed_kernel(place_ref, info_ref, d_ref, wq_ref, wk_ref, wv_ref, base_ref, t_ref, *refs):
    outs, sum_ref = refs[:-1], refs[-1]
    total = base_ref[...]
    for t, w in enumerate((wq_ref, wk_ref, wv_ref)):
        total += dot_nt(d_ref[t], w[...])
    if len(outs) == 1:
        outs[0][...] = total.astype(outs[0].dtype)
    else:
        for r, o_ref in enumerate(outs):

            @pl.when(pl.program_id(0) == r)
            def _(o_ref=o_ref):
                o_ref[...] = total.astype(o_ref.dtype)

    hat, _ = normalize(t_ref[...])
    sums = jnp.concatenate([jnp.sum(total * hat, axis=0, keepdims=True), jnp.sum(total, axis=0, keepdims=True)], axis=0)
    accumulate(sum_ref, sums)


def grad_normed_call(place, info, dmix, w, base, tokens, parts):
    rows, block = base.shape[0], 256
    steps = rows // block
    row = pl.BlockSpec((block, D), lambda r, p, i: (r, 0))
    kind = BF if parts else F32
    count = parts or 1
    return pl.pallas_call(
        grad_normed_kernel,
        grid_spec=pltpu.PrefetchScalarGridSpec(
            num_scalar_prefetch=2,
            grid=(steps,),
            in_specs=[pl.BlockSpec((3, block, HALF), lambda r, p, i: (0, p[0] * steps + r, 0))]
            + [pl.BlockSpec((D, HALF), lambda r, p, i, t=t: (0, 2 * t + i[0])) for t in range(3)]
            + [row, row],
            out_specs=([row] if count == 1 else [pl.BlockSpec((block, D), lambda r, p, i: (0, 0))] * count)
            + [pl.BlockSpec((2, D), lambda r, p, i: (0, 0))],
        ),
        out_shape=[in_hbm((rows // count, D), kind)] * count + [jax.ShapeDtypeStruct((2, D), F32)],
        compiler_params=params(),
        cost_estimate=cost(2 * rows * D * 3 * HALF, 8 * rows * D + 6 * D * HALF + 6 * rows * HALF),
        name="grad_normed",
    )(place, info, dmix, w, w, w, base, tokens)


def assemble_kernel(sources, width, info_ref, mine_ref, their_ref, o_ref):
    first = info_ref[0] == 0
    rows = o_ref.shape[0]
    for k, at in enumerate(sources):
        mine = mine_ref[:, at : at + width]
        theirs = their_ref[:rows, at : at + width].astype(F32)
        o_ref[:, 2 * k * width : (2 * k + 1) * width] = jnp.where(first, mine, theirs)
        o_ref[:, (2 * k + 1) * width : (2 * k + 2) * width] = jnp.where(first, theirs, mine)


def assemble_call(info, mine, theirs, sources, width):
    whole = lambda v: pl.BlockSpec(v.shape, lambda s, i: (0, 0))
    shape = (mine.shape[0], 2 * width * len(sources))
    return pl.pallas_call(
        functools.partial(assemble_kernel, sources, width),
        grid_spec=pltpu.PrefetchScalarGridSpec(
            num_scalar_prefetch=1,
            grid=(1,),
            in_specs=[whole(mine), whole(theirs)],
            out_specs=pl.BlockSpec(shape, lambda s, i: (0, 0)),
        ),
        out_shape=in_hbm(shape, F32),
        compiler_params=params(),
        cost_estimate=cost(1000, 1000),
        name="assemble",
    )(info, mine, theirs)


def finish_grad_kernel(gn_ref, r_ref, t_ref, g_ref, gain_ref, o_ref):
    hat, rstd = normalize(t_ref[...])
    u = (gn_ref[...] + r_ref[...].astype(F32)) * gain_ref[...].astype(F32)
    inner = u - jnp.mean(u, axis=1, keepdims=True) - hat * jnp.mean(u * hat, axis=1, keepdims=True)
    o_ref[...] = g_ref[...].astype(F32) + inner * rstd


def finish_grad_call(grad_normed, received, tokens, grads, gain):
    rows, block = tokens.shape[0], 256
    row = pl.BlockSpec((block, D), lambda r: (r, 0))
    return pl.pallas_call(
        finish_grad_kernel,
        grid=(rows // block,),
        in_specs=[row, row, row, row, pl.BlockSpec((1, D), lambda r: (0, 0))],
        out_specs=row,
        out_shape=in_hbm((rows, D), F32),
        compiler_params=params(),
        cost_estimate=cost(20 * rows * D, 14 * rows * D),
        name="finish_grad",
    )(grad_normed, received, tokens, grads, gain)


class Reduction:
    def __init__(self, keep, send, stages, n_dp):
        self.keep, self.sends, self.stages, self.n_dp = keep, [send], list(stages), n_dp
        self.start()

    def start(self):
        offsets = self.stages.pop(0)
        self.flying = [
            lax.ppermute(part, "dp", [(i, i ^ offset) for i in range(self.n_dp)])
            for part, offset in zip(self.sends, offsets, strict=True)
        ]

    def land(self, *first):
        if first:
            self.keep = after(self.keep, *first)
        kind = self.flying[0].dtype
        pieces = self.keep.shape[0]
        count = pieces // (len(self.stages[0]) + 1) if self.stages else pieces
        parts = []
        for i in range(0, pieces, count):
            total = self.keep[i : i + count].astype(F32)
            for part in self.flying:
                total = total + part[i : i + count].astype(F32)
            parts.append(total)
        if not self.stages:
            self.keep, self.sends = parts[0][0], []
            return (self.keep,)
        parts = [part.astype(kind) for part in parts]
        self.keep, self.sends = parts[0], parts[1:]
        self.start()
        return tuple(parts)

    def finish(self, *first):
        self.land(*first)
        while self.sends:
            self.land()
        return self.keep


def after(x, *done):
    return lax.optimization_barrier((x, *done))[0]


def send_order(stages, me):
    table = [0]
    for offsets in stages:
        table = [r ^ offset for r in table for offset in (0, *offsets)]
    return jnp.bitwise_xor(jnp.array(table, jnp.int32), me)


def pairs_of_bits(bits):
    stages = []
    for i in range(0, len(bits), 2):
        if i + 1 < len(bits):
            stages.append((bits[i], bits[i + 1], bits[i] ^ bits[i + 1]))
        else:
            stages.append((bits[i],))
    return stages


def on_device(n_dp, tokens, lengths, norm_gain, norm_shift, qkv_weight, proj_weight, up_weight, inner_bias,
              down_weight, outer_bias, cotangent):
    j = lax.axis_index("branch").astype(jnp.int32)
    me = lax.axis_index("dp").astype(jnp.int32)
    other = [(0, 1), (1, 0)]
    tokens_their = lax.ppermute(tokens, "branch", other)
    cotangent_their = lax.ppermute(cotangent, "branch", other)
    own, their = j.reshape(1), (1 - j).reshape(1)
    info = jnp.stack([j, lengths[0].astype(jnp.int32)])
    gain, shift = norm_gain.reshape(1, D), norm_shift.reshape(1, D)

    bits = [1 << i for i in range(n_dp.bit_length() - 1)]
    high_stages = pairs_of_bits(bits[2:])
    low_first = [(1,), (2,)] + high_stages
    halvings = [(bit,) for bit in bits]
    order = send_order(low_first, me)
    ffb = FF_HALF // n_dp
    fast = ffb == LANES
    if fast:
        splits = FB // LANES
        plan = {
            "splits": splits,
            "pieces": n_dp,
            "pick": lambda s, a, i: 2 * (4 * i + a[1][s]) + a[0][0],
            "classes": jnp.array([1, 3, 0, 2], jnp.int32) ^ (me & 3),
            "subs": jnp.arange(4, dtype=jnp.int32) ^ (me >> 2),
            "weights": (up_weight, down_weight, inner_bias.reshape(1, FF)),
        }
    else:
        plan = {
            "splits": 1,
            "pieces": 0,
            "pick": lambda s, a, i: s,
            "classes": jnp.arange(FF_HALF // FB, dtype=jnp.int32),
            "subs": jnp.zeros((1,), jnp.int32),
            "weights": (
                lax.dynamic_index_in_dim(up_weight.reshape(D, n_dp, 2, ffb), j, 2, False).reshape(D, FF_HALF),
                lax.dynamic_index_in_dim(down_weight.reshape(n_dp, 2, ffb, D), j, 1, False).reshape(FF_HALF, D),
                lax.dynamic_index_in_dim(inner_bias.reshape(n_dp, 2, ffb), j, 1, False).reshape(1, FF_HALF),
            ),
        }
    plan["order"], plan["halved"] = order, send_order(halvings, me)

    def pieces_of(grads, table):
        if len(grads) == 2:
            return grads
        whole = grads[0]
        ordered = jnp.take(whole.reshape(n_dp, whole.shape[0] // n_dp, whole.shape[1]), table, axis=0)
        return ordered[: n_dp // 2], ordered[n_dp // 2 :]

    plan["weights"] = tuple(pltpu.with_memory_space_constraint(w, pltpu.HBM) for w in plan["weights"][:2]) + plan["weights"][2:]
    qkv_weight = pltpu.with_memory_space_constraint(qkv_weight, pltpu.HBM)
    proj_weight = pltpu.with_memory_space_constraint(proj_weight, pltpu.HBM)

    cosine, sine = rotary_tables()
    normed, hidden, grads_own, gb_own, expanded_own, gn_own, outer = mlp_own_call(
        info, plan, tokens, cotangent, gain, shift
    )
    qkv = qkv_half_call(own, info, 0, normed, qkv_weight, cosine, sine)
    info = after(info, qkv)
    normed, hidden, slope, expanded_their = mlp_forward_call(info, plan, tokens_their, gain, shift, normed, hidden)
    info = after(info, slope)
    grads, *down = down_grad_call(info, plan, stay(hidden), grads_own, cotangent_their)
    down = Reduction(*pieces_of(down, order), low_first, n_dp)
    info = after(info, grads)
    gn_their, inner, *up = mlp_back_call(info, plan, normed, stay(slope), grads, stay(gb_own))

    up = Reduction(*pieces_of(up, plan["halved"]), halvings, n_dp)
    info = after(info, *down.land(gn_their), *up.land(gn_their))
    qkv = qkv_half_call(their, info, 1, normed, qkv_weight, cosine, sine, qkv)
    context, qe = attend_call(info, stay(qkv))
    out_their = out_call(their, info, stay(context), proj_weight, expanded_their)

    info = after(info, *down.land(out_their))
    out_received = lax.ppermute(out_their, "branch", other)
    grad_context, *proj = proj_back_call(info, plan, order, grads, context, proj_weight)
    info = after(info, *up.land(grad_context))
    dmix = attend_back_call(info, qe, qkv, stay(context), stay(grad_context), cosine, sine)

    down_grad = down.finish(dmix)
    info = after(info, out_received, down_grad, *up.land(dmix))
    small = D // n_dp
    shard = small // 2
    first = qkv_grad_call(info, plan, normed, dmix, 0, 2, proj)
    if not fast:
        first = jnp.concatenate([first[0].reshape(n_dp, small, D), proj[0].reshape(n_dp, shard, D)], axis=1)
        first = jnp.take(first, order, axis=0)
        first = first[: n_dp // 2], first[n_dp // 2 :]
    info = after(info, *first)
    first = Reduction(*first, low_first, n_dp)
    *gn_send, sums_their = grad_normed_call(their, info, dmix, qkv_weight, gn_their, tokens_their, 1)

    info = after(info, *first.land(*gn_send))
    gn_first = lax.ppermute(gn_send[0], "branch", other)
    gn_own, sums_own = grad_normed_call(own, info, dmix, qkv_weight, gn_own, tokens, 0)
    info = after(info, gn_own)
    layer_out = out_call(
        own, info, context, proj_weight, expanded_own, (tokens, out_received, outer_bias.reshape(1, D))
    )
    info = after(info, layer_out)
    if fast:
        value = qkv_grad_call(info, plan, normed, dmix, 2, 1, (sums_own, sums_their, outer, inner))
    else:
        sums = sums_own + sums_their
        lines = jnp.concatenate([v.reshape(n_dp, small) for v in (sums[0], sums[1], outer)], axis=1)
        lines = jnp.concatenate(
            [jnp.pad(lines, ((0, 0), (0, 2 * LANES - 3 * small))), inner.reshape(n_dp, ffb)], axis=1
        )
        lines = jnp.pad(lines, ((0, 0), (0, HALF - lines.shape[1]))).astype(BF)
        lines = jnp.broadcast_to(lines[:, None], (n_dp, 16, HALF))
        value = qkv_grad_call(info, plan, normed, dmix, 2, 1)[0].reshape(n_dp, small, HALF)
        value = jnp.take(jnp.concatenate([value, lines], axis=1), order, axis=0)
        value = value[: n_dp // 2], value[n_dp // 2 :]
    up.finish(*value)
    landed = first.land(*value)
    value, up.keep, _ = lax.optimization_barrier((tuple(value), up.keep, landed))
    value = Reduction(*value, low_first, n_dp)
    up_mine = lax.dynamic_slice_in_dim(up.keep, j * shard, shard, 0)
    up_their = lax.dynamic_slice_in_dim(up.keep, (1 - j) * shard, shard, 0).astype(BF)
    up_their = lax.ppermute(up_their, "branch", other)
    value.keep, gn_first = lax.optimization_barrier((value.keep, gn_first))
    landed = value.land()
    tokens_grad = finish_grad_call(gn_own, after(gn_first, *landed), tokens, grads_own, gain)
    up_mine, up_their, tokens_grad = lax.optimization_barrier((up_mine, up_their, tokens_grad))
    if fast:
        sources = tuple(p % 4 * HALF + p // 4 * LANES for p in range(n_dp))
        up_grad = assemble_call(info, up_mine, up_their, sources, LANES)
    else:
        up_their = up_their.astype(F32)
        low, high = jnp.where(j == 0, up_mine, up_their), jnp.where(j == 0, up_their, up_mine)
        up_grad = jnp.stack([low.reshape(shard, n_dp, ffb), high.reshape(shard, n_dp, ffb)], axis=2).reshape(shard, FF)
    first = first.finish(up_grad)
    value.land(first)
    value = value.finish()
    query_key, proj_piece = first[:small], first[small:]
    piece = jnp.concatenate([query_key, value[:small]], axis=1)
    line = value[small:]
    theirs = lax.dynamic_slice_in_dim(piece, (1 - j) * shard, shard, 0)
    theirs = jnp.concatenate([theirs, jnp.concatenate([line, line, line], axis=1)], axis=0).astype(BF)
    route = [(2 * p + h, n_dp * h + p) for h in range(2) for p in range(n_dp)]
    proj_grad = lax.ppermute(after(proj_piece.astype(BF), theirs), ("dp", "branch"), route).astype(F32)
    theirs = lax.ppermute(theirs, "branch", other)
    mine = lax.dynamic_slice_in_dim(piece, j * shard, shard, 0)
    qkv_grad = assemble_call(info, mine, theirs, (0, HALF, 2 * HALF), HALF) if fast else None
    triple = (line[0] + theirs[shard, :HALF].astype(F32))[: 3 * small].reshape(3, 2, shard)
    triple = lax.dynamic_index_in_dim(triple, j, 1, False)
    if not fast:
        mine = mine.reshape(shard, 3, HALF)
        theirs = theirs[:shard].astype(F32).reshape(shard, 3, HALF)
        qkv_grad = jnp.stack([jnp.where(j == 0, mine, theirs), jnp.where(j == 0, theirs, mine)], axis=2)
        qkv_grad = qkv_grad.reshape(shard, 3 * D)
    return (
        layer_out,
        tokens_grad,
        triple[0],
        triple[1],
        qkv_grad,
        proj_grad,
        up_grad,
        line[0, 2 * LANES : 2 * LANES + ffb],
        down_grad,
        triple[2],
    )


def solution(mesh):
    rows = P(("dp", "branch"), None)
    flat = P(("dp", "branch"))
    return jax.shard_map(
        functools.partial(on_device, mesh.shape["dp"]),
        mesh=mesh,
        in_specs=(rows, P("dp"), P(), P(), P(), P(), P(), P(), P(), P(), rows),
        out_specs=(rows, rows, flat, flat, rows, rows, rows, flat, rows, flat),
        check_vma=False,
    )
```
